32 devices in a mesh: dp: 4 (over x, core), expert: 8 (over z, y).
Axes of the slice: x: 2, y: 2, z: 4, core: 2. Of those that a mesh axis runs over, the one named last changes fastest.
Arguments:
- patches: bfloat16 [3, 16384, 384], P(None, ('dp', 'expert')), may hold values from -6 to 6
- out_grad: bfloat16 [3, 16384, 384], P(None, ('dp', 'expert')), may hold values from -6 to 6
- item_ids: int32 [3, 32, 512], P(None, ('dp', 'expert')), may hold values from 0 to 7, never falling along the last dimension, each value on 1 to 128 neighbouring positions
- expert_ids: int32 [3, 16384, 2], P(None, ('dp', 'expert')), may hold values from 0 to 7, all different within a row; in each aligned block of 512 rows (0 to 511, 512 to 1023, ..., all dimensions but the last counted through in order) at most 256 rows name the same one
- qkv_master: float32 [384, 1152], replicated, may hold values from -0.3125 to 0.3125
- qkv_first: float32 [384, 1152], replicated
- qkv_second: float32 [384, 1152], replicated, as said below
- proj_master: float32 [384, 384], replicated, may hold values from -1.25 to 1.25
- proj_first: float32 [384, 384], replicated
- proj_second: float32 [384, 384], replicated, as said below
- router_master: float32 [384, 8], replicated, may hold values from -0.21875 to 0.21875
- router_first: float32 [384, 8], replicated
- router_second: float32 [384, 8], replicated, as said below
- gains_master: float32 [2, 384], replicated, may hold values from 0.5 to 1.5
- gains_first: float32 [2, 384], replicated
- gains_second: float32 [2, 384], replicated, as said below
- inner_master: float32 [8, 384, 1536], P('expert', 'dp'), may hold values from -0.3125 to 0.3125
- inner_first: float32 [8, 384, 1536], P('expert', 'dp')
- inner_second: float32 [8, 384, 1536], P('expert', 'dp'), as said below
- down_master: float32 [8, 768, 384], P('expert', 'dp'), may hold values from -0.4375 to 0.4375
- down_first: float32 [8, 768, 384], P('expert', 'dp')
- down_second: float32 [8, 768, 384], P('expert', 'dp'), as said below
Outputs:
- block_out: bfloat16 [3, 16384, 384], P(None, ('dp', 'expert'))
- patch_grad: float32 [3, 16384, 384], P(None, ('dp', 'expert'))
- qkv_updated: float32 [384, 1152], replicated
- qkv_first_new: float32 [384, 1152], replicated
- qkv_second_new: float32 [384, 1152], replicated
- proj_updated: float32 [384, 384], replicated
- proj_first_new: float32 [384, 384], replicated
- proj_second_new: float32 [384, 384], replicated
- router_updated: float32 [384, 8], replicated
- router_first_new: float32 [384, 8], replicated
- router_second_new: float32 [384, 8], replicated
- gains_updated: float32 [2, 384], replicated
- gains_first_new: float32 [2, 384], replicated
- gains_second_new: float32 [2, 384], replicated
- inner_updated: float32 [8, 384, 1536], P('expert', 'dp')
- inner_first_new: float32 [8, 384, 1536], P('expert', 'dp')
- inner_second_new: float32 [8, 384, 1536], P('expert', 'dp')
- down_updated: float32 [8, 768, 384], P('expert', 'dp')
- down_first_new: float32 [8, 768, 384], P('expert', 'dp')
- down_second_new: float32 [8, 768, 384], P('expert', 'dp')
The draws below stay inside these ranges and needn't reach their ends.
Inputs may be any that keep to these rules, and one draw needn't show every extreme that they name: `expert_ids`: each row names 2 different experts. In each aligned block of 512 rows of a micro-batch (the rows of one device) no expert is named by more than 256 rows, and some expert reaches 256. `item_ids`: within each pack of 512 tokens the item numbers never fall; an item holds 1 to 128 tokens, and some item holds exactly 128. `qkv_second`: all entries positive. `proj_second`: all entries positive. `router_second`: all entries positive. `gains_second`: all entries positive. `inner_second`: all entries positive. `down_second`: all entries positive.
All inputs are finite; a program needn't handle non-finite values.
Results may differ from the reference program's by a relative error of at most 0.013.
The reference program's roundings to bfloat16 on the way count: a program that leaves them out, or rounds other values in their place, can miss the bound.
Values may be sent and summed in bfloat16 or wider, within the bound.
A program may use at most 128 MiB of HBM per device.

```python
import math
import jax
import jax.numpy as jnp
import numpy as np
from jax import lax

D = 384
HEADS = 6
HEAD = 64
FF = 768
TOP = 2
ITEMS = 8
TOK_DEV = 512
MICRO = 3
EXPERTS = 8
CAP = 256
ITEM_MAX = 128
TOKENS = 16384
N_DP = 4
N_EXPERT = 8
DEVICES = 32


def token_root():
    return math.sqrt(MICRO * TOKENS)


def expert_root():
    return math.sqrt(MICRO * TOKENS * TOP / EXPERTS)


def first_moment(key, shape, level, tag):
    sub = jax.random.fold_in(key, tag)
    return level * jax.random.truncated_normal(sub, -3.0, 3.0, shape, jnp.float32)


def second_moment(key, shape, level, tag):
    sub = jax.random.fold_in(key, tag)
    factor = jnp.exp(jax.random.uniform(sub, shape, jnp.float32) * math.log(4.0))
    return level * level * factor


def draw_qkv_first(key, part):
    return first_moment(key, (D, 3 * D), 0.8 * token_root(), 11)


def draw_qkv_second(key, part):
    return second_moment(key, (D, 3 * D), 0.8 * token_root(), 12)


def draw_proj_first(key, part):
    return first_moment(key, (D, D), 0.4 * token_root(), 21)


def draw_proj_second(key, part):
    return second_moment(key, (D, D), 0.4 * token_root(), 22)


def draw_router_first(key, part):
    return first_moment(key, (D, EXPERTS), 8.0 * expert_root(), 31)


def draw_router_second(key, part):
    return second_moment(key, (D, EXPERTS), 8.0 * expert_root(), 32)


def draw_gains_first(key, part):
    return first_moment(key, (2, D), 1.4 * token_root(), 41)


def draw_gains_second(key, part):
    return second_moment(key, (2, D), 1.4 * token_root(), 42)


def draw_inner_first(key, part):
    return first_moment(key, (EXPERTS, D, 2 * FF), 0.45 * expert_root(), 51)


def draw_inner_second(key, part):
    return second_moment(key, (EXPERTS, D, 2 * FF), 0.45 * expert_root(), 52)


def draw_down_first(key, part):
    return first_moment(key, (EXPERTS, FF, D), 0.3 * expert_root(), 61)


def draw_down_second(key, part):
    return second_moment(key, (EXPERTS, FF, D), 0.3 * expert_root(), 62)


def block_levels(rng, dims, pieces, smallest, high):
    level = 1.0
    for position, shards_of in pieces:
        draws = jax.random.uniform(jax.random.fold_in(jax.random.fold_in(rng, 6), position), (shards_of,), jnp.float32, smallest / len(pieces), high / len(pieces))
        level = level * jnp.repeat(jnp.exp(draws), dims[position] // shards_of).reshape((-1,) + (1,) * (len(dims) - 1 - position))
    return level


def split_up(count, total, limit, skew):
    portions = [(1 << 20) // math.isqrt(standing ** skew) + 1 for standing in range(2, count + 1)]
    spare, counts = total - limit - (count - 1), [1] * (count - 1)
    while spare > 0:
        movable = [i for i in range(count - 1) if counts[i] < limit]
        pool, budget = sum([portions[i] for i in movable]), spare
        for i in movable:
            more = min(limit - counts[i], max(1, budget * portions[i] // pool), spare)
            counts[i] = counts[i] + more
            spare = spare - more
    return np.array([limit] + counts)


def uneven(rng, count, total, bound, slope):
    if count == 2:
        one = jax.random.randint(rng, (), max(1, total - bound), min(bound, total - 1) + 1)
        return jnp.stack([one, total - one])
    lengths = jnp.asarray(split_up(count, total, bound, slope), jnp.int32)
    pairs = (count - 1) // 2
    giver, taker = lengths[1:1 + 2 * pairs:2], lengths[2:2 + 2 * pairs:2]
    room = jnp.minimum(giver - 1, bound - taker)
    passed = jax.random.randint(jax.random.fold_in(rng, 1), (pairs,), 0, 1 << 20) % (room + 1)
    lengths = lengths.at[1:1 + 2 * pairs:2].set(giver - passed).at[2:2 + 2 * pairs:2].set(taker + passed)
    return lengths[jax.random.permutation(jax.random.fold_in(rng, 2), count)]


def deal_out(key, own, number, rows, count, top, most, skew):
    order = jax.random.permutation(key, count)
    crowded, common = portions_of(count, rows * top, most, skew, True), portions_of(count, rows * top, most, skew, False)
    places = jnp.arange(count)

    def named(sizes, rotation):
        used = int((sizes > 0).sum())
        fixed = max(1, used // 4)
        shifted = fixed + (places - fixed + rotation * (used - fixed)) % max(1, count - fixed)
        return jnp.zeros((count,), jnp.int32).at[order[jnp.where(places < fixed, places, shifted)]].set(jnp.asarray(sizes, jnp.int32))

    sizes = jnp.where(number % 4 == 0, named(crowded, number // 4), named(common, number - number // 4 - 1))
    mixed = jax.random.permutation(jax.random.fold_in(own, 3), count)
    source_of, taker = mixed[0:count // 2 * 2:2], mixed[1:count // 2 * 2:2]
    room = jnp.minimum(sizes[source_of] - 1, most - sizes[taker]) // 2
    room = jnp.where((source_of == order[0]) | (taker == order[0]) | (sizes[taker] == 0), 0, jnp.maximum(room, 0))
    shifted = jax.random.randint(jax.random.fold_in(own, 4), (count // 2,), 0, 1 << 20) % (room + 1)
    sizes = sizes.at[source_of].add(-shifted).at[taker].add(shifted)
    labels = jnp.searchsorted(jnp.cumsum(sizes), jnp.arange(rows * top), side="right").astype(jnp.int32)
    grid = labels.reshape(top, rows).T
    grid = grid[jax.random.permutation(jax.random.fold_in(own, 1), rows)]
    rotation = jax.random.randint(jax.random.fold_in(own, 2), (rows, 1), 0, top)
    return jnp.take_along_axis(grid, (jnp.arange(top)[None, :] + rotation) % top, axis=1)


def portions_of(amount, total, limit, skew, full):
    portions = [(1 << 20) // math.isqrt(grade ** skew) + 1 for grade in range(1, amount + 1)]
    largest = limit if full else min(limit, max(-(-total // amount), total * portions[0] // sum(portions)))
    least = 1 if total - largest >= amount - 1 else 0
    holding, spare = [largest] + [least] * (amount - 1), total - largest - least * (amount - 1)
    while spare > 0:
        candidates = [i for i in range(1, amount) if holding[i] < largest] or [i for i in range(1, amount) if holding[i] < limit]
        pool, left = sum([portions[i] for i in candidates]), spare
        for i in candidates:
            more = min(limit - holding[i], max(1, left * portions[i] // pool), spare)
            holding[i] = holding[i] + more
            spare = spare - more
    return np.array(holding)


def centred(stream_key, shape, scale, reach, pieces=(), kind=jnp.bfloat16):
    entries = jax.random.normal(stream_key, shape, jnp.float32) * scale
    if len(pieces) > 0:
        entries = block_levels(stream_key, shape, pieces, -0.22, 0.18) * entries
    return jnp.clip(entries, min=-reach, max=reach).astype(kind)


def setup_inputs(seed: int = 0) -> dict:
    seeds = jax.random.split(jax.random.key(seed), 23)
    patches = centred(seeds[0], (MICRO, TOKENS, D), 1.0, 6.0, ((1, 32),))
    out_grad = centred(seeds[1], (MICRO, TOKENS, D), 1.0, 6.0, ((1, 32),))
    item_ids = jax.vmap(lambda own: jnp.searchsorted(jnp.cumsum(uneven(own, ITEMS, TOK_DEV, ITEM_MAX, 1)), jnp.arange(TOK_DEV), side="right"))(jax.random.split(seeds[2], MICRO * DEVICES)).reshape((MICRO, DEVICES, TOK_DEV)).astype(jnp.int32)
    expert_ids_keys = jax.random.split(jax.random.fold_in(seeds[3], 1), MICRO * TOKENS // TOK_DEV)
    expert_ids_turns = jax.random.permutation(jax.random.fold_in(seeds[3], 3), MICRO * TOKENS // TOK_DEV)
    expert_ids = jax.vmap(lambda own, number: deal_out(jax.random.fold_in(seeds[3], 2), own, number, TOK_DEV, EXPERTS, TOP, CAP, 1))(expert_ids_keys, expert_ids_turns).reshape((MICRO, TOKENS, TOP))
    qkv_master = centred(seeds[4], (D, 3 * D), D ** -0.5, 0.3125, (), jnp.float32)
    qkv_first = draw_qkv_first(jax.random.fold_in(seeds[22], 71), 0)
    qkv_second = draw_qkv_second(jax.random.fold_in(seeds[22], 71), 0)
    proj_master = centred(seeds[7], (D, D), (D // 16) ** -0.5, 1.25, (), jnp.float32)
    proj_first = draw_proj_first(jax.random.fold_in(seeds[22], 71), 0)
    proj_second = draw_proj_second(jax.random.fold_in(seeds[22], 71), 0)
    router_master = centred(seeds[10], (D, EXPERTS), (2 * D) ** -0.5, 0.21875, (), jnp.float32)
    router_first = draw_router_first(jax.random.fold_in(seeds[22], 71), 0)
    router_second = draw_router_second(jax.random.fold_in(seeds[22], 71), 0)
    gains_master = jnp.clip(1.0 + 0.1 * jax.random.normal(seeds[13], (2, D), jnp.float32), 0.5, 1.5)
    gains_first = draw_gains_first(jax.random.fold_in(seeds[22], 71), 0)
    gains_second = draw_gains_second(jax.random.fold_in(seeds[22], 71), 0)
    inner_master = centred(seeds[16], (EXPERTS, D, 2 * FF), D ** -0.5, 0.3125, ((0, 8), (1, 4)), jnp.float32)
    inner_first = draw_inner_first(jax.random.fold_in(seeds[22], 71), 0)
    inner_second = draw_inner_second(jax.random.fold_in(seeds[22], 71), 0)
    down_master = centred(seeds[19], (EXPERTS, FF, D), (FF // 4) ** -0.5, 0.4375, ((0, 8), (1, 4)), jnp.float32)
    down_first = draw_down_first(jax.random.fold_in(seeds[22], 71), 0)
    down_second = draw_down_second(jax.random.fold_in(seeds[22], 71), 0)
    return dict(patches=patches, out_grad=out_grad, item_ids=item_ids, expert_ids=expert_ids, qkv_master=qkv_master, qkv_first=qkv_first, qkv_second=qkv_second, proj_master=proj_master, proj_first=proj_first, proj_second=proj_second, router_master=router_master, router_first=router_first, router_second=router_second, gains_master=gains_master, gains_first=gains_first, gains_second=gains_second, inner_master=inner_master, inner_first=inner_first, inner_second=inner_second, down_master=down_master, down_first=down_first, down_second=down_second)


@jax.custom_vjp
def low(v):
    return lax.optimization_barrier(v.astype(jnp.bfloat16)).astype(jnp.float32)

@jax.custom_vjp
def low_back(v):
    return v

def low_keep(v):
    return (low(v), None)

def low_pass(kept, grad):
    return (grad,)

def back_keep(v):
    return (v, None)

def back_low(kept, grad):
    return (low(grad),)
low.defvjp(low_keep, low_pass)
low_back.defvjp(back_keep, back_low)
norm_eps = 1e-06
adam_eps = 1e-08
correction = 0.875
high = lax.Precision.HIGHEST

def unit_rows(values):
    return values * lax.rsqrt(lax.optimization_barrier(jnp.mean(values * values, axis=-1, keepdims=True)) + norm_eps)

def rotary_tables(item_row):
    length = item_row.shape[0]
    places = jnp.arange(length, dtype=jnp.int32)
    starts = jnp.concatenate([jnp.ones((1,), dtype=bool), item_row[1:] != item_row[:-1]])
    first = lax.cummax(jnp.where(starts, places, 0), axis=0)
    offset = (places - first).astype(jnp.float32)
    half = HEAD // 2
    freqs = 10000.0 ** (-jnp.arange(half, dtype=jnp.float32) / half)
    angles = offset[:, None] * freqs[None, :]
    return (jnp.cos(angles), jnp.sin(angles))

def rotate(vectors, cosine, sine):
    half = vectors.shape[-1] // 2
    first_half = vectors[..., :half]
    second_half = vectors[..., half:]
    cos_part = cosine[:, None, :]
    sin_part = sine[:, None, :]
    return jnp.concatenate([first_half * cos_part - second_half * sin_part, second_half * cos_part + first_half * sin_part], axis=-1)

def attend_pack(normed, item_row, qkv_low):
    length = normed.shape[0]
    cosine, sine = rotary_tables(item_row)
    mixed = low_back(jnp.dot(normed, qkv_low, precision=high))
    query = low(rotate(mixed[:, :D].reshape(length, HEADS, HEAD), cosine, sine))
    keys = low(rotate(mixed[:, D:2 * D].reshape(length, HEADS, HEAD), cosine, sine))
    values = low(mixed[:, 2 * D:].reshape(length, HEADS, HEAD))
    scores = low_back(jnp.einsum('qhe,khe->hqk', query, keys, precision=high) * 0.125)
    same_item = item_row[:, None] == item_row[None, :]
    scores = jnp.where(same_item[None], scores, -1e+30)
    peak = lax.optimization_barrier(jnp.max(scores, axis=-1, keepdims=True))
    weights = jnp.exp(scores - peak)
    probs = low(weights / lax.optimization_barrier(jnp.sum(weights, axis=-1, keepdims=True)))
    attended = jnp.einsum('hqk,khe->qhe', probs, values, precision=high).reshape(length, D)
    return low_back(low(attended))

def expert_apply(operands):
    group, inner, down = operands
    both = low_back(jnp.dot(group, inner, precision=high))
    hidden = low(jax.nn.silu(both[:, :FF]) * both[:, FF:])
    return low_back(low(jnp.dot(hidden, down, precision=high)))

def adamw(weight, first, second, grad, rate, decay):
    first_new = 0.5 * first + 0.5 * grad
    second_new = 0.5 * second + 0.5 * grad * grad
    update = first_new / correction / (jnp.sqrt(second_new / correction) + adam_eps)
    return (weight - rate * (update + decay * weight), first_new, second_new)

def reference(patches, out_grad, item_ids, expert_ids, qkv_master, qkv_first, qkv_second, proj_master, proj_first, proj_second, router_master, router_first, router_second, gains_master, gains_first, gains_second, inner_master, inner_first, inner_second, down_master, down_first, down_second):
    packs = MICRO * N_DP * N_EXPERT
    length = TOK_DEV
    rows = patches.reshape(packs * length, D).astype(jnp.float32)
    item_rows = item_ids.reshape(packs, length)
    choose = expert_ids.reshape(packs * length, TOP)
    ids_block = choose.reshape(packs, length * TOP)
    hits = (ids_block[:, :, None] == jnp.arange(EXPERTS, dtype=jnp.int32)[None, None, :]).astype(jnp.int32)
    rank = lax.optimization_barrier(jnp.sum(jnp.cumsum(hits, axis=1) * hits, axis=2)) - 1
    slot_rows = packs * CAP
    pack_index = jnp.arange(packs, dtype=jnp.int32)[:, None]
    flat_slots = (ids_block * slot_rows + pack_index * CAP + rank).reshape(-1).astype(jnp.int32)

    def forward(source, qkv_w, proj_w, router_w, gains_w, inner_w, down_w):
        normed_in = low(unit_rows(source) * gains_w[0])
        qkv_low = low(qkv_w)

        def attend_one(pair):
            return attend_pack(pair[0], pair[1], qkv_low)
        attended = lax.map(jax.checkpoint(attend_one), (normed_in.reshape(packs, length, D), item_rows))
        branch = low_back(jnp.dot(attended.reshape(-1, D), low(proj_w), precision=high))
        middle = source + branch
        normed_mid = low(unit_rows(middle) * gains_w[1])
        logits = low_back(jnp.dot(normed_mid, low(router_w), precision=high))
        chosen = jnp.take_along_axis(logits, choose, axis=1)
        gates = jax.nn.softmax(chosen, axis=1)
        copies = jnp.stack([low_back(normed_mid) for turn in range(TOP)], axis=1).reshape(-1, D)
        buffers = jnp.zeros((EXPERTS * slot_rows, D), jnp.float32).at[flat_slots].set(copies)
        buffers = buffers.reshape(EXPERTS, slot_rows, D)
        results = lax.map(jax.checkpoint(expert_apply), (buffers, low(inner_w), low(down_w)))
        picked = results.reshape(EXPERTS * slot_rows, D)[flat_slots].reshape(-1, TOP, D)
        combined = lax.optimization_barrier(jnp.sum(gates[:, :, None] * picked, axis=1))
        return middle + combined
    out_value, pull = jax.vjp(forward, rows, qkv_master, proj_master, router_master, gains_master, inner_master, down_master)
    grads = pull(out_grad.reshape(-1, D).astype(jnp.float32))
    qkv_new = adamw(qkv_master, qkv_first, qkv_second, grads[1], 0.1, 0.1)
    proj_new = adamw(proj_master, proj_first, proj_second, grads[2], 0.4, 0.1)
    router_new = adamw(router_master, router_first, router_second, grads[3], 0.07, 0.1)
    gains_new = adamw(gains_master, gains_first, gains_second, grads[4], 0.4, 0.0)
    inner_new = adamw(inner_master, inner_first, inner_second, grads[5], 0.1, 0.1)
    down_new = adamw(down_master, down_first, down_second, grads[6], 0.15, 0.1)
    block_out = out_value.astype(jnp.bfloat16).reshape(MICRO, TOKENS, D)
    patch_grad = grads[0].reshape(MICRO, TOKENS, D)
    return (block_out, patch_grad, qkv_new[0], qkv_new[1], qkv_new[2], proj_new[0], proj_new[1], proj_new[2], router_new[0], router_new[1], router_new[2], gains_new[0], gains_new[1], gains_new[2], inner_new[0], inner_new[1], inner_new[2], down_new[0], down_new[1], down_new[2])
```

```python
import jax
import jax.numpy as jnp
import numpy as np
from jax import lax
from jax.experimental import pallas as pl
from jax.experimental.pallas import tpu as pltpu
from jax.sharding import PartitionSpec as P

HEADS = 6
HEAD = 64


norm_eps = 1e-06
adam_eps = 1e-08
correction = 0.875


def rotary_tables(item_row):
    length = item_row.shape[0]
    places = jnp.arange(length, dtype=jnp.int32)
    starts = jnp.concatenate([jnp.ones((1,), dtype=bool), item_row[1:] != item_row[:-1]])
    first = lax.cummax(jnp.where(starts, places, 0), axis=0)
    offset = (places - first).astype(jnp.float32)
    half = HEAD // 2
    freqs = 10000.0 ** (-jnp.arange(half, dtype=jnp.float32) / half)
    angles = offset[:, None] * freqs[None, :]
    return (jnp.cos(angles), jnp.sin(angles))


def rotate(vectors, cosine, sine):
    half = vectors.shape[-1] // 2
    first_half = vectors[..., :half]
    second_half = vectors[..., half:]
    cos_part = cosine[:, None, :]
    sin_part = sine[:, None, :]
    return jnp.concatenate(
        [
            first_half * cos_part - second_half * sin_part,
            second_half * cos_part + first_half * sin_part,
        ],
        axis=-1,
    )


def masked_scores(query, keys, same_item):
    scores = jnp.einsum("qhe,khe->hqk", query, keys, preferred_element_type=jnp.float32) * 0.125
    return jnp.where(same_item[None], scores, -1e30)


def adamw(weight, first, second, grad, rate, decay):
    first_new = 0.5 * first + 0.5 * grad
    second_new = 0.5 * second + 0.5 * grad * grad
    update = first_new / correction / (jnp.sqrt(second_new / correction) + adam_eps)
    return (weight - rate * (update + decay * weight), first_new, second_new)


def local(
    patches,
    out_grad,
    item_ids,
    expert_ids,
    qkv_master,
    qkv_first,
    qkv_second,
    proj_master,
    proj_first,
    proj_second,
    router_master,
    router_first,
    router_second,
    gains_master,
    gains_first,
    gains_second,
    inner_master,
    inner_first,
    inner_second,
    down_master,
    down_first,
    down_second,
):
    expert_count = lax.axis_size("expert")
    local_experts = inner_master.shape[0]
    experts = expert_count * local_experts
    length = patches.shape[1]
    width = patches.shape[2]
    top = expert_ids.shape[2]
    capacity = 2 * length * top // experts
    hidden_width = down_master.shape[1] * lax.axis_size("dp")
    inner_low, down_low = (
        lax.all_gather(inner_master.astype(jnp.bfloat16), "dp", axis=1, tiled=True),
        lax.all_gather(down_master.astype(jnp.bfloat16), "dp", axis=1, tiled=True),
    )
    qkv_low = qkv_master.astype(jnp.bfloat16)
    proj_low = proj_master.astype(jnp.bfloat16)
    router_low = router_master.astype(jnp.bfloat16)
    gain_attn = gains_master[0]
    gain_ffn = gains_master[1]
    expert_numbers = jnp.arange(experts, dtype=jnp.int32)

    def expert_forward(received):
        count = received.shape[1]
        grid = received.reshape(expert_count, local_experts, count, width)
        both = jnp.einsum("sjcd,jdf->sjcf", grid, inner_low, preferred_element_type=jnp.float32)
        hidden = (jax.nn.silu(both[..., :hidden_width]) * both[..., hidden_width:]).astype(
            jnp.bfloat16
        )
        result = jnp.einsum("sjcf,jfd->sjcd", hidden, down_low, preferred_element_type=jnp.float32)
        result = result.astype(jnp.bfloat16).reshape(experts, count, width)
        returned = lax.all_to_all(result, "expert", split_axis=0, concat_axis=0, tiled=True)
        return (returned, received)

    def micro_step(carry, inputs):
        grad_qkv, grad_proj, grad_router, grad_gains, grad_inner, grad_down = carry
        patch, upstream, item_block, routes = inputs
        items = item_block[0]
        source = patch.astype(jnp.float32)
        inv_first = lax.rsqrt(jnp.mean(source * source, axis=1, keepdims=True) + norm_eps)
        unit_first = source * inv_first
        normed_in = (unit_first * gain_attn).astype(jnp.bfloat16)
        mixed = jnp.dot(normed_in, qkv_low, preferred_element_type=jnp.float32)
        cosine, sine = rotary_tables(items)
        query = rotate(mixed[:, :width].reshape(length, HEADS, HEAD), cosine, sine).astype(
            jnp.bfloat16
        )
        keys = rotate(
            mixed[:, width : 2 * width].reshape(length, HEADS, HEAD), cosine, sine
        ).astype(jnp.bfloat16)
        values = mixed[:, 2 * width :].reshape(length, HEADS, HEAD).astype(jnp.bfloat16)
        same_item = items[:, None] == items[None, :]
        scores = masked_scores(query, keys, same_item)
        peak = jnp.max(scores, axis=2, keepdims=True)
        weights = jnp.exp(scores - peak)
        totals = jnp.sum(weights, axis=2, keepdims=True)
        probs_low = (weights / totals).astype(jnp.bfloat16)
        log_total = peak + jnp.log(totals)
        attended = jnp.einsum("hqk,khe->qhe", probs_low, values, preferred_element_type=jnp.float32)
        attended = attended.reshape(length, width).astype(jnp.bfloat16)
        middle = source + jnp.dot(attended, proj_low, preferred_element_type=jnp.float32)
        inv_second = lax.rsqrt(jnp.mean(middle * middle, axis=1, keepdims=True) + norm_eps)
        unit_second = middle * inv_second
        normed_mid = (unit_second * gain_ffn).astype(jnp.bfloat16)
        logits = jnp.dot(normed_mid, router_low, preferred_element_type=jnp.float32)
        chosen = jnp.take_along_axis(logits, routes, axis=1)
        gates = jax.nn.softmax(chosen, axis=1)
        flat_ids = routes.reshape(length * top)
        hits = (flat_ids[:, None] == expert_numbers[None, :]).astype(jnp.int32)
        rank = jnp.sum(jnp.cumsum(hits, axis=0) * hits, axis=1) - 1
        slots = flat_ids * capacity + rank
        copies = jnp.repeat(normed_mid, top, axis=0)
        outgoing = jnp.zeros((experts * capacity, width), jnp.bfloat16).at[slots].set(copies)
        outgoing = outgoing.reshape(experts, capacity, width)
        returned, kept_inputs = expert_forward(
            lax.all_to_all(outgoing, "expert", split_axis=0, concat_axis=0, tiled=True)
        )
        picked = (
            returned.reshape(experts * capacity, width)[slots]
            .reshape(length, top, width)
            .astype(jnp.float32)
        )
        combined = jnp.sum(gates[:, :, None] * picked, axis=1)
        block_out = (middle + combined).astype(jnp.bfloat16)
        upstream_full = upstream.astype(jnp.float32)
        grad_gate = jnp.sum(upstream_full[:, None, :] * picked, axis=2)
        grad_chosen = gates * (grad_gate - jnp.sum(gates * grad_gate, axis=1, keepdims=True))
        route_hits = (routes[:, :, None] == expert_numbers[None, None, :]).astype(jnp.float32)
        grad_logits = jnp.sum(grad_chosen[:, :, None] * route_hits, axis=1).astype(jnp.bfloat16)
        grad_router_now = jnp.dot(normed_mid.T, grad_logits, preferred_element_type=jnp.float32)
        grad_mid = jnp.dot(grad_logits, router_low.T, preferred_element_type=jnp.float32)
        grad_slots = (
            (gates[:, :, None] * upstream_full[:, None, :])
            .astype(jnp.bfloat16)
            .reshape(length * top, width)
        )
        grad_outgoing = (
            jnp.zeros((experts * capacity, width), jnp.bfloat16).at[slots].set(grad_slots)
        )
        grad_outgoing = grad_outgoing.reshape(experts, capacity, width)
        incoming, inputs_back = (
            lax.all_to_all(grad_outgoing, "expert", split_axis=0, concat_axis=0, tiled=True),
            lax.all_to_all(outgoing, "expert", split_axis=0, concat_axis=0, tiled=True),
        )
        grid_in = inputs_back.reshape(expert_count, local_experts, capacity, width)
        grid_grad = incoming.reshape(expert_count, local_experts, capacity, width)
        both = jnp.einsum("sjcd,jdf->sjcf", grid_in, inner_low, preferred_element_type=jnp.float32)
        gate_part = both[..., :hidden_width]
        up_part = both[..., hidden_width:]
        sigma = jax.nn.sigmoid(gate_part)
        activated = jax.nn.silu(gate_part)
        hidden = (activated * up_part).astype(jnp.bfloat16)
        grad_hidden = jnp.einsum(
            "sjcd,jfd->sjcf", grid_grad, down_low, preferred_element_type=jnp.float32
        )
        grad_down_now = jnp.einsum(
            "sjcf,sjcd->jfd", hidden, grid_grad, preferred_element_type=jnp.float32
        )
        grad_both = jnp.concatenate(
            [
                grad_hidden * up_part * sigma * (1.0 + gate_part * (1.0 - sigma)),
                grad_hidden * activated,
            ],
            axis=3,
        ).astype(jnp.bfloat16)
        grad_inner_now = jnp.einsum(
            "sjcd,sjcf->jdf", grid_in, grad_both, preferred_element_type=jnp.float32
        )
        grad_copies = jnp.einsum(
            "sjcf,jdf->sjcd", grad_both, inner_low, preferred_element_type=jnp.float32
        )
        grad_copies = grad_copies.astype(jnp.bfloat16).reshape(experts, capacity, width)
        grad_back = lax.all_to_all(grad_copies, "expert", split_axis=0, concat_axis=0, tiled=True)
        grad_picked = grad_back.reshape(experts * capacity, width)[slots].reshape(
            length, top, width
        )
        grad_mid = grad_mid + jnp.sum(grad_picked.astype(jnp.float32), axis=1)
        grad_unit_second = grad_mid * gain_ffn
        grad_gain_ffn = jnp.sum(grad_mid * unit_second, axis=0)
        grad_middle = upstream_full + inv_second * (
            grad_unit_second
            - unit_second * jnp.mean(grad_unit_second * unit_second, axis=1, keepdims=True)
        )
        grad_branch = grad_middle.astype(jnp.bfloat16)
        grad_proj_now = jnp.dot(attended.T, grad_branch, preferred_element_type=jnp.float32)
        grad_attended = jnp.dot(grad_branch, proj_low.T, preferred_element_type=jnp.float32)
        grad_attended = grad_attended.astype(jnp.bfloat16).reshape(length, HEADS, HEAD)
        probs_again = jnp.exp(masked_scores(query, keys, same_item) - log_total)
        grad_probs = jnp.einsum(
            "qhe,khe->hqk", grad_attended, values, preferred_element_type=jnp.float32
        )
        grad_values = jnp.einsum(
            "hqk,qhe->khe", probs_low, grad_attended, preferred_element_type=jnp.float32
        )
        grad_scores = probs_again * (
            grad_probs - jnp.sum(probs_again * grad_probs, axis=2, keepdims=True)
        )
        grad_scores = grad_scores.astype(jnp.bfloat16)
        grad_query = (
            jnp.einsum("hqk,khe->qhe", grad_scores, keys, preferred_element_type=jnp.float32)
            * 0.125
        )
        grad_keys = (
            jnp.einsum("hqk,qhe->khe", grad_scores, query, preferred_element_type=jnp.float32)
            * 0.125
        )
        grad_mixed = jnp.concatenate(
            [
                rotate(grad_query, cosine, -sine).reshape(length, width),
                rotate(grad_keys, cosine, -sine).reshape(length, width),
                grad_values.reshape(length, width),
            ],
            axis=1,
        ).astype(jnp.bfloat16)
        grad_qkv_now = jnp.dot(normed_in.T, grad_mixed, preferred_element_type=jnp.float32)
        grad_normed = jnp.dot(grad_mixed, qkv_low.T, preferred_element_type=jnp.float32)
        grad_unit_first = grad_normed * gain_attn
        grad_gain_attn = jnp.sum(grad_normed * unit_first, axis=0)
        patch_grad = grad_middle + inv_first * (
            grad_unit_first
            - unit_first * jnp.mean(grad_unit_first * unit_first, axis=1, keepdims=True)
        )
        new_carry = (
            grad_qkv + grad_qkv_now,
            grad_proj + grad_proj_now,
            grad_router + grad_router_now,
            grad_gains + jnp.stack([grad_gain_attn, grad_gain_ffn]),
            grad_inner + grad_inner_now,
            grad_down + grad_down_now,
        )
        return (new_carry, (block_out, patch_grad))

    start = (
        jnp.zeros(qkv_master.shape, jnp.float32),
        jnp.zeros(proj_master.shape, jnp.float32),
        jnp.zeros(router_master.shape, jnp.float32),
        jnp.zeros(gains_master.shape, jnp.float32),
        jnp.zeros(inner_low.shape, jnp.float32),
        jnp.zeros(down_low.shape, jnp.float32),
    )
    totals, outputs = lax.scan(micro_step, start, (patches, out_grad, item_ids, expert_ids))
    grad_qkv, grad_proj, grad_router, grad_gains = lax.psum(
        (totals[0], totals[1], totals[2], totals[3]), ("dp", "expert")
    )
    grad_inner, grad_down = (
        lax.psum_scatter(totals[4], "dp", scatter_dimension=1, tiled=True),
        lax.psum_scatter(totals[5], "dp", scatter_dimension=1, tiled=True),
    )
    qkv_new = adamw(qkv_master, qkv_first, qkv_second, grad_qkv, 0.1, 0.1)
    proj_new = adamw(proj_master, proj_first, proj_second, grad_proj, 0.4, 0.1)
    router_new = adamw(router_master, router_first, router_second, grad_router, 0.07, 0.1)
    gains_new = adamw(gains_master, gains_first, gains_second, grad_gains, 0.4, 0.0)
    inner_new = adamw(inner_master, inner_first, inner_second, grad_inner, 0.1, 0.1)
    down_new = adamw(down_master, down_first, down_second, grad_down, 0.15, 0.1)
    return (
        outputs[0],
        outputs[1],
        qkv_new[0],
        qkv_new[1],
        qkv_new[2],
        proj_new[0],
        proj_new[1],
        proj_new[2],
        router_new[0],
        router_new[1],
        router_new[2],
        gains_new[0],
        gains_new[1],
        gains_new[2],
        inner_new[0],
        inner_new[1],
        inner_new[2],
        down_new[0],
        down_new[1],
        down_new[2],
    )


F32 = jnp.float32
BF16 = jnp.bfloat16
QB = 128


def iota(shape, axis):
    return lax.broadcasted_iota(jnp.int32, shape, axis)


def dot_nn(a, b):
    return jnp.dot(a, b, preferred_element_type=F32)


def dot_nt(a, b):
    return lax.dot_general(a, b, (((1,), (1,)), ((), ())), preferred_element_type=F32)


def dot_tn(a, b):
    return lax.dot_general(a, b, (((0,), (0,)), ((), ())), preferred_element_type=F32)


def swap_halves(v, low_lane):
    width = v.shape[1]
    half = HEAD // 2
    return jnp.where(low_lane, pltpu.roll(v, width - half, 1), pltpu.roll(v, half, 1))


def turn(v, cos_row, sin_row, low_lane):
    return v * cos_row + swap_halves(v, low_lane) * sin_row


def rope_table(item_max):
    half = HEAD // 2
    offset = np.arange(item_max, dtype=np.float32)
    freqs = np.float32(10000.0) ** (-np.arange(half, dtype=np.float32) / np.float32(half))
    angles = (offset[:, None] * freqs[None, :]).astype(np.float32)
    cosine, sine = np.cos(angles), np.sin(angles)
    return np.concatenate([cosine] * 4 + [-sine, sine] * 2, axis=1).astype(np.float32)


def windows(length):
    found = []
    for start in range(0, length, QB):
        low = max(0, start - QB)
        high = min(length, start + 2 * QB)
        found.append((start, low, high))
    return found


def row_norm(values):
    return lax.rsqrt(jnp.mean(values * values, axis=1, keepdims=True) + norm_eps)


def positions(item_row, length):
    eye = iota((length, length), 0) == iota((length, length), 1)
    col = jnp.sum(jnp.where(eye, item_row, 0.0), axis=1, keepdims=True)
    before = jnp.sum(jnp.where(item_row < col, 1.0, 0.0), axis=1, keepdims=True)
    offset = iota((length, 1), 0) - before.astype(jnp.int32)
    return col, offset


def rope_rows(offset, table, length, width):
    spots = table.shape[0]
    pick = jnp.where(iota((length, spots), 1) == offset, 1.0, 0.0)
    both = jnp.dot(pick, table, precision=lax.Precision.HIGHEST, preferred_element_type=F32)
    copies = width // 128
    return (
        jnp.concatenate([both[:, :128]] * copies, axis=1),
        jnp.concatenate([both[:, 128:]] * copies, axis=1),
    )


def attend_kernel(patches, items, qkv_w, proj_w, gains, table, mixed_o, probs_o, att_o, mid_o, nm_o):
    packs, length, width = patches.shape
    pairs = width // 128
    low_lane = iota((1, width), 1) % HEAD < HEAD // 2
    first_head = iota((1, 128), 1) < HEAD
    mask_a = jnp.where(first_head, 1.0, 0.0).astype(BF16)
    mask_b = jnp.where(first_head, 0.0, 1.0).astype(BF16)
    top_rows = iota((128, 1), 0) < HEAD

    def pack(p, carry):
        source = patches[p].astype(F32)
        normed = (source * row_norm(source) * gains[0:1, :]).astype(BF16)
        mixed = dot_nn(normed, qkv_w[...])
        item_row = items[p].astype(F32)
        item_col, offset = positions(item_row, length)
        cos_row, sin_row = rope_rows(offset, table[...], length, width)
        mixed_o[p, :, :width] = turn(mixed[:, :width], cos_row, sin_row, low_lane).astype(BF16)
        mixed_o[p, :, width : 2 * width] = turn(
            mixed[:, width : 2 * width], cos_row, sin_row, low_lane
        ).astype(BF16)
        mixed_o[p, :, 2 * width :] = mixed[:, 2 * width :].astype(BF16)
        for pair in range(pairs):
            lanes = slice(128 * pair, 128 * pair + 128)
            key_lanes = slice(width + 128 * pair, width + 128 * pair + 128)
            values_t = mixed[:, 2 * width + 128 * pair : 2 * width + 128 * pair + 128].T.astype(BF16)
            for block, (start, low, high) in enumerate(windows(length)):
                query = mixed_o[p, start : start + QB, lanes] * 0.125
                query = jnp.concatenate([query * mask_a, query * mask_b], axis=0)
                scores = dot_nt(mixed_o[p, low:high, key_lanes], query)
                here = item_row[:, start : start + QB]
                same = item_col[low:high] == jnp.concatenate([here, here], axis=1)
                scores = jnp.where(same, scores, -1e30)
                peak = jnp.max(scores, axis=0, keepdims=True)
                weights = jnp.exp(scores - peak)
                total = jnp.sum(weights, axis=0, keepdims=True)
                probs = (weights * (1.0 / total)).astype(BF16)
                probs_o[p, pair, block, : high - low] = probs
                out = dot_nn(values_t[:, low:high], probs)
                out = jnp.where(top_rows, out[:, :QB], out[:, QB:])
                att_o[p, start : start + QB, lanes] = out.T.astype(BF16)
        middle = source + dot_nn(att_o[p], proj_w[...])
        mid_o[p] = middle
        nm_o[p] = (middle * row_norm(middle) * gains[1:2, :]).astype(BF16)
        return carry

    lax.fori_loop(0, packs, pack, 0)


def expert_kernel(
    nm, upstream, ids, router_w, inner_w, down_w,
    inner_g, down_g, back_o, glog_o,
    both_s, rank_s, gate_s, gg_s, x_s, hid_s, go_s, gb_s, y_s,
):
    packs, length, width = nm.shape
    experts = router_w.shape[0]
    hidden_width = down_w.shape[1]
    cap = x_s.shape[0] // packs
    expert = pl.program_id(0)

    @pl.when(expert == 0)
    def _():
        earlier = jnp.where(iota((length, length), 0) < iota((length, length), 1), 1.0, 0.0).astype(BF16)

        def prepare(p, carry):
            both_s[p, :, :width] = nm[p]
            both_s[p, :, width:] = upstream[p]
            logits = dot_nt(router_w[...], nm[p])
            number = iota((experts, length), 0)
            hit0 = number == ids[p, 0:1, :]
            hit1 = number == ids[p, 1:2, :]
            chosen0 = jnp.sum(jnp.where(hit0, logits, 0.0), axis=0, keepdims=True)
            chosen1 = jnp.sum(jnp.where(hit1, logits, 0.0), axis=0, keepdims=True)
            peak = jnp.maximum(chosen0, chosen1)
            e0 = jnp.exp(chosen0 - peak)
            e1 = jnp.exp(chosen1 - peak)
            total = e0 + e1
            gate_s[p] = jnp.where(hit0, e0 / total, 0.0) + jnp.where(hit1, e1 / total, 0.0)
            named = jnp.where(hit0, 1.0, jnp.where(hit1, 1.0, 0.0))
            rank = dot_nn(named.astype(BF16), earlier)
            rank_s[p] = jnp.where(named > 0.5, rank, -1.0)
            return carry

        lax.fori_loop(0, packs, prepare, 0)

    def rows(p, carry):
        here = pl.ds(pl.multiple_of(p * cap, cap), cap)
        rank = rank_s[p, pl.ds(expert, 1), :]
        gate_row = gate_s[p, pl.ds(expert, 1), :]
        pick = iota((cap, length), 0).astype(F32) == rank
        chosen = jnp.where(pick, 1.0, 0.0).astype(BF16)
        taken = dot_nn(chosen, both_s[p])
        gate_col = jnp.sum(jnp.where(pick, gate_row, 0.0), axis=1, keepdims=True)
        x = taken[:, :width].astype(BF16)
        g = taken[:, width:]
        x_s[here, :] = x
        grad_out = (gate_col * g).astype(BF16)
        go_s[here, :] = grad_out
        gate = dot_nn(x, inner_w[0, :, :hidden_width])
        up = dot_nn(x, inner_w[0, :, hidden_width:])
        sigma = 1.0 / (1.0 + jnp.exp(-gate))
        active = gate * sigma
        hidden = (active * up).astype(BF16)
        hid_s[here, :] = hidden
        result = dot_nn(hidden, down_w[0]).astype(BF16).astype(F32)
        spot = pl.ds(pl.multiple_of(expert * cap, cap), cap)
        y_s[p, spot, :width] = (gate_col * result).astype(BF16)
        grad_gate = jnp.sum(g * result, axis=1, keepdims=True)
        gg_s[p, pl.ds(expert, 1), :] = jnp.sum(jnp.where(pick, grad_gate, 0.0), axis=0, keepdims=True)
        grad_hidden = dot_nt(grad_out, down_w[0])
        gb_s[here, :hidden_width] = (grad_hidden * up * sigma * (1.0 + gate * (1.0 - sigma))).astype(BF16)
        gb_s[here, hidden_width:] = (grad_hidden * active).astype(BF16)
        y_s[p, spot, width:] = dot_nt(gb_s[here, :], inner_w[0]).astype(BF16)
        return carry

    lax.fori_loop(0, packs, rows, 0)
    inner_g[0] = dot_tn(x_s[...], gb_s[...]).astype(BF16)
    down_g[0] = dot_tn(hid_s[...], go_s[...]).astype(BF16)

    @pl.when(expert == experts - 1)
    def _():
        def finish(p, carry):
            ranks = rank_s[p].T
            slot = iota((length, cap), 1).astype(F32)
            pieces = [
                jnp.where(ranks[:, e : e + 1] == slot, 1.0, 0.0).astype(BF16) for e in range(experts)
            ]
            back = dot_nn(jnp.concatenate(pieces, axis=1), y_s[p])
            number = iota((experts, length), 0)
            gate = gate_s[p]
            grad_gate = gg_s[p]
            mean = jnp.sum(gate * grad_gate, axis=0, keepdims=True)
            hit = rank_s[p] > -0.5
            grad_logits = jnp.where(hit, gate * (grad_gate - mean), 0.0).astype(BF16)
            glog_o[p] = grad_logits
            back_o[p, :, :width] = back[:, :width]
            back_o[p, :, width:] = back[:, width:] + dot_tn(grad_logits, router_w[...])
            return carry

        lax.fori_loop(0, packs, finish, 0)


def return_kernel(
    patches, upstream, items, qkv_w, proj_w, gains, table, mixed, probs, att, mid, nm, back, glog,
    block_o, patch_o, attn_g, small_g,
    normed_s, branch_s, datt_s, dmix_s, dkv_s,
):
    packs, length, width = patches.shape
    pairs = width // 128
    experts = glog.shape[1]
    low_lane = iota((1, width), 1) % HEAD < HEAD // 2
    first_head = iota((1, 128), 1) < HEAD
    mask_a = jnp.where(first_head, 1.0, 0.0).astype(BF16)
    mask_b = jnp.where(first_head, 0.0, 1.0).astype(BF16)
    top_rows = iota((128, 1), 0) < HEAD
    small_g[...] = jnp.zeros(small_g.shape, F32)

    def pack(p, carry):
        rows = pl.ds(pl.multiple_of(p * length, length), length)
        source = patches[p].astype(F32)
        gain0, gain1 = gains[0:1, :], gains[1:2, :]
        middle = mid[p]
        inv = row_norm(middle)
        unit = middle * inv
        block_o[p] = (middle + back[p, :, :width]).astype(BF16)
        grad_mid = back[p, :, width:]
        small_g[experts : experts + 1, :] += jnp.zeros((1, width), F32)
        small_g[experts + 1 : experts + 2, :] += jnp.sum(grad_mid * unit, axis=0, keepdims=True)
        small_g[0:experts, :] += dot_nn(glog[p], nm[p])
        grad_unit = grad_mid * gain1
        grad_middle = upstream[p].astype(F32) + inv * (
            grad_unit - unit * jnp.mean(grad_unit * unit, axis=1, keepdims=True)
        )
        patch_o[p] = grad_middle
        branch = grad_middle.astype(BF16)
        branch_s[rows, :] = branch
        datt_s[...] = dot_nt(branch, proj_w[...]).astype(BF16)
        dkv_s[...] = jnp.zeros(dkv_s.shape, F32)
        item_row = items[p].astype(F32)
        item_col, offset = positions(item_row, length)
        cos_row, sin_row = rope_rows(offset, table[...], length, width)
        for pair in range(pairs):
            lanes = slice(128 * pair, 128 * pair + 128)
            key_lanes = slice(width + 128 * pair, width + 128 * pair + 128)
            value_lanes = slice(2 * width + 128 * pair, 2 * width + 128 * pair + 128)
            keys_t = mixed[p, :, key_lanes].astype(F32).T.astype(BF16)
            for block, (start, low, high) in enumerate(windows(length)):
                query = mixed[p, start : start + QB, lanes] * 0.125
                query = jnp.concatenate([query * mask_a, query * mask_b], axis=0)
                datt = datt_s[start : start + QB, lanes]
                datt = jnp.concatenate([datt * mask_a, datt * mask_b], axis=0)
                prob = probs[p, pair, block, : high - low]
                dprob = dot_nt(mixed[p, low:high, value_lanes], datt)
                weight = prob.astype(F32)
                mean = jnp.sum(weight * dprob, axis=0, keepdims=True)
                dscore = (weight * (dprob - mean)).astype(BF16)
                dkv_s[low:high, key_lanes] += dot_nn(dscore, query)
                dkv_s[low:high, value_lanes] += dot_nn(prob, datt)
                dquery = dot_nn(keys_t[:, low:high], dscore)
                dquery = jnp.where(top_rows, dquery[:, :QB], dquery[:, QB:])
                dkv_s[start : start + QB, lanes] = dquery.T * 0.125
        dmix_s[rows, :width] = turn(dkv_s[:, :width], cos_row, -sin_row, low_lane).astype(BF16)
        dmix_s[rows, width : 2 * width] = turn(
            dkv_s[:, width : 2 * width], cos_row, -sin_row, low_lane
        ).astype(BF16)
        dmix_s[rows, 2 * width :] = dkv_s[:, 2 * width :].astype(BF16)
        grad_normed = dot_nt(dmix_s[rows, :], qkv_w[...])
        inv_in = row_norm(source)
        unit_in = source * inv_in
        normed_s[rows, :] = (unit_in * gain0).astype(BF16)
        small_g[experts : experts + 1, :] += jnp.sum(grad_normed * unit_in, axis=0, keepdims=True)
        grad_unit_in = grad_normed * gain0
        patch_o[p] += inv_in * (
            grad_unit_in - unit_in * jnp.mean(grad_unit_in * unit_in, axis=1, keepdims=True)
        )
        return carry

    lax.fori_loop(0, packs, pack, 0)
    attn_g[:, : 3 * width] = dot_tn(normed_s[...], dmix_s[...])
    for p in range(packs):
        pass
    flat = jnp.concatenate([att[p] for p in range(packs)], axis=0)
    attn_g[:, 3 * width :] = dot_tn(flat, branch_s[...])


def whole(count):
    return [pl.BlockSpec(memory_space=pltpu.VMEM)] * count


LIMIT = pltpu.CompilerParams(vmem_limit_bytes=60 * 1024 * 1024)


def run_attend(patches, items, qkv_w, proj_w, gains, table):
    packs, length, width = patches.shape
    pairs = width // 128
    blocks = length // QB
    shapes = (
        jax.ShapeDtypeStruct((packs, length, 3 * width), BF16),
        jax.ShapeDtypeStruct((packs, pairs, blocks, 3 * QB, 2 * QB), BF16),
        jax.ShapeDtypeStruct((packs, length, width), BF16),
        jax.ShapeDtypeStruct((packs, length, width), F32),
        jax.ShapeDtypeStruct((packs, length, width), BF16),
    )
    return pl.pallas_call(
        attend_kernel,
        out_shape=shapes,
        in_specs=whole(6),
        out_specs=tuple(whole(5)),
        compiler_params=LIMIT,
        name="attend",
    )(patches, items, qkv_w, proj_w, gains, table)


def run_experts(nm, upstream, ids, router_w, inner_w, down_w):
    packs, length, width = nm.shape
    experts = router_w.shape[0]
    hidden = down_w.shape[1]
    cap = 2 * length * 2 // experts
    fixed3 = lambda e: (0, 0, 0)
    each = lambda e: (e, 0, 0)
    grid_spec = pltpu.PrefetchScalarGridSpec(
        num_scalar_prefetch=0,
        grid=(experts,),
        in_specs=[
            pl.BlockSpec((packs, length, width), fixed3),
            pl.BlockSpec((packs, length, width), fixed3),
            pl.BlockSpec((packs, 2, length), fixed3),
            pl.BlockSpec((experts, width), lambda e: (0, 0)),
            pl.BlockSpec((1, width, 2 * hidden), each),
            pl.BlockSpec((1, hidden, width), each),
        ],
        out_specs=(
            pl.BlockSpec((1, width, 2 * hidden), each),
            pl.BlockSpec((1, hidden, width), each),
            pl.BlockSpec((packs, length, 2 * width), fixed3),
            pl.BlockSpec((packs, experts, length), fixed3),
        ),
        scratch_shapes=[
            pltpu.VMEM((packs, length, 2 * width), BF16),
            pltpu.VMEM((packs, experts, length), F32),
            pltpu.VMEM((packs, experts, length), F32),
            pltpu.VMEM((packs, experts, length), F32),
            pltpu.VMEM((packs * cap, width), BF16),
            pltpu.VMEM((packs * cap, hidden), BF16),
            pltpu.VMEM((packs * cap, width), BF16),
            pltpu.VMEM((packs * cap, 2 * hidden), BF16),
            pltpu.VMEM((packs, experts * cap, 2 * width), BF16),
        ],
    )
    return pl.pallas_call(
        expert_kernel,
        out_shape=(
            jax.ShapeDtypeStruct((experts, width, 2 * hidden), BF16),
            jax.ShapeDtypeStruct((experts, hidden, width), BF16),
            jax.ShapeDtypeStruct((packs, length, 2 * width), F32),
            jax.ShapeDtypeStruct((packs, experts, length), BF16),
        ),
        grid_spec=grid_spec,
        compiler_params=LIMIT,
        name="experts",
    )(nm, upstream, ids, router_w, inner_w, down_w)


def run_return(patches, upstream, items, qkv_w, proj_w, gains, table, mixed, probs, att, mid, nm, back, glog):
    packs, length, width = patches.shape
    shapes = (
        jax.ShapeDtypeStruct((packs, length, width), BF16),
        jax.ShapeDtypeStruct((packs, length, width), F32),
        jax.ShapeDtypeStruct((width, 4 * width), F32),
        jax.ShapeDtypeStruct((16, width), F32),
    )
    return pl.pallas_call(
        return_kernel,
        out_shape=shapes,
        in_specs=whole(14),
        out_specs=tuple(whole(4)),
        scratch_shapes=[
            pltpu.VMEM((packs * length, width), BF16),
            pltpu.VMEM((packs * length, width), BF16),
            pltpu.VMEM((length, width), BF16),
            pltpu.VMEM((packs * length, 3 * width), BF16),
            pltpu.VMEM((length, 3 * width), F32),
        ],
        compiler_params=LIMIT,
        name="backward",
    )(patches, upstream, items, qkv_w, proj_w, gains, table, mixed, probs, att, mid, nm, back, glog)


def fast(
    patches, out_grad, item_ids, expert_ids,
    qkv_master, qkv_first, qkv_second,
    proj_master, proj_first, proj_second,
    router_master, router_first, router_second,
    gains_master, gains_first, gains_second,
    inner_master, inner_first, inner_second,
    down_master, down_first, down_second,
):
    width = patches.shape[2]
    experts = router_master.shape[1]
    inner_w = lax.all_gather(inner_master.astype(BF16), "dp", axis=1, tiled=True)
    inner_w = lax.all_gather(inner_w, "expert", axis=0, tiled=True)
    down_w = lax.all_gather(down_master.astype(BF16), "dp", axis=1, tiled=True)
    down_w = lax.all_gather(down_w, "expert", axis=0, tiled=True)
    qkv_w = qkv_master.astype(BF16)
    proj_w = proj_master.astype(BF16)
    router_w = router_master.T.astype(BF16)
    ids = jnp.swapaxes(expert_ids, 1, 2)
    table = jnp.asarray(rope_table(QB))
    mixed, probs, att, mid, nm = run_attend(patches, item_ids, qkv_w, proj_w, gains_master, table)
    inner_g, down_g, back, glog = run_experts(nm, out_grad, ids, router_w, inner_w, down_w)
    block_out, patch_grad, attn_g, small_g = run_return(
        patches, out_grad, item_ids, qkv_w, proj_w, gains_master, table, mixed, probs, att, mid, nm, back, glog
    )
    grad_inner = lax.psum_scatter(inner_g, "expert", scatter_dimension=0, tiled=True)
    grad_inner = lax.psum_scatter(grad_inner, "dp", scatter_dimension=1, tiled=True).astype(F32)
    grad_down = lax.psum_scatter(down_g, "expert", scatter_dimension=0, tiled=True)
    grad_down = lax.psum_scatter(grad_down, "dp", scatter_dimension=1, tiled=True).astype(F32)
    attn_g, small_g = lax.psum((attn_g, small_g), ("dp", "expert"))
    qkv_new = adamw(qkv_master, qkv_first, qkv_second, attn_g[:, : 3 * width], 0.1, 0.1)
    proj_new = adamw(proj_master, proj_first, proj_second, attn_g[:, 3 * width :], 0.4, 0.1)
    router_new = adamw(router_master, router_first, router_second, small_g[:experts].T, 0.07, 0.1)
    gains_new = adamw(gains_master, gains_first, gains_second, small_g[experts : experts + 2], 0.4, 0.0)
    inner_new = adamw(inner_master, inner_first, inner_second, grad_inner, 0.1, 0.1)
    down_new = adamw(down_master, down_first, down_second, grad_down, 0.15, 0.1)
    return (block_out, patch_grad) + qkv_new + proj_new + router_new + gains_new + inner_new + down_new


GATHER_LIMIT = 16 * 1024 * 1024


def step(*args):
    inner_master, down_master = args[16], args[19]
    experts = inner_master.shape[0] * lax.axis_size("expert")
    entries = inner_master.shape[1] * inner_master.shape[2] + down_master.shape[1] * down_master.shape[2]
    weight_bytes = 2 * experts * entries * lax.axis_size("dp")
    return (fast if weight_bytes <= GATHER_LIMIT else local)(*args)


def solution(mesh):
    in_specs = (
        P(None, ("dp", "expert"), None),
        P(None, ("dp", "expert"), None),
        P(None, ("dp", "expert"), None),
        P(None, ("dp", "expert"), None),
        P(),
        P(),
        P(),
        P(),
        P(),
        P(),
        P(),
        P(),
        P(),
        P(),
        P(),
        P(),
        P("expert", "dp", None),
        P("expert", "dp", None),
        P("expert", "dp", None),
        P("expert", "dp", None),
        P("expert", "dp", None),
        P("expert", "dp", None),
    )
    out_specs = (
        P(None, ("dp", "expert"), None),
        P(None, ("dp", "expert"), None),
        P(),
        P(),
        P(),
        P(),
        P(),
        P(),
        P(),
        P(),
        P(),
        P(),
        P(),
        P(),
        P("expert", "dp", None),
        P("expert", "dp", None),
        P("expert", "dp", None),
        P("expert", "dp", None),
        P("expert", "dp", None),
        P("expert", "dp", None),
    )
    return jax.shard_map(step, mesh=mesh, in_specs=in_specs, out_specs=out_specs, check_vma=False)
```

```python
import functools

import jax
import jax.numpy as jnp
import numpy as np
from jax import lax
from jax.experimental import pallas as pl
from jax.experimental.pallas import tpu as pltpu
from jax.sharding import PartitionSpec as P

HEADS = 6
HEAD = 64


norm_eps = 1e-06
adam_eps = 1e-08
correction = 0.875


def rotary_tables(item_row):
    length = item_row.shape[0]
    places = jnp.arange(length, dtype=jnp.int32)
    starts = jnp.concatenate([jnp.ones((1,), dtype=bool), item_row[1:] != item_row[:-1]])
    first = lax.cummax(jnp.where(starts, places, 0), axis=0)
    offset = (places - first).astype(jnp.float32)
    half = HEAD // 2
    freqs = 10000.0 ** (-jnp.arange(half, dtype=jnp.float32) / half)
    angles = offset[:, None] * freqs[None, :]
    return (jnp.cos(angles), jnp.sin(angles))


def rotate(vectors, cosine, sine):
    half = vectors.shape[-1] // 2
    first_half = vectors[..., :half]
    second_half = vectors[..., half:]
    cos_part = cosine[:, None, :]
    sin_part = sine[:, None, :]
    return jnp.concatenate(
        [
            first_half * cos_part - second_half * sin_part,
            second_half * cos_part + first_half * sin_part,
        ],
        axis=-1,
    )


def masked_scores(query, keys, same_item):
    scores = jnp.einsum("qhe,khe->hqk", query, keys, preferred_element_type=jnp.float32) * 0.125
    return jnp.where(same_item[None], scores, -1e30)


def adamw(weight, first, second, grad, rate, decay):
    first_new = 0.5 * first + 0.5 * grad
    second_new = 0.5 * second + 0.5 * grad * grad
    update = first_new / correction / (jnp.sqrt(second_new / correction) + adam_eps)
    return (weight - rate * (update + decay * weight), first_new, second_new)


def local(
    patches,
    out_grad,
    item_ids,
    expert_ids,
    qkv_master,
    qkv_first,
    qkv_second,
    proj_master,
    proj_first,
    proj_second,
    router_master,
    router_first,
    router_second,
    gains_master,
    gains_first,
    gains_second,
    inner_master,
    inner_first,
    inner_second,
    down_master,
    down_first,
    down_second,
):
    expert_count = lax.axis_size("expert")
    local_experts = inner_master.shape[0]
    experts = expert_count * local_experts
    length = patches.shape[1]
    width = patches.shape[2]
    top = expert_ids.shape[2]
    capacity = 2 * length * top // experts
    hidden_width = down_master.shape[1] * lax.axis_size("dp")
    inner_low, down_low = (
        lax.all_gather(inner_master.astype(jnp.bfloat16), "dp", axis=1, tiled=True),
        lax.all_gather(down_master.astype(jnp.bfloat16), "dp", axis=1, tiled=True),
    )
    qkv_low = qkv_master.astype(jnp.bfloat16)
    proj_low = proj_master.astype(jnp.bfloat16)
    router_low = router_master.astype(jnp.bfloat16)
    gain_attn = gains_master[0]
    gain_ffn = gains_master[1]
    expert_numbers = jnp.arange(experts, dtype=jnp.int32)

    def expert_forward(received):
        count = received.shape[1]
        grid = received.reshape(expert_count, local_experts, count, width)
        both = jnp.einsum("sjcd,jdf->sjcf", grid, inner_low, preferred_element_type=jnp.float32)
        hidden = (jax.nn.silu(both[..., :hidden_width]) * both[..., hidden_width:]).astype(
            jnp.bfloat16
        )
        result = jnp.einsum("sjcf,jfd->sjcd", hidden, down_low, preferred_element_type=jnp.float32)
        result = result.astype(jnp.bfloat16).reshape(experts, count, width)
        returned = lax.all_to_all(result, "expert", split_axis=0, concat_axis=0, tiled=True)
        return (returned, received)

    def micro_step(carry, inputs):
        grad_qkv, grad_proj, grad_router, grad_gains, grad_inner, grad_down = carry
        patch, upstream, item_block, routes = inputs
        items = item_block[0]
        source = patch.astype(jnp.float32)
        inv_first = lax.rsqrt(jnp.mean(source * source, axis=1, keepdims=True) + norm_eps)
        unit_first = source * inv_first
        normed_in = (unit_first * gain_attn).astype(jnp.bfloat16)
        mixed = jnp.dot(normed_in, qkv_low, preferred_element_type=jnp.float32)
        cosine, sine = rotary_tables(items)
        query = rotate(mixed[:, :width].reshape(length, HEADS, HEAD), cosine, sine).astype(
            jnp.bfloat16
        )
        keys = rotate(
            mixed[:, width : 2 * width].reshape(length, HEADS, HEAD), cosine, sine
        ).astype(jnp.bfloat16)
        values = mixed[:, 2 * width :].reshape(length, HEADS, HEAD).astype(jnp.bfloat16)
        same_item = items[:, None] == items[None, :]
        scores = masked_scores(query, keys, same_item)
        peak = jnp.max(scores, axis=2, keepdims=True)
        weights = jnp.exp(scores - peak)
        totals = jnp.sum(weights, axis=2, keepdims=True)
        probs_low = (weights / totals).astype(jnp.bfloat16)
        log_total = peak + jnp.log(totals)
        attended = jnp.einsum("hqk,khe->qhe", probs_low, values, preferred_element_type=jnp.float32)
        attended = attended.reshape(length, width).astype(jnp.bfloat16)
        middle = source + jnp.dot(attended, proj_low, preferred_element_type=jnp.float32)
        inv_second = lax.rsqrt(jnp.mean(middle * middle, axis=1, keepdims=True) + norm_eps)
        unit_second = middle * inv_second
        normed_mid = (unit_second * gain_ffn).astype(jnp.bfloat16)
        logits = jnp.dot(normed_mid, router_low, preferred_element_type=jnp.float32)
        chosen = jnp.take_along_axis(logits, routes, axis=1)
        gates = jax.nn.softmax(chosen, axis=1)
        flat_ids = routes.reshape(length * top)
        hits = (flat_ids[:, None] == expert_numbers[None, :]).astype(jnp.int32)
        rank = jnp.sum(jnp.cumsum(hits, axis=0) * hits, axis=1) - 1
        slots = flat_ids * capacity + rank
        copies = jnp.repeat(normed_mid, top, axis=0)
        outgoing = jnp.zeros((experts * capacity, width), jnp.bfloat16).at[slots].set(copies)
        outgoing = outgoing.reshape(experts, capacity, width)
        returned, kept_inputs = expert_forward(
            lax.all_to_all(outgoing, "expert", split_axis=0, concat_axis=0, tiled=True)
        )
        picked = (
            returned.reshape(experts * capacity, width)[slots]
            .reshape(length, top, width)
            .astype(jnp.float32)
        )
        combined = jnp.sum(gates[:, :, None] * picked, axis=1)
        block_out = (middle + combined).astype(jnp.bfloat16)
        upstream_full = upstream.astype(jnp.float32)
        grad_gate = jnp.sum(upstream_full[:, None, :] * picked, axis=2)
        grad_chosen = gates * (grad_gate - jnp.sum(gates * grad_gate, axis=1, keepdims=True))
        route_hits = (routes[:, :, None] == expert_numbers[None, None, :]).astype(jnp.float32)
        grad_logits = jnp.sum(grad_chosen[:, :, None] * route_hits, axis=1).astype(jnp.bfloat16)
        grad_router_now = jnp.dot(normed_mid.T, grad_logits, preferred_element_type=jnp.float32)
        grad_mid = jnp.dot(grad_logits, router_low.T, preferred_element_type=jnp.float32)
        grad_slots = (
            (gates[:, :, None] * upstream_full[:, None, :])
            .astype(jnp.bfloat16)
            .reshape(length * top, width)
        )
        grad_outgoing = (
            jnp.zeros((experts * capacity, width), jnp.bfloat16).at[slots].set(grad_slots)
        )
        grad_outgoing = grad_outgoing.reshape(experts, capacity, width)
        incoming, inputs_back = (
            lax.all_to_all(grad_outgoing, "expert", split_axis=0, concat_axis=0, tiled=True),
            lax.all_to_all(outgoing, "expert", split_axis=0, concat_axis=0, tiled=True),
        )
        grid_in = inputs_back.reshape(expert_count, local_experts, capacity, width)
        grid_grad = incoming.reshape(expert_count, local_experts, capacity, width)
        both = jnp.einsum("sjcd,jdf->sjcf", grid_in, inner_low, preferred_element_type=jnp.float32)
        gate_part = both[..., :hidden_width]
        up_part = both[..., hidden_width:]
        sigma = jax.nn.sigmoid(gate_part)
        activated = jax.nn.silu(gate_part)
        hidden = (activated * up_part).astype(jnp.bfloat16)
        grad_hidden = jnp.einsum(
            "sjcd,jfd->sjcf", grid_grad, down_low, preferred_element_type=jnp.float32
        )
        grad_down_now = jnp.einsum(
            "sjcf,sjcd->jfd", hidden, grid_grad, preferred_element_type=jnp.float32
        )
        grad_both = jnp.concatenate(
            [
                grad_hidden * up_part * sigma * (1.0 + gate_part * (1.0 - sigma)),
                grad_hidden * activated,
            ],
            axis=3,
        ).astype(jnp.bfloat16)
        grad_inner_now = jnp.einsum(
            "sjcd,sjcf->jdf", grid_in, grad_both, preferred_element_type=jnp.float32
        )
        grad_copies = jnp.einsum(
            "sjcf,jdf->sjcd", grad_both, inner_low, preferred_element_type=jnp.float32
        )
        grad_copies = grad_copies.astype(jnp.bfloat16).reshape(experts, capacity, width)
        grad_back = lax.all_to_all(grad_copies, "expert", split_axis=0, concat_axis=0, tiled=True)
        grad_picked = grad_back.reshape(experts * capacity, width)[slots].reshape(
            length, top, width
        )
        grad_mid = grad_mid + jnp.sum(grad_picked.astype(jnp.float32), axis=1)
        grad_unit_second = grad_mid * gain_ffn
        grad_gain_ffn = jnp.sum(grad_mid * unit_second, axis=0)
        grad_middle = upstream_full + inv_second * (
            grad_unit_second
            - unit_second * jnp.mean(grad_unit_second * unit_second, axis=1, keepdims=True)
        )
        grad_branch = grad_middle.astype(jnp.bfloat16)
        grad_proj_now = jnp.dot(attended.T, grad_branch, preferred_element_type=jnp.float32)
        grad_attended = jnp.dot(grad_branch, proj_low.T, preferred_element_type=jnp.float32)
        grad_attended = grad_attended.astype(jnp.bfloat16).reshape(length, HEADS, HEAD)
        probs_again = jnp.exp(masked_scores(query, keys, same_item) - log_total)
        grad_probs = jnp.einsum(
            "qhe,khe->hqk", grad_attended, values, preferred_element_type=jnp.float32
        )
        grad_values = jnp.einsum(
            "hqk,qhe->khe", probs_low, grad_attended, preferred_element_type=jnp.float32
        )
        grad_scores = probs_again * (
            grad_probs - jnp.sum(probs_again * grad_probs, axis=2, keepdims=True)
        )
        grad_scores = grad_scores.astype(jnp.bfloat16)
        grad_query = (
            jnp.einsum("hqk,khe->qhe", grad_scores, keys, preferred_element_type=jnp.float32)
            * 0.125
        )
        grad_keys = (
            jnp.einsum("hqk,qhe->khe", grad_scores, query, preferred_element_type=jnp.float32)
            * 0.125
        )
        grad_mixed = jnp.concatenate(
            [
                rotate(grad_query, cosine, -sine).reshape(length, width),
                rotate(grad_keys, cosine, -sine).reshape(length, width),
                grad_values.reshape(length, width),
            ],
            axis=1,
        ).astype(jnp.bfloat16)
        grad_qkv_now = jnp.dot(normed_in.T, grad_mixed, preferred_element_type=jnp.float32)
        grad_normed = jnp.dot(grad_mixed, qkv_low.T, preferred_element_type=jnp.float32)
        grad_unit_first = grad_normed * gain_attn
        grad_gain_attn = jnp.sum(grad_normed * unit_first, axis=0)
        patch_grad = grad_middle + inv_first * (
            grad_unit_first
            - unit_first * jnp.mean(grad_unit_first * unit_first, axis=1, keepdims=True)
        )
        new_carry = (
            grad_qkv + grad_qkv_now,
            grad_proj + grad_proj_now,
            grad_router + grad_router_now,
            grad_gains + jnp.stack([grad_gain_attn, grad_gain_ffn]),
            grad_inner + grad_inner_now,
            grad_down + grad_down_now,
        )
        return (new_carry, (block_out, patch_grad))

    start = (
        jnp.zeros(qkv_master.shape, jnp.float32),
        jnp.zeros(proj_master.shape, jnp.float32),
        jnp.zeros(router_master.shape, jnp.float32),
        jnp.zeros(gains_master.shape, jnp.float32),
        jnp.zeros(inner_low.shape, jnp.float32),
        jnp.zeros(down_low.shape, jnp.float32),
    )
    totals, outputs = lax.scan(micro_step, start, (patches, out_grad, item_ids, expert_ids))
    grad_qkv, grad_proj, grad_router, grad_gains = lax.psum(
        (totals[0], totals[1], totals[2], totals[3]), ("dp", "expert")
    )
    grad_inner, grad_down = (
        lax.psum_scatter(totals[4], "dp", scatter_dimension=1, tiled=True),
        lax.psum_scatter(totals[5], "dp", scatter_dimension=1, tiled=True),
    )
    qkv_new = adamw(qkv_master, qkv_first, qkv_second, grad_qkv, 0.1, 0.1)
    proj_new = adamw(proj_master, proj_first, proj_second, grad_proj, 0.4, 0.1)
    router_new = adamw(router_master, router_first, router_second, grad_router, 0.07, 0.1)
    gains_new = adamw(gains_master, gains_first, gains_second, grad_gains, 0.4, 0.0)
    inner_new = adamw(inner_master, inner_first, inner_second, grad_inner, 0.1, 0.1)
    down_new = adamw(down_master, down_first, down_second, grad_down, 0.15, 0.1)
    return (
        outputs[0],
        outputs[1],
        qkv_new[0],
        qkv_new[1],
        qkv_new[2],
        proj_new[0],
        proj_new[1],
        proj_new[2],
        router_new[0],
        router_new[1],
        router_new[2],
        gains_new[0],
        gains_new[1],
        gains_new[2],
        inner_new[0],
        inner_new[1],
        inner_new[2],
        down_new[0],
        down_new[1],
        down_new[2],
    )


F32 = jnp.float32
BF16 = jnp.bfloat16
QB = 128


def iota(shape, axis):
    return lax.broadcasted_iota(jnp.int32, shape, axis)


def dot_nn(a, b):
    return jnp.dot(a, b, preferred_element_type=F32)


def dot_nt(a, b):
    return lax.dot_general(a, b, (((1,), (1,)), ((), ())), preferred_element_type=F32)


def dot_tn(a, b):
    return lax.dot_general(a, b, (((0,), (0,)), ((), ())), preferred_element_type=F32)


def swap_halves(v, low_lane):
    width = v.shape[1]
    half = HEAD // 2
    return jnp.where(low_lane, pltpu.roll(v, width - half, 1), pltpu.roll(v, half, 1))


def turn(v, cos_row, sin_row, low_lane):
    return v * cos_row + swap_halves(v, low_lane) * sin_row


def rope_table(item_max):
    half = HEAD // 2
    offset = np.arange(item_max, dtype=np.float32)
    freqs = np.float32(10000.0) ** (-np.arange(half, dtype=np.float32) / np.float32(half))
    angles = (offset[:, None] * freqs[None, :]).astype(np.float32)
    cosine, sine = np.cos(angles), np.sin(angles)
    return np.concatenate([cosine] * 4 + [-sine, sine] * 2, axis=1).astype(np.float32)


def windows(length):
    found = []
    for start in range(0, length, QB):
        low = max(0, start - QB)
        high = min(length, start + 2 * QB)
        found.append((start, low, high))
    return found


def row_norm(values):
    return lax.rsqrt(jnp.mean(values * values, axis=1, keepdims=True) + norm_eps)


def positions(item_row, length):
    eye = iota((length, length), 0) == iota((length, length), 1)
    col = jnp.sum(jnp.where(eye, item_row, 0.0), axis=1, keepdims=True)
    before = jnp.sum(jnp.where(item_row < col, 1.0, 0.0), axis=1, keepdims=True)
    offset = iota((length, 1), 0) - before.astype(jnp.int32)
    return col, offset


def rope_rows(offset, table, length, width):
    spots = table.shape[0]
    pick = jnp.where(iota((length, spots), 1) == offset, 1.0, 0.0)
    both = jnp.dot(pick, table, precision=lax.Precision.HIGHEST, preferred_element_type=F32)
    copies = width // 128
    return (
        jnp.concatenate([both[:, :128]] * copies, axis=1),
        jnp.concatenate([both[:, 128:]] * copies, axis=1),
    )


def attend_kernel(patches, items, qkv_w, proj_w, gains, table, mixed_o, probs_o, att_o, mid_o, nm_o):
    packs, length, width = patches.shape
    pairs = width // 128
    low_lane = iota((1, width), 1) % HEAD < HEAD // 2
    first_head = iota((1, 128), 1) < HEAD
    mask_a = jnp.where(first_head, 1.0, 0.0).astype(BF16)
    mask_b = jnp.where(first_head, 0.0, 1.0).astype(BF16)
    top_rows = iota((128, 1), 0) < HEAD

    def pack(p, carry):
        source = patches[p].astype(F32)
        normed = (source * row_norm(source) * gains[0:1, :]).astype(BF16)
        mixed = dot_nn(normed, qkv_w[...])
        item_row = items[p].astype(F32)
        item_col, offset = positions(item_row, length)
        cos_row, sin_row = rope_rows(offset, table[...], length, width)
        mixed_o[p, :, :width] = turn(mixed[:, :width], cos_row, sin_row, low_lane).astype(BF16)
        mixed_o[p, :, width : 2 * width] = turn(
            mixed[:, width : 2 * width], cos_row, sin_row, low_lane
        ).astype(BF16)
        mixed_o[p, :, 2 * width :] = mixed[:, 2 * width :].astype(BF16)
        for pair in range(pairs):
            lanes = slice(128 * pair, 128 * pair + 128)
            key_lanes = slice(width + 128 * pair, width + 128 * pair + 128)
            values_t = mixed[:, 2 * width + 128 * pair : 2 * width + 128 * pair + 128].T.astype(BF16)
            for block, (start, low, high) in enumerate(windows(length)):
                query = mixed_o[p, start : start + QB, lanes] * 0.125
                query = jnp.concatenate([query * mask_a, query * mask_b], axis=0)
                scores = dot_nt(mixed_o[p, low:high, key_lanes], query)
                here = item_row[:, start : start + QB]
                same = item_col[low:high] == jnp.concatenate([here, here], axis=1)
                scores = jnp.where(same, scores, -1e30)
                peak = jnp.max(scores, axis=0, keepdims=True)
                weights = jnp.exp(scores - peak)
                total = jnp.sum(weights, axis=0, keepdims=True)
                probs = (weights * (1.0 / total)).astype(BF16)
                probs_o[p, pair, block, : high - low] = probs
                out = dot_nn(values_t[:, low:high], probs)
                out = jnp.where(top_rows, out[:, :QB], out[:, QB:])
                att_o[p, start : start + QB, lanes] = out.T.astype(BF16)
        middle = source + dot_nn(att_o[p], proj_w[...])
        mid_o[p] = middle
        nm_o[p] = (middle * row_norm(middle) * gains[1:2, :]).astype(BF16)
        return carry

    lax.fori_loop(0, packs, pack, 0)


def unpack(weights, inner_w, down_w):
    copies, width = weights.shape[1], inner_w.shape[0]
    deep, span = width // copies, down_w.shape[0] // copies
    for d in range(copies):
        for block in range(inner_w.shape[1] // width):
            inner_w[d * deep : d * deep + deep, block * width : block * width + width] = weights[
                0, d, block * deep : block * deep + deep, :
            ]
        down_w[d * span : d * span + span, :] = weights[0, d, width:, :]


def expert_kernel(
    nm, upstream, ids, router_w, weights,
    part, back_o, glog_o,
    both_s, rank_s, gate_s, gg_s, x_s, hid_s, go_s, gb_s, y_s, inner_w, down_w,
):
    packs, length, width = nm.shape
    experts = router_w.shape[0]
    hidden_width = down_w.shape[0]
    cap = x_s.shape[0] // packs
    expert = pl.program_id(0)

    @pl.when(expert == 0)
    def _():
        earlier = jnp.where(iota((length, length), 0) < iota((length, length), 1), 1.0, 0.0).astype(BF16)

        def prepare(p, carry):
            both_s[p, :, :width] = nm[p]
            both_s[p, :, width:] = upstream[p]
            logits = dot_nt(router_w[...], nm[p])
            number = iota((experts, length), 0)
            hit0 = number == ids[p, 0:1, :]
            hit1 = number == ids[p, 1:2, :]
            chosen0 = jnp.sum(jnp.where(hit0, logits, 0.0), axis=0, keepdims=True)
            chosen1 = jnp.sum(jnp.where(hit1, logits, 0.0), axis=0, keepdims=True)
            peak = jnp.maximum(chosen0, chosen1)
            e0 = jnp.exp(chosen0 - peak)
            e1 = jnp.exp(chosen1 - peak)
            total = e0 + e1
            gate_s[p] = jnp.where(hit0, e0 / total, 0.0) + jnp.where(hit1, e1 / total, 0.0)
            named = jnp.where(hit0, 1.0, jnp.where(hit1, 1.0, 0.0))
            rank = dot_nn(named.astype(BF16), earlier)
            rank_s[p] = jnp.where(named > 0.5, rank, -1.0)
            return carry

        lax.fori_loop(0, packs, prepare, 0)

    unpack(weights, inner_w, down_w)

    def rows(p, carry):
        here = pl.ds(pl.multiple_of(p * cap, cap), cap)
        rank = rank_s[p, pl.ds(expert, 1), :]
        gate_row = gate_s[p, pl.ds(expert, 1), :]
        pick = iota((cap, length), 0).astype(F32) == rank
        chosen = jnp.where(pick, 1.0, 0.0).astype(BF16)
        taken = dot_nn(chosen, both_s[p])
        gate_col = jnp.sum(jnp.where(pick, gate_row, 0.0), axis=1, keepdims=True)
        x = taken[:, :width].astype(BF16)
        g = taken[:, width:]
        x_s[here, :] = x
        grad_out = (gate_col * g).astype(BF16)
        go_s[here, :] = grad_out
        gate = dot_nn(x, inner_w[:, :hidden_width])
        up = dot_nn(x, inner_w[:, hidden_width:])
        sigma = 1.0 / (1.0 + jnp.exp(-gate))
        active = gate * sigma
        hidden = (active * up).astype(BF16)
        hid_s[here, :] = hidden
        result = dot_nn(hidden, down_w[...]).astype(BF16).astype(F32)
        spot = pl.ds(pl.multiple_of(expert * cap, cap), cap)
        y_s[p, spot, :width] = (gate_col * result).astype(BF16)
        grad_gate = jnp.sum(g * result, axis=1, keepdims=True)
        gg_s[p, pl.ds(expert, 1), :] = jnp.sum(jnp.where(pick, grad_gate, 0.0), axis=0, keepdims=True)
        grad_hidden = dot_nt(grad_out, down_w[...])
        gb_s[here, :hidden_width] = (grad_hidden * up * sigma * (1.0 + gate * (1.0 - sigma))).astype(BF16)
        gb_s[here, hidden_width:] = (grad_hidden * active).astype(BF16)
        y_s[p, spot, width:] = dot_nt(gb_s[here, :], inner_w[...]).astype(BF16)
        return carry

    lax.fori_loop(0, packs, rows, 0)
    copies = part.shape[1]
    deep, span = width // copies, hidden_width // copies
    for block in range(2 * hidden_width // width):
        lanes = slice(block * width, block * width + width)
        grad = dot_tn(x_s[...], gb_s[:, lanes]).astype(BF16)
        for d in range(copies):
            part[0, d, block * deep : block * deep + deep, :] = grad[d * deep : d * deep + deep]
    grad = dot_tn(hid_s[...], go_s[...]).astype(BF16)
    for d in range(copies):
        part[0, d, width:, :] = grad[d * span : d * span + span]

    @pl.when(expert == experts - 1)
    def _():
        def finish(p, carry):
            ranks = rank_s[p].T
            slot = iota((length, cap), 1).astype(F32)
            pieces = [
                jnp.where(ranks[:, e : e + 1] == slot, 1.0, 0.0).astype(BF16) for e in range(experts)
            ]
            back = dot_nn(jnp.concatenate(pieces, axis=1), y_s[p])
            number = iota((experts, length), 0)
            gate = gate_s[p]
            grad_gate = gg_s[p]
            mean = jnp.sum(gate * grad_gate, axis=0, keepdims=True)
            hit = rank_s[p] > -0.5
            grad_logits = jnp.where(hit, gate * (grad_gate - mean), 0.0).astype(BF16)
            glog_o[p] = grad_logits
            back_o[p, :, :width] = back[:, :width]
            back_o[p, :, width:] = back[:, width:] + dot_tn(grad_logits, router_w[...])
            return carry

        lax.fori_loop(0, packs, finish, 0)


def return_kernel(
    patches, upstream, items, qkv_w, proj_w, gains, table, mixed, probs, att, mid, nm, back, glog,
    block_o, patch_o, tail_o,
    normed_s, branch_s, datt_s, dmix_s, dkv_s, small_g,
):
    packs, length, width = patches.shape
    pairs = width // 128
    experts = glog.shape[1]
    low_lane = iota((1, width), 1) % HEAD < HEAD // 2
    first_head = iota((1, 128), 1) < HEAD
    mask_a = jnp.where(first_head, 1.0, 0.0).astype(BF16)
    mask_b = jnp.where(first_head, 0.0, 1.0).astype(BF16)
    top_rows = iota((128, 1), 0) < HEAD
    small_g[...] = jnp.zeros(small_g.shape, F32)

    def pack(p, carry):
        rows = pl.ds(pl.multiple_of(p * length, length), length)
        source = patches[p].astype(F32)
        gain0, gain1 = gains[0:1, :], gains[1:2, :]
        middle = mid[p]
        inv = row_norm(middle)
        unit = middle * inv
        block_o[p] = (middle + back[p, :, :width]).astype(BF16)
        grad_mid = back[p, :, width:]
        small_g[experts : experts + 1, :] += jnp.zeros((1, width), F32)
        small_g[experts + 1 : experts + 2, :] += jnp.sum(grad_mid * unit, axis=0, keepdims=True)
        small_g[0:experts, :] += dot_nn(glog[p], nm[p])
        grad_unit = grad_mid * gain1
        grad_middle = upstream[p].astype(F32) + inv * (
            grad_unit - unit * jnp.mean(grad_unit * unit, axis=1, keepdims=True)
        )
        patch_o[p] = grad_middle
        branch = grad_middle.astype(BF16)
        branch_s[rows, :] = branch
        datt_s[...] = dot_nt(branch, proj_w[...]).astype(BF16)
        dkv_s[...] = jnp.zeros(dkv_s.shape, F32)
        item_row = items[p].astype(F32)
        item_col, offset = positions(item_row, length)
        cos_row, sin_row = rope_rows(offset, table[...], length, width)
        for pair in range(pairs):
            lanes = slice(128 * pair, 128 * pair + 128)
            key_lanes = slice(width + 128 * pair, width + 128 * pair + 128)
            value_lanes = slice(2 * width + 128 * pair, 2 * width + 128 * pair + 128)
            keys_t = mixed[p, :, key_lanes].astype(F32).T.astype(BF16)
            for block, (start, low, high) in enumerate(windows(length)):
                query = mixed[p, start : start + QB, lanes] * 0.125
                query = jnp.concatenate([query * mask_a, query * mask_b], axis=0)
                datt = datt_s[start : start + QB, lanes]
                datt = jnp.concatenate([datt * mask_a, datt * mask_b], axis=0)
                prob = probs[p, pair, block, : high - low]
                dprob = dot_nt(mixed[p, low:high, value_lanes], datt)
                weight = prob.astype(F32)
                mean = jnp.sum(weight * dprob, axis=0, keepdims=True)
                dscore = (weight * (dprob - mean)).astype(BF16)
                dkv_s[low:high, key_lanes] += dot_nn(dscore, query)
                dkv_s[low:high, value_lanes] += dot_nn(prob, datt)
                dquery = dot_nn(keys_t[:, low:high], dscore)
                dquery = jnp.where(top_rows, dquery[:, :QB], dquery[:, QB:])
                dkv_s[start : start + QB, lanes] = dquery.T * 0.125
        dmix_s[rows, :width] = turn(dkv_s[:, :width], cos_row, -sin_row, low_lane).astype(BF16)
        dmix_s[rows, width : 2 * width] = turn(
            dkv_s[:, width : 2 * width], cos_row, -sin_row, low_lane
        ).astype(BF16)
        dmix_s[rows, 2 * width :] = dkv_s[:, 2 * width :].astype(BF16)
        grad_normed = dot_nt(dmix_s[rows, :], qkv_w[...])
        inv_in = row_norm(source)
        unit_in = source * inv_in
        normed_s[rows, :] = (unit_in * gain0).astype(BF16)
        small_g[experts : experts + 1, :] += jnp.sum(grad_normed * unit_in, axis=0, keepdims=True)
        grad_unit_in = grad_normed * gain0
        patch_o[p] += inv_in * (
            grad_unit_in - unit_in * jnp.mean(grad_unit_in * unit_in, axis=1, keepdims=True)
        )
        return carry

    lax.fori_loop(0, packs, pack, 0)
    flat = jnp.concatenate([att[p] for p in range(packs)], axis=0)
    tail_o[...] = jnp.zeros(tail_o.shape, BF16)
    for block in range(4):
        if block < 3:
            grad = dot_tn(normed_s[...], dmix_s[:, block * width : block * width + width])
        else:
            grad = dot_tn(flat, branch_s[...])
        lay_tail(tail_o, block, grad.astype(BF16))
    tail_o[0, 0, tail_o.shape[2] - 16 :, :] = small_g[...].astype(BF16)


def tail_rows(width, devices):
    return 4 * width // devices + 16


def lay_tail(tail, block, grad):
    ex, dp, rows, width = tail.shape
    rows = rows - 16
    each = width // rows
    for piece in range(each):
        number = block * each + piece
        tail[number // dp, number % dp, :rows, :] = grad[piece * rows : piece * rows + rows]


MESH_ID = pl.DeviceIdType.MESH


class Place:
    def __init__(self, line):
        self.line = line
        dp, ex = lax.axis_index("dp"), lax.axis_index("expert")
        self.x, self.core = lax.div(dp, 2), lax.rem(dp, 2)
        self.z, self.y = lax.div(ex, 2), lax.rem(ex, 2)

    def device(self, flip_x=0, flip_y=0, flip_core=0, z=None):
        x = 1 - self.x if flip_x else self.x
        y = 1 - self.y if flip_y else self.y
        core = 1 - self.core if flip_core else self.core
        return (2 * x + core, 2 * (self.z if z is None else z) + y)

    def levels(self):
        found = [(0, self.z, None)]
        for away in range(1, self.line):
            found.append((away, self.z - away, self.z >= away))
            found.append((away, self.z + away, self.z + away < self.line))
        return found

    def greet(self):
        barrier = pltpu.get_barrier_semaphore()

        def signal(device):
            pl.semaphore_signal(barrier, inc=1, device_id=device, device_id_type=MESH_ID)

        for device in (self.device(1), self.device(0, 1), self.device(0, 0, 1)):
            signal(device)
        pl.when(self.z > 0)(lambda: signal(self.device(z=self.z - 1)))
        pl.when(self.z + 1 < self.line)(lambda: signal(self.device(z=self.z + 1)))
        ends = (self.z == 0).astype(jnp.int32) + (self.z + 1 == self.line).astype(jnp.int32)
        pl.semaphore_wait(barrier, 5 - ends)


def both(*tests):
    tests = [t for t in tests if t is not None]
    if not tests:
        return None
    found = tests[0]
    for t in tests[1:]:
        found = jnp.logical_and(found, t)
    return found


def only(test, body):
    if test is None:
        body()
    else:
        pl.when(test)(body)


class Wires:
    def __init__(self, send_sem):
        self.send_sem = send_sem
        self.sent = []

    def send(self, source, target, arrival, device, test=None):
        copy = pltpu.make_async_remote_copy(
            src_ref=source,
            dst_ref=target,
            send_sem=self.send_sem.at[len(self.sent)],
            recv_sem=arrival,
            device_id=device,
            device_id_type=MESH_ID,
        )
        only(test, copy.start)
        self.sent.append((copy, test))

    def arrived(self, target, arrival, device, test=None):
        copy = pltpu.make_async_remote_copy(
            src_ref=target,
            dst_ref=target,
            send_sem=self.send_sem.at[0],
            recv_sem=arrival,
            device_id=device,
            device_id_type=MESH_ID,
        )
        only(test, copy.wait_recv)

    def finish(self):
        for copy, test in self.sent:
            only(test, copy.wait_send)


class Gather:
    def __init__(self, place, shard, full, send_sem, recv_sem, copy_sem):
        self.place, self.shard, self.full = place, shard, full
        self.recv_sem, self.copy_sem = recv_sem, copy_sem
        self.wires = Wires(send_sem)

    def at(self, device):
        return self.full.at[device[1], device[0]]

    def ready(self, device):
        return self.recv_sem.at[device[1], device[0]]

    def pass_on(self, origin, to, test=None, source=None):
        source = self.at(origin) if source is None else source
        self.wires.send(source, self.at(origin), self.ready(origin), to, test)

    def wait(self, origin, test=None):
        self.wires.arrived(self.at(origin), self.ready(origin), self.place.device(0, 0, 1), test)

    def start(self):
        place = self.place
        me = place.device()
        up, down = place.z + 1 < place.line, place.z > 0
        self.pass_on(me, place.device(z=place.z + 1), up, self.shard)
        self.pass_on(me, place.device(z=place.z - 1), down, self.shard)
        self.pass_on(me, place.device(1), None, self.shard)
        self.pass_on(me, place.device(0, 1), None, self.shard)
        self.pass_on(me, place.device(0, 0, 1), None, self.shard)
        self.own = pltpu.make_async_copy(self.shard, self.at(me), self.copy_sem)
        self.own.start()

    def column(self, away):
        place = self.place
        for dist, level, test in place.levels():
            if dist != away:
                continue
            origin = place.device(z=level)
            self.wait(origin, test)
            if level is not place.z:
                upward = jnp.logical_and(level < place.z, place.z + 1 < place.line)
                downward = jnp.logical_and(level > place.z, place.z > 0)
                self.pass_on(origin, place.device(z=place.z + 1), both(test, upward))
                self.pass_on(origin, place.device(z=place.z - 1), both(test, downward))
            self.pass_on(origin, place.device(1), test)
            self.pass_on(origin, place.device(0, 1), test)
            self.pass_on(origin, place.device(0, 0, 1), test)

    def square(self, away):
        place = self.place
        for dist, level, test in place.levels():
            if dist != away:
                continue
            over_x, over_y = place.device(1, z=level), place.device(0, 1, z=level)
            self.wait(over_x, test)
            if dist % 2 == 0:
                self.pass_on(over_x, place.device(0, 1), test)
            self.pass_on(over_x, place.device(0, 0, 1), test)
            self.wait(over_y, test)
            if dist % 2 == 1:
                self.pass_on(over_y, place.device(1), test)
            self.pass_on(over_y, place.device(0, 0, 1), test)

    def corner(self, away):
        place = self.place
        for dist, level, test in place.levels():
            if dist != away:
                continue
            across = place.device(1, 1, z=level)
            self.wait(across, test)
            self.pass_on(across, place.device(0, 0, 1), test)

    def partner(self, flip_x, flip_y, away):
        place = self.place
        for dist, level, test in place.levels():
            if dist == away:
                self.wait(place.device(flip_x, flip_y, 1, z=level), test)


def gather_kernel(line, shard, full, send_sem, recv_sem, copy_sem):
    place = Place(line)
    place.greet()
    gather = Gather(place, shard, full, send_sem, recv_sem, copy_sem)
    gather.start()
    for away in range(1, line):
        gather.column(away)
        gather.square(away - 1)
    gather.square(line - 1)
    for away in range(line):
        gather.corner(away)
    for flip_x in range(2):
        for flip_y in range(2):
            for away in range(line):
                gather.partner(flip_x, flip_y, away)
    gather.own.wait()
    gather.wires.finish()


def run_gather(shard, slot):
    rows, width = shard.shape
    dp, ex = lax.axis_size("dp"), lax.axis_size("expert")
    line = ex // 2
    return pl.pallas_call(
        functools.partial(gather_kernel, line),
        out_shape=jax.ShapeDtypeStruct((ex, dp, rows, width), shard.dtype),
        in_specs=[pl.BlockSpec(memory_space=pltpu.VMEM)],
        out_specs=pl.BlockSpec(memory_space=pl.ANY),
        scratch_shapes=[
            pltpu.SemaphoreType.DMA((32 * line,)),
            pltpu.SemaphoreType.DMA((ex, dp)),
            pltpu.SemaphoreType.DMA,
        ],
        compiler_params=pltpu.CompilerParams(
            collective_id=slot, has_side_effects=True, vmem_limit_bytes=60 * 1024 * 1024
        ),
        name="gather",
    )(shard)


OWN, OVER_X, OVER_Y, ACROSS = 0, 1, 2, 3
FLIPS = ((0, 0), (1, 0), (0, 1), (1, 1))


class Reduce:
    def __init__(self, place, part, sums, core_in, diag_in, side_in, line_in, send_sem, recv, copy_sem):
        self.place, self.part, self.sums = place, part, sums
        self.core_in, self.diag_in, self.side_in, self.line_in = core_in, diag_in, side_in, line_in
        self.core_sem, self.diag_sem, self.side_sem, self.line_sem = recv
        self.copy_sem = copy_sem
        self.wires = Wires(send_sem)
        self.loads = []

    def shard(self, group, level, flip_core=0):
        device = self.place.device(*FLIPS[group], flip_core, z=level)
        return self.part.at[device[1], device[0]]

    def pick(self, away):
        return [(level, test) for dist, level, test in self.place.levels() if dist == away]

    def share(self, group, away):
        for level, test in self.pick(away):
            load = pltpu.make_async_copy(
                self.shard(group, level), self.sums.at[group, level], self.copy_sem.at[group, level]
            )
            only(test, load.start)
            self.wires.send(
                self.shard(group, level, 1),
                self.core_in.at[group, level],
                self.core_sem.at[group, level],
                self.place.device(0, 0, 1),
                test,
            )

    def add(self, group, level, value):
        self.sums[group, level] = (self.sums[group, level].astype(F32) + value.astype(F32)).astype(BF16)

    def merge(self, group, away):
        place = self.place
        for level, test in self.pick(away):

            def body(level=level):
                pltpu.make_async_copy(
                    self.shard(group, level), self.sums.at[group, level], self.copy_sem.at[group, level]
                ).wait()
                self.wires.arrived(
                    self.core_in.at[group, level],
                    self.core_sem.at[group, level],
                    place.device(0, 0, 1),
                )
                self.add(group, level, self.core_in[group, level])

            only(test, body)

    def send_across(self, away):
        place = self.place
        side = OVER_Y if away % 2 == 0 else OVER_X
        for level, test in self.pick(away):
            self.wires.send(
                self.sums.at[ACROSS, level],
                self.diag_in.at[level],
                self.diag_sem.at[level],
                place.device(*FLIPS[side]),
                test,
            )

    def send_side(self, away):
        place = self.place
        group = OVER_X if away % 2 == 0 else OVER_Y
        for level, test in self.pick(away):

            def body(level=level):
                self.wires.arrived(self.diag_in.at[level], self.diag_sem.at[level], place.device(1))
                self.add(group, level, self.diag_in[level])

            only(test, body)
            for side in (OVER_X, OVER_Y):
                self.wires.send(
                    self.sums.at[side, level],
                    self.side_in.at[side - 1, level],
                    self.side_sem.at[side - 1, level],
                    place.device(*FLIPS[side]),
                    test,
                )

    def collect(self, level, test):
        place = self.place

        def body():
            total = self.sums[OWN, level].astype(F32)
            for side in range(2):
                self.wires.arrived(
                    self.side_in.at[side, level], self.side_sem.at[side, level], place.device(1)
                )
                total = total + self.side_in[side, level].astype(F32)
            self.sums[OWN, level] = total.astype(BF16)

        only(test, body)

    def send_line(self, away):
        place = self.place
        for level, test in self.pick(away):
            self.collect(level, test)
            below = level is not place.z and level < place.z
            for way, test_way, far in (
                (0, jnp.logical_and(test, level < place.z), place.z + 1 < place.line),
                (1, jnp.logical_and(test, level > place.z), place.z > 0),
            ):

                def body(level=level, way=way):
                    self.wires.arrived(
                        self.line_in.at[way, level], self.line_sem.at[way, level], place.device(1)
                    )
                    self.add(OWN, level, self.line_in[way, level])

                only(jnp.logical_and(test_way, far), body)
                self.wires.send(
                    self.sums.at[OWN, level],
                    self.line_in.at[way, level],
                    self.line_sem.at[way, level],
                    place.device(z=place.z - 1 if way == 0 else place.z + 1),
                    test_way,
                )

    def finish(self, out):
        place = self.place
        level = place.z
        total = self.sums[OWN, level].astype(F32)
        for side in range(2):
            self.wires.arrived(
                self.side_in.at[side, level], self.side_sem.at[side, level], place.device(1)
            )
            total = total + self.side_in[side, level].astype(F32)
        out[...] = total
        for way, far in ((0, place.z + 1 < place.line), (1, place.z > 0)):

            def body(way=way):
                self.wires.arrived(
                    self.line_in.at[way, level], self.line_sem.at[way, level], place.device(1)
                )
                out[...] += self.line_in[way, level].astype(F32)

            only(far, body)
        self.wires.finish()


def reduce_kernel(
    line, part, out, sums, core_in, diag_in, side_in, line_in,
    send_sem, core_sem, diag_sem, side_sem, line_sem, copy_sem,
):
    place = Place(line)
    place.greet()
    reduce = Reduce(
        place, part, sums, core_in, diag_in, side_in, line_in,
        send_sem, (core_sem, diag_sem, side_sem, line_sem), copy_sem,
    )
    order = list(range(line - 1, -1, -1))
    for group in (ACROSS, OVER_X, OVER_Y, OWN):
        for away in order:
            reduce.share(group, away)
    for away in order:
        reduce.merge(ACROSS, away)
        reduce.send_across(away)
    for group in (OVER_X, OVER_Y, OWN):
        for away in order:
            reduce.merge(group, away)
    for away in order:
        reduce.send_side(away)
    for away in order[:-1]:
        reduce.send_line(away)
    reduce.finish(out)


def run_reduce(part, slot):
    ex, dp, rows, width = part.shape
    line = ex // 2
    dma = pltpu.SemaphoreType.DMA
    slab = lambda *dims: pltpu.VMEM(dims + (rows, width), part.dtype)
    return pl.pallas_call(
        functools.partial(reduce_kernel, line),
        out_shape=jax.ShapeDtypeStruct((rows, width), F32),
        in_specs=[pl.BlockSpec(memory_space=pl.ANY)],
        out_specs=pl.BlockSpec(memory_space=pltpu.VMEM),
        scratch_shapes=[
            slab(4, line), slab(4, line), slab(line), slab(2, line), slab(2, line),
            dma((32 * line,)), dma((4, line)), dma((line,)), dma((2, line)), dma((2, line)), dma((4, line)),
        ],
        compiler_params=pltpu.CompilerParams(
            collective_id=slot, has_side_effects=True, vmem_limit_bytes=60 * 1024 * 1024
        ),
        name="reduce",
    )(part)


def whole(count):
    return [pl.BlockSpec(memory_space=pltpu.VMEM)] * count


LIMIT = pltpu.CompilerParams(vmem_limit_bytes=60 * 1024 * 1024)


def run_attend(patches, items, qkv_w, proj_w, gains, table):
    packs, length, width = patches.shape
    pairs = width // 128
    blocks = length // QB
    shapes = (
        jax.ShapeDtypeStruct((packs, length, 3 * width), BF16),
        jax.ShapeDtypeStruct((packs, pairs, blocks, 3 * QB, 2 * QB), BF16),
        jax.ShapeDtypeStruct((packs, length, width), BF16),
        jax.ShapeDtypeStruct((packs, length, width), F32),
        jax.ShapeDtypeStruct((packs, length, width), BF16),
    )
    return pl.pallas_call(
        attend_kernel,
        out_shape=shapes,
        in_specs=whole(6),
        out_specs=tuple(whole(5)),
        compiler_params=LIMIT,
        name="attend",
    )(patches, items, qkv_w, proj_w, gains, table)


def run_experts(nm, upstream, ids, router_w, weights, hidden):
    packs, length, width = nm.shape
    experts, copies, rows, _ = weights.shape
    cap = 2 * length * 2 // experts
    fixed3 = lambda e: (0, 0, 0)
    each = lambda e: (e, 0, 0, 0)
    grid_spec = pltpu.PrefetchScalarGridSpec(
        num_scalar_prefetch=0,
        grid=(experts,),
        in_specs=[
            pl.BlockSpec((packs, length, width), fixed3),
            pl.BlockSpec((packs, length, width), fixed3),
            pl.BlockSpec((packs, 2, length), fixed3),
            pl.BlockSpec((experts, width), lambda e: (0, 0)),
            pl.BlockSpec((1, copies, rows, width), each),
        ],
        out_specs=(
            pl.BlockSpec((1, copies, rows, width), each),
            pl.BlockSpec((packs, length, 2 * width), fixed3),
            pl.BlockSpec((packs, experts, length), fixed3),
        ),
        scratch_shapes=[
            pltpu.VMEM((packs, length, 2 * width), BF16),
            pltpu.VMEM((packs, experts, length), F32),
            pltpu.VMEM((packs, experts, length), F32),
            pltpu.VMEM((packs, experts, length), F32),
            pltpu.VMEM((packs * cap, width), BF16),
            pltpu.VMEM((packs * cap, hidden), BF16),
            pltpu.VMEM((packs * cap, width), BF16),
            pltpu.VMEM((packs * cap, 2 * hidden), BF16),
            pltpu.VMEM((packs, experts * cap, 2 * width), BF16),
            pltpu.VMEM((width, 2 * hidden), BF16),
            pltpu.VMEM((hidden, width), BF16),
        ],
    )
    return pl.pallas_call(
        expert_kernel,
        out_shape=(
            jax.ShapeDtypeStruct(weights.shape, BF16),
            jax.ShapeDtypeStruct((packs, length, 2 * width), F32),
            jax.ShapeDtypeStruct((packs, experts, length), BF16),
        ),
        grid_spec=grid_spec,
        compiler_params=LIMIT,
        name="experts",
    )(nm, upstream, ids, router_w, weights)


def run_return(
    tail_shape, patches, upstream, items, qkv_w, proj_w, gains, table, mixed, probs, att, mid, nm, back, glog
):
    packs, length, width = patches.shape
    shapes = (
        jax.ShapeDtypeStruct((packs, length, width), BF16),
        jax.ShapeDtypeStruct((packs, length, width), F32),
        jax.ShapeDtypeStruct(tail_shape, BF16),
    )
    return pl.pallas_call(
        return_kernel,
        out_shape=shapes,
        in_specs=whole(14),
        out_specs=tuple(whole(3)),
        scratch_shapes=[
            pltpu.VMEM((packs * length, width), BF16),
            pltpu.VMEM((packs * length, width), BF16),
            pltpu.VMEM((length, width), BF16),
            pltpu.VMEM((packs * length, 3 * width), BF16),
            pltpu.VMEM((length, 3 * width), F32),
            pltpu.VMEM((16, width), F32),
        ],
        compiler_params=LIMIT,
        name="backward",
    )(patches, upstream, items, qkv_w, proj_w, gains, table, mixed, probs, att, mid, nm, back, glog)


def fast(
    patches, out_grad, item_ids, expert_ids,
    qkv_master, qkv_first, qkv_second,
    proj_master, proj_first, proj_second,
    router_master, router_first, router_second,
    gains_master, gains_first, gains_second,
    inner_master, inner_first, inner_second,
    down_master, down_first, down_second,
):
    width = patches.shape[2]
    experts = router_master.shape[1]
    hidden = down_master.shape[1] * lax.axis_size("dp")
    devices = lax.axis_size("dp") * lax.axis_size("expert")
    deep = inner_master.shape[1]
    blocks = inner_master.shape[2] // width
    shard = jnp.concatenate(
        [
            jnp.swapaxes(inner_master[0].reshape(deep, blocks, width), 0, 1).reshape(blocks * deep, width),
            down_master[0],
        ],
        axis=0,
    ).astype(BF16)
    weights = run_gather(shard, 0)
    qkv_w = qkv_master.astype(BF16)
    proj_w = proj_master.astype(BF16)
    router_w = router_master.T.astype(BF16)
    ids = jnp.swapaxes(expert_ids, 1, 2)
    table = jnp.asarray(rope_table(QB))
    tail_shape = (lax.axis_size("expert"), lax.axis_size("dp"), tail_rows(width, devices), width)
    mixed, probs, att, mid, nm = run_attend(patches, item_ids, qkv_w, proj_w, gains_master, table)
    part, back, glog = run_experts(nm, out_grad, ids, router_w, weights, hidden)
    block_out, patch_grad, tail = run_return(
        tail_shape,
        patches, out_grad, item_ids, qkv_w, proj_w, gains_master, table, mixed, probs, att, mid, nm, back, glog
    )
    grad = run_reduce(part, 1)
    grad_inner = jnp.swapaxes(grad[: blocks * deep].reshape(blocks, deep, width), 0, 1).reshape(
        inner_master.shape
    )
    grad_down = grad[blocks * deep :].reshape(down_master.shape)
    tail = run_gather(run_reduce(tail, 2).astype(BF16), 3).astype(F32)
    small = tail[0, 0, tail_shape[2] - 16 :]
    attn = tail[:, :, : tail_shape[2] - 16].reshape(4, width, width)
    grad_qkv = jnp.swapaxes(attn[:3], 0, 1).reshape(width, 3 * width)
    qkv_new = adamw(qkv_master, qkv_first, qkv_second, grad_qkv, 0.1, 0.1)
    proj_new = adamw(proj_master, proj_first, proj_second, attn[3], 0.4, 0.1)
    router_new = adamw(router_master, router_first, router_second, small[:experts].T, 0.07, 0.1)
    gains_new = adamw(gains_master, gains_first, gains_second, small[experts : experts + 2], 0.4, 0.0)
    inner_new = adamw(inner_master, inner_first, inner_second, grad_inner, 0.1, 0.1)
    down_new = adamw(down_master, down_first, down_second, grad_down, 0.15, 0.1)
    return (block_out, patch_grad) + qkv_new + proj_new + router_new + gains_new + inner_new + down_new


GATHER_LIMIT = 16 * 1024 * 1024


def step(*args):
    inner_master, down_master = args[16], args[19]
    experts = inner_master.shape[0] * lax.axis_size("expert")
    entries = inner_master.shape[1] * inner_master.shape[2] + down_master.shape[1] * down_master.shape[2]
    weight_bytes = 2 * experts * entries * lax.axis_size("dp")
    square = lax.axis_size("dp") == 4 and inner_master.shape[0] == 1 and lax.axis_size("expert") == experts
    return (fast if square and weight_bytes <= GATHER_LIMIT else local)(*args)


def solution(mesh):
    in_specs = (
        P(None, ("dp", "expert"), None),
        P(None, ("dp", "expert"), None),
        P(None, ("dp", "expert"), None),
        P(None, ("dp", "expert"), None),
        P(),
        P(),
        P(),
        P(),
        P(),
        P(),
        P(),
        P(),
        P(),
        P(),
        P(),
        P(),
        P("expert", "dp", None),
        P("expert", "dp", None),
        P("expert", "dp", None),
        P("expert", "dp", None),
        P("expert", "dp", None),
        P("expert", "dp", None),
    )
    out_specs = (
        P(None, ("dp", "expert"), None),
        P(None, ("dp", "expert"), None),
        P(),
        P(),
        P(),
        P(),
        P(),
        P(),
        P(),
        P(),
        P(),
        P(),
        P(),
        P(),
        P("expert", "dp", None),
        P("expert", "dp", None),
        P("expert", "dp", None),
        P("expert", "dp", None),
        P("expert", "dp", None),
        P("expert", "dp", None),
    )
    return jax.shard_map(step, mesh=mesh, in_specs=in_specs, out_specs=out_specs, check_vma=False)
```

```python
import functools

import jax
import jax.numpy as jnp
import numpy as np
from jax import lax
from jax.experimental import pallas as pl
from jax.experimental.pallas import tpu as pltpu
from jax.sharding import PartitionSpec as P

HEADS = 6
HEAD = 64


norm_eps = 1e-06
adam_eps = 1e-08
correction = 0.875


def rotary_tables(item_row):
    length = item_row.shape[0]
    places = jnp.arange(length, dtype=jnp.int32)
    starts = jnp.concatenate([jnp.ones((1,), dtype=bool), item_row[1:] != item_row[:-1]])
    first = lax.cummax(jnp.where(starts, places, 0), axis=0)
    offset = (places - first).astype(jnp.float32)
    half = HEAD // 2
    freqs = 10000.0 ** (-jnp.arange(half, dtype=jnp.float32) / half)
    angles = offset[:, None] * freqs[None, :]
    return (jnp.cos(angles), jnp.sin(angles))


def rotate(vectors, cosine, sine):
    half = vectors.shape[-1] // 2
    first_half = vectors[..., :half]
    second_half = vectors[..., half:]
    cos_part = cosine[:, None, :]
    sin_part = sine[:, None, :]
    return jnp.concatenate(
        [
            first_half * cos_part - second_half * sin_part,
            second_half * cos_part + first_half * sin_part,
        ],
        axis=-1,
    )


def masked_scores(query, keys, same_item):
    scores = jnp.einsum("qhe,khe->hqk", query, keys, preferred_element_type=jnp.float32) * 0.125
    return jnp.where(same_item[None], scores, -1e30)


def adamw(weight, first, second, grad, rate, decay):
    first_new = 0.5 * first + 0.5 * grad
    second_new = 0.5 * second + 0.5 * grad * grad
    update = first_new / correction / (jnp.sqrt(second_new / correction) + adam_eps)
    return (weight - rate * (update + decay * weight), first_new, second_new)


def local(
    patches,
    out_grad,
    item_ids,
    expert_ids,
    qkv_master,
    qkv_first,
    qkv_second,
    proj_master,
    proj_first,
    proj_second,
    router_master,
    router_first,
    router_second,
    gains_master,
    gains_first,
    gains_second,
    inner_master,
    inner_first,
    inner_second,
    down_master,
    down_first,
    down_second,
):
    expert_count = lax.axis_size("expert")
    local_experts = inner_master.shape[0]
    experts = expert_count * local_experts
    length = patches.shape[1]
    width = patches.shape[2]
    top = expert_ids.shape[2]
    capacity = 2 * length * top // experts
    hidden_width = down_master.shape[1] * lax.axis_size("dp")
    inner_low, down_low = (
        lax.all_gather(inner_master.astype(jnp.bfloat16), "dp", axis=1, tiled=True),
        lax.all_gather(down_master.astype(jnp.bfloat16), "dp", axis=1, tiled=True),
    )
    qkv_low = qkv_master.astype(jnp.bfloat16)
    proj_low = proj_master.astype(jnp.bfloat16)
    router_low = router_master.astype(jnp.bfloat16)
    gain_attn = gains_master[0]
    gain_ffn = gains_master[1]
    expert_numbers = jnp.arange(experts, dtype=jnp.int32)

    def expert_forward(received):
        count = received.shape[1]
        grid = received.reshape(expert_count, local_experts, count, width)
        both = jnp.einsum("sjcd,jdf->sjcf", grid, inner_low, preferred_element_type=jnp.float32)
        hidden = (jax.nn.silu(both[..., :hidden_width]) * both[..., hidden_width:]).astype(
            jnp.bfloat16
        )
        result = jnp.einsum("sjcf,jfd->sjcd", hidden, down_low, preferred_element_type=jnp.float32)
        result = result.astype(jnp.bfloat16).reshape(experts, count, width)
        returned = lax.all_to_all(result, "expert", split_axis=0, concat_axis=0, tiled=True)
        return (returned, received)

    def micro_step(carry, inputs):
        grad_qkv, grad_proj, grad_router, grad_gains, grad_inner, grad_down = carry
        patch, upstream, item_block, routes = inputs
        items = item_block[0]
        source = patch.astype(jnp.float32)
        inv_first = lax.rsqrt(jnp.mean(source * source, axis=1, keepdims=True) + norm_eps)
        unit_first = source * inv_first
        normed_in = (unit_first * gain_attn).astype(jnp.bfloat16)
        mixed = jnp.dot(normed_in, qkv_low, preferred_element_type=jnp.float32)
        cosine, sine = rotary_tables(items)
        query = rotate(mixed[:, :width].reshape(length, HEADS, HEAD), cosine, sine).astype(
            jnp.bfloat16
        )
        keys = rotate(
            mixed[:, width : 2 * width].reshape(length, HEADS, HEAD), cosine, sine
        ).astype(jnp.bfloat16)
        values = mixed[:, 2 * width :].reshape(length, HEADS, HEAD).astype(jnp.bfloat16)
        same_item = items[:, None] == items[None, :]
        scores = masked_scores(query, keys, same_item)
        peak = jnp.max(scores, axis=2, keepdims=True)
        weights = jnp.exp(scores - peak)
        totals = jnp.sum(weights, axis=2, keepdims=True)
        probs_low = (weights / totals).astype(jnp.bfloat16)
        log_total = peak + jnp.log(totals)
        attended = jnp.einsum("hqk,khe->qhe", probs_low, values, preferred_element_type=jnp.float32)
        attended = attended.reshape(length, width).astype(jnp.bfloat16)
        middle = source + jnp.dot(attended, proj_low, preferred_element_type=jnp.float32)
        inv_second = lax.rsqrt(jnp.mean(middle * middle, axis=1, keepdims=True) + norm_eps)
        unit_second = middle * inv_second
        normed_mid = (unit_second * gain_ffn).astype(jnp.bfloat16)
        logits = jnp.dot(normed_mid, router_low, preferred_element_type=jnp.float32)
        chosen = jnp.take_along_axis(logits, routes, axis=1)
        gates = jax.nn.softmax(chosen, axis=1)
        flat_ids = routes.reshape(length * top)
        hits = (flat_ids[:, None] == expert_numbers[None, :]).astype(jnp.int32)
        rank = jnp.sum(jnp.cumsum(hits, axis=0) * hits, axis=1) - 1
        slots = flat_ids * capacity + rank
        copies = jnp.repeat(normed_mid, top, axis=0)
        outgoing = jnp.zeros((experts * capacity, width), jnp.bfloat16).at[slots].set(copies)
        outgoing = outgoing.reshape(experts, capacity, width)
        returned, kept_inputs = expert_forward(
            lax.all_to_all(outgoing, "expert", split_axis=0, concat_axis=0, tiled=True)
        )
        picked = (
            returned.reshape(experts * capacity, width)[slots]
            .reshape(length, top, width)
            .astype(jnp.float32)
        )
        combined = jnp.sum(gates[:, :, None] * picked, axis=1)
        block_out = (middle + combined).astype(jnp.bfloat16)
        upstream_full = upstream.astype(jnp.float32)
        grad_gate = jnp.sum(upstream_full[:, None, :] * picked, axis=2)
        grad_chosen = gates * (grad_gate - jnp.sum(gates * grad_gate, axis=1, keepdims=True))
        route_hits = (routes[:, :, None] == expert_numbers[None, None, :]).astype(jnp.float32)
        grad_logits = jnp.sum(grad_chosen[:, :, None] * route_hits, axis=1).astype(jnp.bfloat16)
        grad_router_now = jnp.dot(normed_mid.T, grad_logits, preferred_element_type=jnp.float32)
        grad_mid = jnp.dot(grad_logits, router_low.T, preferred_element_type=jnp.float32)
        grad_slots = (
            (gates[:, :, None] * upstream_full[:, None, :])
            .astype(jnp.bfloat16)
            .reshape(length * top, width)
        )
        grad_outgoing = (
            jnp.zeros((experts * capacity, width), jnp.bfloat16).at[slots].set(grad_slots)
        )
        grad_outgoing = grad_outgoing.reshape(experts, capacity, width)
        incoming, inputs_back = (
            lax.all_to_all(grad_outgoing, "expert", split_axis=0, concat_axis=0, tiled=True),
            lax.all_to_all(outgoing, "expert", split_axis=0, concat_axis=0, tiled=True),
        )
        grid_in = inputs_back.reshape(expert_count, local_experts, capacity, width)
        grid_grad = incoming.reshape(expert_count, local_experts, capacity, width)
        both = jnp.einsum("sjcd,jdf->sjcf", grid_in, inner_low, preferred_element_type=jnp.float32)
        gate_part = both[..., :hidden_width]
        up_part = both[..., hidden_width:]
        sigma = jax.nn.sigmoid(gate_part)
        activated = jax.nn.silu(gate_part)
        hidden = (activated * up_part).astype(jnp.bfloat16)
        grad_hidden = jnp.einsum(
            "sjcd,jfd->sjcf", grid_grad, down_low, preferred_element_type=jnp.float32
        )
        grad_down_now = jnp.einsum(
            "sjcf,sjcd->jfd", hidden, grid_grad, preferred_element_type=jnp.float32
        )
        grad_both = jnp.concatenate(
            [
                grad_hidden * up_part * sigma * (1.0 + gate_part * (1.0 - sigma)),
                grad_hidden * activated,
            ],
            axis=3,
        ).astype(jnp.bfloat16)
        grad_inner_now = jnp.einsum(
            "sjcd,sjcf->jdf", grid_in, grad_both, preferred_element_type=jnp.float32
        )
        grad_copies = jnp.einsum(
            "sjcf,jdf->sjcd", grad_both, inner_low, preferred_element_type=jnp.float32
        )
        grad_copies = grad_copies.astype(jnp.bfloat16).reshape(experts, capacity, width)
        grad_back = lax.all_to_all(grad_copies, "expert", split_axis=0, concat_axis=0, tiled=True)
        grad_picked = grad_back.reshape(experts * capacity, width)[slots].reshape(
            length, top, width
        )
        grad_mid = grad_mid + jnp.sum(grad_picked.astype(jnp.float32), axis=1)
        grad_unit_second = grad_mid * gain_ffn
        grad_gain_ffn = jnp.sum(grad_mid * unit_second, axis=0)
        grad_middle = upstream_full + inv_second * (
            grad_unit_second
            - unit_second * jnp.mean(grad_unit_second * unit_second, axis=1, keepdims=True)
        )
        grad_branch = grad_middle.astype(jnp.bfloat16)
        grad_proj_now = jnp.dot(attended.T, grad_branch, preferred_element_type=jnp.float32)
        grad_attended = jnp.dot(grad_branch, proj_low.T, preferred_element_type=jnp.float32)
        grad_attended = grad_attended.astype(jnp.bfloat16).reshape(length, HEADS, HEAD)
        probs_again = jnp.exp(masked_scores(query, keys, same_item) - log_total)
        grad_probs = jnp.einsum(
            "qhe,khe->hqk", grad_attended, values, preferred_element_type=jnp.float32
        )
        grad_values = jnp.einsum(
            "hqk,qhe->khe", probs_low, grad_attended, preferred_element_type=jnp.float32
        )
        grad_scores = probs_again * (
            grad_probs - jnp.sum(probs_again * grad_probs, axis=2, keepdims=True)
        )
        grad_scores = grad_scores.astype(jnp.bfloat16)
        grad_query = (
            jnp.einsum("hqk,khe->qhe", grad_scores, keys, preferred_element_type=jnp.float32)
            * 0.125
        )
        grad_keys = (
            jnp.einsum("hqk,qhe->khe", grad_scores, query, preferred_element_type=jnp.float32)
            * 0.125
        )
        grad_mixed = jnp.concatenate(
            [
                rotate(grad_query, cosine, -sine).reshape(length, width),
                rotate(grad_keys, cosine, -sine).reshape(length, width),
                grad_values.reshape(length, width),
            ],
            axis=1,
        ).astype(jnp.bfloat16)
        grad_qkv_now = jnp.dot(normed_in.T, grad_mixed, preferred_element_type=jnp.float32)
        grad_normed = jnp.dot(grad_mixed, qkv_low.T, preferred_element_type=jnp.float32)
        grad_unit_first = grad_normed * gain_attn
        grad_gain_attn = jnp.sum(grad_normed * unit_first, axis=0)
        patch_grad = grad_middle + inv_first * (
            grad_unit_first
            - unit_first * jnp.mean(grad_unit_first * unit_first, axis=1, keepdims=True)
        )
        new_carry = (
            grad_qkv + grad_qkv_now,
            grad_proj + grad_proj_now,
            grad_router + grad_router_now,
            grad_gains + jnp.stack([grad_gain_attn, grad_gain_ffn]),
            grad_inner + grad_inner_now,
            grad_down + grad_down_now,
        )
        return (new_carry, (block_out, patch_grad))

    start = (
        jnp.zeros(qkv_master.shape, jnp.float32),
        jnp.zeros(proj_master.shape, jnp.float32),
        jnp.zeros(router_master.shape, jnp.float32),
        jnp.zeros(gains_master.shape, jnp.float32),
        jnp.zeros(inner_low.shape, jnp.float32),
        jnp.zeros(down_low.shape, jnp.float32),
    )
    totals, outputs = lax.scan(micro_step, start, (patches, out_grad, item_ids, expert_ids))
    grad_qkv, grad_proj, grad_router, grad_gains = lax.psum(
        (totals[0], totals[1], totals[2], totals[3]), ("dp", "expert")
    )
    grad_inner, grad_down = (
        lax.psum_scatter(totals[4], "dp", scatter_dimension=1, tiled=True),
        lax.psum_scatter(totals[5], "dp", scatter_dimension=1, tiled=True),
    )
    qkv_new = adamw(qkv_master, qkv_first, qkv_second, grad_qkv, 0.1, 0.1)
    proj_new = adamw(proj_master, proj_first, proj_second, grad_proj, 0.4, 0.1)
    router_new = adamw(router_master, router_first, router_second, grad_router, 0.07, 0.1)
    gains_new = adamw(gains_master, gains_first, gains_second, grad_gains, 0.4, 0.0)
    inner_new = adamw(inner_master, inner_first, inner_second, grad_inner, 0.1, 0.1)
    down_new = adamw(down_master, down_first, down_second, grad_down, 0.15, 0.1)
    return (
        outputs[0],
        outputs[1],
        qkv_new[0],
        qkv_new[1],
        qkv_new[2],
        proj_new[0],
        proj_new[1],
        proj_new[2],
        router_new[0],
        router_new[1],
        router_new[2],
        gains_new[0],
        gains_new[1],
        gains_new[2],
        inner_new[0],
        inner_new[1],
        inner_new[2],
        down_new[0],
        down_new[1],
        down_new[2],
    )


F32 = jnp.float32
BF16 = jnp.bfloat16
QB = 128


def iota(shape, axis):
    return lax.broadcasted_iota(jnp.int32, shape, axis)


def dot_nn(a, b):
    return jnp.dot(a, b, preferred_element_type=F32)


def dot_nt(a, b):
    return lax.dot_general(a, b, (((1,), (1,)), ((), ())), preferred_element_type=F32)


def dot_tn(a, b):
    return lax.dot_general(a, b, (((0,), (0,)), ((), ())), preferred_element_type=F32)


def swap_halves(v, low_lane):
    width = v.shape[1]
    half = HEAD // 2
    return jnp.where(low_lane, pltpu.roll(v, width - half, 1), pltpu.roll(v, half, 1))


def turn(v, cos_row, sin_row, low_lane):
    return v * cos_row + swap_halves(v, low_lane) * sin_row


def rope_table(item_max):
    half = HEAD // 2
    offset = np.arange(item_max, dtype=np.float32)
    freqs = np.float32(10000.0) ** (-np.arange(half, dtype=np.float32) / np.float32(half))
    angles = (offset[:, None] * freqs[None, :]).astype(np.float32)
    cosine, sine = np.cos(angles), np.sin(angles)
    return np.concatenate([cosine] * 4 + [-sine, sine] * 2, axis=1).astype(np.float32)


def windows(length):
    found = []
    for start in range(0, length, QB):
        low = max(0, start - QB)
        high = min(length, start + 2 * QB)
        found.append((start, low, high))
    return found


def row_norm(values):
    return lax.rsqrt(jnp.mean(values * values, axis=1, keepdims=True) + norm_eps)


def positions(item_row, length):
    eye = iota((length, length), 0) == iota((length, length), 1)
    col = jnp.sum(jnp.where(eye, item_row, 0.0), axis=1, keepdims=True)
    before = jnp.sum(jnp.where(item_row < col, 1.0, 0.0), axis=1, keepdims=True)
    offset = iota((length, 1), 0) - before.astype(jnp.int32)
    return col, offset


def rope_rows(offset, table, length, width):
    spots = table.shape[0]
    pick = jnp.where(iota((length, spots), 1) == offset, 1.0, 0.0)
    both = jnp.dot(pick, table, precision=lax.Precision.HIGHEST, preferred_element_type=F32)
    copies = width // 128
    return (
        jnp.concatenate([both[:, :128]] * copies, axis=1),
        jnp.concatenate([both[:, 128:]] * copies, axis=1),
    )


VMEM_BYTES = 64 * 1024 * 1024 - 512 * 1024


MESH_ID = pl.DeviceIdType.MESH


class Place:
    def __init__(self, line):
        self.line = line
        dp, ex = lax.axis_index("dp"), lax.axis_index("expert")
        self.x, self.core = lax.div(dp, 2), lax.rem(dp, 2)
        self.z, self.y = lax.div(ex, 2), lax.rem(ex, 2)

    def device(self, flip_x=0, flip_y=0, flip_core=0, z=None):
        x = 1 - self.x if flip_x else self.x
        y = 1 - self.y if flip_y else self.y
        core = 1 - self.core if flip_core else self.core
        return (2 * x + core, 2 * (self.z if z is None else z) + y)

    def levels(self):
        found = [(0, self.z, None, 0)]
        for away in range(1, self.line):
            found.append((away, self.z - away, lambda a=away: self.z >= a, -1))
            found.append((away, self.z + away, lambda a=away: self.z + a < self.line, 1))
        return found

    def up(self):
        return self.z + 1 < self.line

    def down(self):
        return self.z > 0

    def by_distance(self, i):
        found = 0
        for z in range(self.line):
            order = sorted(range(self.line), key=lambda level: (abs(level - z), level))
            for place, level in enumerate(order):
                hit = jnp.logical_and(self.z == z, i == place).astype(jnp.int32)
                found = found + hit * level
        return found

    def greet(self):
        barrier = pltpu.get_barrier_semaphore()

        def signal(device):
            pl.semaphore_signal(barrier, inc=1, device_id=device, device_id_type=MESH_ID)

        for device in (self.device(1), self.device(0, 1), self.device(0, 0, 1)):
            signal(device)
        pl.when(self.z > 0)(lambda: signal(self.device(z=self.z - 1)))
        pl.when(self.z + 1 < self.line)(lambda: signal(self.device(z=self.z + 1)))
        ends = (self.z == 0).astype(jnp.int32) + (self.z + 1 == self.line).astype(jnp.int32)
        pl.semaphore_wait(barrier, 5 - ends)


def both(*tests):
    tests = [t for t in tests if t is not None]

    def all_of():
        found = tests[0]()
        for t in tests[1:]:
            found = jnp.logical_and(found, t())
        return found

    return all_of if tests else None


def only(test, body):
    if test is None:
        body()
    else:
        pl.when(test())(body)


class Wires:
    def __init__(self, send_sem, like):
        self.send_sem, self.like = send_sem, like
        self.sent = []

    def send(self, source, target, arrival, device, test=None):
        copy = pltpu.make_async_remote_copy(
            src_ref=source,
            dst_ref=target,
            send_sem=self.send_sem.at[len(self.sent)],
            recv_sem=arrival,
            device_id=device,
            device_id_type=MESH_ID,
        )
        only(test, copy.start)
        self.sent.append(test)

    def arrived(self, target, arrival, device, test=None):
        copy = pltpu.make_async_remote_copy(
            src_ref=target,
            dst_ref=target,
            send_sem=self.send_sem.at[0],
            recv_sem=arrival,
            device_id=device,
            device_id_type=MESH_ID,
        )
        only(test, copy.wait_recv)

    def finish(self):
        for number, test in enumerate(self.sent):
            copy = pltpu.make_async_remote_copy(
                src_ref=self.like,
                dst_ref=self.like,
                send_sem=self.send_sem.at[number],
                recv_sem=self.send_sem.at[number],
                device_id=(0, 0),
                device_id_type=MESH_ID,
            )
            only(test, copy.wait_send)


class Gather:
    def __init__(self, place, shard, full, send_sem, recv_sem, copy_sem):
        self.place, self.shard, self.full = place, shard, full
        self.recv_sem, self.copy_sem = recv_sem, copy_sem
        self.wires = Wires(send_sem, shard)

    def at(self, device):
        return self.full.at[device[1], device[0]]

    def ready(self, device):
        return self.recv_sem.at[device[1], device[0]]

    def pass_on(self, origin, to, test=None, source=None):
        source = self.at(origin) if source is None else source
        self.wires.send(source, self.at(origin), self.ready(origin), to, test)

    def wait(self, origin, test=None):
        self.wires.arrived(self.at(origin), self.ready(origin), self.place.device(0, 0, 1), test)

    def start(self):
        place = self.place
        me = place.device()
        self.pass_on(me, place.device(z=place.z + 1), place.up, self.shard)
        self.pass_on(me, place.device(z=place.z - 1), place.down, self.shard)
        self.pass_on(me, place.device(1), None, self.shard)
        self.pass_on(me, place.device(0, 1), None, self.shard)
        self.pass_on(me, place.device(0, 0, 1), None, self.shard)
        self.own = pltpu.make_async_copy(self.shard, self.at(me), self.copy_sem)
        self.own.start()

    def column(self, away):
        place = self.place
        for dist, level, test, way in place.levels():
            if dist != away:
                continue
            origin = place.device(z=level)
            self.wait(origin, test)
            if way < 0:
                self.pass_on(origin, place.device(z=place.z + 1), both(test, place.up))
            if way > 0:
                self.pass_on(origin, place.device(z=place.z - 1), both(test, place.down))
            self.pass_on(origin, place.device(1), test)
            self.pass_on(origin, place.device(0, 1), test)
            self.pass_on(origin, place.device(0, 0, 1), test)

    def square(self, away):
        place = self.place
        for dist, level, test, way in place.levels():
            if dist != away:
                continue
            over_x, over_y = place.device(1, z=level), place.device(0, 1, z=level)
            self.wait(over_x, test)
            if dist % 2 == 0:
                self.pass_on(over_x, place.device(0, 1), test)
            self.pass_on(over_x, place.device(0, 0, 1), test)
            self.wait(over_y, test)
            if dist % 2 == 1:
                self.pass_on(over_y, place.device(1), test)
            self.pass_on(over_y, place.device(0, 0, 1), test)

    def corner(self, away):
        place = self.place
        for dist, level, test, way in place.levels():
            if dist != away:
                continue
            across = place.device(1, 1, z=level)
            self.wait(across, test)
            self.pass_on(across, place.device(0, 0, 1), test)

    def partner(self, flip_x, flip_y, level):
        self.wait(self.place.device(flip_x, flip_y, 1, z=level))


OWN, OVER_X, OVER_Y, ACROSS = 0, 1, 2, 3
FLIPS = ((0, 0), (1, 0), (0, 1), (1, 1))


class Reduce:
    def __init__(self, place, part, sums, core_in, diag_in, side_in, line_in, send_sem, recv, copy_sem):
        self.place, self.part, self.sums = place, part, sums
        self.core_in, self.diag_in, self.side_in, self.line_in = core_in, diag_in, side_in, line_in
        self.core_sem, self.diag_sem, self.side_sem, self.line_sem = recv
        self.copy_sem = copy_sem
        self.wires = Wires(send_sem, core_in.at[0, 0])

    def shard(self, group, level, flip_core=0):
        device = self.place.device(*FLIPS[group], flip_core, z=level)
        return self.part.at[device[1], device[0]]

    def pick(self, away):
        return [(level, test, way) for dist, level, test, way in self.place.levels() if dist == away]

    def share(self, group, away):
        for level, test, way in self.pick(away):
            load = pltpu.make_async_copy(
                self.shard(group, level), self.sums.at[group, level], self.copy_sem.at[group, level]
            )
            only(test, load.start)
            self.wires.send(
                self.shard(group, level, 1),
                self.core_in.at[group, level],
                self.core_sem.at[group, level],
                self.place.device(0, 0, 1),
                test,
            )

    def add(self, group, level, value):
        self.sums[group, level] = (self.sums[group, level].astype(F32) + value.astype(F32)).astype(BF16)

    def merge(self, group, away):
        place = self.place
        for level, test, way in self.pick(away):

            def body(level=level):
                pltpu.make_async_copy(
                    self.shard(group, level), self.sums.at[group, level], self.copy_sem.at[group, level]
                ).wait()
                self.wires.arrived(
                    self.core_in.at[group, level],
                    self.core_sem.at[group, level],
                    place.device(0, 0, 1),
                )
                self.add(group, level, self.core_in[group, level])

            only(test, body)

    def send_across(self, away):
        place = self.place
        side = OVER_Y if away % 2 == 0 else OVER_X
        for level, test, way in self.pick(away):
            self.wires.send(
                self.sums.at[ACROSS, level],
                self.diag_in.at[level],
                self.diag_sem.at[level],
                place.device(*FLIPS[side]),
                test,
            )

    def send_side(self, away):
        place = self.place
        group = OVER_X if away % 2 == 0 else OVER_Y
        for level, test, way in self.pick(away):

            def body(level=level):
                self.wires.arrived(self.diag_in.at[level], self.diag_sem.at[level], place.device(1))
                self.add(group, level, self.diag_in[level])

            only(test, body)
            for side in (OVER_X, OVER_Y):
                self.wires.send(
                    self.sums.at[side, level],
                    self.side_in.at[side - 1, level],
                    self.side_sem.at[side - 1, level],
                    place.device(*FLIPS[side]),
                    test,
                )

    def collect(self, level, test):
        place = self.place

        def body():
            total = self.sums[OWN, level].astype(F32)
            for side in range(2):
                self.wires.arrived(
                    self.side_in.at[side, level], self.side_sem.at[side, level], place.device(1)
                )
                total = total + self.side_in[side, level].astype(F32)
            self.sums[OWN, level] = total.astype(BF16)

        only(test, body)

    def send_line(self, away):
        place = self.place
        for level, test, way in self.pick(away):
            self.collect(level, test)
            lane = 0 if way < 0 else 1

            def body(level=level, lane=lane):
                self.wires.arrived(
                    self.line_in.at[lane, level], self.line_sem.at[lane, level], place.device(1)
                )
                self.add(OWN, level, self.line_in[lane, level])

            only(both(test, place.up if way < 0 else place.down), body)
            self.wires.send(
                self.sums.at[OWN, level],
                self.line_in.at[lane, level],
                self.line_sem.at[lane, level],
                place.device(z=place.z + way),
                test,
            )

    def finish(self, out):
        place = self.place
        level = place.z
        total = self.sums[OWN, level].astype(F32)
        for side in range(2):
            self.wires.arrived(
                self.side_in.at[side, level], self.side_sem.at[side, level], place.device(1)
            )
            total = total + self.side_in[side, level].astype(F32)
        out[...] = total
        for way, far in ((0, place.up), (1, place.down)):

            def body(way=way):
                self.wires.arrived(
                    self.line_in.at[way, level], self.line_sem.at[way, level], place.device(1)
                )
                out[...] += self.line_in[way, level].astype(F32)

            only(far, body)
        self.wires.finish()


def copy_all(copies):
    for copy in copies:
        copy.start()


def attend_pack(p, patches, items, gains, table, qkv_s, proj_s, mixed_s, probs_s, att_s, mid_s, nm_s):
    _, length, width = patches.shape
    pairs = width // 128
    low_lane = iota((1, width), 1) % HEAD < HEAD // 2
    first_head = iota((1, 128), 1) < HEAD
    mask_a = jnp.where(first_head, 1.0, 0.0).astype(BF16)
    mask_b = jnp.where(first_head, 0.0, 1.0).astype(BF16)
    top_rows = iota((128, 1), 0) < HEAD
    source = patches[p].astype(F32)
    normed = (source * row_norm(source) * gains[0:1, :]).astype(BF16)
    mixed = dot_nn(normed, qkv_s[...])
    item_row = items[p].astype(F32)
    item_col, offset = positions(item_row, length)
    cos_row, sin_row = rope_rows(offset, table[...], length, width)
    mixed_s[p, :, :width] = turn(mixed[:, :width], cos_row, sin_row, low_lane).astype(BF16)
    mixed_s[p, :, width : 2 * width] = turn(
        mixed[:, width : 2 * width], cos_row, sin_row, low_lane
    ).astype(BF16)
    mixed_s[p, :, 2 * width :] = mixed[:, 2 * width :].astype(BF16)
    for pair in range(pairs):
        lanes = slice(128 * pair, 128 * pair + 128)
        key_lanes = slice(width + 128 * pair, width + 128 * pair + 128)
        values_t = mixed[:, 2 * width + 128 * pair : 2 * width + 128 * pair + 128].T.astype(BF16)
        for block, (start, low, high) in enumerate(windows(length)):
            query = mixed_s[p, start : start + QB, lanes] * 0.125
            query = jnp.concatenate([query * mask_a, query * mask_b], axis=0)
            scores = dot_nt(mixed_s[p, low:high, key_lanes], query)
            here = item_row[:, start : start + QB]
            same = item_col[low:high] == jnp.concatenate([here, here], axis=1)
            scores = jnp.where(same, scores, -1e30)
            peak = jnp.max(scores, axis=0, keepdims=True)
            weights = jnp.exp(scores - peak)
            total = jnp.sum(weights, axis=0, keepdims=True)
            probs = (weights * (1.0 / total)).astype(BF16)
            probs_s[p, pair, block, : high - low] = probs
            out = dot_nn(values_t[:, low:high], probs)
            out = jnp.where(top_rows, out[:, :QB], out[:, QB:])
            att_s[p, start : start + QB, lanes] = out.T.astype(BF16)
    middle = source + dot_nn(att_s[p], proj_s[...])
    mid_s[p] = middle
    nm_s[p] = (middle * row_norm(middle) * gains[1:2, :]).astype(BF16)


class Experts:
    def __init__(self, refs, cap):
        (
            self.both_s, self.rank_s, self.gate_s, self.gg_s, self.x_s, self.hid_s, self.go_s, self.gb_s,
            self.y_s, self.inner_w, self.down_w,
        ) = refs
        self.cap = cap

    def prepare(self, p, nm, upstream, ids, router_w):
        _, length, width = nm.shape
        experts = router_w.shape[0]
        earlier = jnp.where(iota((length, length), 0) < iota((length, length), 1), 1.0, 0.0).astype(BF16)
        self.both_s[p, :, :width] = nm[p]
        self.both_s[p, :, width:] = upstream[p]
        logits = dot_nt(router_w[...], nm[p])
        number = iota((experts, length), 0)
        hit0 = number == ids[p, 0:1, :]
        hit1 = number == ids[p, 1:2, :]
        chosen0 = jnp.sum(jnp.where(hit0, logits, 0.0), axis=0, keepdims=True)
        chosen1 = jnp.sum(jnp.where(hit1, logits, 0.0), axis=0, keepdims=True)
        peak = jnp.maximum(chosen0, chosen1)
        e0 = jnp.exp(chosen0 - peak)
        e1 = jnp.exp(chosen1 - peak)
        total = e0 + e1
        self.gate_s[p] = jnp.where(hit0, e0 / total, 0.0) + jnp.where(hit1, e1 / total, 0.0)
        named = jnp.where(hit0, 1.0, jnp.where(hit1, 1.0, 0.0))
        rank = dot_nn(named.astype(BF16), earlier)
        self.rank_s[p] = jnp.where(named > 0.5, rank, -1.0)

    def rows(self, p, expert):
        cap = self.cap
        _, length, wide = self.both_s.shape
        width, hidden_width = wide // 2, self.hid_s.shape[1]
        here = pl.ds(pl.multiple_of(p * cap, cap), cap)
        rank = self.rank_s[p, pl.ds(expert, 1), :]
        gate_row = self.gate_s[p, pl.ds(expert, 1), :]
        pick = iota((cap, length), 0).astype(F32) == rank
        chosen = jnp.where(pick, 1.0, 0.0).astype(BF16)
        taken = dot_nn(chosen, self.both_s[p])
        gate_col = jnp.sum(jnp.where(pick, gate_row, 0.0), axis=1, keepdims=True)
        x = taken[:, :width].astype(BF16)
        g = taken[:, width:]
        self.x_s[here, :] = x
        grad_out = (gate_col * g).astype(BF16)
        self.go_s[here, :] = grad_out
        gate = dot_nn(x, self.inner_w[:, :hidden_width])
        up = dot_nn(x, self.inner_w[:, hidden_width:])
        sigma = 1.0 / (1.0 + jnp.exp(-gate))
        active = gate * sigma
        hidden = (active * up).astype(BF16)
        self.hid_s[here, :] = hidden
        result = dot_nn(hidden, self.down_w[...]).astype(BF16).astype(F32)
        spot = pl.ds(pl.multiple_of(expert * cap, cap), cap)
        self.y_s[p, spot, :width] = (gate_col * result).astype(BF16)
        grad_gate = jnp.sum(g * result, axis=1, keepdims=True)
        self.gg_s[p, pl.ds(expert, 1), :] = jnp.sum(
            jnp.where(pick, grad_gate, 0.0), axis=0, keepdims=True
        )
        grad_hidden = dot_nt(grad_out, self.down_w[...])
        self.gb_s[here, :hidden_width] = (
            grad_hidden * up * sigma * (1.0 + gate * (1.0 - sigma))
        ).astype(BF16)
        self.gb_s[here, hidden_width:] = (grad_hidden * active).astype(BF16)
        self.y_s[p, spot, width:] = dot_nt(self.gb_s[here, :], self.inner_w[...]).astype(BF16)

    def grads(self, part):
        copies, _, width = part.shape
        hidden_width = self.hid_s.shape[1]
        deep, span = width // copies, hidden_width // copies
        for block in range(2 * hidden_width // width):
            lanes = slice(block * width, block * width + width)
            grad = dot_tn(self.x_s[...], self.gb_s[:, lanes]).astype(BF16)
            for d in range(copies):
                part[d, block * deep : block * deep + deep, :] = grad[d * deep : d * deep + deep]
        grad = dot_tn(self.hid_s[...], self.go_s[...]).astype(BF16)
        for d in range(copies):
            part[d, width:, :] = grad[d * span : d * span + span]

    def finish(self, p, router_w, mid, block_o, gmid_o, glog_o):
        cap = self.cap
        _, length, wide = self.both_s.shape
        width = wide // 2
        experts = router_w.shape[0]
        ranks = self.rank_s[p].T
        slot = iota((length, cap), 1).astype(F32)
        pieces = [
            jnp.where(ranks[:, e : e + 1] == slot, 1.0, 0.0).astype(BF16) for e in range(experts)
        ]
        back = dot_nn(jnp.concatenate(pieces, axis=1), self.y_s[p])
        gate = self.gate_s[p]
        grad_gate = self.gg_s[p]
        mean = jnp.sum(gate * grad_gate, axis=0, keepdims=True)
        hit = self.rank_s[p] > -0.5
        grad_logits = jnp.where(hit, gate * (grad_gate - mean), 0.0).astype(BF16)
        glog_o[p] = grad_logits
        block_o[p] = (mid[p] + back[:, :width]).astype(BF16)
        gmid_o[p] = back[:, width:] + dot_tn(grad_logits, router_w[...])


def unpack(weights, inner_w, down_w):
    copies, _, width = weights.shape
    deep, span = width // copies, down_w.shape[0] // copies
    for d in range(copies):
        for block in range(inner_w.shape[1] // width):
            inner_w[d * deep : d * deep + deep, block * width : block * width + width] = weights[
                d, block * deep : block * deep + deep, :
            ]
        down_w[d * span : d * span + span, :] = weights[d, width:, :]


def forward_kernel(
    line, cap,
    shard, patches, upstream, items, ids, qkv_w, proj_w, router_w, gains, table,
    full, part, mixed_o, probs_o, att_o, mid_o, nm_o, block_o, gmid_o, glog_o,
    qkv_s, proj_s, mixed_s, probs_s, att_s, mid_s, nm_s, wbuf, pbuf,
    both_s, rank_s, gate_s, gg_s, x_s, hid_s, go_s, gb_s, y_s, inner_s, down_s,
    send_sem, recv_sem, own_sem, save_sem, fetch_sem, part_sem,
):
    packs = patches.shape[0]
    experts = router_w.shape[0]
    place = Place(line)
    place.greet()
    gather = Gather(place, shard, full, send_sem, recv_sem, own_sem)
    gather.start()
    qkv_s[...] = qkv_w[...].astype(BF16)
    proj_s[...] = proj_w[...].astype(BF16)
    work = Experts((both_s, rank_s, gate_s, gg_s, x_s, hid_s, go_s, gb_s, y_s, inner_s, down_s), cap)
    saves = ((mixed_s, mixed_o), (probs_s, probs_o), (att_s, att_o), (mid_s, mid_o), (nm_s, nm_o))

    def save(n, p):
        return pltpu.make_async_copy(saves[n][0].at[p], saves[n][1].at[p], save_sem.at[n, p])

    def pack(p, carry):
        attend_pack(p, patches, items, gains, table, qkv_s, proj_s, mixed_s, probs_s, att_s, mid_s, nm_s)
        for n in range(len(saves)):
            save(n, p).start()
        work.prepare(p, nm_s, upstream, ids, router_w)
        for k in range(1, line):

            def relay(k=k):
                gather.column(k)
                gather.square(k - 1)

            pl.when(p == min(k - 1, packs - 1))(relay)
        return carry

    lax.fori_loop(0, packs, pack, 0)

    def number(i):
        near = int(i < line) if isinstance(i, int) else (i < line).astype(jnp.int32)
        level = place.by_distance(i - (1 - near) * line)
        side = near * place.y + (1 - near) * (1 - place.y)
        return level, 2 * level + side

    def fetch(i):
        return pltpu.make_async_copy(full.at[number(i)[1]], wbuf.at[lax.rem(i, 2)], fetch_sem.at[lax.rem(i, 2)])

    def store(i):
        return pltpu.make_async_copy(pbuf.at[lax.rem(i, 2)], part.at[number(i)[1]], part_sem.at[lax.rem(i, 2)])

    def arrive(i):
        level = number(i)[0]

        def near():
            gather.partner(0, 0, level)
            gather.partner(1, 0, level)

        def far():
            gather.partner(0, 1, level)
            gather.partner(1, 1, level)

        if isinstance(i, int):
            (near if i < line else far)()
        else:
            pl.when(i < line)(near)
            pl.when(i >= line)(far)

    gather.own.wait()
    arrive(0)
    fetch(0).start()

    def one(i, carry):
        pl.when(i == line - 2)(lambda: gather.square(line - 1))

        def corners(found):
            for k in found:
                gather.corner(k)

        pl.when(i == line - 1)(lambda: corners((0, 1)))
        pl.when(i == line)(lambda: corners(range(2, line)))

        def ahead():
            arrive(i + 1)
            fetch(i + 1).start()

        pl.when(i + 1 < experts)(ahead)
        fetch(i).wait()
        unpack(wbuf.at[lax.rem(i, 2)], inner_s, down_s)
        expert = number(i)[1]

        def rows(p, inner_carry):
            work.rows(p, expert)
            return inner_carry

        lax.fori_loop(0, packs, rows, 0)
        pl.when(i >= 2)(lambda: store(i - 2).wait())
        work.grads(pbuf.at[lax.rem(i, 2)])
        store(i).start()
        return carry

    lax.fori_loop(0, experts, one, 0)

    def finish(p, carry):
        work.finish(p, router_w, mid_s, block_o, gmid_o, glog_o)
        return carry

    lax.fori_loop(0, packs, finish, 0)
    store(experts - 2).wait()
    store(experts - 1).wait()
    for n in range(len(saves)):
        for p in range(packs):
            save(n, p).wait()
    gather.wires.finish()


def run_forward(shard, patches, upstream, items, ids, qkv_w, proj_w, router_w, gains, table, hidden, slot):
    packs, length, width = patches.shape
    experts = router_w.shape[0]
    dp, ex = lax.axis_size("dp"), lax.axis_size("expert")
    line = ex // 2
    cap = 2 * length * ids.shape[1] // experts
    pairs, blocks = width // 128, length // QB
    rows = shard.shape[0]
    dma = pltpu.SemaphoreType.DMA
    here = pl.BlockSpec(memory_space=pltpu.VMEM)
    away = pl.BlockSpec(memory_space=pl.ANY)
    saved = (
        ((packs, length, 3 * width), BF16),
        ((packs, pairs, blocks, 3 * QB, 2 * QB), BF16),
        ((packs, length, width), BF16),
        ((packs, length, width), F32),
        ((packs, length, width), BF16),
    )
    shapes = (
        ((ex, dp, rows, width), BF16),
        ((ex, dp, rows, width), BF16),
        *saved,
        ((packs, length, width), BF16),
        ((packs, length, width), F32),
        ((packs, experts, length), BF16),
    )
    scratch = (
        ((width, 3 * width), BF16),
        ((width, width), BF16),
        *saved,
        ((2, dp, rows, width), BF16),
        ((2, dp, rows, width), BF16),
        ((packs, length, 2 * width), BF16),
        ((packs, experts, length), F32),
        ((packs, experts, length), F32),
        ((packs, experts, length), F32),
        ((packs * cap, width), BF16),
        ((packs * cap, hidden), BF16),
        ((packs * cap, width), BF16),
        ((packs * cap, 2 * hidden), BF16),
        ((packs, experts * cap, 2 * width), BF16),
        ((width, 2 * hidden), BF16),
        ((hidden, width), BF16),
    )
    return pl.pallas_call(
        functools.partial(forward_kernel, line, cap),
        out_shape=tuple(jax.ShapeDtypeStruct(*s) for s in shapes),
        in_specs=[here] * 10,
        out_specs=(away,) * 7 + (here,) * 3,
        scratch_shapes=[pltpu.VMEM(*s) for s in scratch]
        + [dma((24 * line,)), dma((ex, dp)), dma, dma((5, packs)), dma((2,)), dma((2,))],
        compiler_params=pltpu.CompilerParams(
            collective_id=slot, has_side_effects=True, vmem_limit_bytes=VMEM_BYTES
        ),
        name="forward",
    )(shard, patches, upstream, items, ids, qkv_w, proj_w, router_w, gains, table)


class Backward:
    def __init__(self, refs):
        (
            self.patches, self.upstream, self.items, self.gains, self.table, self.gmid, self.glog,
            self.qkv_s, self.proj_s, self.mixed, self.probs, self.mid, self.nm,
            self.patch_o, self.normed_s, self.branch_s, self.datt_s, self.dmix_s, self.dkv_s, self.small_g,
        ) = refs

    def pack(self, p):
        packs, length, width = self.patches.shape
        pairs = width // 128
        experts = self.glog.shape[1]
        gains, mixed, dkv_s = self.gains, self.mixed, self.dkv_s
        low_lane = iota((1, width), 1) % HEAD < HEAD // 2
        first_head = iota((1, 128), 1) < HEAD
        mask_a = jnp.where(first_head, 1.0, 0.0).astype(BF16)
        mask_b = jnp.where(first_head, 0.0, 1.0).astype(BF16)
        top_rows = iota((128, 1), 0) < HEAD
        rows = pl.ds(pl.multiple_of(p * length, length), length)
        source = self.patches[p].astype(F32)
        gain0, gain1 = gains[0:1, :], gains[1:2, :]
        slot = lax.rem(p, 2)
        middle = self.mid[slot]
        inv = row_norm(middle)
        unit = middle * inv
        grad_mid = self.gmid[p]
        self.small_g[experts + 1 : experts + 2, :] += jnp.sum(grad_mid * unit, axis=0, keepdims=True)
        self.small_g[0:experts, :] += dot_nn(self.glog[p], self.nm[slot])
        grad_unit = grad_mid * gain1
        grad_middle = self.upstream[p].astype(F32) + inv * (
            grad_unit - unit * jnp.mean(grad_unit * unit, axis=1, keepdims=True)
        )
        self.patch_o[p] = grad_middle
        branch = grad_middle.astype(BF16)
        self.branch_s[rows, :] = branch
        self.datt_s[...] = dot_nt(branch, self.proj_s[...]).astype(BF16)
        dkv_s[...] = jnp.zeros(dkv_s.shape, F32)
        item_row = self.items[p].astype(F32)
        item_col, offset = positions(item_row, length)
        cos_row, sin_row = rope_rows(offset, self.table[...], length, width)
        for pair in range(pairs):
            lanes = slice(128 * pair, 128 * pair + 128)
            key_lanes = slice(width + 128 * pair, width + 128 * pair + 128)
            value_lanes = slice(2 * width + 128 * pair, 2 * width + 128 * pair + 128)
            keys_t = mixed[slot, :, key_lanes].astype(F32).T.astype(BF16)
            for block, (start, low, high) in enumerate(windows(length)):
                query = mixed[slot, start : start + QB, lanes] * 0.125
                query = jnp.concatenate([query * mask_a, query * mask_b], axis=0)
                datt = self.datt_s[start : start + QB, lanes]
                datt = jnp.concatenate([datt * mask_a, datt * mask_b], axis=0)
                prob = self.probs[slot, pair, block, : high - low]
                dprob = dot_nt(mixed[slot, low:high, value_lanes], datt)
                weight = prob.astype(F32)
                mean = jnp.sum(weight * dprob, axis=0, keepdims=True)
                dscore = (weight * (dprob - mean)).astype(BF16)
                dkv_s[low:high, key_lanes] += dot_nn(dscore, query)
                dkv_s[low:high, value_lanes] += dot_nn(prob, datt)
                dquery = dot_nn(keys_t[:, low:high], dscore)
                dquery = jnp.where(top_rows, dquery[:, :QB], dquery[:, QB:])
                dkv_s[start : start + QB, lanes] = dquery.T * 0.125
        dmix_s = self.dmix_s
        dmix_s[rows, :width] = turn(dkv_s[:, :width], cos_row, -sin_row, low_lane).astype(BF16)
        dmix_s[rows, width : 2 * width] = turn(
            dkv_s[:, width : 2 * width], cos_row, -sin_row, low_lane
        ).astype(BF16)
        dmix_s[rows, 2 * width :] = dkv_s[:, 2 * width :].astype(BF16)
        grad_normed = dot_nt(dmix_s[rows, :], self.qkv_s[...])
        inv_in = row_norm(source)
        unit_in = source * inv_in
        self.normed_s[rows, :] = (unit_in * gain0).astype(BF16)
        self.small_g[experts : experts + 1, :] += jnp.sum(grad_normed * unit_in, axis=0, keepdims=True)
        grad_unit_in = grad_normed * gain0
        self.patch_o[p] += inv_in * (
            grad_unit_in - unit_in * jnp.mean(grad_unit_in * unit_in, axis=1, keepdims=True)
        )

    def tail(self, att, tail):
        packs, length, width = self.patches.shape
        tail[...] = jnp.zeros(tail.shape, BF16)
        for block in range(4):
            if block < 3:
                grad = dot_tn(self.normed_s[...], self.dmix_s[:, block * width : block * width + width])
            else:
                flat = jnp.concatenate([att[p] for p in range(packs)], axis=0)
                grad = dot_tn(flat, self.branch_s[...])
            lay_tail(tail, block, grad.astype(BF16))
        tail[0, 0, tail.shape[2] - 16 :, :] = self.small_g[...].astype(BF16)


def tail_rows(width, devices):
    return 4 * width // devices + 16


def lay_tail(tail, block, grad):
    ex, dp, rows, width = tail.shape
    rows = rows - 16
    each = width // rows
    for piece in range(each):
        number = block * each + piece
        tail[number // dp, number % dp, :rows, :] = grad[piece * rows : piece * rows + rows]


def backward_kernel(
    line,
    part, patches, upstream, items, qkv_w, proj_w, gains, table, gmid, glog, mixed_i, probs_i, att_i, mid_i, nm_i,
    patch_o, grad_o, tail_o,
    qkv_s, proj_s, mixed, probs, att, mid, nm,
    normed_s, branch_s, datt_s, dmix_s, dkv_s, small_g, tail, tail_sum, tail_low,
    sums, core_in, diag_in, side_in, line_in,
    tsums, tcore_in, tdiag_in, tside_in, tline_in,
    load_sem, send_sem, core_sem, diag_sem, side_sem, line_sem, copy_sem,
    tsend_sem, tcore_sem, tdiag_sem, tside_sem, tline_sem, tcopy_sem,
    gsend_sem, grecv_sem, gown_sem,
):
    packs = patches.shape[0]
    place = Place(line)
    place.greet()
    reduce = Reduce(
        place, part, sums, core_in, diag_in, side_in, line_in,
        send_sem, (core_sem, diag_sem, side_sem, line_sem), copy_sem,
    )
    small = Reduce(
        place, tail, tsums, tcore_in, tdiag_in, tside_in, tline_in,
        tsend_sem, (tcore_sem, tdiag_sem, tside_sem, tline_sem), tcopy_sem,
    )
    order = list(range(line - 1, -1, -1))
    for group in (ACROSS, OVER_X, OVER_Y, OWN):
        for away in order:
            reduce.share(group, away)
    loads = ((mixed_i, mixed), (mid_i, mid), (nm_i, nm), (probs_i, probs), (att_i, att))

    def load(n, p):
        source, target = loads[n]
        return pltpu.make_async_copy(
            source.at[p], target.at[lax.rem(p, target.shape[0])], load_sem.at[n, p]
        )

    for p in range(packs):
        for n in range(len(loads)):
            if p < loads[n][1].shape[0]:
                load(n, p).start()
    qkv_s[...] = qkv_w[...].astype(BF16)
    proj_s[...] = proj_w[...].astype(BF16)
    small_g[...] = jnp.zeros(small_g.shape, F32)
    work = Backward((
        patches, upstream, items, gains, table, gmid, glog,
        qkv_s, proj_s, mixed, probs, mid, nm,
        patch_o, normed_s, branch_s, datt_s, dmix_s, dkv_s, small_g,
    ))
    for away in order:
        reduce.merge(ACROSS, away)
        reduce.send_across(away)
    for group in (OVER_X, OVER_Y, OWN):
        for away in order:
            reduce.merge(group, away)

    def pack(p, carry):
        for n in range(len(loads)):
            load(n, p).wait()
        work.pack(p)

        def ahead():
            for n in range(len(loads) - 1):
                load(n, p + 2).start()

        pl.when(p + 2 < packs)(ahead)

        def first():
            for away in order[:2]:
                reduce.send_side(away)

        def second():
            for away in order[2:]:
                reduce.send_side(away)
            reduce.send_line(order[0])

        pl.when(p == 0)(first)
        pl.when(p == 1)(second)
        return carry

    lax.fori_loop(0, packs, pack, 0)
    reduce.send_line(order[1])
    work.tail(att, tail)
    for group in (ACROSS, OVER_X, OVER_Y, OWN):
        for away in order:
            small.share(group, away)
    for away in order[2:-1]:
        reduce.send_line(away)
    for away in order:
        small.merge(ACROSS, away)
        small.send_across(away)
    for group in (OVER_X, OVER_Y, OWN):
        for away in order:
            small.merge(group, away)
    for away in order:
        small.send_side(away)
    for away in order[:-1]:
        small.send_line(away)
    small.finish(tail_sum)
    tail_low[...] = tail_sum[...].astype(BF16)
    gather = Gather(place, tail_low, tail_o, gsend_sem, grecv_sem, gown_sem)
    gather.start()
    reduce.finish(grad_o)
    for away in range(1, line):
        gather.column(away)
        gather.square(away - 1)
    gather.square(line - 1)
    for away in range(line):
        gather.corner(away)
    for flip_x in range(2):
        for flip_y in range(2):
            for away in range(line):
                for dist, level, test, way in place.levels():
                    if dist == away:
                        only(test, lambda: gather.partner(flip_x, flip_y, level))
    gather.own.wait()
    gather.wires.finish()


def run_backward(
    part, patches, upstream, items, qkv_w, proj_w, gains, table, gmid, glog, mixed, probs, att, mid, nm, slot
):
    packs, length, width = patches.shape
    ex, dp, rows, _ = part.shape
    line = ex // 2
    few = tail_rows(width, ex * dp)
    dma = pltpu.SemaphoreType.DMA
    here = pl.BlockSpec(memory_space=pltpu.VMEM)
    away = pl.BlockSpec(memory_space=pl.ANY)
    shapes = (
        ((packs, length, width), F32),
        ((rows, width), F32),
        ((ex, dp, few, width), BF16),
    )
    slabs = lambda r: tuple(
        (dims + (r, width), BF16) for dims in ((4, line), (4, line), (line,), (2, line), (2, line))
    )
    scratch = (
        ((width, 3 * width), BF16),
        ((width, width), BF16),
        ((2,) + mixed.shape[1:], BF16),
        ((2,) + probs.shape[1:], BF16),
        (att.shape, BF16),
        ((2,) + mid.shape[1:], F32),
        ((2,) + nm.shape[1:], BF16),
        ((packs * length, width), BF16),
        ((packs * length, width), BF16),
        ((length, width), BF16),
        ((packs * length, 3 * width), BF16),
        ((length, 3 * width), F32),
        ((16, width), F32),
        ((ex, dp, few, width), BF16),
        ((few, width), F32),
        ((few, width), BF16),
        *slabs(rows),
        *slabs(few),
    )
    reduce_sems = [dma((20 * line,)), dma((4, line)), dma((line,)), dma((2, line)), dma((2, line)), dma((4, line))]
    return pl.pallas_call(
        functools.partial(backward_kernel, line),
        out_shape=tuple(jax.ShapeDtypeStruct(*s) for s in shapes),
        in_specs=[away] + [here] * 9 + [away] * 5,
        out_specs=(here, here, here),
        scratch_shapes=[pltpu.VMEM(*s) for s in scratch]
        + [dma((5, packs))] + reduce_sems + reduce_sems
        + [dma((24 * line,)), dma((ex, dp)), dma],
        compiler_params=pltpu.CompilerParams(
            collective_id=slot, has_side_effects=True, vmem_limit_bytes=VMEM_BYTES
        ),
        name="backward",
    )(part, patches, upstream, items, qkv_w, proj_w, gains, table, gmid, glog, mixed, probs, att, mid, nm)


def fast(
    patches, out_grad, item_ids, expert_ids,
    qkv_master, qkv_first, qkv_second,
    proj_master, proj_first, proj_second,
    router_master, router_first, router_second,
    gains_master, gains_first, gains_second,
    inner_master, inner_first, inner_second,
    down_master, down_first, down_second,
):
    width = patches.shape[2]
    experts = router_master.shape[1]
    hidden = down_master.shape[1] * lax.axis_size("dp")
    deep = inner_master.shape[1]
    blocks = inner_master.shape[2] // width
    shard = jnp.concatenate(
        [
            jnp.swapaxes(inner_master[0].reshape(deep, blocks, width), 0, 1).reshape(blocks * deep, width),
            down_master[0],
        ],
        axis=0,
    ).astype(BF16)
    router_w = router_master.T.astype(BF16)
    ids = jnp.swapaxes(expert_ids, 1, 2)
    table = jnp.asarray(rope_table(QB))
    full, part, mixed, probs, att, mid, nm, block_out, gmid, glog = run_forward(
        shard, patches, out_grad, item_ids, ids, qkv_master, proj_master, router_w, gains_master, table, hidden, 0
    )
    patch_grad, grad, tail = run_backward(
        part, patches, out_grad, item_ids, qkv_master, proj_master, gains_master, table,
        gmid, glog, mixed, probs, att, mid, nm, 1,
    )
    grad_inner = jnp.swapaxes(grad[: blocks * deep].reshape(blocks, deep, width), 0, 1).reshape(
        inner_master.shape
    )
    grad_down = grad[blocks * deep :].reshape(down_master.shape)
    tail = tail.astype(F32)
    few = tail.shape[2]
    small = tail[0, 0, few - 16 :]
    attn = tail[:, :, : few - 16].reshape(4, width, width)
    grad_qkv = jnp.swapaxes(attn[:3], 0, 1).reshape(width, 3 * width)
    qkv_new = adamw(qkv_master, qkv_first, qkv_second, grad_qkv, 0.1, 0.1)
    proj_new = adamw(proj_master, proj_first, proj_second, attn[3], 0.4, 0.1)
    router_new = adamw(router_master, router_first, router_second, small[:experts].T, 0.07, 0.1)
    gains_new = adamw(gains_master, gains_first, gains_second, small[experts : experts + 2], 0.4, 0.0)
    inner_new = adamw(inner_master, inner_first, inner_second, grad_inner, 0.1, 0.1)
    down_new = adamw(down_master, down_first, down_second, grad_down, 0.15, 0.1)
    return (block_out, patch_grad) + qkv_new + proj_new + router_new + gains_new + inner_new + down_new


GATHER_LIMIT = 16 * 1024 * 1024


def step(*args):
    inner_master, down_master = args[16], args[19]
    experts = inner_master.shape[0] * lax.axis_size("expert")
    entries = inner_master.shape[1] * inner_master.shape[2] + down_master.shape[1] * down_master.shape[2]
    weight_bytes = 2 * experts * entries * lax.axis_size("dp")
    square = lax.axis_size("dp") == 4 and inner_master.shape[0] == 1 and lax.axis_size("expert") == experts
    return (fast if square and weight_bytes <= GATHER_LIMIT else local)(*args)


def solution(mesh):
    in_specs = (
        P(None, ("dp", "expert"), None),
        P(None, ("dp", "expert"), None),
        P(None, ("dp", "expert"), None),
        P(None, ("dp", "expert"), None),
        P(),
        P(),
        P(),
        P(),
        P(),
        P(),
        P(),
        P(),
        P(),
        P(),
        P(),
        P(),
        P("expert", "dp", None),
        P("expert", "dp", None),
        P("expert", "dp", None),
        P("expert", "dp", None),
        P("expert", "dp", None),
        P("expert", "dp", None),
    )
    out_specs = (
        P(None, ("dp", "expert"), None),
        P(None, ("dp", "expert"), None),
        P(),
        P(),
        P(),
        P(),
        P(),
        P(),
        P(),
        P(),
        P(),
        P(),
        P(),
        P(),
        P("expert", "dp", None),
        P("expert", "dp", None),
        P("expert", "dp", None),
        P("expert", "dp", None),
        P("expert", "dp", None),
        P("expert", "dp", None),
    )
    return jax.shard_map(step, mesh=mesh, in_specs=in_specs, out_specs=out_specs, check_vma=False)
```

```python
import functools

import jax
import jax.numpy as jnp
import numpy as np
from jax import lax
from jax.experimental import pallas as pl
from jax.experimental.pallas import tpu as pltpu
from jax.sharding import PartitionSpec as P

HEADS = 6
HEAD = 64


norm_eps = 1e-06
adam_eps = 1e-08
correction = 0.875


def rotary_tables(item_row):
    length = item_row.shape[0]
    places = jnp.arange(length, dtype=jnp.int32)
    starts = jnp.concatenate([jnp.ones((1,), dtype=bool), item_row[1:] != item_row[:-1]])
    first = lax.cummax(jnp.where(starts, places, 0), axis=0)
    offset = (places - first).astype(jnp.float32)
    half = HEAD // 2
    freqs = 10000.0 ** (-jnp.arange(half, dtype=jnp.float32) / half)
    angles = offset[:, None] * freqs[None, :]
    return (jnp.cos(angles), jnp.sin(angles))


def rotate(vectors, cosine, sine):
    half = vectors.shape[-1] // 2
    first_half = vectors[..., :half]
    second_half = vectors[..., half:]
    cos_part = cosine[:, None, :]
    sin_part = sine[:, None, :]
    return jnp.concatenate(
        [
            first_half * cos_part - second_half * sin_part,
            second_half * cos_part + first_half * sin_part,
        ],
        axis=-1,
    )


def masked_scores(query, keys, same_item):
    scores = jnp.einsum("qhe,khe->hqk", query, keys, preferred_element_type=jnp.float32) * 0.125
    return jnp.where(same_item[None], scores, -1e30)


def adamw(weight, first, second, grad, rate, decay):
    first_new = 0.5 * first + 0.5 * grad
    second_new = 0.5 * second + 0.5 * grad * grad
    update = first_new / correction / (jnp.sqrt(second_new / correction) + adam_eps)
    return (weight - rate * (update + decay * weight), first_new, second_new)


def local(
    patches,
    out_grad,
    item_ids,
    expert_ids,
    qkv_master,
    qkv_first,
    qkv_second,
    proj_master,
    proj_first,
    proj_second,
    router_master,
    router_first,
    router_second,
    gains_master,
    gains_first,
    gains_second,
    inner_master,
    inner_first,
    inner_second,
    down_master,
    down_first,
    down_second,
):
    expert_count = lax.axis_size("expert")
    local_experts = inner_master.shape[0]
    experts = expert_count * local_experts
    length = patches.shape[1]
    width = patches.shape[2]
    top = expert_ids.shape[2]
    capacity = 2 * length * top // experts
    hidden_width = down_master.shape[1] * lax.axis_size("dp")
    inner_low, down_low = (
        lax.all_gather(inner_master.astype(jnp.bfloat16), "dp", axis=1, tiled=True),
        lax.all_gather(down_master.astype(jnp.bfloat16), "dp", axis=1, tiled=True),
    )
    qkv_low = qkv_master.astype(jnp.bfloat16)
    proj_low = proj_master.astype(jnp.bfloat16)
    router_low = router_master.astype(jnp.bfloat16)
    gain_attn = gains_master[0]
    gain_ffn = gains_master[1]
    expert_numbers = jnp.arange(experts, dtype=jnp.int32)

    def expert_forward(received):
        count = received.shape[1]
        grid = received.reshape(expert_count, local_experts, count, width)
        both = jnp.einsum("sjcd,jdf->sjcf", grid, inner_low, preferred_element_type=jnp.float32)
        hidden = (jax.nn.silu(both[..., :hidden_width]) * both[..., hidden_width:]).astype(
            jnp.bfloat16
        )
        result = jnp.einsum("sjcf,jfd->sjcd", hidden, down_low, preferred_element_type=jnp.float32)
        result = result.astype(jnp.bfloat16).reshape(experts, count, width)
        returned = lax.all_to_all(result, "expert", split_axis=0, concat_axis=0, tiled=True)
        return (returned, received)

    def micro_step(carry, inputs):
        grad_qkv, grad_proj, grad_router, grad_gains, grad_inner, grad_down = carry
        patch, upstream, item_block, routes = inputs
        items = item_block[0]
        source = patch.astype(jnp.float32)
        inv_first = lax.rsqrt(jnp.mean(source * source, axis=1, keepdims=True) + norm_eps)
        unit_first = source * inv_first
        normed_in = (unit_first * gain_attn).astype(jnp.bfloat16)
        mixed = jnp.dot(normed_in, qkv_low, preferred_element_type=jnp.float32)
        cosine, sine = rotary_tables(items)
        query = rotate(mixed[:, :width].reshape(length, HEADS, HEAD), cosine, sine).astype(
            jnp.bfloat16
        )
        keys = rotate(
            mixed[:, width : 2 * width].reshape(length, HEADS, HEAD), cosine, sine
        ).astype(jnp.bfloat16)
        values = mixed[:, 2 * width :].reshape(length, HEADS, HEAD).astype(jnp.bfloat16)
        same_item = items[:, None] == items[None, :]
        scores = masked_scores(query, keys, same_item)
        peak = jnp.max(scores, axis=2, keepdims=True)
        weights = jnp.exp(scores - peak)
        totals = jnp.sum(weights, axis=2, keepdims=True)
        probs_low = (weights / totals).astype(jnp.bfloat16)
        log_total = peak + jnp.log(totals)
        attended = jnp.einsum("hqk,khe->qhe", probs_low, values, preferred_element_type=jnp.float32)
        attended = attended.reshape(length, width).astype(jnp.bfloat16)
        middle = source + jnp.dot(attended, proj_low, preferred_element_type=jnp.float32)
        inv_second = lax.rsqrt(jnp.mean(middle * middle, axis=1, keepdims=True) + norm_eps)
        unit_second = middle * inv_second
        normed_mid = (unit_second * gain_ffn).astype(jnp.bfloat16)
        logits = jnp.dot(normed_mid, router_low, preferred_element_type=jnp.float32)
        chosen = jnp.take_along_axis(logits, routes, axis=1)
        gates = jax.nn.softmax(chosen, axis=1)
        flat_ids = routes.reshape(length * top)
        hits = (flat_ids[:, None] == expert_numbers[None, :]).astype(jnp.int32)
        rank = jnp.sum(jnp.cumsum(hits, axis=0) * hits, axis=1) - 1
        slots = flat_ids * capacity + rank
        copies = jnp.repeat(normed_mid, top, axis=0)
        outgoing = jnp.zeros((experts * capacity, width), jnp.bfloat16).at[slots].set(copies)
        outgoing = outgoing.reshape(experts, capacity, width)
        returned, kept_inputs = expert_forward(
            lax.all_to_all(outgoing, "expert", split_axis=0, concat_axis=0, tiled=True)
        )
        picked = (
            returned.reshape(experts * capacity, width)[slots]
            .reshape(length, top, width)
            .astype(jnp.float32)
        )
        combined = jnp.sum(gates[:, :, None] * picked, axis=1)
        block_out = (middle + combined).astype(jnp.bfloat16)
        upstream_full = upstream.astype(jnp.float32)
        grad_gate = jnp.sum(upstream_full[:, None, :] * picked, axis=2)
        grad_chosen = gates * (grad_gate - jnp.sum(gates * grad_gate, axis=1, keepdims=True))
        route_hits = (routes[:, :, None] == expert_numbers[None, None, :]).astype(jnp.float32)
        grad_logits = jnp.sum(grad_chosen[:, :, None] * route_hits, axis=1).astype(jnp.bfloat16)
        grad_router_now = jnp.dot(normed_mid.T, grad_logits, preferred_element_type=jnp.float32)
        grad_mid = jnp.dot(grad_logits, router_low.T, preferred_element_type=jnp.float32)
        grad_slots = (
            (gates[:, :, None] * upstream_full[:, None, :])
            .astype(jnp.bfloat16)
            .reshape(length * top, width)
        )
        grad_outgoing = (
            jnp.zeros((experts * capacity, width), jnp.bfloat16).at[slots].set(grad_slots)
        )
        grad_outgoing = grad_outgoing.reshape(experts, capacity, width)
        incoming, inputs_back = (
            lax.all_to_all(grad_outgoing, "expert", split_axis=0, concat_axis=0, tiled=True),
            lax.all_to_all(outgoing, "expert", split_axis=0, concat_axis=0, tiled=True),
        )
        grid_in = inputs_back.reshape(expert_count, local_experts, capacity, width)
        grid_grad = incoming.reshape(expert_count, local_experts, capacity, width)
        both = jnp.einsum("sjcd,jdf->sjcf", grid_in, inner_low, preferred_element_type=jnp.float32)
        gate_part = both[..., :hidden_width]
        up_part = both[..., hidden_width:]
        sigma = jax.nn.sigmoid(gate_part)
        activated = jax.nn.silu(gate_part)
        hidden = (activated * up_part).astype(jnp.bfloat16)
        grad_hidden = jnp.einsum(
            "sjcd,jfd->sjcf", grid_grad, down_low, preferred_element_type=jnp.float32
        )
        grad_down_now = jnp.einsum(
            "sjcf,sjcd->jfd", hidden, grid_grad, preferred_element_type=jnp.float32
        )
        grad_both = jnp.concatenate(
            [
                grad_hidden * up_part * sigma * (1.0 + gate_part * (1.0 - sigma)),
                grad_hidden * activated,
            ],
            axis=3,
        ).astype(jnp.bfloat16)
        grad_inner_now = jnp.einsum(
            "sjcd,sjcf->jdf", grid_in, grad_both, preferred_element_type=jnp.float32
        )
        grad_copies = jnp.einsum(
            "sjcf,jdf->sjcd", grad_both, inner_low, preferred_element_type=jnp.float32
        )
        grad_copies = grad_copies.astype(jnp.bfloat16).reshape(experts, capacity, width)
        grad_back = lax.all_to_all(grad_copies, "expert", split_axis=0, concat_axis=0, tiled=True)
        grad_picked = grad_back.reshape(experts * capacity, width)[slots].reshape(
            length, top, width
        )
        grad_mid = grad_mid + jnp.sum(grad_picked.astype(jnp.float32), axis=1)
        grad_unit_second = grad_mid * gain_ffn
        grad_gain_ffn = jnp.sum(grad_mid * unit_second, axis=0)
        grad_middle = upstream_full + inv_second * (
            grad_unit_second
            - unit_second * jnp.mean(grad_unit_second * unit_second, axis=1, keepdims=True)
        )
        grad_branch = grad_middle.astype(jnp.bfloat16)
        grad_proj_now = jnp.dot(attended.T, grad_branch, preferred_element_type=jnp.float32)
        grad_attended = jnp.dot(grad_branch, proj_low.T, preferred_element_type=jnp.float32)
        grad_attended = grad_attended.astype(jnp.bfloat16).reshape(length, HEADS, HEAD)
        probs_again = jnp.exp(masked_scores(query, keys, same_item) - log_total)
        grad_probs = jnp.einsum(
            "qhe,khe->hqk", grad_attended, values, preferred_element_type=jnp.float32
        )
        grad_values = jnp.einsum(
            "hqk,qhe->khe", probs_low, grad_attended, preferred_element_type=jnp.float32
        )
        grad_scores = probs_again * (
            grad_probs - jnp.sum(probs_again * grad_probs, axis=2, keepdims=True)
        )
        grad_scores = grad_scores.astype(jnp.bfloat16)
        grad_query = (
            jnp.einsum("hqk,khe->qhe", grad_scores, keys, preferred_element_type=jnp.float32)
            * 0.125
        )
        grad_keys = (
            jnp.einsum("hqk,qhe->khe", grad_scores, query, preferred_element_type=jnp.float32)
            * 0.125
        )
        grad_mixed = jnp.concatenate(
            [
                rotate(grad_query, cosine, -sine).reshape(length, width),
                rotate(grad_keys, cosine, -sine).reshape(length, width),
                grad_values.reshape(length, width),
            ],
            axis=1,
        ).astype(jnp.bfloat16)
        grad_qkv_now = jnp.dot(normed_in.T, grad_mixed, preferred_element_type=jnp.float32)
        grad_normed = jnp.dot(grad_mixed, qkv_low.T, preferred_element_type=jnp.float32)
        grad_unit_first = grad_normed * gain_attn
        grad_gain_attn = jnp.sum(grad_normed * unit_first, axis=0)
        patch_grad = grad_middle + inv_first * (
            grad_unit_first
            - unit_first * jnp.mean(grad_unit_first * unit_first, axis=1, keepdims=True)
        )
        new_carry = (
            grad_qkv + grad_qkv_now,
            grad_proj + grad_proj_now,
            grad_router + grad_router_now,
            grad_gains + jnp.stack([grad_gain_attn, grad_gain_ffn]),
            grad_inner + grad_inner_now,
            grad_down + grad_down_now,
        )
        return (new_carry, (block_out, patch_grad))

    start = (
        jnp.zeros(qkv_master.shape, jnp.float32),
        jnp.zeros(proj_master.shape, jnp.float32),
        jnp.zeros(router_master.shape, jnp.float32),
        jnp.zeros(gains_master.shape, jnp.float32),
        jnp.zeros(inner_low.shape, jnp.float32),
        jnp.zeros(down_low.shape, jnp.float32),
    )
    totals, outputs = lax.scan(micro_step, start, (patches, out_grad, item_ids, expert_ids))
    grad_qkv, grad_proj, grad_router, grad_gains = lax.psum(
        (totals[0], totals[1], totals[2], totals[3]), ("dp", "expert")
    )
    grad_inner, grad_down = (
        lax.psum_scatter(totals[4], "dp", scatter_dimension=1, tiled=True),
        lax.psum_scatter(totals[5], "dp", scatter_dimension=1, tiled=True),
    )
    qkv_new = adamw(qkv_master, qkv_first, qkv_second, grad_qkv, 0.1, 0.1)
    proj_new = adamw(proj_master, proj_first, proj_second, grad_proj, 0.4, 0.1)
    router_new = adamw(router_master, router_first, router_second, grad_router, 0.07, 0.1)
    gains_new = adamw(gains_master, gains_first, gains_second, grad_gains, 0.4, 0.0)
    inner_new = adamw(inner_master, inner_first, inner_second, grad_inner, 0.1, 0.1)
    down_new = adamw(down_master, down_first, down_second, grad_down, 0.15, 0.1)
    return (
        outputs[0],
        outputs[1],
        qkv_new[0],
        qkv_new[1],
        qkv_new[2],
        proj_new[0],
        proj_new[1],
        proj_new[2],
        router_new[0],
        router_new[1],
        router_new[2],
        gains_new[0],
        gains_new[1],
        gains_new[2],
        inner_new[0],
        inner_new[1],
        inner_new[2],
        down_new[0],
        down_new[1],
        down_new[2],
    )


F32 = jnp.float32
BF16 = jnp.bfloat16
QB = 128


def iota(shape, axis):
    return lax.broadcasted_iota(jnp.int32, shape, axis)


def dot_nn(a, b):
    return jnp.dot(a, b, preferred_element_type=F32)


def dot_nt(a, b):
    return lax.dot_general(a, b, (((1,), (1,)), ((), ())), preferred_element_type=F32)


def dot_tn(a, b):
    return lax.dot_general(a, b, (((0,), (0,)), ((), ())), preferred_element_type=F32)


def swap_halves(v, low_lane):
    width = v.shape[1]
    half = HEAD // 2
    return jnp.where(low_lane, pltpu.roll(v, width - half, 1), pltpu.roll(v, half, 1))


def turn(v, cos_row, sin_row, low_lane):
    return v * cos_row + swap_halves(v, low_lane) * sin_row


def rope_table(item_max):
    half = HEAD // 2
    offset = np.arange(item_max, dtype=np.float32)
    freqs = np.float32(10000.0) ** (-np.arange(half, dtype=np.float32) / np.float32(half))
    angles = (offset[:, None] * freqs[None, :]).astype(np.float32)
    cosine, sine = np.cos(angles), np.sin(angles)
    return np.concatenate([cosine] * 4 + [-sine, sine] * 2, axis=1).astype(np.float32)


def windows(length):
    found = []
    for start in range(0, length, QB):
        low = max(0, start - QB)
        high = min(length, start + 2 * QB)
        found.append((start, low, high))
    return found


def row_norm(values):
    return lax.rsqrt(jnp.mean(values * values, axis=1, keepdims=True) + norm_eps)


def positions(item_row, length):
    eye = iota((length, length), 0) == iota((length, length), 1)
    col = jnp.sum(jnp.where(eye, item_row, 0.0), axis=1, keepdims=True)
    before = jnp.sum(jnp.where(item_row < col, 1.0, 0.0), axis=1, keepdims=True)
    offset = iota((length, 1), 0) - before.astype(jnp.int32)
    return col, offset


def rope_rows(offset, table, length, width):
    spots = table.shape[0]
    pick = jnp.where(iota((length, spots), 1) == offset, 1.0, 0.0)
    both = jnp.dot(pick, table, precision=lax.Precision.HIGHEST, preferred_element_type=F32)
    copies = width // 128
    return (
        jnp.concatenate([both[:, :128]] * copies, axis=1),
        jnp.concatenate([both[:, 128:]] * copies, axis=1),
    )


VMEM_BYTES = 64 * 1024 * 1024 - 512 * 1024


MESH_ID = pl.DeviceIdType.MESH


class Place:
    def __init__(self, line):
        self.line = line
        dp, ex = lax.axis_index("dp"), lax.axis_index("expert")
        self.x, self.core = lax.div(dp, 2), lax.rem(dp, 2)
        self.z, self.y = lax.div(ex, 2), lax.rem(ex, 2)

    def device(self, flip_x=0, flip_y=0, flip_core=0, z=None):
        x = 1 - self.x if flip_x else self.x
        y = 1 - self.y if flip_y else self.y
        core = 1 - self.core if flip_core else self.core
        return (2 * x + core, 2 * (self.z if z is None else z) + y)

    def levels(self):
        found = [(0, self.z, None, 0)]
        for away in range(1, self.line):
            found.append((away, self.z - away, lambda a=away: self.z >= a, -1))
            found.append((away, self.z + away, lambda a=away: self.z + a < self.line, 1))
        return found

    def up(self):
        return self.z + 1 < self.line

    def down(self):
        return self.z > 0

    def by_distance(self, i):
        found = 0
        for z in range(self.line):
            order = sorted(range(self.line), key=lambda level: (abs(level - z), level))
            for place, level in enumerate(order):
                hit = jnp.logical_and(self.z == z, i == place).astype(jnp.int32)
                found = found + hit * level
        return found

    def greet(self):
        barrier = pltpu.get_barrier_semaphore()

        def signal(device):
            pl.semaphore_signal(barrier, inc=1, device_id=device, device_id_type=MESH_ID)

        for device in (self.device(1), self.device(0, 1), self.device(0, 0, 1)):
            signal(device)
        for step in range(1, self.line):
            signal(self.device(z=lax.rem(self.z + step, self.line)))
        pl.semaphore_wait(barrier, self.line + 2)


def both(*tests):
    tests = [t for t in tests if t is not None]

    def all_of():
        found = tests[0]()
        for t in tests[1:]:
            found = jnp.logical_and(found, t())
        return found

    return all_of if tests else None


def only(test, body):
    if test is None:
        body()
    else:
        pl.when(test())(body)


def remote(source, target, departure, arrival, device):
    return pltpu.make_async_remote_copy(
        src_ref=source,
        dst_ref=target,
        send_sem=departure,
        recv_sem=arrival,
        device_id=device,
        device_id_type=MESH_ID,
    )


class Wires:
    def __init__(self, send_sem, like):
        self.send_sem, self.like = send_sem, like
        self.sent = []

    def send(self, source, target, arrival, device, test=None):
        copy = pltpu.make_async_remote_copy(
            src_ref=source,
            dst_ref=target,
            send_sem=self.send_sem.at[len(self.sent)],
            recv_sem=arrival,
            device_id=device,
            device_id_type=MESH_ID,
        )
        only(test, copy.start)
        self.sent.append(test)

    def arrived(self, target, arrival, device, test=None):
        copy = pltpu.make_async_remote_copy(
            src_ref=target,
            dst_ref=target,
            send_sem=self.send_sem.at[0],
            recv_sem=arrival,
            device_id=device,
            device_id_type=MESH_ID,
        )
        only(test, copy.wait_recv)

    def finish(self):
        for number, test in enumerate(self.sent):
            copy = pltpu.make_async_remote_copy(
                src_ref=self.like,
                dst_ref=self.like,
                send_sem=self.send_sem.at[number],
                recv_sem=self.send_sem.at[number],
                device_id=(0, 0),
                device_id_type=MESH_ID,
            )
            only(test, copy.wait_send)


class Gather:
    def __init__(self, place, shard, full, send_sem, recv_sem, copy_sem):
        self.place, self.shard, self.full = place, shard, full
        self.recv_sem, self.copy_sem = recv_sem, copy_sem
        self.wires = Wires(send_sem, shard)

    def at(self, device):
        return self.full.at[device[1], device[0]]

    def ready(self, device):
        return self.recv_sem.at[device[1], device[0]]

    def pass_on(self, origin, to, test=None, source=None):
        source = self.at(origin) if source is None else source
        self.wires.send(source, self.at(origin), self.ready(origin), to, test)

    def wait(self, origin, test=None):
        self.wires.arrived(self.at(origin), self.ready(origin), self.place.device(0, 0, 1), test)

    def start(self):
        place = self.place
        me = place.device()
        self.pass_on(me, place.device(z=place.z + 1), place.up, self.shard)
        self.pass_on(me, place.device(z=place.z - 1), place.down, self.shard)
        self.pass_on(me, place.device(1), None, self.shard)
        self.pass_on(me, place.device(0, 1), None, self.shard)
        self.pass_on(me, place.device(0, 0, 1), None, self.shard)
        self.own = pltpu.make_async_copy(self.shard, self.at(me), self.copy_sem)
        self.own.start()

    def column(self, away):
        place = self.place
        for dist, level, test, way in place.levels():
            if dist != away:
                continue
            origin = place.device(z=level)
            self.wait(origin, test)
            if way < 0:
                self.pass_on(origin, place.device(z=place.z + 1), both(test, place.up))
            if way > 0:
                self.pass_on(origin, place.device(z=place.z - 1), both(test, place.down))
            self.pass_on(origin, place.device(1), test)
            self.pass_on(origin, place.device(0, 1), test)
            self.pass_on(origin, place.device(0, 0, 1), test)

    def square(self, away):
        place = self.place
        for dist, level, test, way in place.levels():
            if dist != away:
                continue
            over_x, over_y = place.device(1, z=level), place.device(0, 1, z=level)
            self.wait(over_x, test)
            if dist % 2 == 0:
                self.pass_on(over_x, place.device(0, 1), test)
            self.pass_on(over_x, place.device(0, 0, 1), test)
            self.wait(over_y, test)
            if dist % 2 == 1:
                self.pass_on(over_y, place.device(1), test)
            self.pass_on(over_y, place.device(0, 0, 1), test)

    def corner(self, away):
        place = self.place
        for dist, level, test, way in place.levels():
            if dist != away:
                continue
            across = place.device(1, 1, z=level)
            self.wait(across, test)
            self.pass_on(across, place.device(0, 0, 1), test)

    def partner(self, flip_x, flip_y, level):
        self.wait(self.place.device(flip_x, flip_y, 1, z=level))


OWN, OVER_X, OVER_Y, ACROSS = 0, 1, 2, 3
FLIPS = ((0, 0), (1, 0), (0, 1), (1, 1))


class Reduce:
    def __init__(self, place, part, sums, core_in, diag_in, side_in, line_in, send_sem, recv, copy_sem):
        self.place, self.part, self.sums = place, part, sums
        self.core_in, self.diag_in, self.side_in, self.line_in = core_in, diag_in, side_in, line_in
        self.core_sem, self.diag_sem, self.side_sem, self.line_sem = recv
        self.copy_sem = copy_sem
        self.wires = Wires(send_sem, core_in.at[0, 0])

    def shard(self, group, level, flip_core=0):
        device = self.place.device(*FLIPS[group], flip_core, z=level)
        return self.part.at[device[1], device[0]]

    def pick(self, away):
        return [(level, test, way) for dist, level, test, way in self.place.levels() if dist == away]

    def share(self, group, away):
        for level, test, way in self.pick(away):
            load = pltpu.make_async_copy(
                self.shard(group, level), self.sums.at[group, level], self.copy_sem.at[group, level]
            )
            only(test, load.start)
            self.wires.send(
                self.shard(group, level, 1),
                self.core_in.at[group, level],
                self.core_sem.at[group, level],
                self.place.device(0, 0, 1),
                test,
            )

    def add(self, group, level, value):
        self.sums[group, level] = (self.sums[group, level].astype(F32) + value.astype(F32)).astype(BF16)

    def merge(self, group, away):
        place = self.place
        for level, test, way in self.pick(away):

            def body(level=level):
                pltpu.make_async_copy(
                    self.shard(group, level), self.sums.at[group, level], self.copy_sem.at[group, level]
                ).wait()
                self.wires.arrived(
                    self.core_in.at[group, level],
                    self.core_sem.at[group, level],
                    place.device(0, 0, 1),
                )
                self.add(group, level, self.core_in[group, level])

            only(test, body)

    def send_across(self, away):
        place = self.place
        side = OVER_Y if away % 2 == 0 else OVER_X
        for level, test, way in self.pick(away):
            self.wires.send(
                self.sums.at[ACROSS, level],
                self.diag_in.at[level],
                self.diag_sem.at[level],
                place.device(*FLIPS[side]),
                test,
            )

    def send_side(self, away):
        place = self.place
        group = OVER_X if away % 2 == 0 else OVER_Y
        for level, test, way in self.pick(away):

            def body(level=level):
                self.wires.arrived(self.diag_in.at[level], self.diag_sem.at[level], place.device(1))
                self.add(group, level, self.diag_in[level])

            only(test, body)
            for side in (OVER_X, OVER_Y):
                self.wires.send(
                    self.sums.at[side, level],
                    self.side_in.at[side - 1, level],
                    self.side_sem.at[side - 1, level],
                    place.device(*FLIPS[side]),
                    test,
                )

    def collect(self, level, test):
        place = self.place

        def body():
            total = self.sums[OWN, level].astype(F32)
            for side in range(2):
                self.wires.arrived(
                    self.side_in.at[side, level], self.side_sem.at[side, level], place.device(1)
                )
                total = total + self.side_in[side, level].astype(F32)
            self.sums[OWN, level] = total.astype(BF16)

        only(test, body)

    def send_line(self, away):
        place = self.place
        for level, test, way in self.pick(away):
            self.collect(level, test)
            lane = 0 if way < 0 else 1

            def body(level=level, lane=lane):
                self.wires.arrived(
                    self.line_in.at[lane, level], self.line_sem.at[lane, level], place.device(1)
                )
                self.add(OWN, level, self.line_in[lane, level])

            only(both(test, place.up if way < 0 else place.down), body)
            self.wires.send(
                self.sums.at[OWN, level],
                self.line_in.at[lane, level],
                self.line_sem.at[lane, level],
                place.device(z=place.z + way),
                test,
            )

    def finish(self, out):
        place = self.place
        level = place.z
        total = self.sums[OWN, level].astype(F32)
        for side in range(2):
            self.wires.arrived(
                self.side_in.at[side, level], self.side_sem.at[side, level], place.device(1)
            )
            total = total + self.side_in[side, level].astype(F32)
        out[...] = total
        for way, far in ((0, place.up), (1, place.down)):

            def body(way=way):
                self.wires.arrived(
                    self.line_in.at[way, level], self.line_sem.at[way, level], place.device(1)
                )
                out[...] += self.line_in[way, level].astype(F32)

            only(far, body)
        self.wires.finish()


EARLY = 1


class Close:
    def __init__(self, place, kept, owns, sides, diag_in, side_in, line_in, load_sem, sems):
        self.place, self.kept, self.owns, self.sides = place, kept, owns, sides
        self.diag_in, self.side_in, self.line_in, self.load_sem = diag_in, side_in, line_in, load_sem
        self.diag_send, self.diag_sem, self.side_send, self.side_sem, self.line_send, self.line_sem = sems

    def level(self, slot):
        return self.place.by_distance(self.place.line - 1 - slot)

    def load(self, which, slot):
        target = self.owns if which == 0 else self.sides
        return pltpu.make_async_copy(
            self.kept.at[which, self.level(slot)], target.at[slot], self.load_sem.at[which, slot]
        )

    def across(self, slot):
        level = self.level(slot)
        return remote(
            self.kept.at[2, level], self.diag_in.at[slot], self.diag_send.at[slot], self.diag_sem.at[slot],
            self.place.device(1),
        )

    def aside(self, slot):
        level = self.level(slot)
        source = self.kept.at[1, level] if slot < EARLY else self.sides.at[slot]
        return remote(
            source, self.side_in.at[slot], self.side_send.at[slot], self.side_sem.at[slot],
            self.place.device(0, 1),
        )

    def along(self, slot):
        return remote(
            self.owns.at[slot], self.line_in.at[self.place.z], self.line_send.at[slot],
            self.line_sem.at[self.place.z], self.place.device(z=self.level(slot)),
        )

    def start(self):
        for slot in range(self.place.line):
            (self.aside(slot) if slot < EARLY else self.across(slot)).start()
            self.load(0, slot).start()
            if slot >= EARLY:
                self.load(1, slot).start()

    def send_side(self, slot):
        self.load(1, slot).wait()
        self.across(slot).wait_recv()
        self.sides[slot] = (self.sides[slot].astype(F32) + self.diag_in[slot].astype(F32)).astype(BF16)
        self.aside(slot).start()

    def collect(self, slot):
        self.load(0, slot).wait()
        self.aside(slot).wait_recv()
        return self.owns[slot].astype(F32) + self.side_in[slot].astype(F32)

    def send_line(self, slot):
        self.owns[slot] = self.collect(slot).astype(BF16)
        self.along(slot).start()

    def finish(self, out):
        place = self.place
        last = place.line - 1
        out[...] = self.collect(last)
        for step in range(1, place.line):
            z = lax.rem(place.z + step, place.line)
            remote(
                self.owns.at[0], self.line_in.at[z], self.line_send.at[0], self.line_sem.at[z],
                place.device(z=z),
            ).wait_recv()
            out[...] += self.line_in[z].astype(F32)
        for slot in range(place.line):
            self.aside(slot).wait_send()
            if slot >= EARLY:
                self.across(slot).wait_send()
            if slot < last:
                self.along(slot).wait_send()


def copy_all(copies):
    for copy in copies:
        copy.start()


def attend_pack(p, patches, items, gains, table, qkv_s, proj_s, mixed_s, probs_s, att_s, mid_s, nm_s):
    _, length, width = patches.shape
    pairs = width // 128
    slot = lax.rem(p, mixed_s.shape[0])
    low_lane = iota((1, width), 1) % HEAD < HEAD // 2
    first_head = iota((1, 128), 1) < HEAD
    mask_a = jnp.where(first_head, 1.0, 0.0).astype(BF16)
    mask_b = jnp.where(first_head, 0.0, 1.0).astype(BF16)
    top_rows = iota((128, 1), 0) < HEAD
    source = patches[p].astype(F32)
    normed = (source * row_norm(source) * gains[0:1, :]).astype(BF16)
    mixed = dot_nn(normed, qkv_s[...])
    item_row = items[p].astype(F32)
    item_col, offset = positions(item_row, length)
    cos_row, sin_row = rope_rows(offset, table[...], length, width)
    mixed_s[slot, :, :width] = turn(mixed[:, :width], cos_row, sin_row, low_lane).astype(BF16)
    mixed_s[slot, :, width : 2 * width] = turn(
        mixed[:, width : 2 * width], cos_row, sin_row, low_lane
    ).astype(BF16)
    mixed_s[slot, :, 2 * width :] = mixed[:, 2 * width :].astype(BF16)
    for pair in range(pairs):
        lanes = slice(128 * pair, 128 * pair + 128)
        key_lanes = slice(width + 128 * pair, width + 128 * pair + 128)
        values_t = mixed[:, 2 * width + 128 * pair : 2 * width + 128 * pair + 128].T.astype(BF16)
        for block, (start, low, high) in enumerate(windows(length)):
            query = mixed_s[slot, start : start + QB, lanes] * 0.125
            query = jnp.concatenate([query * mask_a, query * mask_b], axis=0)
            scores = dot_nt(mixed_s[slot, low:high, key_lanes], query)
            here = item_row[:, start : start + QB]
            same = item_col[low:high] == jnp.concatenate([here, here], axis=1)
            scores = jnp.where(same, scores, -1e30)
            peak = jnp.max(scores, axis=0, keepdims=True)
            weights = jnp.exp(scores - peak)
            total = jnp.sum(weights, axis=0, keepdims=True)
            probs = (weights * (1.0 / total)).astype(BF16)
            probs_s[p, pair, block, : high - low] = probs
            out = dot_nn(values_t[:, low:high], probs)
            out = jnp.where(top_rows, out[:, :QB], out[:, QB:])
            att_s[p, start : start + QB, lanes] = out.T.astype(BF16)
    middle = source + dot_nn(att_s[p], proj_s[...])
    mid_s[p] = middle
    nm_s[p] = (middle * row_norm(middle) * gains[1:2, :]).astype(BF16)


class Experts:
    def __init__(self, refs, cap):
        (
            self.nm, self.upstream, self.rank_s, self.gate_s, self.gg_s, self.x_s, self.hid_s, self.go_s,
            self.gb_s, self.y_s, self.inner_w, self.down_w,
        ) = refs
        self.cap = cap

    def prepare(self, p, ids, router_w):
        nm = self.nm
        _, length, width = nm.shape
        experts = router_w.shape[0]
        earlier = jnp.where(iota((length, length), 0) < iota((length, length), 1), 1.0, 0.0).astype(BF16)
        logits = dot_nt(router_w[...], nm[p])
        number = iota((experts, length), 0)
        hit0 = number == ids[p, 0:1, :]
        hit1 = number == ids[p, 1:2, :]
        chosen0 = jnp.sum(jnp.where(hit0, logits, 0.0), axis=0, keepdims=True)
        chosen1 = jnp.sum(jnp.where(hit1, logits, 0.0), axis=0, keepdims=True)
        peak = jnp.maximum(chosen0, chosen1)
        e0 = jnp.exp(chosen0 - peak)
        e1 = jnp.exp(chosen1 - peak)
        total = e0 + e1
        self.gate_s[p] = jnp.where(hit0, e0 / total, 0.0) + jnp.where(hit1, e1 / total, 0.0)
        named = jnp.where(hit0, 1.0, jnp.where(hit1, 1.0, 0.0))
        rank = dot_nn(named.astype(BF16), earlier)
        self.rank_s[p] = jnp.where(named > 0.5, rank, -1.0)

    def rows(self, p, expert):
        cap = self.cap
        _, length, width = self.nm.shape
        hidden_width = self.hid_s.shape[1]
        here = pl.ds(pl.multiple_of(p * cap, cap), cap)
        rank = self.rank_s[p, pl.ds(expert, 1), :]
        gate_row = self.gate_s[p, pl.ds(expert, 1), :]
        pick = iota((cap, length), 0).astype(F32) == rank
        chosen = jnp.where(pick, 1.0, 0.0).astype(BF16)
        taken = dot_nn(chosen, jnp.concatenate([self.nm[p], self.upstream[p]], axis=1))
        gate_col = jnp.sum(jnp.where(pick, gate_row, 0.0), axis=1, keepdims=True)
        x = taken[:, :width].astype(BF16)
        g = taken[:, width:]
        self.x_s[here, :] = x
        grad_out = (gate_col * g).astype(BF16)
        self.go_s[here, :] = grad_out
        gate = dot_nn(x, self.inner_w[:, :hidden_width])
        up = dot_nn(x, self.inner_w[:, hidden_width:])
        sigma = 1.0 / (1.0 + jnp.exp(-gate))
        active = gate * sigma
        hidden = (active * up).astype(BF16)
        self.hid_s[here, :] = hidden
        result = dot_nn(hidden, self.down_w[...]).astype(BF16).astype(F32)
        spot = pl.ds(pl.multiple_of(expert * cap, cap), cap)
        self.y_s[p, spot, :width] = (gate_col * result).astype(BF16)
        grad_gate = jnp.sum(g * result, axis=1, keepdims=True)
        self.gg_s[p, pl.ds(expert, 1), :] = jnp.sum(
            jnp.where(pick, grad_gate, 0.0), axis=0, keepdims=True
        )
        grad_hidden = dot_nt(grad_out, self.down_w[...])
        self.gb_s[here, :hidden_width] = (
            grad_hidden * up * sigma * (1.0 + gate * (1.0 - sigma))
        ).astype(BF16)
        self.gb_s[here, hidden_width:] = (grad_hidden * active).astype(BF16)
        self.y_s[p, spot, width:] = dot_nt(self.gb_s[here, :], self.inner_w[...]).astype(BF16)

    def grads(self, part):
        copies, _, width = part.shape
        hidden_width = self.hid_s.shape[1]
        deep, span = width // copies, hidden_width // copies
        for block in range(2 * hidden_width // width):
            lanes = slice(block * width, block * width + width)
            grad = dot_tn(self.x_s[...], self.gb_s[:, lanes]).astype(BF16)
            for d in range(copies):
                part[d, block * deep : block * deep + deep, :] = grad[d * deep : d * deep + deep]
        grad = dot_tn(self.hid_s[...], self.go_s[...]).astype(BF16)
        for d in range(copies):
            part[d, width:, :] = grad[d * span : d * span + span]

    def finish(self, p, router_w, mid, block_o, gmid_o, glog_o):
        cap = self.cap
        _, length, width = self.nm.shape
        experts = router_w.shape[0]
        ranks = self.rank_s[p].T
        slot = iota((length, cap), 1).astype(F32)
        pieces = [
            jnp.where(ranks[:, e : e + 1] == slot, 1.0, 0.0).astype(BF16) for e in range(experts)
        ]
        back = dot_nn(jnp.concatenate(pieces, axis=1), self.y_s[p])
        gate = self.gate_s[p]
        grad_gate = self.gg_s[p]
        mean = jnp.sum(gate * grad_gate, axis=0, keepdims=True)
        hit = self.rank_s[p] > -0.5
        grad_logits = jnp.where(hit, gate * (grad_gate - mean), 0.0).astype(BF16)
        glog_o[p] = grad_logits
        block_o[p] = (mid[p] + back[:, :width]).astype(BF16)
        gmid_o[p] = back[:, width:] + dot_tn(grad_logits, router_w[...])


def unpack(weights, inner_w, down_w):
    copies, _, width = weights.shape
    deep, span = width // copies, down_w.shape[0] // copies
    for d in range(copies):
        for block in range(inner_w.shape[1] // width):
            inner_w[d * deep : d * deep + deep, block * width : block * width + width] = weights[
                d, block * deep : block * deep + deep, :
            ]
        down_w[d * span : d * span + span, :] = weights[d, width:, :]


def forward_kernel(
    line, cap,
    shard, patches, upstream, items, ids, qkv_w, proj_w, router_w, gains, table,
    full, kept_o, mixed_o, probs_o, att_o, mid_o, nm_o, block_o, gmid_o, glog_o,
    qkv_s, proj_s, mixed_s, probs_s, att_s, mid_s, nm_s, wbuf, pbuf,
    rank_s, gate_s, gg_s, x_s, hid_s, go_s, gb_s, y_s, inner_s, down_s,
    sums, core_in, diag_in, side_in,
    send_sem, recv_sem, own_sem, save_sem, fetch_sem, keep_sem,
    core_send, core_sem, diag_send, diag_sem, side_send, side_sem, credit_sem,
):
    packs = patches.shape[0]
    experts = router_w.shape[0]
    place = Place(line)
    place.greet()
    gather = Gather(place, shard, full, send_sem, recv_sem, own_sem)
    gather.start()
    qkv_s[...] = qkv_w[...].astype(BF16)
    proj_s[...] = proj_w[...].astype(BF16)
    work = Experts(
        (nm_s, upstream, rank_s, gate_s, gg_s, x_s, hid_s, go_s, gb_s, y_s, inner_s, down_s), cap
    )
    saves = ((mixed_s, mixed_o), (probs_s, probs_o), (att_s, att_o), (mid_s, mid_o), (nm_s, nm_o))

    def save(n, p):
        source, target = saves[n]
        return pltpu.make_async_copy(
            source.at[lax.rem(p, source.shape[0])], target.at[p], save_sem.at[n, p]
        )

    def pack(p, carry):
        pl.when(p >= 2)(lambda: save(0, p - 2).wait())
        attend_pack(p, patches, items, gains, table, qkv_s, proj_s, mixed_s, probs_s, att_s, mid_s, nm_s)
        for n in range(len(saves)):
            save(n, p).start()
        work.prepare(p, ids, router_w)
        for k in range(1, line):

            def relay(k=k):
                gather.column(k)
                gather.square(k - 1)

            pl.when(p == min(k - 1, packs - 1))(relay)
        return carry

    lax.fori_loop(0, packs, pack, 0)

    def near(i):
        return int(i < line) if isinstance(i, int) else (i < line).astype(jnp.int32)

    def number(i):
        level = place.by_distance(near(i) * i + (1 - near(i)) * (2 * line - 1 - i))
        side = near(i) * place.y + (1 - near(i)) * (1 - place.y)
        return level, 2 * level + side

    def fetch(i):
        return pltpu.make_async_copy(full.at[number(i)[1]], wbuf.at[lax.rem(i, 2)], fetch_sem.at[lax.rem(i, 2)])

    def arrive(i):
        level = number(i)[0]

        def close():
            gather.partner(0, 0, level)
            gather.partner(1, 0, level)

        def far():
            gather.partner(0, 1, level)
            gather.partner(1, 1, level)

        if isinstance(i, int):
            (close if i < line else far)()
        else:
            pl.when(i < line)(close)
            pl.when(i >= line)(far)

    def piece(q, flip_core):
        return place.device(q, 0, flip_core)[0]

    def swap(i, q):
        slot = lax.rem(i, 2)
        return remote(
            pbuf.at[slot, piece(q, 1)], core_in.at[slot, q], core_send.at[slot, q], core_sem.at[slot, q],
            place.device(0, 0, 1),
        )

    def across(n):
        level = number(line + n)[0]
        return remote(
            sums.at[ACROSS, level], diag_in.at[n], diag_send.at[n], diag_sem.at[n], place.device(1)
        )

    def aside(level):
        return remote(
            sums.at[OVER_X, level], side_in.at[level], side_send.at[level], side_sem.at[level],
            place.device(1),
        )

    def keep(which, group, level):
        return pltpu.make_async_copy(sums.at[group, level], kept_o.at[which, level], keep_sem.at[which, level])

    def merge(i):
        slot = lax.rem(i, 2)
        level = number(i)[0]
        group = 2 * (1 - near(i))
        for q in range(2):
            swap(i, q).wait_recv()
            total = pbuf[slot, piece(q, 0)].astype(F32) + core_in[slot, q].astype(F32)
            sums[group + q, level] = total.astype(BF16)
        pl.semaphore_signal(credit_sem, inc=1, device_id=place.device(0, 0, 1), device_id_type=MESH_ID)
        pl.when(i < line)(lambda: aside(level).start())
        for n in range(EARLY):
            pl.when(i == line + n)(lambda n=n: across(n).start())

        def put_away():
            keep(1, OVER_Y, level).start()
            keep(2, ACROSS, level).start()

        pl.when(i >= line + EARLY)(put_away)

    gather.own.wait()
    arrive(0)
    fetch(0).start()

    def one(i, carry):
        fetch(i).wait()
        unpack(wbuf.at[lax.rem(i, 2)], inner_s, down_s)
        expert = number(i)[1]

        def rows(p, inner_carry):
            work.rows(p, expert)
            pl.when(jnp.logical_and(p == 0, i >= 1))(lambda: merge(i - 1))
            return inner_carry

        lax.fori_loop(0, packs, rows, 0)

        def corners(found):
            for k in found:
                gather.corner(k)

        pl.when(i == line - 3)(lambda: gather.square(line - 1))
        pl.when(i == line - 2)(lambda: corners(range(line - 1)))
        pl.when(i == line - 1)(lambda: corners((line - 1,)))

        def ahead():
            arrive(i + 1)
            fetch(i + 1).start()

        pl.when(i + 1 < experts)(ahead)

        def free():
            pl.semaphore_wait(credit_sem, 1)
            for q in range(2):
                swap(i, q).wait_send()

        pl.when(i >= 2)(free)
        work.grads(pbuf.at[lax.rem(i, 2)])
        for q in range(2):
            swap(i, q).start()
        return carry

    lax.fori_loop(0, experts, one, 0)

    def last(i, carry):
        merge(i)
        return carry

    lax.fori_loop(experts - 1, experts, last, 0)

    def finish(p, carry):
        work.finish(p, router_w, mid_s, block_o, gmid_o, glog_o)
        return carry

    lax.fori_loop(0, packs, finish, 0)

    def settle(level, carry):
        aside(level).wait_recv()
        sums[OWN, level] = (sums[OWN, level].astype(F32) + side_in[level].astype(F32)).astype(BF16)
        keep(0, OWN, level).start()
        return carry

    lax.fori_loop(0, line, settle, 0)
    for n in range(EARLY):
        level = number(line + n)[0]
        across(n).wait_recv()
        sums[OVER_Y, level] = (sums[OVER_Y, level].astype(F32) + diag_in[n].astype(F32)).astype(BF16)
        keep(1, OVER_Y, level).start()
        across(n).wait_send()

    def drain(level, carry):
        keep(0, OWN, level).wait()
        keep(1, OVER_Y, level).wait()
        aside(level).wait_send()
        return carry

    lax.fori_loop(0, line, drain, 0)
    for n in range(EARLY, line):
        keep(2, ACROSS, number(line + n)[0]).wait()
    pl.semaphore_wait(credit_sem, 2)
    for i in range(experts - 2, experts):
        for q in range(2):
            swap(i, q).wait_send()
    for n in range(len(saves)):
        for p in range(packs - 2 if n == 0 else 0, packs):
            save(n, p).wait()
    gather.wires.finish()


def run_forward(shard, patches, upstream, items, ids, qkv_w, proj_w, router_w, gains, table, hidden, slot):
    packs, length, width = patches.shape
    experts = router_w.shape[0]
    dp, ex = lax.axis_size("dp"), lax.axis_size("expert")
    line = ex // 2
    cap = 2 * length * ids.shape[1] // experts
    pairs, blocks = width // 128, length // QB
    rows = shard.shape[0]
    dma = pltpu.SemaphoreType.DMA
    here = pl.BlockSpec(memory_space=pltpu.VMEM)
    away = pl.BlockSpec(memory_space=pl.ANY)
    saved = (
        ((packs, length, 3 * width), BF16),
        ((packs, pairs, blocks, 3 * QB, 2 * QB), BF16),
        ((packs, length, width), BF16),
        ((packs, length, width), F32),
        ((packs, length, width), BF16),
    )
    shapes = (
        ((ex, dp, rows, width), BF16),
        ((3, line, rows, width), BF16),
        *saved,
        ((packs, length, width), BF16),
        ((packs, length, width), F32),
        ((packs, experts, length), BF16),
    )
    scratch = (
        ((width, 3 * width), BF16),
        ((width, width), BF16),
        ((2, length, 3 * width), BF16),
        *saved[1:],
        ((2, dp, rows, width), BF16),
        ((2, dp, rows, width), BF16),
        ((packs, experts, length), F32),
        ((packs, experts, length), F32),
        ((packs, experts, length), F32),
        ((packs * cap, width), BF16),
        ((packs * cap, hidden), BF16),
        ((packs * cap, width), BF16),
        ((packs * cap, 2 * hidden), BF16),
        ((packs, experts * cap, 2 * width), BF16),
        ((width, 2 * hidden), BF16),
        ((hidden, width), BF16),
        ((4, line, rows, width), BF16),
        ((2, 2, rows, width), BF16),
        ((EARLY, rows, width), BF16),
        ((line, rows, width), BF16),
    )
    return pl.pallas_call(
        functools.partial(forward_kernel, line, cap),
        out_shape=tuple(jax.ShapeDtypeStruct(*s) for s in shapes),
        in_specs=[here] * 10,
        out_specs=(away,) * 7 + (here,) * 3,
        scratch_shapes=[pltpu.VMEM(*s) for s in scratch]
        + [dma((24 * line,)), dma((ex, dp)), dma, dma((5, packs)), dma((2,)), dma((3, line))]
        + [dma((2, 2))] * 2 + [dma((EARLY,))] * 2 + [dma((line,))] * 2 + [pltpu.SemaphoreType.REGULAR],
        compiler_params=pltpu.CompilerParams(
            collective_id=slot, has_side_effects=True, vmem_limit_bytes=VMEM_BYTES
        ),
        name="forward",
    )(shard, patches, upstream, items, ids, qkv_w, proj_w, router_w, gains, table)


class Backward:
    def __init__(self, refs):
        (
            self.patches, self.upstream, self.items, self.gains, self.table, self.gmid, self.glog,
            self.qkv_s, self.proj_s, self.mixed, self.probs, self.mid, self.nm,
            self.patch_o, self.normed_s, self.branch_s, self.datt_s, self.dmix_s, self.dkv_s, self.small_g,
        ) = refs

    def pack(self, p):
        packs, length, width = self.patches.shape
        pairs = width // 128
        experts = self.glog.shape[1]
        gains, mixed, dkv_s = self.gains, self.mixed, self.dkv_s
        low_lane = iota((1, width), 1) % HEAD < HEAD // 2
        first_head = iota((1, 128), 1) < HEAD
        mask_a = jnp.where(first_head, 1.0, 0.0).astype(BF16)
        mask_b = jnp.where(first_head, 0.0, 1.0).astype(BF16)
        top_rows = iota((128, 1), 0) < HEAD
        rows = pl.ds(pl.multiple_of(p * length, length), length)
        source = self.patches[p].astype(F32)
        gain0, gain1 = gains[0:1, :], gains[1:2, :]
        slot = lax.rem(p, 2)
        middle = self.mid[slot]
        inv = row_norm(middle)
        unit = middle * inv
        grad_mid = self.gmid[p]
        self.small_g[experts + 1 : experts + 2, :] += jnp.sum(grad_mid * unit, axis=0, keepdims=True)
        self.small_g[0:experts, :] += dot_nn(self.glog[p], self.nm[slot])
        grad_unit = grad_mid * gain1
        grad_middle = self.upstream[p].astype(F32) + inv * (
            grad_unit - unit * jnp.mean(grad_unit * unit, axis=1, keepdims=True)
        )
        self.patch_o[p] = grad_middle
        branch = grad_middle.astype(BF16)
        self.branch_s[rows, :] = branch
        self.datt_s[...] = dot_nt(branch, self.proj_s[...]).astype(BF16)
        dkv_s[...] = jnp.zeros(dkv_s.shape, F32)
        item_row = self.items[p].astype(F32)
        item_col, offset = positions(item_row, length)
        cos_row, sin_row = rope_rows(offset, self.table[...], length, width)
        for pair in range(pairs):
            lanes = slice(128 * pair, 128 * pair + 128)
            key_lanes = slice(width + 128 * pair, width + 128 * pair + 128)
            value_lanes = slice(2 * width + 128 * pair, 2 * width + 128 * pair + 128)
            keys_t = mixed[slot, :, key_lanes].astype(F32).T.astype(BF16)
            for block, (start, low, high) in enumerate(windows(length)):
                query = mixed[slot, start : start + QB, lanes] * 0.125
                query = jnp.concatenate([query * mask_a, query * mask_b], axis=0)
                datt = self.datt_s[start : start + QB, lanes]
                datt = jnp.concatenate([datt * mask_a, datt * mask_b], axis=0)
                prob = self.probs[slot, pair, block, : high - low]
                dprob = dot_nt(mixed[slot, low:high, value_lanes], datt)
                weight = prob.astype(F32)
                mean = jnp.sum(weight * dprob, axis=0, keepdims=True)
                dscore = (weight * (dprob - mean)).astype(BF16)
                dkv_s[low:high, key_lanes] += dot_nn(dscore, query)
                dkv_s[low:high, value_lanes] += dot_nn(prob, datt)
                dquery = dot_nn(keys_t[:, low:high], dscore)
                dquery = jnp.where(top_rows, dquery[:, :QB], dquery[:, QB:])
                dkv_s[start : start + QB, lanes] = dquery.T * 0.125
        dmix_s = self.dmix_s
        dmix_s[rows, :width] = turn(dkv_s[:, :width], cos_row, -sin_row, low_lane).astype(BF16)
        dmix_s[rows, width : 2 * width] = turn(
            dkv_s[:, width : 2 * width], cos_row, -sin_row, low_lane
        ).astype(BF16)
        dmix_s[rows, 2 * width :] = dkv_s[:, 2 * width :].astype(BF16)
        grad_normed = dot_nt(dmix_s[rows, :], self.qkv_s[...])
        inv_in = row_norm(source)
        unit_in = source * inv_in
        self.normed_s[rows, :] = (unit_in * gain0).astype(BF16)
        self.small_g[experts : experts + 1, :] += jnp.sum(grad_normed * unit_in, axis=0, keepdims=True)
        grad_unit_in = grad_normed * gain0
        self.patch_o[p] += inv_in * (
            grad_unit_in - unit_in * jnp.mean(grad_unit_in * unit_in, axis=1, keepdims=True)
        )

    def tail(self, att, tail):
        packs, length, width = self.patches.shape
        tail[...] = jnp.zeros(tail.shape, BF16)
        for block in range(4):
            if block < 3:
                grad = dot_tn(self.normed_s[...], self.dmix_s[:, block * width : block * width + width])
            else:
                flat = jnp.concatenate([att[p] for p in range(packs)], axis=0)
                grad = dot_tn(flat, self.branch_s[...])
            lay_tail(tail, block, grad.astype(BF16))
        tail[0, 0, tail.shape[2] - 16 :, :] = self.small_g[...].astype(BF16)


def tail_rows(width, devices):
    return 4 * width // devices + 16


def lay_tail(tail, block, grad):
    ex, dp, rows, width = tail.shape
    rows = rows - 16
    each = width // rows
    for piece in range(each):
        number = block * each + piece
        tail[number // dp, number % dp, :rows, :] = grad[piece * rows : piece * rows + rows]


def backward_kernel(
    line,
    kept, patches, upstream, items, qkv_w, proj_w, gains, table, gmid, glog, mixed_i, probs_i, att_i, mid_i, nm_i,
    patch_o, grad_o, tail_o,
    qkv_s, proj_s, mixed, probs, att, mid, nm,
    normed_s, branch_s, datt_s, dmix_s, dkv_s, small_g, tail, tail_sum, tail_low,
    owns, sides, diag_in, side_in, line_in,
    tsums, tcore_in, tdiag_in, tside_in, tline_in,
    load_sem, own_sem, diag_send, diag_sem, side_send, side_sem, line_send, line_sem,
    tsend_sem, tcore_sem, tdiag_sem, tside_sem, tline_sem, tcopy_sem,
    gsend_sem, grecv_sem, gown_sem,
):
    packs = patches.shape[0]
    place = Place(line)
    place.greet()
    reduce = Close(
        place, kept, owns, sides, diag_in, side_in, line_in, own_sem,
        (diag_send, diag_sem, side_send, side_sem, line_send, line_sem),
    )
    small = Reduce(
        place, tail, tsums, tcore_in, tdiag_in, tside_in, tline_in,
        tsend_sem, (tcore_sem, tdiag_sem, tside_sem, tline_sem), tcopy_sem,
    )
    order = list(range(line - 1, -1, -1))
    reduce.start()
    loads = ((mixed_i, mixed), (mid_i, mid), (nm_i, nm), (probs_i, probs), (att_i, att))

    def load(n, p):
        source, target = loads[n]
        return pltpu.make_async_copy(
            source.at[p], target.at[lax.rem(p, target.shape[0])], load_sem.at[n, p]
        )

    for p in range(packs):
        for n in range(len(loads)):
            if p < loads[n][1].shape[0]:
                load(n, p).start()
    qkv_s[...] = qkv_w[...].astype(BF16)
    proj_s[...] = proj_w[...].astype(BF16)
    small_g[...] = jnp.zeros(small_g.shape, F32)
    work = Backward((
        patches, upstream, items, gains, table, gmid, glog,
        qkv_s, proj_s, mixed, probs, mid, nm,
        patch_o, normed_s, branch_s, datt_s, dmix_s, dkv_s, small_g,
    ))
    def pack(p, carry):
        for n in range(len(loads)):
            load(n, p).wait()
        work.pack(p)

        def ahead():
            for n in range(len(loads) - 1):
                load(n, p + 2).start()

        pl.when(p + 2 < packs)(ahead)

        def advance(n):
            if n + 1 < line:
                reduce.send_side(n + 1)
            reduce.send_line(n)

        for n in range(min(packs, line - 1)):
            pl.when(p == n)(lambda n=n: advance(n))
        return carry

    lax.fori_loop(0, packs, pack, 0)
    work.tail(att, tail)
    for group in (ACROSS, OVER_X, OVER_Y, OWN):
        for away in order:
            small.share(group, away)
    for away in order:
        small.merge(ACROSS, away)
        small.send_across(away)
    for group in (OVER_X, OVER_Y, OWN):
        for away in order:
            small.merge(group, away)
    for away in order:
        small.send_side(away)
    for away in order[:-1]:
        small.send_line(away)
    small.finish(tail_sum)
    tail_low[...] = tail_sum[...].astype(BF16)
    gather = Gather(place, tail_low, tail_o, gsend_sem, grecv_sem, gown_sem)
    gather.start()
    reduce.finish(grad_o)
    for away in range(1, line):
        gather.column(away)
        gather.square(away - 1)
    gather.square(line - 1)
    for away in range(line):
        gather.corner(away)
    for flip_x in range(2):
        for flip_y in range(2):
            for away in range(line):
                for dist, level, test, way in place.levels():
                    if dist == away:
                        only(test, lambda: gather.partner(flip_x, flip_y, level))
    gather.own.wait()
    gather.wires.finish()


def run_backward(
    kept, patches, upstream, items, qkv_w, proj_w, gains, table, gmid, glog, mixed, probs, att, mid, nm, slot
):
    packs, length, width = patches.shape
    _, line, rows, _ = kept.shape
    dp, ex = lax.axis_size("dp"), lax.axis_size("expert")
    few = tail_rows(width, ex * dp)
    dma = pltpu.SemaphoreType.DMA
    here = pl.BlockSpec(memory_space=pltpu.VMEM)
    away = pl.BlockSpec(memory_space=pl.ANY)
    shapes = (
        ((packs, length, width), F32),
        ((rows, width), F32),
        ((ex, dp, few, width), BF16),
    )
    slabs = lambda r: tuple(
        (dims + (r, width), BF16) for dims in ((4, line), (4, line), (line,), (2, line), (2, line))
    )
    scratch = (
        ((width, 3 * width), BF16),
        ((width, width), BF16),
        ((2,) + mixed.shape[1:], BF16),
        ((2,) + probs.shape[1:], BF16),
        (att.shape, BF16),
        ((2,) + mid.shape[1:], F32),
        ((2,) + nm.shape[1:], BF16),
        ((packs * length, width), BF16),
        ((packs * length, width), BF16),
        ((length, width), BF16),
        ((packs * length, 3 * width), BF16),
        ((length, 3 * width), F32),
        ((16, width), F32),
        ((ex, dp, few, width), BF16),
        ((few, width), F32),
        ((few, width), BF16),
        *([((line, rows, width), BF16)] * 5),
        *slabs(few),
    )
    reduce_sems = [dma((20 * line,)), dma((4, line)), dma((line,)), dma((2, line)), dma((2, line)), dma((4, line))]
    return pl.pallas_call(
        functools.partial(backward_kernel, line),
        out_shape=tuple(jax.ShapeDtypeStruct(*s) for s in shapes),
        in_specs=[away] + [here] * 9 + [away] * 5,
        out_specs=(here, here, here),
        scratch_shapes=[pltpu.VMEM(*s) for s in scratch]
        + [dma((5, packs)), dma((2, line))] + [dma((line,))] * 6 + reduce_sems
        + [dma((24 * line,)), dma((ex, dp)), dma],
        compiler_params=pltpu.CompilerParams(
            collective_id=slot, has_side_effects=True, vmem_limit_bytes=VMEM_BYTES
        ),
        name="backward",
    )(kept, patches, upstream, items, qkv_w, proj_w, gains, table, gmid, glog, mixed, probs, att, mid, nm)


def update_kernel(
    tail, inner_g, down_g,
    qkv_w, qkv_f, qkv_s, proj_w, proj_f, proj_s, router_w, router_f, router_s,
    gains_w, gains_f, gains_s, inner_w, inner_f, inner_s, down_w, down_f, down_s,
    qkv_wo, qkv_fo, qkv_so, proj_wo, proj_fo, proj_so, router_wo, router_fo, router_so,
    gains_wo, gains_fo, gains_so, inner_wo, inner_fo, inner_so, down_wo, down_fo, down_so,
):
    step = pl.program_id(0)
    ex, dp, few, width = tail.shape
    rows = few - 16
    experts = router_w.shape[1]
    attn = tail[:, :, :rows, :].reshape(ex * dp * rows, width).astype(F32)

    def write(outs, values):
        for out, value in zip(outs, values):
            out[...] = value

    def qkv():
        write((qkv_wo, qkv_fo, qkv_so), adamw(qkv_w[...], qkv_f[...], qkv_s[...], attn, 0.1, 0.1))

    def proj():
        write((proj_wo, proj_fo, proj_so), adamw(proj_w[...], proj_f[...], proj_s[...], attn, 0.4, 0.1))

    def rest():
        small = tail[0, 0, rows:, :].astype(F32)
        router_g = small.T[:, :experts]
        gains_g = small[experts : experts + 2]
        write(
            (router_wo, router_fo, router_so),
            adamw(router_w[...], router_f[...], router_s[...], router_g, 0.07, 0.1),
        )
        write(
            (gains_wo, gains_fo, gains_so),
            adamw(gains_w[...], gains_f[...], gains_s[...], gains_g, 0.4, 0.0),
        )

    pl.when(step < 3)(qkv)
    pl.when(step == 3)(proj)
    pl.when(step == 0)(rest)
    write(
        (inner_wo, inner_fo, inner_so),
        adamw(inner_w[...], inner_f[...], inner_s[...], inner_g[...], 0.1, 0.1),
    )
    write((down_wo, down_fo, down_so), adamw(down_w[...], down_f[...], down_s[...], down_g[...], 0.15, 0.1))


def run_update(tail, grad, weights):
    ex, dp, few, width = tail.shape
    qkv, router, inner, down = weights[0], weights[6], weights[12], weights[15]
    deep, span = inner.shape[0], down.shape[0] // 4
    of_qkv = pl.BlockSpec((width, width), lambda j: (0, jnp.minimum(j, 2)))
    of_proj = pl.BlockSpec((width, width), lambda j: (0, 0))
    of_router = pl.BlockSpec(router.shape, lambda j: (0, 0))
    of_gains = pl.BlockSpec((2, width), lambda j: (0, 0))
    of_inner = pl.BlockSpec((deep, width), lambda j: (0, j))
    of_down = pl.BlockSpec((span, width), lambda j: (j, 0))
    specs = []
    for spec in (of_qkv, of_proj, of_router, of_gains, of_inner, of_down):
        specs += [spec] * 3
    first_down = 4 * deep // span
    return pl.pallas_call(
        update_kernel,
        out_shape=tuple(jax.ShapeDtypeStruct(w.shape, F32) for w in weights),
        grid=(4,),
        in_specs=[
            pl.BlockSpec((ex // 4, dp, few, width), lambda j: (j, 0, 0, 0)),
            pl.BlockSpec((deep, width), lambda j: (j, 0)),
            pl.BlockSpec((span, width), lambda j: (first_down + j, 0)),
        ] + specs,
        out_specs=tuple(specs),
        compiler_params=pltpu.CompilerParams(vmem_limit_bytes=VMEM_BYTES),
        name="update",
    )(tail, grad, grad, *weights)


def fast(
    patches, out_grad, item_ids, expert_ids,
    qkv_master, qkv_first, qkv_second,
    proj_master, proj_first, proj_second,
    router_master, router_first, router_second,
    gains_master, gains_first, gains_second,
    inner_master, inner_first, inner_second,
    down_master, down_first, down_second,
):
    width = patches.shape[2]
    experts = router_master.shape[1]
    hidden = down_master.shape[1] * lax.axis_size("dp")
    deep = inner_master.shape[1]
    blocks = inner_master.shape[2] // width
    shard = jnp.concatenate(
        [
            jnp.swapaxes(inner_master[0].reshape(deep, blocks, width), 0, 1).reshape(blocks * deep, width),
            down_master[0],
        ],
        axis=0,
    ).astype(BF16)
    router_w = router_master.T.astype(BF16)
    ids = jnp.swapaxes(expert_ids, 1, 2)
    table = jnp.asarray(rope_table(QB))
    full, kept, mixed, probs, att, mid, nm, block_out, gmid, glog = run_forward(
        shard, patches, out_grad, item_ids, ids, qkv_master, proj_master, router_w, gains_master, table, hidden, 0
    )
    patch_grad, grad, tail = run_backward(
        kept, patches, out_grad, item_ids, qkv_master, proj_master, gains_master, table,
        gmid, glog, mixed, probs, att, mid, nm, 1,
    )
    weights = (
        qkv_master, qkv_first, qkv_second,
        proj_master, proj_first, proj_second,
        router_master, router_first, router_second,
        gains_master, gains_first, gains_second,
        inner_master[0], inner_first[0], inner_second[0],
        down_master[0], down_first[0], down_second[0],
    )
    new = run_update(tail, grad, weights)
    return (block_out, patch_grad, *new[:12], *(value[None] for value in new[12:]))


GATHER_LIMIT = 16 * 1024 * 1024


def step(*args):
    inner_master, down_master = args[16], args[19]
    experts = inner_master.shape[0] * lax.axis_size("expert")
    entries = inner_master.shape[1] * inner_master.shape[2] + down_master.shape[1] * down_master.shape[2]
    weight_bytes = 2 * experts * entries * lax.axis_size("dp")
    square = lax.axis_size("dp") == 4 and inner_master.shape[0] == 1 and lax.axis_size("expert") == experts
    return (fast if square and weight_bytes <= GATHER_LIMIT else local)(*args)


def solution(mesh):
    in_specs = (
        P(None, ("dp", "expert"), None),
        P(None, ("dp", "expert"), None),
        P(None, ("dp", "expert"), None),
        P(None, ("dp", "expert"), None),
        P(),
        P(),
        P(),
        P(),
        P(),
        P(),
        P(),
        P(),
        P(),
        P(),
        P(),
        P(),
        P("expert", "dp", None),
        P("expert", "dp", None),
        P("expert", "dp", None),
        P("expert", "dp", None),
        P("expert", "dp", None),
        P("expert", "dp", None),
    )
    out_specs = (
        P(None, ("dp", "expert"), None),
        P(None, ("dp", "expert"), None),
        P(),
        P(),
        P(),
        P(),
        P(),
        P(),
        P(),
        P(),
        P(),
        P(),
        P(),
        P(),
        P("expert", "dp", None),
        P("expert", "dp", None),
        P("expert", "dp", None),
        P("expert", "dp", None),
        P("expert", "dp", None),
        P("expert", "dp", None),
    )
    return jax.shard_map(step, mesh=mesh, in_specs=in_specs, out_specs=out_specs, check_vma=False)
```

```python
import functools

import jax
import jax.numpy as jnp
import numpy as np
from jax import lax
from jax.experimental import pallas as pl
from jax.experimental.pallas import tpu as pltpu
from jax.sharding import PartitionSpec as P

HEADS = 6
HEAD = 64


norm_eps = 1e-06
adam_eps = 1e-08
correction = 0.875


def rotary_tables(item_row):
    length = item_row.shape[0]
    places = jnp.arange(length, dtype=jnp.int32)
    starts = jnp.concatenate([jnp.ones((1,), dtype=bool), item_row[1:] != item_row[:-1]])
    first = lax.cummax(jnp.where(starts, places, 0), axis=0)
    offset = (places - first).astype(jnp.float32)
    half = HEAD // 2
    freqs = 10000.0 ** (-jnp.arange(half, dtype=jnp.float32) / half)
    angles = offset[:, None] * freqs[None, :]
    return (jnp.cos(angles), jnp.sin(angles))


def rotate(vectors, cosine, sine):
    half = vectors.shape[-1] // 2
    first_half = vectors[..., :half]
    second_half = vectors[..., half:]
    cos_part = cosine[:, None, :]
    sin_part = sine[:, None, :]
    return jnp.concatenate(
        [
            first_half * cos_part - second_half * sin_part,
            second_half * cos_part + first_half * sin_part,
        ],
        axis=-1,
    )


def masked_scores(query, keys, same_item):
    scores = jnp.einsum("qhe,khe->hqk", query, keys, preferred_element_type=jnp.float32) * 0.125
    return jnp.where(same_item[None], scores, -1e30)


def adamw(weight, first, second, grad, rate, decay):
    first_new = 0.5 * first + 0.5 * grad
    second_new = 0.5 * second + 0.5 * grad * grad
    update = first_new / correction / (jnp.sqrt(second_new / correction) + adam_eps)
    return (weight - rate * (update + decay * weight), first_new, second_new)


def local(
    patches,
    out_grad,
    item_ids,
    expert_ids,
    qkv_master,
    qkv_first,
    qkv_second,
    proj_master,
    proj_first,
    proj_second,
    router_master,
    router_first,
    router_second,
    gains_master,
    gains_first,
    gains_second,
    inner_master,
    inner_first,
    inner_second,
    down_master,
    down_first,
    down_second,
):
    expert_count = lax.axis_size("expert")
    local_experts = inner_master.shape[0]
    experts = expert_count * local_experts
    length = patches.shape[1]
    width = patches.shape[2]
    top = expert_ids.shape[2]
    capacity = 2 * length * top // experts
    hidden_width = down_master.shape[1] * lax.axis_size("dp")
    inner_low, down_low = (
        lax.all_gather(inner_master.astype(jnp.bfloat16), "dp", axis=1, tiled=True),
        lax.all_gather(down_master.astype(jnp.bfloat16), "dp", axis=1, tiled=True),
    )
    qkv_low = qkv_master.astype(jnp.bfloat16)
    proj_low = proj_master.astype(jnp.bfloat16)
    router_low = router_master.astype(jnp.bfloat16)
    gain_attn = gains_master[0]
    gain_ffn = gains_master[1]
    expert_numbers = jnp.arange(experts, dtype=jnp.int32)

    def expert_forward(received):
        count = received.shape[1]
        grid = received.reshape(expert_count, local_experts, count, width)
        both = jnp.einsum("sjcd,jdf->sjcf", grid, inner_low, preferred_element_type=jnp.float32)
        hidden = (jax.nn.silu(both[..., :hidden_width]) * both[..., hidden_width:]).astype(
            jnp.bfloat16
        )
        result = jnp.einsum("sjcf,jfd->sjcd", hidden, down_low, preferred_element_type=jnp.float32)
        result = result.astype(jnp.bfloat16).reshape(experts, count, width)
        returned = lax.all_to_all(result, "expert", split_axis=0, concat_axis=0, tiled=True)
        return (returned, received)

    def micro_step(carry, inputs):
        grad_qkv, grad_proj, grad_router, grad_gains, grad_inner, grad_down = carry
        patch, upstream, item_block, routes = inputs
        items = item_block[0]
        source = patch.astype(jnp.float32)
        inv_first = lax.rsqrt(jnp.mean(source * source, axis=1, keepdims=True) + norm_eps)
        unit_first = source * inv_first
        normed_in = (unit_first * gain_attn).astype(jnp.bfloat16)
        mixed = jnp.dot(normed_in, qkv_low, preferred_element_type=jnp.float32)
        cosine, sine = rotary_tables(items)
        query = rotate(mixed[:, :width].reshape(length, HEADS, HEAD), cosine, sine).astype(
            jnp.bfloat16
        )
        keys = rotate(
            mixed[:, width : 2 * width].reshape(length, HEADS, HEAD), cosine, sine
        ).astype(jnp.bfloat16)
        values = mixed[:, 2 * width :].reshape(length, HEADS, HEAD).astype(jnp.bfloat16)
        same_item = items[:, None] == items[None, :]
        scores = masked_scores(query, keys, same_item)
        peak = jnp.max(scores, axis=2, keepdims=True)
        weights = jnp.exp(scores - peak)
        totals = jnp.sum(weights, axis=2, keepdims=True)
        probs_low = (weights / totals).astype(jnp.bfloat16)
        log_total = peak + jnp.log(totals)
        attended = jnp.einsum("hqk,khe->qhe", probs_low, values, preferred_element_type=jnp.float32)
        attended = attended.reshape(length, width).astype(jnp.bfloat16)
        middle = source + jnp.dot(attended, proj_low, preferred_element_type=jnp.float32)
        inv_second = lax.rsqrt(jnp.mean(middle * middle, axis=1, keepdims=True) + norm_eps)
        unit_second = middle * inv_second
        normed_mid = (unit_second * gain_ffn).astype(jnp.bfloat16)
        logits = jnp.dot(normed_mid, router_low, preferred_element_type=jnp.float32)
        chosen = jnp.take_along_axis(logits, routes, axis=1)
        gates = jax.nn.softmax(chosen, axis=1)
        flat_ids = routes.reshape(length * top)
        hits = (flat_ids[:, None] == expert_numbers[None, :]).astype(jnp.int32)
        rank = jnp.sum(jnp.cumsum(hits, axis=0) * hits, axis=1) - 1
        slots = flat_ids * capacity + rank
        copies = jnp.repeat(normed_mid, top, axis=0)
        outgoing = jnp.zeros((experts * capacity, width), jnp.bfloat16).at[slots].set(copies)
        outgoing = outgoing.reshape(experts, capacity, width)
        returned, kept_inputs = expert_forward(
            lax.all_to_all(outgoing, "expert", split_axis=0, concat_axis=0, tiled=True)
        )
        picked = (
            returned.reshape(experts * capacity, width)[slots]
            .reshape(length, top, width)
            .astype(jnp.float32)
        )
        combined = jnp.sum(gates[:, :, None] * picked, axis=1)
        block_out = (middle + combined).astype(jnp.bfloat16)
        upstream_full = upstream.astype(jnp.float32)
        grad_gate = jnp.sum(upstream_full[:, None, :] * picked, axis=2)
        grad_chosen = gates * (grad_gate - jnp.sum(gates * grad_gate, axis=1, keepdims=True))
        route_hits = (routes[:, :, None] == expert_numbers[None, None, :]).astype(jnp.float32)
        grad_logits = jnp.sum(grad_chosen[:, :, None] * route_hits, axis=1).astype(jnp.bfloat16)
        grad_router_now = jnp.dot(normed_mid.T, grad_logits, preferred_element_type=jnp.float32)
        grad_mid = jnp.dot(grad_logits, router_low.T, preferred_element_type=jnp.float32)
        grad_slots = (
            (gates[:, :, None] * upstream_full[:, None, :])
            .astype(jnp.bfloat16)
            .reshape(length * top, width)
        )
        grad_outgoing = (
            jnp.zeros((experts * capacity, width), jnp.bfloat16).at[slots].set(grad_slots)
        )
        grad_outgoing = grad_outgoing.reshape(experts, capacity, width)
        incoming, inputs_back = (
            lax.all_to_all(grad_outgoing, "expert", split_axis=0, concat_axis=0, tiled=True),
            lax.all_to_all(outgoing, "expert", split_axis=0, concat_axis=0, tiled=True),
        )
        grid_in = inputs_back.reshape(expert_count, local_experts, capacity, width)
        grid_grad = incoming.reshape(expert_count, local_experts, capacity, width)
        both = jnp.einsum("sjcd,jdf->sjcf", grid_in, inner_low, preferred_element_type=jnp.float32)
        gate_part = both[..., :hidden_width]
        up_part = both[..., hidden_width:]
        sigma = jax.nn.sigmoid(gate_part)
        activated = jax.nn.silu(gate_part)
        hidden = (activated * up_part).astype(jnp.bfloat16)
        grad_hidden = jnp.einsum(
            "sjcd,jfd->sjcf", grid_grad, down_low, preferred_element_type=jnp.float32
        )
        grad_down_now = jnp.einsum(
            "sjcf,sjcd->jfd", hidden, grid_grad, preferred_element_type=jnp.float32
        )
        grad_both = jnp.concatenate(
            [
                grad_hidden * up_part * sigma * (1.0 + gate_part * (1.0 - sigma)),
                grad_hidden * activated,
            ],
            axis=3,
        ).astype(jnp.bfloat16)
        grad_inner_now = jnp.einsum(
            "sjcd,sjcf->jdf", grid_in, grad_both, preferred_element_type=jnp.float32
        )
        grad_copies = jnp.einsum(
            "sjcf,jdf->sjcd", grad_both, inner_low, preferred_element_type=jnp.float32
        )
        grad_copies = grad_copies.astype(jnp.bfloat16).reshape(experts, capacity, width)
        grad_back = lax.all_to_all(grad_copies, "expert", split_axis=0, concat_axis=0, tiled=True)
        grad_picked = grad_back.reshape(experts * capacity, width)[slots].reshape(
            length, top, width
        )
        grad_mid = grad_mid + jnp.sum(grad_picked.astype(jnp.float32), axis=1)
        grad_unit_second = grad_mid * gain_ffn
        grad_gain_ffn = jnp.sum(grad_mid * unit_second, axis=0)
        grad_middle = upstream_full + inv_second * (
            grad_unit_second
            - unit_second * jnp.mean(grad_unit_second * unit_second, axis=1, keepdims=True)
        )
        grad_branch = grad_middle.astype(jnp.bfloat16)
        grad_proj_now = jnp.dot(attended.T, grad_branch, preferred_element_type=jnp.float32)
        grad_attended = jnp.dot(grad_branch, proj_low.T, preferred_element_type=jnp.float32)
        grad_attended = grad_attended.astype(jnp.bfloat16).reshape(length, HEADS, HEAD)
        probs_again = jnp.exp(masked_scores(query, keys, same_item) - log_total)
        grad_probs = jnp.einsum(
            "qhe,khe->hqk", grad_attended, values, preferred_element_type=jnp.float32
        )
        grad_values = jnp.einsum(
            "hqk,qhe->khe", probs_low, grad_attended, preferred_element_type=jnp.float32
        )
        grad_scores = probs_again * (
            grad_probs - jnp.sum(probs_again * grad_probs, axis=2, keepdims=True)
        )
        grad_scores = grad_scores.astype(jnp.bfloat16)
        grad_query = (
            jnp.einsum("hqk,khe->qhe", grad_scores, keys, preferred_element_type=jnp.float32)
            * 0.125
        )
        grad_keys = (
            jnp.einsum("hqk,qhe->khe", grad_scores, query, preferred_element_type=jnp.float32)
            * 0.125
        )
        grad_mixed = jnp.concatenate(
            [
                rotate(grad_query, cosine, -sine).reshape(length, width),
                rotate(grad_keys, cosine, -sine).reshape(length, width),
                grad_values.reshape(length, width),
            ],
            axis=1,
        ).astype(jnp.bfloat16)
        grad_qkv_now = jnp.dot(normed_in.T, grad_mixed, preferred_element_type=jnp.float32)
        grad_normed = jnp.dot(grad_mixed, qkv_low.T, preferred_element_type=jnp.float32)
        grad_unit_first = grad_normed * gain_attn
        grad_gain_attn = jnp.sum(grad_normed * unit_first, axis=0)
        patch_grad = grad_middle + inv_first * (
            grad_unit_first
            - unit_first * jnp.mean(grad_unit_first * unit_first, axis=1, keepdims=True)
        )
        new_carry = (
            grad_qkv + grad_qkv_now,
            grad_proj + grad_proj_now,
            grad_router + grad_router_now,
            grad_gains + jnp.stack([grad_gain_attn, grad_gain_ffn]),
            grad_inner + grad_inner_now,
            grad_down + grad_down_now,
        )
        return (new_carry, (block_out, patch_grad))

    start = (
        jnp.zeros(qkv_master.shape, jnp.float32),
        jnp.zeros(proj_master.shape, jnp.float32),
        jnp.zeros(router_master.shape, jnp.float32),
        jnp.zeros(gains_master.shape, jnp.float32),
        jnp.zeros(inner_low.shape, jnp.float32),
        jnp.zeros(down_low.shape, jnp.float32),
    )
    totals, outputs = lax.scan(micro_step, start, (patches, out_grad, item_ids, expert_ids))
    grad_qkv, grad_proj, grad_router, grad_gains = lax.psum(
        (totals[0], totals[1], totals[2], totals[3]), ("dp", "expert")
    )
    grad_inner, grad_down = (
        lax.psum_scatter(totals[4], "dp", scatter_dimension=1, tiled=True),
        lax.psum_scatter(totals[5], "dp", scatter_dimension=1, tiled=True),
    )
    qkv_new = adamw(qkv_master, qkv_first, qkv_second, grad_qkv, 0.1, 0.1)
    proj_new = adamw(proj_master, proj_first, proj_second, grad_proj, 0.4, 0.1)
    router_new = adamw(router_master, router_first, router_second, grad_router, 0.07, 0.1)
    gains_new = adamw(gains_master, gains_first, gains_second, grad_gains, 0.4, 0.0)
    inner_new = adamw(inner_master, inner_first, inner_second, grad_inner, 0.1, 0.1)
    down_new = adamw(down_master, down_first, down_second, grad_down, 0.15, 0.1)
    return (
        outputs[0],
        outputs[1],
        qkv_new[0],
        qkv_new[1],
        qkv_new[2],
        proj_new[0],
        proj_new[1],
        proj_new[2],
        router_new[0],
        router_new[1],
        router_new[2],
        gains_new[0],
        gains_new[1],
        gains_new[2],
        inner_new[0],
        inner_new[1],
        inner_new[2],
        down_new[0],
        down_new[1],
        down_new[2],
    )


F32 = jnp.float32
BF16 = jnp.bfloat16
QB = 128


def iota(shape, axis):
    return lax.broadcasted_iota(jnp.int32, shape, axis)


def dot_nn(a, b):
    return jnp.dot(a, b, preferred_element_type=F32)


def dot_nt(a, b):
    return lax.dot_general(a, b, (((1,), (1,)), ((), ())), preferred_element_type=F32)


def dot_tn(a, b):
    return lax.dot_general(a, b, (((0,), (0,)), ((), ())), preferred_element_type=F32)


def swap_halves(v, low_lane):
    width = v.shape[1]
    half = HEAD // 2
    return jnp.where(low_lane, pltpu.roll(v, width - half, 1), pltpu.roll(v, half, 1))


def turn(v, cos_row, sin_row, low_lane):
    return v * cos_row + swap_halves(v, low_lane) * sin_row


def rope_table(item_max):
    half = HEAD // 2
    offset = np.arange(item_max, dtype=np.float32)
    freqs = np.float32(10000.0) ** (-np.arange(half, dtype=np.float32) / np.float32(half))
    angles = (offset[:, None] * freqs[None, :]).astype(np.float32)
    cosine, sine = np.cos(angles), np.sin(angles)
    return np.concatenate([cosine] * 4 + [-sine, sine] * 2, axis=1).astype(np.float32)


def windows(length):
    found = []
    for start in range(0, length, QB):
        low = max(0, start - QB)
        high = min(length, start + 2 * QB)
        found.append((start, low, high))
    return found


def row_norm(values):
    return lax.rsqrt(jnp.mean(values * values, axis=1, keepdims=True) + norm_eps)


def positions(item_row, length):
    eye = iota((length, length), 0) == iota((length, length), 1)
    col = jnp.sum(jnp.where(eye, item_row, 0.0), axis=1, keepdims=True)
    before = jnp.sum(jnp.where(item_row < col, 1.0, 0.0), axis=1, keepdims=True)
    offset = iota((length, 1), 0) - before.astype(jnp.int32)
    return col, offset


def rope_rows(offset, table, length, width):
    spots = table.shape[0]
    pick = jnp.where(iota((length, spots), 1) == offset, 1.0, 0.0)
    both = jnp.dot(pick, table, precision=lax.Precision.HIGHEST, preferred_element_type=F32)
    copies = width // 128
    return (
        jnp.concatenate([both[:, :128]] * copies, axis=1),
        jnp.concatenate([both[:, 128:]] * copies, axis=1),
    )


VMEM_BYTES = 64 * 1024 * 1024 - 512 * 1024


MESH_ID = pl.DeviceIdType.MESH


class Place:
    def __init__(self, line):
        self.line = line
        dp, ex = lax.axis_index("dp"), lax.axis_index("expert")
        self.x, self.core = lax.div(dp, 2), lax.rem(dp, 2)
        self.z, self.y = lax.div(ex, 2), lax.rem(ex, 2)

    def device(self, flip_x=0, flip_y=0, flip_core=0, z=None):
        x = 1 - self.x if flip_x else self.x
        y = 1 - self.y if flip_y else self.y
        core = 1 - self.core if flip_core else self.core
        return (2 * x + core, 2 * (self.z if z is None else z) + y)

    def levels(self):
        found = [(0, self.z, None, 0)]
        for away in range(1, self.line):
            found.append((away, self.z - away, lambda a=away: self.z >= a, -1))
            found.append((away, self.z + away, lambda a=away: self.z + a < self.line, 1))
        return found

    def up(self):
        return self.z + 1 < self.line

    def down(self):
        return self.z > 0

    def by_distance(self, i):
        found = 0
        for z in range(self.line):
            order = sorted(range(self.line), key=lambda level: (abs(level - z), level))
            for place, level in enumerate(order):
                hit = jnp.logical_and(self.z == z, i == place).astype(jnp.int32)
                found = found + hit * level
        return found

    def greet(self):
        barrier = pltpu.get_barrier_semaphore()

        def signal(device):
            pl.semaphore_signal(barrier, inc=1, device_id=device, device_id_type=MESH_ID)

        for device in (self.device(1), self.device(0, 1), self.device(1, 1), self.device(0, 0, 1)):
            signal(device)
        for step in range(1, self.line):
            signal(self.device(z=lax.rem(self.z + step, self.line)))
        pl.semaphore_wait(barrier, self.line + 3)


def both(*tests):
    tests = [t for t in tests if t is not None]

    def all_of():
        found = tests[0]()
        for t in tests[1:]:
            found = jnp.logical_and(found, t())
        return found

    return all_of if tests else None


def only(test, body):
    if test is None:
        body()
    else:
        pl.when(test())(body)


def remote(source, target, departure, arrival, device):
    return pltpu.make_async_remote_copy(
        src_ref=source,
        dst_ref=target,
        send_sem=departure,
        recv_sem=arrival,
        device_id=device,
        device_id_type=MESH_ID,
    )


class Wires:
    def __init__(self, send_sem, like):
        self.send_sem, self.like = send_sem, like
        self.sent = []

    def send(self, source, target, arrival, device, test=None):
        copy = pltpu.make_async_remote_copy(
            src_ref=source,
            dst_ref=target,
            send_sem=self.send_sem.at[len(self.sent)],
            recv_sem=arrival,
            device_id=device,
            device_id_type=MESH_ID,
        )
        only(test, copy.start)
        self.sent.append(test)

    def arrived(self, target, arrival, device, test=None):
        copy = pltpu.make_async_remote_copy(
            src_ref=target,
            dst_ref=target,
            send_sem=self.send_sem.at[0],
            recv_sem=arrival,
            device_id=device,
            device_id_type=MESH_ID,
        )
        only(test, copy.wait_recv)

    def finish(self):
        for number, test in enumerate(self.sent):
            copy = pltpu.make_async_remote_copy(
                src_ref=self.like,
                dst_ref=self.like,
                send_sem=self.send_sem.at[number],
                recv_sem=self.send_sem.at[number],
                device_id=(0, 0),
                device_id_type=MESH_ID,
            )
            only(test, copy.wait_send)


class Gather:
    def __init__(self, place, shard, full, send_sem, recv_sem, copy_sem):
        self.place, self.shard, self.full = place, shard, full
        self.recv_sem, self.copy_sem = recv_sem, copy_sem
        self.wires = Wires(send_sem, shard)

    def at(self, device):
        return self.full.at[device[1], device[0]]

    def ready(self, device):
        return self.recv_sem.at[device[1], device[0]]

    def pass_on(self, origin, to, test=None, source=None):
        source = self.at(origin) if source is None else source
        self.wires.send(source, self.at(origin), self.ready(origin), to, test)

    def wait(self, origin, test=None):
        self.wires.arrived(self.at(origin), self.ready(origin), self.place.device(0, 0, 1), test)

    def start(self):
        place = self.place
        me = place.device()
        self.pass_on(me, place.device(z=place.z + 1), place.up, self.shard)
        self.pass_on(me, place.device(z=place.z - 1), place.down, self.shard)
        self.pass_on(me, place.device(1), None, self.shard)
        self.pass_on(me, place.device(0, 1), None, self.shard)
        self.pass_on(me, place.device(0, 0, 1), None, self.shard)
        self.own = pltpu.make_async_copy(self.shard, self.at(me), self.copy_sem)
        self.own.start()

    def column(self, away):
        place = self.place
        for dist, level, test, way in place.levels():
            if dist != away:
                continue
            origin = place.device(z=level)
            self.wait(origin, test)
            if way < 0:
                self.pass_on(origin, place.device(z=place.z + 1), both(test, place.up))
            if way > 0:
                self.pass_on(origin, place.device(z=place.z - 1), both(test, place.down))
            self.pass_on(origin, place.device(1), test)
            self.pass_on(origin, place.device(0, 1), test)
            self.pass_on(origin, place.device(0, 0, 1), test)

    def square(self, away):
        place = self.place
        for dist, level, test, way in place.levels():
            if dist != away:
                continue
            over_x, over_y = place.device(1, z=level), place.device(0, 1, z=level)
            self.wait(over_x, test)
            if dist % 2 == 0:
                self.pass_on(over_x, place.device(0, 1), test)
            self.pass_on(over_x, place.device(0, 0, 1), test)
            self.wait(over_y, test)
            if dist % 2 == 1:
                self.pass_on(over_y, place.device(1), test)
            self.pass_on(over_y, place.device(0, 0, 1), test)

    def corner(self, away):
        place = self.place
        for dist, level, test, way in place.levels():
            if dist != away:
                continue
            across = place.device(1, 1, z=level)
            self.wait(across, test)
            self.pass_on(across, place.device(0, 0, 1), test)

    def partner(self, flip_x, flip_y, level):
        self.wait(self.place.device(flip_x, flip_y, 1, z=level))


OWN, OVER_X, OVER_Y, ACROSS = 0, 1, 2, 3
EARLY = 2


class Close:
    def __init__(self, place, kept, owns, sides, diag_in, side_in, line_in, load_sem, sems):
        self.place, self.kept, self.owns, self.sides = place, kept, owns, sides
        self.diag_in, self.side_in, self.line_in, self.load_sem = diag_in, side_in, line_in, load_sem
        self.diag_send, self.diag_sem, self.side_send, self.side_sem, self.line_send, self.line_sem = sems

    def level(self, slot):
        return self.place.by_distance(self.place.line - 1 - slot)

    def load(self, which, slot):
        target = self.owns if which == 0 else self.sides
        return pltpu.make_async_copy(
            self.kept.at[which, self.level(slot)], target.at[slot], self.load_sem.at[which, slot]
        )

    def across(self, slot):
        level = self.level(slot)
        return remote(
            self.kept.at[2, level], self.diag_in.at[slot], self.diag_send.at[slot], self.diag_sem.at[slot],
            self.place.device(1),
        )

    def aside(self, slot):
        level = self.level(slot)
        source = self.kept.at[1, level] if slot < EARLY else self.sides.at[slot]
        return remote(
            source, self.side_in.at[slot], self.side_send.at[slot], self.side_sem.at[slot],
            self.place.device(1) if slot == 0 else self.place.device(0, 1),
        )

    def along(self, slot):
        return remote(
            self.owns.at[slot], self.line_in.at[self.place.z], self.line_send.at[slot],
            self.line_sem.at[self.place.z], self.place.device(z=self.level(slot)),
        )

    def start(self):
        for slot in range(self.place.line):
            (self.aside(slot) if slot < EARLY else self.across(slot)).start()
            self.load(0, slot).start()
            if slot >= EARLY:
                self.load(1, slot).start()

    def send_side(self, slot):
        self.load(1, slot).wait()
        self.across(slot).wait_recv()
        self.sides[slot] = (self.sides[slot].astype(F32) + self.diag_in[slot].astype(F32)).astype(BF16)
        self.aside(slot).start()

    def collect(self, slot):
        self.load(0, slot).wait()
        self.aside(slot).wait_recv()
        return self.owns[slot].astype(F32) + self.side_in[slot].astype(F32)

    def send_line(self, slot):
        self.owns[slot] = self.collect(slot).astype(BF16)
        self.along(slot).start()

    def finish(self, out):
        place = self.place
        last = place.line - 1
        out[...] = self.collect(last)
        for step in range(1, place.line):
            z = lax.rem(place.z + step, place.line)
            remote(
                self.owns.at[0], self.line_in.at[z], self.line_send.at[0], self.line_sem.at[z],
                place.device(z=z),
            ).wait_recv()
            out[...] += self.line_in[z].astype(F32)
        for slot in range(place.line):
            self.aside(slot).wait_send()
            if slot >= EARLY:
                self.across(slot).wait_send()
            if slot < last:
                self.along(slot).wait_send()


class Small:
    def __init__(self, place, part, low, out, sums, core_in, square_in, line_in, sems):
        self.place, self.part, self.low, self.out = place, part, low, out
        self.sums, self.core_in, self.square_in, self.line_in = sums, core_in, square_in, line_in
        (
            self.core_send, self.core_sem, self.square_send, self.square_sem, self.line_send, self.line_sem,
            self.up_send, self.up_sem, self.back_send, self.back_sem, self.last_send, self.last_sem,
        ) = sems

    def lane(self, group, flip_core=0):
        place = self.place
        x = 1 - place.x if group in (OVER_X, ACROSS) else place.x
        y = 1 - place.y if group in (OVER_Y, ACROSS) else place.y
        core = 1 - place.core if flip_core else place.core
        return y, 2 * x + core

    def to(self, group):
        return self.place.device(int(group in (OVER_X, ACROSS)), int(group in (OVER_Y, ACROSS)))

    def core(self, group):
        y, d = self.lane(group, 1)
        return remote(
            self.part.at[y, d], self.core_in.at[group], self.core_send.at[group], self.core_sem.at[group],
            self.place.device(0, 0, 1),
        )

    def over(self, group):
        return remote(
            self.sums.at[group], self.square_in.at[group - 1], self.square_send.at[group - 1],
            self.square_sem.at[group - 1], self.to(group),
        )

    def along(self, z):
        return remote(
            self.sums.at[OWN, z], self.line_in.at[self.place.z], self.line_send.at[z],
            self.line_sem.at[self.place.z], self.place.device(z=z),
        )

    def landed(self, z):
        return remote(
            self.sums.at[OWN, z], self.line_in.at[z], self.line_send.at[z], self.line_sem.at[z],
            self.place.device(z=z),
        )

    def up(self, z):
        y, d = self.lane(OWN)
        return remote(
            self.low, self.out.at[y, d, self.place.z], self.up_send.at[z], self.up_sem.at[self.place.z],
            self.place.device(z=z),
        )

    def risen(self, z):
        y, d = self.lane(OWN)
        return remote(self.low, self.out.at[y, d, z], self.up_send.at[z], self.up_sem.at[z], self.place.device(z=z))

    def back(self, group):
        y, d = self.lane(OWN)
        return remote(
            self.out.at[y, d], self.out.at[y, d], self.back_send.at[group - 1], self.back_sem.at[group - 1],
            self.to(group),
        )

    def last(self, group):
        y, d = self.lane(group)
        return remote(
            self.out.at[y, d], self.out.at[y, d], self.last_send.at[group], self.last_sem.at[group],
            self.place.device(0, 0, 1),
        )

    def others(self):
        return [lax.rem(self.place.z + step, self.place.line) for step in range(1, self.place.line)]

    def start(self):
        for group in (ACROSS, OVER_X, OVER_Y, OWN):
            self.core(group).start()

    def run(self):
        place = self.place
        for group in (ACROSS, OVER_X, OVER_Y, OWN):
            self.core(group).wait_recv()
            total = self.part[self.lane(group)].astype(F32) + self.core_in[group].astype(F32)
            self.sums[group] = total.astype(BF16)
            if group != OWN:
                self.over(group).start()
        total = self.sums[OWN].astype(F32)
        for group in (OVER_X, OVER_Y, ACROSS):
            self.over(group).wait_recv()
            total = total + self.square_in[group - 1].astype(F32)
        self.sums[OWN] = total.astype(BF16)
        for z in self.others():
            self.along(z).start()
        total = self.sums[OWN, place.z].astype(F32)
        for z in self.others():
            self.landed(z).wait_recv()
            total = total + self.line_in[z].astype(F32)
        self.low[...] = total.astype(BF16)
        for z in self.others():
            self.up(z).start()
        y, d = self.lane(OWN)
        self.out[y, d, place.z] = total.astype(BF16)
        for z in self.others():
            self.risen(z).wait_recv()
        for group in (ACROSS, OVER_X, OVER_Y):
            self.back(group).start()
        self.last(OWN).start()

    def finish(self):
        for group in (OVER_X, OVER_Y, ACROSS):
            self.back(group).wait_recv()
            self.last(group).start()
        for group in (OWN, OVER_X, OVER_Y, ACROSS):
            self.last(group).wait_recv()
        for group in (OWN, OVER_X, OVER_Y, ACROSS):
            self.core(group).wait_send()
            self.last(group).wait_send()
            if group != OWN:
                self.over(group).wait_send()
                self.back(group).wait_send()
        for z in self.others():
            self.along(z).wait_send()
            self.up(z).wait_send()


def copy_all(copies):
    for copy in copies:
        copy.start()


def attend_pack(p, patches, items, gains, table, qkv_s, proj_s, mixed_s, probs_s, att_s, mid_s, nm_s):
    _, length, width = patches.shape
    pairs = width // 128
    slot = lax.rem(p, mixed_s.shape[0])
    low_lane = iota((1, width), 1) % HEAD < HEAD // 2
    first_head = iota((1, 128), 1) < HEAD
    mask_a = jnp.where(first_head, 1.0, 0.0).astype(BF16)
    mask_b = jnp.where(first_head, 0.0, 1.0).astype(BF16)
    top_rows = iota((128, 1), 0) < HEAD
    source = patches[p].astype(F32)
    normed = (source * row_norm(source) * gains[0:1, :]).astype(BF16)
    mixed = dot_nn(normed, qkv_s[...])
    item_row = items[p].astype(F32)
    item_col, offset = positions(item_row, length)
    cos_row, sin_row = rope_rows(offset, table[...], length, width)
    mixed_s[slot, :, :width] = turn(mixed[:, :width], cos_row, sin_row, low_lane).astype(BF16)
    mixed_s[slot, :, width : 2 * width] = turn(
        mixed[:, width : 2 * width], cos_row, sin_row, low_lane
    ).astype(BF16)
    mixed_s[slot, :, 2 * width :] = mixed[:, 2 * width :].astype(BF16)
    for pair in range(pairs):
        lanes = slice(128 * pair, 128 * pair + 128)
        key_lanes = slice(width + 128 * pair, width + 128 * pair + 128)
        values_t = mixed[:, 2 * width + 128 * pair : 2 * width + 128 * pair + 128].T.astype(BF16)
        for block, (start, low, high) in enumerate(windows(length)):
            query = mixed_s[slot, start : start + QB, lanes] * 0.125
            query = jnp.concatenate([query * mask_a, query * mask_b], axis=0)
            scores = dot_nt(mixed_s[slot, low:high, key_lanes], query)
            here = item_row[:, start : start + QB]
            same = item_col[low:high] == jnp.concatenate([here, here], axis=1)
            scores = jnp.where(same, scores, -1e30)
            peak = jnp.max(scores, axis=0, keepdims=True)
            weights = jnp.exp(scores - peak)
            total = jnp.sum(weights, axis=0, keepdims=True)
            probs = (weights * (1.0 / total)).astype(BF16)
            probs_s[slot, pair, block, : high - low] = probs
            out = dot_nn(values_t[:, low:high], probs)
            out = jnp.where(top_rows, out[:, :QB], out[:, QB:])
            att_s[p, start : start + QB, lanes] = out.T.astype(BF16)
    middle = source + dot_nn(att_s[p], proj_s[...])
    mid_s[p] = middle
    nm_s[p] = (middle * row_norm(middle) * gains[1:2, :]).astype(BF16)


class Experts:
    def __init__(self, refs, cap):
        (
            self.nm, self.upstream, self.rank_s, self.gate_s, self.gg_s, self.x_s, self.hid_s, self.go_s,
            self.gb_s, self.y_s, self.inner_w, self.down_w,
        ) = refs
        self.cap = cap

    def prepare(self, p, ids, router_w):
        nm = self.nm
        _, length, width = nm.shape
        experts = router_w.shape[0]
        earlier = jnp.where(iota((length, length), 0) < iota((length, length), 1), 1.0, 0.0).astype(BF16)
        logits = dot_nt(router_w[...], nm[p])
        number = iota((experts, length), 0)
        hit0 = number == ids[p, 0:1, :]
        hit1 = number == ids[p, 1:2, :]
        chosen0 = jnp.sum(jnp.where(hit0, logits, 0.0), axis=0, keepdims=True)
        chosen1 = jnp.sum(jnp.where(hit1, logits, 0.0), axis=0, keepdims=True)
        peak = jnp.maximum(chosen0, chosen1)
        e0 = jnp.exp(chosen0 - peak)
        e1 = jnp.exp(chosen1 - peak)
        total = e0 + e1
        self.gate_s[p] = jnp.where(hit0, e0 / total, 0.0) + jnp.where(hit1, e1 / total, 0.0)
        named = jnp.where(hit0, 1.0, jnp.where(hit1, 1.0, 0.0))
        rank = dot_nn(named.astype(BF16), earlier)
        self.rank_s[p] = jnp.where(named > 0.5, rank, -1.0)

    def rows(self, p, expert):
        cap = self.cap
        _, length, width = self.nm.shape
        hidden_width = self.hid_s.shape[1]
        here = pl.ds(pl.multiple_of(p * cap, cap), cap)
        rank = self.rank_s[p, pl.ds(expert, 1), :]
        gate_row = self.gate_s[p, pl.ds(expert, 1), :]
        pick = iota((cap, length), 0).astype(F32) == rank
        chosen = jnp.where(pick, 1.0, 0.0).astype(BF16)
        taken = dot_nn(chosen, jnp.concatenate([self.nm[p], self.upstream[p]], axis=1))
        gate_col = jnp.sum(jnp.where(pick, gate_row, 0.0), axis=1, keepdims=True)
        x = taken[:, :width].astype(BF16)
        g = taken[:, width:]
        self.x_s[here, :] = x
        grad_out = (gate_col * g).astype(BF16)
        self.go_s[here, :] = grad_out
        gate = dot_nn(x, self.inner_w[:, :hidden_width])
        up = dot_nn(x, self.inner_w[:, hidden_width:])
        sigma = 1.0 / (1.0 + jnp.exp(-gate))
        active = gate * sigma
        hidden = (active * up).astype(BF16)
        self.hid_s[here, :] = hidden
        result = dot_nn(hidden, self.down_w[...]).astype(BF16).astype(F32)
        spot = pl.ds(pl.multiple_of(expert * cap, cap), cap)
        self.y_s[p, spot, :width] = (gate_col * result).astype(BF16)
        grad_gate = jnp.sum(g * result, axis=1, keepdims=True)
        self.gg_s[p, pl.ds(expert, 1), :] = jnp.sum(
            jnp.where(pick, grad_gate, 0.0), axis=0, keepdims=True
        )
        grad_hidden = dot_nt(grad_out, self.down_w[...])
        self.gb_s[here, :hidden_width] = (
            grad_hidden * up * sigma * (1.0 + gate * (1.0 - sigma))
        ).astype(BF16)
        self.gb_s[here, hidden_width:] = (grad_hidden * active).astype(BF16)
        self.y_s[p, spot, width:] = dot_nt(self.gb_s[here, :], self.inner_w[...]).astype(BF16)

    def grads(self, part):
        copies, _, width = part.shape
        hidden_width = self.hid_s.shape[1]
        deep, span = width // copies, hidden_width // copies
        for block in range(2 * hidden_width // width):
            lanes = slice(block * width, block * width + width)
            grad = dot_tn(self.x_s[...], self.gb_s[:, lanes]).astype(BF16)
            for d in range(copies):
                part[d, block * deep : block * deep + deep, :] = grad[d * deep : d * deep + deep]
        grad = dot_tn(self.hid_s[...], self.go_s[...]).astype(BF16)
        for d in range(copies):
            part[d, width:, :] = grad[d * span : d * span + span]

    def finish(self, p, router_w, mid, block_o, gmid_o, glog_o):
        cap = self.cap
        _, length, width = self.nm.shape
        experts = router_w.shape[0]
        ranks = self.rank_s[p].T
        slot = iota((length, cap), 1).astype(F32)
        pieces = [
            jnp.where(ranks[:, e : e + 1] == slot, 1.0, 0.0).astype(BF16) for e in range(experts)
        ]
        back = dot_nn(jnp.concatenate(pieces, axis=1), self.y_s[p])
        gate = self.gate_s[p]
        grad_gate = self.gg_s[p]
        mean = jnp.sum(gate * grad_gate, axis=0, keepdims=True)
        hit = self.rank_s[p] > -0.5
        grad_logits = jnp.where(hit, gate * (grad_gate - mean), 0.0).astype(BF16)
        glog_o[p] = grad_logits
        block_o[p] = (mid[p] + back[:, :width]).astype(BF16)
        gmid_o[p] = back[:, width:] + dot_tn(grad_logits, router_w[...])


def unpack(weights, inner_w, down_w):
    copies, _, width = weights.shape
    deep, span = width // copies, down_w.shape[0] // copies
    for d in range(copies):
        for block in range(inner_w.shape[1] // width):
            inner_w[d * deep : d * deep + deep, block * width : block * width + width] = weights[
                d, block * deep : block * deep + deep, :
            ]
        down_w[d * span : d * span + span, :] = weights[d, width:, :]


def forward_kernel(
    line, cap,
    shard, patches, upstream, items, ids, qkv_w, proj_w, router_w, gains, table,
    full, kept_o, mixed_o, probs_o, att_o, mid_o, nm_o, block_o, gmid_o, glog_o,
    qkv_s, proj_s, mixed_s, probs_s, att_s, mid_s, nm_s, wbuf, pbuf,
    rank_s, gate_s, gg_s, x_s, hid_s, go_s, gb_s, y_s, inner_s, down_s,
    sums, core_in, diag_in, side_in,
    send_sem, recv_sem, own_sem, save_sem, fetch_sem, keep_sem,
    core_send, core_sem, diag_send, diag_sem, side_send, side_sem, credit_sem,
):
    packs = patches.shape[0]
    experts = router_w.shape[0]
    place = Place(line)
    place.greet()
    gather = Gather(place, shard, full, send_sem, recv_sem, own_sem)
    gather.start()
    qkv_s[...] = qkv_w[...].astype(BF16)
    proj_s[...] = proj_w[...].astype(BF16)
    work = Experts(
        (nm_s, upstream, rank_s, gate_s, gg_s, x_s, hid_s, go_s, gb_s, y_s, inner_s, down_s), cap
    )
    saves = ((mixed_s, mixed_o), (probs_s, probs_o), (att_s, att_o), (mid_s, mid_o), (nm_s, nm_o))

    def save(n, p):
        source, target = saves[n]
        return pltpu.make_async_copy(
            source.at[lax.rem(p, source.shape[0])], target.at[p], save_sem.at[n, p]
        )

    def pack(p, carry):
        def reuse():
            save(0, p - 2).wait()
            save(1, p - 2).wait()

        pl.when(p >= 2)(reuse)
        attend_pack(p, patches, items, gains, table, qkv_s, proj_s, mixed_s, probs_s, att_s, mid_s, nm_s)
        for n in range(len(saves)):
            save(n, p).start()
        work.prepare(p, ids, router_w)
        for k in range(1, line):

            def relay(k=k):
                gather.column(k)
                if k != 2:
                    gather.square(k // 2)

            pl.when(p == min(k - 1, packs - 1))(relay)
        return carry

    lax.fori_loop(0, packs, pack, 0)

    def near(i):
        return int(i < line) if isinstance(i, int) else (i < line).astype(jnp.int32)

    def number(i):
        level = place.by_distance(near(i) * i + (1 - near(i)) * (2 * line - 1 - i))
        side = near(i) * place.y + (1 - near(i)) * (1 - place.y)
        return level, 2 * level + side

    def fetch(i):
        return pltpu.make_async_copy(full.at[number(i)[1]], wbuf.at[lax.rem(i, 2)], fetch_sem.at[lax.rem(i, 2)])

    def arrive(i):
        level = number(i)[0]

        def close():
            gather.partner(0, 0, level)
            gather.partner(1, 0, level)

        def far():
            gather.partner(0, 1, level)
            gather.partner(1, 1, level)

        if isinstance(i, int):
            (close if i < line else far)()
        else:
            pl.when(i < line)(close)
            pl.when(i >= line)(far)

    def piece(q, flip_core):
        return place.device(q, 0, flip_core)[0]

    def swap(i, q):
        slot = lax.rem(i, 2)
        return remote(
            pbuf.at[slot, piece(q, 1)], core_in.at[slot, q], core_send.at[slot, q], core_sem.at[slot, q],
            place.device(0, 0, 1),
        )

    def across(n):
        level = number(line + n)[0]
        return remote(
            sums.at[ACROSS, level], diag_in.at[n], diag_send.at[n], diag_sem.at[n],
            place.device(0, 1) if n == 0 else place.device(1),
        )

    def aside(level, group=OVER_X):
        return remote(
            sums.at[group, level], side_in.at[level], side_send.at[level], side_sem.at[level],
            place.device(1) if group == OVER_X else place.device(0, 1),
        )

    def keep(which, group, level):
        return pltpu.make_async_copy(sums.at[group, level], kept_o.at[which, level], keep_sem.at[which, level])

    def merge(i):
        slot = lax.rem(i, 2)
        level = number(i)[0]
        group = 2 * (1 - near(i))
        for q in range(2):
            swap(i, q).wait_recv()
            total = pbuf[slot, piece(q, 0)].astype(F32) + core_in[slot, q].astype(F32)
            sums[group + q, level] = total.astype(BF16)
        pl.semaphore_signal(credit_sem, inc=1, device_id=place.device(0, 0, 1), device_id_type=MESH_ID)
        pl.when(jnp.logical_and(i >= 2, i < line - 1))(lambda: aside(level).start())

        def early(n):
            across(n).start()
            if n == 0:
                aside(level, OVER_Y).start()

        for n in range(EARLY):
            pl.when(i == line + n)(lambda n=n: early(n))

        def put_away():
            keep(1, OVER_Y, level).start()
            keep(2, ACROSS, level).start()

        pl.when(i >= line + EARLY)(put_away)

    gather.own.wait()
    arrive(0)
    fetch(0).start()

    def last_square():
        gather.square(line - 1)
        for i in range(2):
            aside(number(i)[0]).start()

    def two_corners():
        gather.corner(0)
        gather.corner(1)

    events = (
        (1, 0, lambda: gather.square(line - 2)),
        (2, 0, last_square),
        (3, 0, two_corners),
        (3, 1, lambda: gather.corner(line - 2)),
        (3, packs - 1, lambda: gather.corner(line - 1)),
    )

    def one(i, carry):
        fetch(i).wait()
        unpack(wbuf.at[lax.rem(i, 2)], inner_s, down_s)
        expert = number(i)[1]

        def rows(p, inner_carry):
            work.rows(p, expert)
            pl.when(jnp.logical_and(p == 0, i >= 1))(lambda: merge(i - 1))
            for slot, turn_at, event in events:
                pl.when(jnp.logical_and(i == slot, p == turn_at))(event)
            return inner_carry

        lax.fori_loop(0, packs, rows, 0)

        def ahead():
            arrive(i + 1)
            fetch(i + 1).start()

        pl.when(i + 1 < experts)(ahead)

        def free():
            pl.semaphore_wait(credit_sem, 1)
            for q in range(2):
                swap(i, q).wait_send()

        pl.when(i >= 2)(free)
        work.grads(pbuf.at[lax.rem(i, 2)])
        for q in range(2):
            swap(i, q).start()
        return carry

    lax.fori_loop(0, experts, one, 0)

    def last(i, carry):
        merge(i)
        return carry

    lax.fori_loop(experts - 1, experts, last, 0)

    def finish(p, carry):
        work.finish(p, router_w, mid_s, block_o, gmid_o, glog_o)
        return carry

    lax.fori_loop(0, packs, finish, 0)

    def settle(level, carry):
        aside(level).wait_recv()
        sums[OWN, level] = (sums[OWN, level].astype(F32) + side_in[level].astype(F32)).astype(BF16)
        keep(0, OWN, level).start()
        return carry

    lax.fori_loop(0, line, settle, 0)
    for n in range(EARLY):
        level = number(line + n)[0]
        across(n).wait_recv()
        group = OVER_X if n == 0 else OVER_Y
        sums[group, level] = (sums[group, level].astype(F32) + diag_in[n].astype(F32)).astype(BF16)
        keep(1, group, level).start()
        across(n).wait_send()

    def drain(level, carry):
        keep(0, OWN, level).wait()
        keep(1, OVER_Y, level).wait()
        aside(level).wait_send()
        return carry

    lax.fori_loop(0, line, drain, 0)
    for n in range(EARLY, line):
        keep(2, ACROSS, number(line + n)[0]).wait()
    pl.semaphore_wait(credit_sem, 2)
    for i in range(experts - 2, experts):
        for q in range(2):
            swap(i, q).wait_send()
    for n in range(len(saves)):
        for p in range(packs - 2 if n < 2 else 0, packs):
            save(n, p).wait()
    gather.wires.finish()


def run_forward(shard, patches, upstream, items, ids, qkv_w, proj_w, router_w, gains, table, hidden, slot):
    packs, length, width = patches.shape
    experts = router_w.shape[0]
    dp, ex = lax.axis_size("dp"), lax.axis_size("expert")
    line = ex // 2
    cap = 2 * length * ids.shape[1] // experts
    pairs, blocks = width // 128, length // QB
    rows = shard.shape[0]
    dma = pltpu.SemaphoreType.DMA
    here = pl.BlockSpec(memory_space=pltpu.VMEM)
    away = pl.BlockSpec(memory_space=pl.ANY)
    saved = (
        ((packs, length, 3 * width), BF16),
        ((packs, pairs, blocks, 3 * QB, 2 * QB), BF16),
        ((packs, length, width), BF16),
        ((packs, length, width), F32),
        ((packs, length, width), BF16),
    )
    shapes = (
        ((ex, dp, rows, width), BF16),
        ((3, line, rows, width), BF16),
        *saved,
        ((packs, length, width), BF16),
        ((packs, length, width), F32),
        ((packs, experts, length), BF16),
    )
    scratch = (
        ((width, 3 * width), BF16),
        ((width, width), BF16),
        ((2, length, 3 * width), BF16),
        ((2, pairs, blocks, 3 * QB, 2 * QB), BF16),
        *saved[2:],
        ((2, dp, rows, width), BF16),
        ((2, dp, rows, width), BF16),
        ((packs, experts, length), F32),
        ((packs, experts, length), F32),
        ((packs, experts, length), F32),
        ((packs * cap, width), BF16),
        ((packs * cap, hidden), BF16),
        ((packs * cap, width), BF16),
        ((packs * cap, 2 * hidden), BF16),
        ((packs, experts * cap, 2 * width), BF16),
        ((width, 2 * hidden), BF16),
        ((hidden, width), BF16),
        ((4, line, rows, width), BF16),
        ((2, 2, rows, width), BF16),
        ((EARLY, rows, width), BF16),
        ((line, rows, width), BF16),
    )
    return pl.pallas_call(
        functools.partial(forward_kernel, line, cap),
        out_shape=tuple(jax.ShapeDtypeStruct(*s) for s in shapes),
        in_specs=[here] * 10,
        out_specs=(away,) * 7 + (here,) * 3,
        scratch_shapes=[pltpu.VMEM(*s) for s in scratch]
        + [dma((24 * line,)), dma((ex, dp)), dma, dma((5, packs)), dma((2,)), dma((3, line))]
        + [dma((2, 2))] * 2 + [dma((EARLY,))] * 2 + [dma((line,))] * 2 + [pltpu.SemaphoreType.REGULAR],
        compiler_params=pltpu.CompilerParams(
            collective_id=slot, has_side_effects=True, vmem_limit_bytes=VMEM_BYTES
        ),
        name="forward",
    )(shard, patches, upstream, items, ids, qkv_w, proj_w, router_w, gains, table)


class Backward:
    def __init__(self, refs):
        (
            self.patches, self.upstream, self.items, self.gains, self.table, self.gmid, self.glog,
            self.qkv_s, self.proj_s, self.mixed, self.probs, self.mid, self.nm,
            self.patch_o, self.normed_s, self.branch_s, self.datt_s, self.dmix_s, self.dkv_s, self.small_g,
        ) = refs

    def pack(self, p, midway):
        packs, length, width = self.patches.shape
        pairs = width // 128
        experts = self.glog.shape[1]
        gains, mixed, dkv_s = self.gains, self.mixed, self.dkv_s
        low_lane = iota((1, width), 1) % HEAD < HEAD // 2
        first_head = iota((1, 128), 1) < HEAD
        mask_a = jnp.where(first_head, 1.0, 0.0).astype(BF16)
        mask_b = jnp.where(first_head, 0.0, 1.0).astype(BF16)
        top_rows = iota((128, 1), 0) < HEAD
        rows = pl.ds(pl.multiple_of(p * length, length), length)
        source = self.patches[p].astype(F32)
        gain0, gain1 = gains[0:1, :], gains[1:2, :]
        slot = lax.rem(p, 2)
        middle = self.mid[slot]
        inv = row_norm(middle)
        unit = middle * inv
        grad_mid = self.gmid[p]
        self.small_g[experts + 1 : experts + 2, :] += jnp.sum(grad_mid * unit, axis=0, keepdims=True)
        self.small_g[0:experts, :] += dot_nn(self.glog[p], self.nm[slot])
        grad_unit = grad_mid * gain1
        grad_middle = self.upstream[p].astype(F32) + inv * (
            grad_unit - unit * jnp.mean(grad_unit * unit, axis=1, keepdims=True)
        )
        self.patch_o[p] = grad_middle
        branch = grad_middle.astype(BF16)
        self.branch_s[rows, :] = branch
        self.datt_s[...] = dot_nt(branch, self.proj_s[...]).astype(BF16)
        dkv_s[...] = jnp.zeros(dkv_s.shape, F32)
        item_row = self.items[p].astype(F32)
        item_col, offset = positions(item_row, length)
        cos_row, sin_row = rope_rows(offset, self.table[...], length, width)
        for pair in range(pairs):
            if pair == 2:
                midway()
            lanes = slice(128 * pair, 128 * pair + 128)
            key_lanes = slice(width + 128 * pair, width + 128 * pair + 128)
            value_lanes = slice(2 * width + 128 * pair, 2 * width + 128 * pair + 128)
            keys_t = mixed[slot, :, key_lanes].astype(F32).T.astype(BF16)
            for block, (start, low, high) in enumerate(windows(length)):
                query = mixed[slot, start : start + QB, lanes] * 0.125
                query = jnp.concatenate([query * mask_a, query * mask_b], axis=0)
                datt = self.datt_s[start : start + QB, lanes]
                datt = jnp.concatenate([datt * mask_a, datt * mask_b], axis=0)
                prob = self.probs[slot, pair, block, : high - low]
                dprob = dot_nt(mixed[slot, low:high, value_lanes], datt)
                weight = prob.astype(F32)
                mean = jnp.sum(weight * dprob, axis=0, keepdims=True)
                dscore = (weight * (dprob - mean)).astype(BF16)
                dkv_s[low:high, key_lanes] += dot_nn(dscore, query)
                dkv_s[low:high, value_lanes] += dot_nn(prob, datt)
                dquery = dot_nn(keys_t[:, low:high], dscore)
                dquery = jnp.where(top_rows, dquery[:, :QB], dquery[:, QB:])
                dkv_s[start : start + QB, lanes] = dquery.T * 0.125
        dmix_s = self.dmix_s
        dmix_s[rows, :width] = turn(dkv_s[:, :width], cos_row, -sin_row, low_lane).astype(BF16)
        dmix_s[rows, width : 2 * width] = turn(
            dkv_s[:, width : 2 * width], cos_row, -sin_row, low_lane
        ).astype(BF16)
        dmix_s[rows, 2 * width :] = dkv_s[:, 2 * width :].astype(BF16)
        grad_normed = dot_nt(dmix_s[rows, :], self.qkv_s[...])
        inv_in = row_norm(source)
        unit_in = source * inv_in
        self.normed_s[rows, :] = (unit_in * gain0).astype(BF16)
        self.small_g[experts : experts + 1, :] += jnp.sum(grad_normed * unit_in, axis=0, keepdims=True)
        grad_unit_in = grad_normed * gain0
        self.patch_o[p] += inv_in * (
            grad_unit_in - unit_in * jnp.mean(grad_unit_in * unit_in, axis=1, keepdims=True)
        )

    def tail(self, att, tail):
        packs, length, width = self.patches.shape
        tail[...] = jnp.zeros(tail.shape, BF16)
        for block in range(4):
            if block < 3:
                grad = dot_tn(self.normed_s[...], self.dmix_s[:, block * width : block * width + width])
            else:
                flat = jnp.concatenate([att[p] for p in range(packs)], axis=0)
                grad = dot_tn(flat, self.branch_s[...])
            lay_tail(tail, block, grad.astype(BF16))
        tail[0, 0, 0, tail.shape[3] - 16 :, :] = self.small_g[...].astype(BF16)


def tail_rows(width, devices):
    return 4 * width // devices + 16


def lay_tail(tail, block, grad):
    _, dp, line, rows, width = tail.shape
    rows = rows - 16
    each = width // rows
    for piece in range(each):
        number = block * each + piece
        spot = (number // (dp * line), number // line % dp, number % line)
        tail[(*spot, slice(0, rows), slice(None))] = grad[piece * rows : piece * rows + rows]


def backward_kernel(
    line,
    kept, patches, upstream, items, qkv_w, proj_w, gains, table, gmid, glog, mixed_i, probs_i, att_i, mid_i, nm_i,
    patch_o, grad_o, tail_o,
    qkv_s, proj_s, mixed, probs, att, mid, nm,
    normed_s, branch_s, datt_s, dmix_s, dkv_s, small_g, tail, tail_low,
    owns, sides, diag_in, side_in, line_in,
    tsums, tcore_in, tsquare_in, tline_in,
    load_sem, own_sem, diag_send, diag_sem, side_send, side_sem, line_send, line_sem,
    *small_sems,
):
    packs = patches.shape[0]
    place = Place(line)
    place.greet()
    reduce = Close(
        place, kept, owns, sides, diag_in, side_in, line_in, own_sem,
        (diag_send, diag_sem, side_send, side_sem, line_send, line_sem),
    )
    small = Small(place, tail, tail_low, tail_o, tsums, tcore_in, tsquare_in, tline_in, small_sems)
    reduce.start()
    loads = ((mixed_i, mixed), (mid_i, mid), (nm_i, nm), (probs_i, probs), (att_i, att))

    def load(n, p):
        source, target = loads[n]
        return pltpu.make_async_copy(
            source.at[p], target.at[lax.rem(p, target.shape[0])], load_sem.at[n, p]
        )

    for p in range(packs):
        for n in range(len(loads)):
            if p < loads[n][1].shape[0]:
                load(n, p).start()
    qkv_s[...] = qkv_w[...].astype(BF16)
    proj_s[...] = proj_w[...].astype(BF16)
    small_g[...] = jnp.zeros(small_g.shape, F32)
    work = Backward((
        patches, upstream, items, gains, table, gmid, glog,
        qkv_s, proj_s, mixed, probs, mid, nm,
        patch_o, normed_s, branch_s, datt_s, dmix_s, dkv_s, small_g,
    ))
    def pack(p, carry):
        for n in range(len(loads)):
            load(n, p).wait()

        def midway():
            pl.when(p == 1)(lambda: reduce.send_side(2))

            def later():
                reduce.send_side(3)
                reduce.send_line(2)

            pl.when(p == packs - 1)(later)

        work.pack(p, midway)

        def ahead():
            for n in range(len(loads) - 1):
                load(n, p + 2).start()

        pl.when(p + 2 < packs)(ahead)

        def first():
            reduce.send_line(0)
            reduce.send_line(1)

        pl.when(p == 0)(first)
        return carry

    lax.fori_loop(0, packs, pack, 0)
    work.tail(att, tail)
    small.start()
    small.run()
    reduce.finish(grad_o)
    small.finish()


def run_backward(
    kept, patches, upstream, items, qkv_w, proj_w, gains, table, gmid, glog, mixed, probs, att, mid, nm, slot
):
    packs, length, width = patches.shape
    _, line, rows, _ = kept.shape
    dp, ex = lax.axis_size("dp"), lax.axis_size("expert")
    few = tail_rows(width, ex * dp)
    dma = pltpu.SemaphoreType.DMA
    here = pl.BlockSpec(memory_space=pltpu.VMEM)
    away = pl.BlockSpec(memory_space=pl.ANY)
    shapes = (
        ((packs, length, width), F32),
        ((rows, width), F32),
        ((ex // line, dp, line, few, width), BF16),
    )
    scratch = (
        ((width, 3 * width), BF16),
        ((width, width), BF16),
        ((2,) + mixed.shape[1:], BF16),
        ((2,) + probs.shape[1:], BF16),
        (att.shape, BF16),
        ((2,) + mid.shape[1:], F32),
        ((2,) + nm.shape[1:], BF16),
        ((packs * length, width), BF16),
        ((packs * length, width), BF16),
        ((length, width), BF16),
        ((packs * length, 3 * width), BF16),
        ((length, 3 * width), F32),
        ((16, width), F32),
        ((ex // line, dp, line, few, width), BF16),
        ((few, width), BF16),
        *([((line, rows, width), BF16)] * 5),
        ((4, line, few, width), BF16),
        ((4, line, few, width), BF16),
        ((3, line, few, width), BF16),
        ((line, few, width), BF16),
    )
    small_sems = [dma((n,)) for n in (4, 4, 3, 3, line, line, line, line, 3, 3, 4, 4)]
    return pl.pallas_call(
        functools.partial(backward_kernel, line),
        out_shape=tuple(jax.ShapeDtypeStruct(*s) for s in shapes),
        in_specs=[away] + [here] * 9 + [away] * 5,
        out_specs=(here, here, here),
        scratch_shapes=[pltpu.VMEM(*s) for s in scratch]
        + [dma((5, packs)), dma((2, line))] + [dma((line,))] * 6 + small_sems,
        compiler_params=pltpu.CompilerParams(
            collective_id=slot, has_side_effects=True, vmem_limit_bytes=VMEM_BYTES
        ),
        name="backward",
    )(kept, patches, upstream, items, qkv_w, proj_w, gains, table, gmid, glog, mixed, probs, att, mid, nm)


def update_kernel(
    tail, inner_g, down_g,
    qkv_w, qkv_f, qkv_s, proj_w, proj_f, proj_s, router_w, router_f, router_s,
    gains_w, gains_f, gains_s, inner_w, inner_f, inner_s, down_w, down_f, down_s,
    qkv_wo, qkv_fo, qkv_so, proj_wo, proj_fo, proj_so, router_wo, router_fo, router_so,
    gains_wo, gains_fo, gains_so, inner_wo, inner_fo, inner_so, down_wo, down_fo, down_so,
):
    step = pl.program_id(0)
    ex, dp, few, width = tail.shape
    rows = few - 16
    experts = router_w.shape[1]
    attn = tail[:, :, :rows, :].reshape(ex * dp * rows, width).astype(F32)

    def write(outs, values):
        for out, value in zip(outs, values):
            out[...] = value

    def qkv():
        write((qkv_wo, qkv_fo, qkv_so), adamw(qkv_w[...], qkv_f[...], qkv_s[...], attn, 0.1, 0.1))

    def proj():
        write((proj_wo, proj_fo, proj_so), adamw(proj_w[...], proj_f[...], proj_s[...], attn, 0.4, 0.1))

    def rest():
        small = tail[0, 0, rows:, :].astype(F32)
        router_g = small.T[:, :experts]
        gains_g = small[experts : experts + 2]
        write(
            (router_wo, router_fo, router_so),
            adamw(router_w[...], router_f[...], router_s[...], router_g, 0.07, 0.1),
        )
        write(
            (gains_wo, gains_fo, gains_so),
            adamw(gains_w[...], gains_f[...], gains_s[...], gains_g, 0.4, 0.0),
        )

    pl.when(step < 3)(qkv)
    pl.when(step == 3)(proj)
    pl.when(step == 0)(rest)
    write(
        (inner_wo, inner_fo, inner_so),
        adamw(inner_w[...], inner_f[...], inner_s[...], inner_g[...], 0.1, 0.1),
    )
    write((down_wo, down_fo, down_so), adamw(down_w[...], down_f[...], down_s[...], down_g[...], 0.15, 0.1))


def run_update(tail, grad, weights):
    ex, dp, few, width = tail.shape
    qkv, router, inner, down = weights[0], weights[6], weights[12], weights[15]
    deep, span = inner.shape[0], down.shape[0] // 4
    of_qkv = pl.BlockSpec((width, width), lambda j: (0, jnp.minimum(j, 2)))
    of_proj = pl.BlockSpec((width, width), lambda j: (0, 0))
    of_router = pl.BlockSpec(router.shape, lambda j: (0, 0))
    of_gains = pl.BlockSpec((2, width), lambda j: (0, 0))
    of_inner = pl.BlockSpec((deep, width), lambda j: (0, j))
    of_down = pl.BlockSpec((span, width), lambda j: (j, 0))
    specs = []
    for spec in (of_qkv, of_proj, of_router, of_gains, of_inner, of_down):
        specs += [spec] * 3
    first_down = 4 * deep // span
    return pl.pallas_call(
        update_kernel,
        out_shape=tuple(jax.ShapeDtypeStruct(w.shape, F32) for w in weights),
        grid=(4,),
        in_specs=[
            pl.BlockSpec((ex // 4, dp, few, width), lambda j: (j, 0, 0, 0)),
            pl.BlockSpec((deep, width), lambda j: (j, 0)),
            pl.BlockSpec((span, width), lambda j: (first_down + j, 0)),
        ] + specs,
        out_specs=tuple(specs),
        compiler_params=pltpu.CompilerParams(vmem_limit_bytes=VMEM_BYTES),
        name="update",
    )(tail, grad, grad, *weights)


def fast(
    patches, out_grad, item_ids, expert_ids,
    qkv_master, qkv_first, qkv_second,
    proj_master, proj_first, proj_second,
    router_master, router_first, router_second,
    gains_master, gains_first, gains_second,
    inner_master, inner_first, inner_second,
    down_master, down_first, down_second,
):
    width = patches.shape[2]
    experts = router_master.shape[1]
    hidden = down_master.shape[1] * lax.axis_size("dp")
    deep = inner_master.shape[1]
    blocks = inner_master.shape[2] // width
    shard = jnp.concatenate(
        [
            jnp.swapaxes(inner_master[0].reshape(deep, blocks, width), 0, 1).reshape(blocks * deep, width),
            down_master[0],
        ],
        axis=0,
    ).astype(BF16)
    router_w = router_master.T.astype(BF16)
    ids = jnp.swapaxes(expert_ids, 1, 2)
    table = jnp.asarray(rope_table(QB))
    full, kept, mixed, probs, att, mid, nm, block_out, gmid, glog = run_forward(
        shard, patches, out_grad, item_ids, ids, qkv_master, proj_master, router_w, gains_master, table, hidden, 0
    )
    patch_grad, grad, tail = run_backward(
        kept, patches, out_grad, item_ids, qkv_master, proj_master, gains_master, table,
        gmid, glog, mixed, probs, att, mid, nm, 1,
    )
    weights = (
        qkv_master, qkv_first, qkv_second,
        proj_master, proj_first, proj_second,
        router_master, router_first, router_second,
        gains_master, gains_first, gains_second,
        inner_master[0], inner_first[0], inner_second[0],
        down_master[0], down_first[0], down_second[0],
    )
    tail = tail.reshape(-1, lax.axis_size("dp"), *tail.shape[3:])
    new = run_update(tail, grad, weights)
    return (block_out, patch_grad, *new[:12], *(value[None] for value in new[12:]))


GATHER_LIMIT = 16 * 1024 * 1024


def step(*args):
    inner_master, down_master = args[16], args[19]
    experts = inner_master.shape[0] * lax.axis_size("expert")
    entries = inner_master.shape[1] * inner_master.shape[2] + down_master.shape[1] * down_master.shape[2]
    weight_bytes = 2 * experts * entries * lax.axis_size("dp")
    square = lax.axis_size("dp") == 4 and lax.axis_size("expert") == 8 and inner_master.shape[0] == 1 and lax.axis_size("expert") == experts
    return (fast if square and weight_bytes <= GATHER_LIMIT else local)(*args)


def solution(mesh):
    in_specs = (
        P(None, ("dp", "expert"), None),
        P(None, ("dp", "expert"), None),
        P(None, ("dp", "expert"), None),
        P(None, ("dp", "expert"), None),
        P(),
        P(),
        P(),
        P(),
        P(),
        P(),
        P(),
        P(),
        P(),
        P(),
        P(),
        P(),
        P("expert", "dp", None),
        P("expert", "dp", None),
        P("expert", "dp", None),
        P("expert", "dp", None),
        P("expert", "dp", None),
        P("expert", "dp", None),
    )
    out_specs = (
        P(None, ("dp", "expert"), None),
        P(None, ("dp", "expert"), None),
        P(),
        P(),
        P(),
        P(),
        P(),
        P(),
        P(),
        P(),
        P(),
        P(),
        P(),
        P(),
        P("expert", "dp", None),
        P("expert", "dp", None),
        P("expert", "dp", None),
        P("expert", "dp", None),
        P("expert", "dp", None),
        P("expert", "dp", None),
    )
    return jax.shard_map(step, mesh=mesh, in_specs=in_specs, out_specs=out_specs, check_vma=False)
```

```python
import functools

import jax
import jax.numpy as jnp
import numpy as np
from jax import lax
from jax.experimental import pallas as pl
from jax.experimental.pallas import tpu as pltpu
from jax.sharding import PartitionSpec as P

HEADS = 6
HEAD = 64


norm_eps = 1e-06
adam_eps = 1e-08
correction = 0.875


def rotary_tables(item_row):
    length = item_row.shape[0]
    places = jnp.arange(length, dtype=jnp.int32)
    starts = jnp.concatenate([jnp.ones((1,), dtype=bool), item_row[1:] != item_row[:-1]])
    first = lax.cummax(jnp.where(starts, places, 0), axis=0)
    offset = (places - first).astype(jnp.float32)
    half = HEAD // 2
    freqs = 10000.0 ** (-jnp.arange(half, dtype=jnp.float32) / half)
    angles = offset[:, None] * freqs[None, :]
    return (jnp.cos(angles), jnp.sin(angles))


def rotate(vectors, cosine, sine):
    half = vectors.shape[-1] // 2
    first_half = vectors[..., :half]
    second_half = vectors[..., half:]
    cos_part = cosine[:, None, :]
    sin_part = sine[:, None, :]
    return jnp.concatenate(
        [
            first_half * cos_part - second_half * sin_part,
            second_half * cos_part + first_half * sin_part,
        ],
        axis=-1,
    )


def masked_scores(query, keys, same_item):
    scores = jnp.einsum("qhe,khe->hqk", query, keys, preferred_element_type=jnp.float32) * 0.125
    return jnp.where(same_item[None], scores, -1e30)


def adamw(weight, first, second, grad, rate, decay):
    first_new = 0.5 * first + 0.5 * grad
    second_new = 0.5 * second + 0.5 * grad * grad
    update = first_new / correction / (jnp.sqrt(second_new / correction) + adam_eps)
    return (weight - rate * (update + decay * weight), first_new, second_new)


def local(
    patches,
    out_grad,
    item_ids,
    expert_ids,
    qkv_master,
    qkv_first,
    qkv_second,
    proj_master,
    proj_first,
    proj_second,
    router_master,
    router_first,
    router_second,
    gains_master,
    gains_first,
    gains_second,
    inner_master,
    inner_first,
    inner_second,
    down_master,
    down_first,
    down_second,
):
    expert_count = lax.axis_size("expert")
    local_experts = inner_master.shape[0]
    experts = expert_count * local_experts
    length = patches.shape[1]
    width = patches.shape[2]
    top = expert_ids.shape[2]
    capacity = 2 * length * top // experts
    hidden_width = down_master.shape[1] * lax.axis_size("dp")
    inner_low, down_low = (
        lax.all_gather(inner_master.astype(jnp.bfloat16), "dp", axis=1, tiled=True),
        lax.all_gather(down_master.astype(jnp.bfloat16), "dp", axis=1, tiled=True),
    )
    qkv_low = qkv_master.astype(jnp.bfloat16)
    proj_low = proj_master.astype(jnp.bfloat16)
    router_low = router_master.astype(jnp.bfloat16)
    gain_attn = gains_master[0]
    gain_ffn = gains_master[1]
    expert_numbers = jnp.arange(experts, dtype=jnp.int32)

    def expert_forward(received):
        count = received.shape[1]
        grid = received.reshape(expert_count, local_experts, count, width)
        both = jnp.einsum("sjcd,jdf->sjcf", grid, inner_low, preferred_element_type=jnp.float32)
        hidden = (jax.nn.silu(both[..., :hidden_width]) * both[..., hidden_width:]).astype(
            jnp.bfloat16
        )
        result = jnp.einsum("sjcf,jfd->sjcd", hidden, down_low, preferred_element_type=jnp.float32)
        result = result.astype(jnp.bfloat16).reshape(experts, count, width)
        returned = lax.all_to_all(result, "expert", split_axis=0, concat_axis=0, tiled=True)
        return (returned, received)

    def micro_step(carry, inputs):
        grad_qkv, grad_proj, grad_router, grad_gains, grad_inner, grad_down = carry
        patch, upstream, item_block, routes = inputs
        items = item_block[0]
        source = patch.astype(jnp.float32)
        inv_first = lax.rsqrt(jnp.mean(source * source, axis=1, keepdims=True) + norm_eps)
        unit_first = source * inv_first
        normed_in = (unit_first * gain_attn).astype(jnp.bfloat16)
        mixed = jnp.dot(normed_in, qkv_low, preferred_element_type=jnp.float32)
        cosine, sine = rotary_tables(items)
        query = rotate(mixed[:, :width].reshape(length, HEADS, HEAD), cosine, sine).astype(
            jnp.bfloat16
        )
        keys = rotate(
            mixed[:, width : 2 * width].reshape(length, HEADS, HEAD), cosine, sine
        ).astype(jnp.bfloat16)
        values = mixed[:, 2 * width :].reshape(length, HEADS, HEAD).astype(jnp.bfloat16)
        same_item = items[:, None] == items[None, :]
        scores = masked_scores(query, keys, same_item)
        peak = jnp.max(scores, axis=2, keepdims=True)
        weights = jnp.exp(scores - peak)
        totals = jnp.sum(weights, axis=2, keepdims=True)
        probs_low = (weights / totals).astype(jnp.bfloat16)
        log_total = peak + jnp.log(totals)
        attended = jnp.einsum("hqk,khe->qhe", probs_low, values, preferred_element_type=jnp.float32)
        attended = attended.reshape(length, width).astype(jnp.bfloat16)
        middle = source + jnp.dot(attended, proj_low, preferred_element_type=jnp.float32)
        inv_second = lax.rsqrt(jnp.mean(middle * middle, axis=1, keepdims=True) + norm_eps)
        unit_second = middle * inv_second
        normed_mid = (unit_second * gain_ffn).astype(jnp.bfloat16)
        logits = jnp.dot(normed_mid, router_low, preferred_element_type=jnp.float32)
        chosen = jnp.take_along_axis(logits, routes, axis=1)
        gates = jax.nn.softmax(chosen, axis=1)
        flat_ids = routes.reshape(length * top)
        hits = (flat_ids[:, None] == expert_numbers[None, :]).astype(jnp.int32)
        rank = jnp.sum(jnp.cumsum(hits, axis=0) * hits, axis=1) - 1
        slots = flat_ids * capacity + rank
        copies = jnp.repeat(normed_mid, top, axis=0)
        outgoing = jnp.zeros((experts * capacity, width), jnp.bfloat16).at[slots].set(copies)
        outgoing = outgoing.reshape(experts, capacity, width)
        returned, kept_inputs = expert_forward(
            lax.all_to_all(outgoing, "expert", split_axis=0, concat_axis=0, tiled=True)
        )
        picked = (
            returned.reshape(experts * capacity, width)[slots]
            .reshape(length, top, width)
            .astype(jnp.float32)
        )
        combined = jnp.sum(gates[:, :, None] * picked, axis=1)
        block_out = (middle + combined).astype(jnp.bfloat16)
        upstream_full = upstream.astype(jnp.float32)
        grad_gate = jnp.sum(upstream_full[:, None, :] * picked, axis=2)
        grad_chosen = gates * (grad_gate - jnp.sum(gates * grad_gate, axis=1, keepdims=True))
        route_hits = (routes[:, :, None] == expert_numbers[None, None, :]).astype(jnp.float32)
        grad_logits = jnp.sum(grad_chosen[:, :, None] * route_hits, axis=1).astype(jnp.bfloat16)
        grad_router_now = jnp.dot(normed_mid.T, grad_logits, preferred_element_type=jnp.float32)
        grad_mid = jnp.dot(grad_logits, router_low.T, preferred_element_type=jnp.float32)
        grad_slots = (
            (gates[:, :, None] * upstream_full[:, None, :])
            .astype(jnp.bfloat16)
            .reshape(length * top, width)
        )
        grad_outgoing = (
            jnp.zeros((experts * capacity, width), jnp.bfloat16).at[slots].set(grad_slots)
        )
        grad_outgoing = grad_outgoing.reshape(experts, capacity, width)
        incoming, inputs_back = (
            lax.all_to_all(grad_outgoing, "expert", split_axis=0, concat_axis=0, tiled=True),
            lax.all_to_all(outgoing, "expert", split_axis=0, concat_axis=0, tiled=True),
        )
        grid_in = inputs_back.reshape(expert_count, local_experts, capacity, width)
        grid_grad = incoming.reshape(expert_count, local_experts, capacity, width)
        both = jnp.einsum("sjcd,jdf->sjcf", grid_in, inner_low, preferred_element_type=jnp.float32)
        gate_part = both[..., :hidden_width]
        up_part = both[..., hidden_width:]
        sigma = jax.nn.sigmoid(gate_part)
        activated = jax.nn.silu(gate_part)
        hidden = (activated * up_part).astype(jnp.bfloat16)
        grad_hidden = jnp.einsum(
            "sjcd,jfd->sjcf", grid_grad, down_low, preferred_element_type=jnp.float32
        )
        grad_down_now = jnp.einsum(
            "sjcf,sjcd->jfd", hidden, grid_grad, preferred_element_type=jnp.float32
        )
        grad_both = jnp.concatenate(
            [
                grad_hidden * up_part * sigma * (1.0 + gate_part * (1.0 - sigma)),
                grad_hidden * activated,
            ],
            axis=3,
        ).astype(jnp.bfloat16)
        grad_inner_now = jnp.einsum(
            "sjcd,sjcf->jdf", grid_in, grad_both, preferred_element_type=jnp.float32
        )
        grad_copies = jnp.einsum(
            "sjcf,jdf->sjcd", grad_both, inner_low, preferred_element_type=jnp.float32
        )
        grad_copies = grad_copies.astype(jnp.bfloat16).reshape(experts, capacity, width)
        grad_back = lax.all_to_all(grad_copies, "expert", split_axis=0, concat_axis=0, tiled=True)
        grad_picked = grad_back.reshape(experts * capacity, width)[slots].reshape(
            length, top, width
        )
        grad_mid = grad_mid + jnp.sum(grad_picked.astype(jnp.float32), axis=1)
        grad_unit_second = grad_mid * gain_ffn
        grad_gain_ffn = jnp.sum(grad_mid * unit_second, axis=0)
        grad_middle = upstream_full + inv_second * (
            grad_unit_second
            - unit_second * jnp.mean(grad_unit_second * unit_second, axis=1, keepdims=True)
        )
        grad_branch = grad_middle.astype(jnp.bfloat16)
        grad_proj_now = jnp.dot(attended.T, grad_branch, preferred_element_type=jnp.float32)
        grad_attended = jnp.dot(grad_branch, proj_low.T, preferred_element_type=jnp.float32)
        grad_attended = grad_attended.astype(jnp.bfloat16).reshape(length, HEADS, HEAD)
        probs_again = jnp.exp(masked_scores(query, keys, same_item) - log_total)
        grad_probs = jnp.einsum(
            "qhe,khe->hqk", grad_attended, values, preferred_element_type=jnp.float32
        )
        grad_values = jnp.einsum(
            "hqk,qhe->khe", probs_low, grad_attended, preferred_element_type=jnp.float32
        )
        grad_scores = probs_again * (
            grad_probs - jnp.sum(probs_again * grad_probs, axis=2, keepdims=True)
        )
        grad_scores = grad_scores.astype(jnp.bfloat16)
        grad_query = (
            jnp.einsum("hqk,khe->qhe", grad_scores, keys, preferred_element_type=jnp.float32)
            * 0.125
        )
        grad_keys = (
            jnp.einsum("hqk,qhe->khe", grad_scores, query, preferred_element_type=jnp.float32)
            * 0.125
        )
        grad_mixed = jnp.concatenate(
            [
                rotate(grad_query, cosine, -sine).reshape(length, width),
                rotate(grad_keys, cosine, -sine).reshape(length, width),
                grad_values.reshape(length, width),
            ],
            axis=1,
        ).astype(jnp.bfloat16)
        grad_qkv_now = jnp.dot(normed_in.T, grad_mixed, preferred_element_type=jnp.float32)
        grad_normed = jnp.dot(grad_mixed, qkv_low.T, preferred_element_type=jnp.float32)
        grad_unit_first = grad_normed * gain_attn
        grad_gain_attn = jnp.sum(grad_normed * unit_first, axis=0)
        patch_grad = grad_middle + inv_first * (
            grad_unit_first
            - unit_first * jnp.mean(grad_unit_first * unit_first, axis=1, keepdims=True)
        )
        new_carry = (
            grad_qkv + grad_qkv_now,
            grad_proj + grad_proj_now,
            grad_router + grad_router_now,
            grad_gains + jnp.stack([grad_gain_attn, grad_gain_ffn]),
            grad_inner + grad_inner_now,
            grad_down + grad_down_now,
        )
        return (new_carry, (block_out, patch_grad))

    start = (
        jnp.zeros(qkv_master.shape, jnp.float32),
        jnp.zeros(proj_master.shape, jnp.float32),
        jnp.zeros(router_master.shape, jnp.float32),
        jnp.zeros(gains_master.shape, jnp.float32),
        jnp.zeros(inner_low.shape, jnp.float32),
        jnp.zeros(down_low.shape, jnp.float32),
    )
    totals, outputs = lax.scan(micro_step, start, (patches, out_grad, item_ids, expert_ids))
    grad_qkv, grad_proj, grad_router, grad_gains = lax.psum(
        (totals[0], totals[1], totals[2], totals[3]), ("dp", "expert")
    )
    grad_inner, grad_down = (
        lax.psum_scatter(totals[4], "dp", scatter_dimension=1, tiled=True),
        lax.psum_scatter(totals[5], "dp", scatter_dimension=1, tiled=True),
    )
    qkv_new = adamw(qkv_master, qkv_first, qkv_second, grad_qkv, 0.1, 0.1)
    proj_new = adamw(proj_master, proj_first, proj_second, grad_proj, 0.4, 0.1)
    router_new = adamw(router_master, router_first, router_second, grad_router, 0.07, 0.1)
    gains_new = adamw(gains_master, gains_first, gains_second, grad_gains, 0.4, 0.0)
    inner_new = adamw(inner_master, inner_first, inner_second, grad_inner, 0.1, 0.1)
    down_new = adamw(down_master, down_first, down_second, grad_down, 0.15, 0.1)
    return (
        outputs[0],
        outputs[1],
        qkv_new[0],
        qkv_new[1],
        qkv_new[2],
        proj_new[0],
        proj_new[1],
        proj_new[2],
        router_new[0],
        router_new[1],
        router_new[2],
        gains_new[0],
        gains_new[1],
        gains_new[2],
        inner_new[0],
        inner_new[1],
        inner_new[2],
        down_new[0],
        down_new[1],
        down_new[2],
    )


F32 = jnp.float32
BF16 = jnp.bfloat16
QB = 128


def iota(shape, axis):
    return lax.broadcasted_iota(jnp.int32, shape, axis)


def dot_nn(a, b):
    return jnp.dot(a, b, preferred_element_type=F32)


def dot_nt(a, b):
    return lax.dot_general(a, b, (((1,), (1,)), ((), ())), preferred_element_type=F32)


def dot_tn(a, b):
    return lax.dot_general(a, b, (((0,), (0,)), ((), ())), preferred_element_type=F32)


def swap_halves(v, low_lane):
    width = v.shape[1]
    half = HEAD // 2
    return jnp.where(low_lane, pltpu.roll(v, width - half, 1), pltpu.roll(v, half, 1))


def turn(v, cos_row, sin_row, low_lane):
    return v * cos_row + swap_halves(v, low_lane) * sin_row


def rope_table(item_max):
    half = HEAD // 2
    offset = np.arange(item_max, dtype=np.float32)
    freqs = np.float32(10000.0) ** (-np.arange(half, dtype=np.float32) / np.float32(half))
    angles = (offset[:, None] * freqs[None, :]).astype(np.float32)
    cosine, sine = np.cos(angles), np.sin(angles)
    return np.concatenate([cosine] * 4 + [-sine, sine] * 2, axis=1).astype(np.float32)


def windows(length):
    found = []
    for start in range(0, length, QB):
        low = max(0, start - QB)
        high = min(length, start + 2 * QB)
        found.append((start, low, high))
    return found


def row_norm(values):
    return lax.rsqrt(jnp.mean(values * values, axis=1, keepdims=True) + norm_eps)


def positions(item_row, length):
    eye = iota((length, length), 0) == iota((length, length), 1)
    col = jnp.sum(jnp.where(eye, item_row, 0.0), axis=1, keepdims=True)
    before = jnp.sum(jnp.where(item_row < col, 1.0, 0.0), axis=1, keepdims=True)
    offset = iota((length, 1), 0) - before.astype(jnp.int32)
    return col, offset


def rope_rows(offset, table, length, width):
    spots = table.shape[0]
    pick = jnp.where(iota((length, spots), 1) == offset, 1.0, 0.0)
    both = jnp.dot(pick, table, precision=lax.Precision.HIGHEST, preferred_element_type=F32)
    copies = width // 128
    return (
        jnp.concatenate([both[:, :128]] * copies, axis=1),
        jnp.concatenate([both[:, 128:]] * copies, axis=1),
    )


VMEM_BYTES = 64 * 1024 * 1024 - 512 * 1024


MESH_ID = pl.DeviceIdType.MESH


class Place:
    def __init__(self, line):
        self.line = line
        dp, ex = lax.axis_index("dp"), lax.axis_index("expert")
        self.x, self.core = lax.div(dp, 2), lax.rem(dp, 2)
        self.z, self.y = lax.div(ex, 2), lax.rem(ex, 2)

    def device(self, flip_x=0, flip_y=0, flip_core=0, z=None):
        x = 1 - self.x if flip_x else self.x
        y = 1 - self.y if flip_y else self.y
        core = 1 - self.core if flip_core else self.core
        return (2 * x + core, 2 * (self.z if z is None else z) + y)

    def levels(self):
        found = [(0, self.z, None, 0)]
        for away in range(1, self.line):
            found.append((away, self.z - away, lambda a=away: self.z >= a, -1))
            found.append((away, self.z + away, lambda a=away: self.z + a < self.line, 1))
        return found

    def up(self):
        return self.z + 1 < self.line

    def down(self):
        return self.z > 0

    def by_distance(self, i):
        found = 0
        for z in range(self.line):
            order = sorted(range(self.line), key=lambda level: (abs(level - z), level))
            for place, level in enumerate(order):
                hit = jnp.logical_and(self.z == z, i == place).astype(jnp.int32)
                found = found + hit * level
        return found

    def greet(self):
        barrier = pltpu.get_barrier_semaphore()

        def signal(device):
            pl.semaphore_signal(barrier, inc=1, device_id=device, device_id_type=MESH_ID)

        for device in (self.device(1), self.device(0, 1), self.device(1, 1), self.device(0, 0, 1)):
            signal(device)
        for step in range(1, self.line):
            signal(self.device(z=lax.rem(self.z + step, self.line)))
        pl.semaphore_wait(barrier, self.line + 3)


def both(*tests):
    tests = [t for t in tests if t is not None]

    def all_of():
        found = tests[0]()
        for t in tests[1:]:
            found = jnp.logical_and(found, t())
        return found

    return all_of if tests else None


def only(test, body):
    if test is None:
        body()
    else:
        pl.when(test())(body)


def remote(source, target, departure, arrival, device):
    return pltpu.make_async_remote_copy(
        src_ref=source,
        dst_ref=target,
        send_sem=departure,
        recv_sem=arrival,
        device_id=device,
        device_id_type=MESH_ID,
    )


class Wires:
    def __init__(self, send_sem, like):
        self.send_sem, self.like = send_sem, like
        self.sent = []

    def send(self, source, target, arrival, device, test=None):
        copy = pltpu.make_async_remote_copy(
            src_ref=source,
            dst_ref=target,
            send_sem=self.send_sem.at[len(self.sent)],
            recv_sem=arrival,
            device_id=device,
            device_id_type=MESH_ID,
        )
        only(test, copy.start)
        self.sent.append(test)

    def arrived(self, target, arrival, device, test=None):
        copy = pltpu.make_async_remote_copy(
            src_ref=target,
            dst_ref=target,
            send_sem=self.send_sem.at[0],
            recv_sem=arrival,
            device_id=device,
            device_id_type=MESH_ID,
        )
        only(test, copy.wait_recv)

    def finish(self):
        for number, test in enumerate(self.sent):
            copy = pltpu.make_async_remote_copy(
                src_ref=self.like,
                dst_ref=self.like,
                send_sem=self.send_sem.at[number],
                recv_sem=self.send_sem.at[number],
                device_id=(0, 0),
                device_id_type=MESH_ID,
            )
            only(test, copy.wait_send)


class Gather:
    def __init__(self, place, shard, full, send_sem, recv_sem, copy_sem):
        self.place, self.shard, self.full = place, shard, full
        self.recv_sem, self.copy_sem = recv_sem, copy_sem
        self.wires = Wires(send_sem, shard)

    def at(self, device):
        return self.full.at[device[1], device[0]]

    def ready(self, device):
        return self.recv_sem.at[device[1], device[0]]

    def pass_on(self, origin, to, test=None, source=None):
        source = self.at(origin) if source is None else source
        self.wires.send(source, self.at(origin), self.ready(origin), to, test)

    def wait(self, origin, test=None):
        self.wires.arrived(self.at(origin), self.ready(origin), self.place.device(0, 0, 1), test)

    def start(self):
        place = self.place
        me = place.device()
        self.pass_on(me, place.device(z=place.z + 1), place.up, self.shard)
        self.pass_on(me, place.device(z=place.z - 1), place.down, self.shard)
        self.pass_on(me, place.device(1), None, self.shard)
        self.pass_on(me, place.device(0, 1), None, self.shard)
        self.pass_on(me, place.device(0, 0, 1), None, self.shard)
        self.own = pltpu.make_async_copy(self.shard, self.at(me), self.copy_sem)
        self.own.start()

    def column(self, away):
        place = self.place
        for dist, level, test, way in place.levels():
            if dist != away:
                continue
            origin = place.device(z=level)
            self.wait(origin, test)
            if way < 0:
                self.pass_on(origin, place.device(z=place.z + 1), both(test, place.up))
            if way > 0:
                self.pass_on(origin, place.device(z=place.z - 1), both(test, place.down))
            self.pass_on(origin, place.device(1), test)
            self.pass_on(origin, place.device(0, 1), test)
            self.pass_on(origin, place.device(0, 0, 1), test)

    def square(self, away):
        place = self.place
        for dist, level, test, way in place.levels():
            if dist != away:
                continue
            over_x, over_y = place.device(1, z=level), place.device(0, 1, z=level)
            self.wait(over_x, test)
            if dist % 2 == 0:
                self.pass_on(over_x, place.device(0, 1), test)
            self.pass_on(over_x, place.device(0, 0, 1), test)
            self.wait(over_y, test)
            if dist % 2 == 1:
                self.pass_on(over_y, place.device(1), test)
            self.pass_on(over_y, place.device(0, 0, 1), test)

    def corner(self, away):
        place = self.place
        for dist, level, test, way in place.levels():
            if dist != away:
                continue
            across = place.device(1, 1, z=level)
            self.wait(across, test)
            self.pass_on(across, place.device(0, 0, 1), test)

    def partner(self, flip_x, flip_y, level):
        self.wait(self.place.device(flip_x, flip_y, 1, z=level))


OWN, OVER_X, OVER_Y, ACROSS = 0, 1, 2, 3
EARLY = 2


class Close:
    def __init__(self, place, kept, owns, sides, diag_in, side_in, line_in, load_sem, sems):
        self.place, self.kept, self.owns, self.sides = place, kept, owns, sides
        self.diag_in, self.side_in, self.line_in, self.load_sem = diag_in, side_in, line_in, load_sem
        self.diag_send, self.diag_sem, self.side_send, self.side_sem, self.line_send, self.line_sem = sems

    def level(self, slot):
        return self.place.by_distance(self.place.line - 1 - slot)

    def load(self, which, slot):
        target = self.owns if which == 0 else self.sides
        return pltpu.make_async_copy(
            self.kept.at[which, self.level(slot)], target.at[slot], self.load_sem.at[which, slot]
        )

    def across(self, slot):
        level = self.level(slot)
        return remote(
            self.kept.at[2, level], self.diag_in.at[slot], self.diag_send.at[slot], self.diag_sem.at[slot],
            self.place.device(1),
        )

    def aside(self, slot):
        level = self.level(slot)
        source = self.kept.at[1, level] if slot < EARLY else self.sides.at[slot]
        return remote(
            source, self.side_in.at[slot], self.side_send.at[slot], self.side_sem.at[slot],
            self.place.device(1) if slot == 0 else self.place.device(0, 1),
        )

    def along(self, slot):
        return remote(
            self.owns.at[slot], self.line_in.at[self.place.z], self.line_send.at[slot],
            self.line_sem.at[self.place.z], self.place.device(z=self.level(slot)),
        )

    def start(self):
        for slot in range(self.place.line):
            (self.aside(slot) if slot < EARLY else self.across(slot)).start()
            self.load(0, slot).start()
            if slot >= EARLY:
                self.load(1, slot).start()

    def send_side(self, slot):
        self.load(1, slot).wait()
        self.across(slot).wait_recv()
        self.sides[slot] = (self.sides[slot].astype(F32) + self.diag_in[slot].astype(F32)).astype(BF16)
        self.aside(slot).start()

    def collect(self, slot):
        self.load(0, slot).wait()
        self.aside(slot).wait_recv()
        return self.owns[slot].astype(F32) + self.side_in[slot].astype(F32)

    def send_line(self, slot):
        self.owns[slot] = self.collect(slot).astype(BF16)
        self.along(slot).start()

    def finish(self, out):
        place = self.place
        last = place.line - 1
        out[...] = self.collect(last)
        for step in range(1, place.line):
            z = lax.rem(place.z + step, place.line)
            remote(
                self.owns.at[0], self.line_in.at[z], self.line_send.at[0], self.line_sem.at[z],
                place.device(z=z),
            ).wait_recv()
            out[...] += self.line_in[z].astype(F32)
        for slot in range(place.line):
            self.aside(slot).wait_send()
            if slot >= EARLY:
                self.across(slot).wait_send()
            if slot < last:
                self.along(slot).wait_send()


class Small:
    def __init__(self, place, rows, part, low, out, sums, core_in, square_in, line_in, sems):
        self.place, self.rows = place, rows
        self.part, self.low, self.out = part, low, out
        self.sums, self.core_in, self.square_in, self.line_in = sums, core_in, square_in, line_in
        (
            self.core_send, self.core_sem, self.square_send, self.square_sem, self.line_send, self.line_sem,
            self.up_send, self.up_sem, self.back_send, self.back_sem, self.last_send, self.last_sem,
        ) = sems

    def lane(self, group, flip_core=0):
        place = self.place
        x = 1 - place.x if group in (OVER_X, ACROSS) else place.x
        y = 1 - place.y if group in (OVER_Y, ACROSS) else place.y
        core = 1 - place.core if flip_core else place.core
        return y, 2 * x + core

    def to(self, group):
        return self.place.device(int(group in (OVER_X, ACROSS)), int(group in (OVER_Y, ACROSS)))

    def core(self, group):
        y, d = self.lane(group, 1)
        return remote(
            self.part.at[y, d, :, self.rows], self.core_in.at[group, :, self.rows], self.core_send.at[group], self.core_sem.at[group],
            self.place.device(0, 0, 1),
        )

    def over(self, group):
        return remote(
            self.sums.at[group, :, self.rows], self.square_in.at[group - 1, :, self.rows], self.square_send.at[group - 1],
            self.square_sem.at[group - 1], self.to(group),
        )

    def along(self, z):
        return remote(
            self.sums.at[OWN, z, self.rows], self.line_in.at[self.place.z, self.rows], self.line_send.at[z],
            self.line_sem.at[self.place.z], self.place.device(z=z),
        )

    def landed(self, z):
        return remote(
            self.sums.at[OWN, z, self.rows], self.line_in.at[z, self.rows], self.line_send.at[z], self.line_sem.at[z],
            self.place.device(z=z),
        )

    def up(self, z):
        y, d = self.lane(OWN)
        return remote(
            self.low.at[self.rows], self.out.at[y, d, self.place.z, self.rows], self.up_send.at[z], self.up_sem.at[self.place.z],
            self.place.device(z=z),
        )

    def risen(self, z):
        y, d = self.lane(OWN)
        return remote(
            self.low.at[self.rows], self.out.at[y, d, z, self.rows], self.up_send.at[z], self.up_sem.at[z],
            self.place.device(z=z),
        )

    def back(self, group):
        y, d = self.lane(OWN)
        return remote(
            self.out.at[y, d, :, self.rows], self.out.at[y, d, :, self.rows], self.back_send.at[group - 1], self.back_sem.at[group - 1],
            self.to(group),
        )

    def last(self, group):
        y, d = self.lane(group)
        return remote(
            self.out.at[y, d, :, self.rows], self.out.at[y, d, :, self.rows], self.last_send.at[group], self.last_sem.at[group],
            self.place.device(0, 0, 1),
        )

    def others(self):
        return [lax.rem(self.place.z + step, self.place.line) for step in range(1, self.place.line)]

    def start(self):
        for group in (ACROSS, OVER_X, OVER_Y, OWN):
            self.core(group).start()

    def stages(self):
        place, rows = self.place, self.rows
        for group in (ACROSS, OVER_X, OVER_Y, OWN):
            self.core(group).wait_recv()
            y, d = self.lane(group)
            total = self.part[y, d, :, rows].astype(F32) + self.core_in[group, :, rows].astype(F32)
            self.sums[group, :, rows] = total.astype(BF16)
            if group != OWN:
                self.over(group).start()
        yield
        total = self.sums[OWN, :, rows].astype(F32)
        for group in (OVER_X, OVER_Y, ACROSS):
            self.over(group).wait_recv()
            total = total + self.square_in[group - 1, :, rows].astype(F32)
        self.sums[OWN, :, rows] = total.astype(BF16)
        for z in self.others():
            self.along(z).start()
        yield
        total = self.sums[OWN, place.z, rows].astype(F32)
        for z in self.others():
            self.landed(z).wait_recv()
            total = total + self.line_in[z, rows].astype(F32)
        self.low[rows] = total.astype(BF16)
        for z in self.others():
            self.up(z).start()
        y, d = self.lane(OWN)
        self.out[y, d, place.z, rows] = total.astype(BF16)
        yield
        for z in self.others():
            self.risen(z).wait_recv()
        for group in (ACROSS, OVER_X, OVER_Y):
            self.back(group).start()
        self.last(OWN).start()
        yield
        for group in (OVER_X, OVER_Y, ACROSS):
            self.back(group).wait_recv()
            self.last(group).start()
        yield
        for group in (OWN, OVER_X, OVER_Y, ACROSS):
            self.last(group).wait_recv()
        yield

    def finish(self):
        for group in (OWN, OVER_X, OVER_Y, ACROSS):
            self.core(group).wait_send()
            self.last(group).wait_send()
            if group != OWN:
                self.over(group).wait_send()
                self.back(group).wait_send()
        for z in self.others():
            self.along(z).wait_send()
            self.up(z).wait_send()


def copy_all(copies):
    for copy in copies:
        copy.start()


def attend_pack(p, patches, items, gains, table, qkv_s, proj_s, mixed_s, probs_s, att_s, mid_s, nm_s):
    _, length, width = patches.shape
    pairs = width // 128
    slot = lax.rem(p, mixed_s.shape[0])
    low_lane = iota((1, width), 1) % HEAD < HEAD // 2
    first_head = iota((1, 128), 1) < HEAD
    mask_a = jnp.where(first_head, 1.0, 0.0).astype(BF16)
    mask_b = jnp.where(first_head, 0.0, 1.0).astype(BF16)
    top_rows = iota((128, 1), 0) < HEAD
    source = patches[p].astype(F32)
    normed = (source * row_norm(source) * gains[0:1, :]).astype(BF16)
    mixed = dot_nn(normed, qkv_s[...])
    item_row = items[p].astype(F32)
    item_col, offset = positions(item_row, length)
    cos_row, sin_row = rope_rows(offset, table[...], length, width)
    mixed_s[slot, :, :width] = turn(mixed[:, :width], cos_row, sin_row, low_lane).astype(BF16)
    mixed_s[slot, :, width : 2 * width] = turn(
        mixed[:, width : 2 * width], cos_row, sin_row, low_lane
    ).astype(BF16)
    mixed_s[slot, :, 2 * width :] = mixed[:, 2 * width :].astype(BF16)
    for pair in range(pairs):
        lanes = slice(128 * pair, 128 * pair + 128)
        key_lanes = slice(width + 128 * pair, width + 128 * pair + 128)
        values_t = mixed[:, 2 * width + 128 * pair : 2 * width + 128 * pair + 128].T.astype(BF16)
        for block, (start, low, high) in enumerate(windows(length)):
            query = mixed_s[slot, start : start + QB, lanes] * 0.125
            query = jnp.concatenate([query * mask_a, query * mask_b], axis=0)
            scores = dot_nt(mixed_s[slot, low:high, key_lanes], query)
            here = item_row[:, start : start + QB]
            same = item_col[low:high] == jnp.concatenate([here, here], axis=1)
            scores = jnp.where(same, scores, -1e30)
            peak = jnp.max(scores, axis=0, keepdims=True)
            weights = jnp.exp(scores - peak)
            total = jnp.sum(weights, axis=0, keepdims=True)
            probs = (weights * (1.0 / total)).astype(BF16)
            probs_s[slot, pair, block, : high - low] = probs
            out = dot_nn(values_t[:, low:high], probs)
            out = jnp.where(top_rows, out[:, :QB], out[:, QB:])
            att_s[p, start : start + QB, lanes] = out.T.astype(BF16)
    middle = source + dot_nn(att_s[p], proj_s[...])
    mid_s[p] = middle
    nm_s[p] = (middle * row_norm(middle) * gains[1:2, :]).astype(BF16)


class Experts:
    def __init__(self, refs, cap):
        (
            self.nm, self.upstream, self.rank_s, self.gate_s, self.gg_s, self.x_s, self.hid_s, self.go_s,
            self.gb_s, self.y_s, self.inner_w, self.down_w,
        ) = refs
        self.cap = cap

    def prepare(self, p, ids, router_w):
        nm = self.nm
        _, length, width = nm.shape
        experts = router_w.shape[0]
        earlier = jnp.where(iota((length, length), 0) < iota((length, length), 1), 1.0, 0.0).astype(BF16)
        logits = dot_nt(router_w[...], nm[p])
        number = iota((experts, length), 0)
        hit0 = number == ids[p, 0:1, :]
        hit1 = number == ids[p, 1:2, :]
        chosen0 = jnp.sum(jnp.where(hit0, logits, 0.0), axis=0, keepdims=True)
        chosen1 = jnp.sum(jnp.where(hit1, logits, 0.0), axis=0, keepdims=True)
        peak = jnp.maximum(chosen0, chosen1)
        e0 = jnp.exp(chosen0 - peak)
        e1 = jnp.exp(chosen1 - peak)
        total = e0 + e1
        self.gate_s[p] = jnp.where(hit0, e0 / total, 0.0) + jnp.where(hit1, e1 / total, 0.0)
        named = jnp.where(hit0, 1.0, jnp.where(hit1, 1.0, 0.0))
        rank = dot_nn(named.astype(BF16), earlier)
        self.rank_s[p] = jnp.where(named > 0.5, rank, -1.0)

    def rows(self, p, expert):
        cap = self.cap
        _, length, width = self.nm.shape
        hidden_width = self.hid_s.shape[1]
        here = pl.ds(pl.multiple_of(p * cap, cap), cap)
        rank = self.rank_s[p, pl.ds(expert, 1), :]
        gate_row = self.gate_s[p, pl.ds(expert, 1), :]
        pick = iota((cap, length), 0).astype(F32) == rank
        chosen = jnp.where(pick, 1.0, 0.0).astype(BF16)
        taken = dot_nn(chosen, jnp.concatenate([self.nm[p], self.upstream[p]], axis=1))
        gate_col = jnp.sum(jnp.where(pick, gate_row, 0.0), axis=1, keepdims=True)
        x = taken[:, :width].astype(BF16)
        g = taken[:, width:]
        self.x_s[here, :] = x
        grad_out = (gate_col * g).astype(BF16)
        self.go_s[here, :] = grad_out
        gate = dot_nn(x, self.inner_w[:, :hidden_width])
        up = dot_nn(x, self.inner_w[:, hidden_width:])
        sigma = 1.0 / (1.0 + jnp.exp(-gate))
        active = gate * sigma
        hidden = (active * up).astype(BF16)
        self.hid_s[here, :] = hidden
        result = dot_nn(hidden, self.down_w[...]).astype(BF16).astype(F32)
        spot = pl.ds(pl.multiple_of(expert * cap, cap), cap)
        self.y_s[p, spot, :width] = (gate_col * result).astype(BF16)
        grad_gate = jnp.sum(g * result, axis=1, keepdims=True)
        self.gg_s[p, pl.ds(expert, 1), :] = jnp.sum(
            jnp.where(pick, grad_gate, 0.0), axis=0, keepdims=True
        )
        grad_hidden = dot_nt(grad_out, self.down_w[...])
        self.gb_s[here, :hidden_width] = (
            grad_hidden * up * sigma * (1.0 + gate * (1.0 - sigma))
        ).astype(BF16)
        self.gb_s[here, hidden_width:] = (grad_hidden * active).astype(BF16)
        self.y_s[p, spot, width:] = dot_nt(self.gb_s[here, :], self.inner_w[...]).astype(BF16)

    def grads(self, part):
        copies, _, width = part.shape
        hidden_width = self.hid_s.shape[1]
        deep, span = width // copies, hidden_width // copies
        for block in range(2 * hidden_width // width):
            lanes = slice(block * width, block * width + width)
            grad = dot_tn(self.x_s[...], self.gb_s[:, lanes]).astype(BF16)
            for d in range(copies):
                part[d, block * deep : block * deep + deep, :] = grad[d * deep : d * deep + deep]
        grad = dot_tn(self.hid_s[...], self.go_s[...]).astype(BF16)
        for d in range(copies):
            part[d, width:, :] = grad[d * span : d * span + span]

    def finish(self, p, router_w, mid, block_o, gmid_o, glog_o):
        cap = self.cap
        _, length, width = self.nm.shape
        experts = router_w.shape[0]
        ranks = self.rank_s[p].T
        slot = iota((length, cap), 1).astype(F32)
        pieces = [
            jnp.where(ranks[:, e : e + 1] == slot, 1.0, 0.0).astype(BF16) for e in range(experts)
        ]
        back = dot_nn(jnp.concatenate(pieces, axis=1), self.y_s[p])
        gate = self.gate_s[p]
        grad_gate = self.gg_s[p]
        mean = jnp.sum(gate * grad_gate, axis=0, keepdims=True)
        hit = self.rank_s[p] > -0.5
        grad_logits = jnp.where(hit, gate * (grad_gate - mean), 0.0).astype(BF16)
        glog_o[p] = grad_logits
        block_o[p] = (mid[p] + back[:, :width]).astype(BF16)
        gmid_o[p] = back[:, width:] + dot_tn(grad_logits, router_w[...])


def unpack(weights, inner_w, down_w):
    copies, _, width = weights.shape
    deep, span = width // copies, down_w.shape[0] // copies
    for d in range(copies):
        for block in range(inner_w.shape[1] // width):
            inner_w[d * deep : d * deep + deep, block * width : block * width + width] = weights[
                d, block * deep : block * deep + deep, :
            ]
        down_w[d * span : d * span + span, :] = weights[d, width:, :]


def forward_kernel(
    line, cap,
    shard, patches, upstream, items, ids, qkv_w, proj_w, router_w, gains, table,
    full, kept_o, mixed_o, probs_o, att_o, mid_o, nm_o, block_o, gmid_o, glog_o,
    qkv_s, proj_s, mixed_s, probs_s, att_s, mid_s, nm_s, wbuf, pbuf,
    rank_s, gate_s, gg_s, x_s, hid_s, go_s, gb_s, y_s, inner_s, down_s,
    sums, core_in, diag_in, side_in,
    send_sem, recv_sem, own_sem, save_sem, fetch_sem, keep_sem,
    core_send, core_sem, diag_send, diag_sem, side_send, side_sem, credit_sem,
):
    packs = patches.shape[0]
    experts = router_w.shape[0]
    place = Place(line)
    place.greet()
    gather = Gather(place, shard, full, send_sem, recv_sem, own_sem)
    gather.start()
    qkv_s[...] = qkv_w[...].astype(BF16)
    proj_s[...] = proj_w[...].astype(BF16)
    work = Experts(
        (nm_s, upstream, rank_s, gate_s, gg_s, x_s, hid_s, go_s, gb_s, y_s, inner_s, down_s), cap
    )
    saves = ((mixed_s, mixed_o), (probs_s, probs_o), (att_s, att_o), (mid_s, mid_o), (nm_s, nm_o))

    def save(n, p):
        source, target = saves[n]
        return pltpu.make_async_copy(
            source.at[lax.rem(p, source.shape[0])], target.at[p], save_sem.at[n, p]
        )

    def pack(p, carry):
        def reuse():
            save(0, p - 2).wait()
            save(1, p - 2).wait()

        pl.when(p >= 2)(reuse)
        attend_pack(p, patches, items, gains, table, qkv_s, proj_s, mixed_s, probs_s, att_s, mid_s, nm_s)
        for n in range(len(saves)):
            save(n, p).start()
        work.prepare(p, ids, router_w)
        for k in range(1, line - 1):

            def relay(k=k):
                gather.column(k)
                if k == 1:
                    gather.square(0)

            pl.when(p == min(k - 1, packs - 1))(relay)
        return carry

    lax.fori_loop(0, packs, pack, 0)

    def near(i):
        return int(i < line) if isinstance(i, int) else (i < line).astype(jnp.int32)

    def number(i):
        level = place.by_distance(near(i) * i + (1 - near(i)) * (2 * line - 1 - i))
        side = near(i) * place.y + (1 - near(i)) * (1 - place.y)
        return level, 2 * level + side

    def fetch(i):
        return pltpu.make_async_copy(full.at[number(i)[1]], wbuf.at[lax.rem(i, 2)], fetch_sem.at[lax.rem(i, 2)])

    def arrive(i):
        level = number(i)[0]

        def close():
            gather.partner(0, 0, level)
            gather.partner(1, 0, level)

        def far():
            gather.partner(0, 1, level)
            gather.partner(1, 1, level)

        if isinstance(i, int):
            (close if i < line else far)()
        else:
            pl.when(i < line)(close)
            pl.when(i >= line)(far)

    def piece(q, flip_core):
        return place.device(q, 0, flip_core)[0]

    def swap(i, q):
        slot = lax.rem(i, 2)
        return remote(
            pbuf.at[slot, piece(q, 1)], core_in.at[slot, q], core_send.at[slot, q], core_sem.at[slot, q],
            place.device(0, 0, 1),
        )

    def across(n):
        level = number(line + n)[0]
        return remote(
            sums.at[ACROSS, level], diag_in.at[n], diag_send.at[n], diag_sem.at[n],
            place.device(0, 1) if n == 0 else place.device(1),
        )

    def aside(level, group=OVER_X):
        return remote(
            sums.at[group, level], side_in.at[level], side_send.at[level], side_sem.at[level],
            place.device(1) if group == OVER_X else place.device(0, 1),
        )

    def keep(which, group, level):
        return pltpu.make_async_copy(sums.at[group, level], kept_o.at[which, level], keep_sem.at[which, level])

    def merge(i):
        slot = lax.rem(i, 2)
        level = number(i)[0]
        group = 2 * (1 - near(i))
        for q in range(2):
            swap(i, q).wait_recv()
            total = pbuf[slot, piece(q, 0)].astype(F32) + core_in[slot, q].astype(F32)
            sums[group + q, level] = total.astype(BF16)
        pl.semaphore_signal(credit_sem, inc=1, device_id=place.device(0, 0, 1), device_id_type=MESH_ID)
        pl.when(jnp.logical_and(i >= 2, i < line - 1))(lambda: aside(level).start())

        def early(n):
            across(n).start()
            if n == 0:
                aside(level, OVER_Y).start()

        for n in range(EARLY):
            pl.when(i == line + n)(lambda n=n: early(n))

        def put_away():
            keep(1, OVER_Y, level).start()
            keep(2, ACROSS, level).start()

        pl.when(i >= line + EARLY)(put_away)

    gather.own.wait()
    arrive(0)
    fetch(0).start()

    def last_square():
        gather.square(line - 1)
        for i in range(2):
            aside(number(i)[0]).start()

    def two_corners():
        gather.corner(0)
        gather.corner(1)

    def third():
        gather.column(line - 1)
        gather.square(1)

    events = (
        (0, 0, third),
        (1, 1, lambda: gather.square(line - 2)),
        (2, 1, last_square),
        (3, 0, two_corners),
        (3, 1, lambda: gather.corner(line - 2)),
        (3, packs - 1, lambda: gather.corner(line - 1)),
    )

    def one(i, carry):
        fetch(i).wait()
        unpack(wbuf.at[lax.rem(i, 2)], inner_s, down_s)
        expert = number(i)[1]

        def rows(p, inner_carry):
            work.rows(p, expert)
            pl.when(jnp.logical_and(p == 0, i >= 1))(lambda: merge(i - 1))
            for slot, turn_at, event in events:
                pl.when(jnp.logical_and(i == slot, p == turn_at))(event)
            return inner_carry

        lax.fori_loop(0, packs, rows, 0)

        def ahead():
            arrive(i + 1)
            fetch(i + 1).start()

        pl.when(i + 1 < experts)(ahead)

        def free():
            pl.semaphore_wait(credit_sem, 1)
            for q in range(2):
                swap(i, q).wait_send()

        pl.when(i >= 2)(free)
        work.grads(pbuf.at[lax.rem(i, 2)])
        for q in range(2):
            swap(i, q).start()
        return carry

    lax.fori_loop(0, experts, one, 0)

    def last(i, carry):
        merge(i)
        return carry

    lax.fori_loop(experts - 1, experts, last, 0)

    def finish(p, carry):
        work.finish(p, router_w, mid_s, block_o, gmid_o, glog_o)
        return carry

    lax.fori_loop(0, packs, finish, 0)

    def settle(level, carry):
        aside(level).wait_recv()
        sums[OWN, level] = (sums[OWN, level].astype(F32) + side_in[level].astype(F32)).astype(BF16)
        keep(0, OWN, level).start()
        return carry

    lax.fori_loop(0, line, settle, 0)
    for n in range(EARLY):
        level = number(line + n)[0]
        across(n).wait_recv()
        group = OVER_X if n == 0 else OVER_Y
        sums[group, level] = (sums[group, level].astype(F32) + diag_in[n].astype(F32)).astype(BF16)
        keep(1, group, level).start()
        across(n).wait_send()

    def drain(level, carry):
        keep(0, OWN, level).wait()
        keep(1, OVER_Y, level).wait()
        aside(level).wait_send()
        return carry

    lax.fori_loop(0, line, drain, 0)
    for n in range(EARLY, line):
        keep(2, ACROSS, number(line + n)[0]).wait()
    pl.semaphore_wait(credit_sem, 2)
    for i in range(experts - 2, experts):
        for q in range(2):
            swap(i, q).wait_send()
    for n in range(len(saves)):
        for p in range(packs - 2 if n < 2 else 0, packs):
            save(n, p).wait()
    gather.wires.finish()


def run_forward(shard, patches, upstream, items, ids, qkv_w, proj_w, router_w, gains, table, hidden, slot):
    packs, length, width = patches.shape
    experts = router_w.shape[0]
    dp, ex = lax.axis_size("dp"), lax.axis_size("expert")
    line = ex // 2
    cap = 2 * length * ids.shape[1] // experts
    pairs, blocks = width // 128, length // QB
    rows = shard.shape[0]
    dma = pltpu.SemaphoreType.DMA
    here = pl.BlockSpec(memory_space=pltpu.VMEM)
    away = pl.BlockSpec(memory_space=pl.ANY)
    saved = (
        ((packs, length, 3 * width), BF16),
        ((packs, pairs, blocks, 3 * QB, 2 * QB), BF16),
        ((packs, length, width), BF16),
        ((packs, length, width), F32),
        ((packs, length, width), BF16),
    )
    shapes = (
        ((ex, dp, rows, width), BF16),
        ((3, line, rows, width), BF16),
        *saved,
        ((packs, length, width), BF16),
        ((packs, length, width), F32),
        ((packs, experts, length), BF16),
    )
    scratch = (
        ((width, 3 * width), BF16),
        ((width, width), BF16),
        ((2, length, 3 * width), BF16),
        ((2, pairs, blocks, 3 * QB, 2 * QB), BF16),
        *saved[2:],
        ((2, dp, rows, width), BF16),
        ((2, dp, rows, width), BF16),
        ((packs, experts, length), F32),
        ((packs, experts, length), F32),
        ((packs, experts, length), F32),
        ((packs * cap, width), BF16),
        ((packs * cap, hidden), BF16),
        ((packs * cap, width), BF16),
        ((packs * cap, 2 * hidden), BF16),
        ((packs, experts * cap, 2 * width), BF16),
        ((width, 2 * hidden), BF16),
        ((hidden, width), BF16),
        ((4, line, rows, width), BF16),
        ((2, 2, rows, width), BF16),
        ((EARLY, rows, width), BF16),
        ((line, rows, width), BF16),
    )
    return pl.pallas_call(
        functools.partial(forward_kernel, line, cap),
        out_shape=tuple(jax.ShapeDtypeStruct(*s) for s in shapes),
        in_specs=[here] * 10,
        out_specs=(away,) * 7 + (here,) * 3,
        scratch_shapes=[pltpu.VMEM(*s) for s in scratch]
        + [dma((24 * line,)), dma((ex, dp)), dma, dma((5, packs)), dma((2,)), dma((3, line))]
        + [dma((2, 2))] * 2 + [dma((EARLY,))] * 2 + [dma((line,))] * 2 + [pltpu.SemaphoreType.REGULAR],
        compiler_params=pltpu.CompilerParams(
            collective_id=slot, has_side_effects=True, vmem_limit_bytes=VMEM_BYTES
        ),
        name="forward",
    )(shard, patches, upstream, items, ids, qkv_w, proj_w, router_w, gains, table)


class Backward:
    def __init__(self, refs):
        (
            self.patches, self.upstream, self.items, self.gains, self.table, self.gmid, self.glog,
            self.qkv_s, self.proj_s, self.mixed, self.probs, self.mid, self.nm,
            self.patch_o, self.normed_s, self.branch_s, self.datt_s, self.dmix_s, self.dkv_s, self.small_g,
        ) = refs

    def pack(self, p, midway):
        packs, length, width = self.patches.shape
        pairs = width // 128
        experts = self.glog.shape[1]
        gains, mixed, dkv_s = self.gains, self.mixed, self.dkv_s
        low_lane = iota((1, width), 1) % HEAD < HEAD // 2
        first_head = iota((1, 128), 1) < HEAD
        mask_a = jnp.where(first_head, 1.0, 0.0).astype(BF16)
        mask_b = jnp.where(first_head, 0.0, 1.0).astype(BF16)
        top_rows = iota((128, 1), 0) < HEAD
        rows = pl.ds(pl.multiple_of(p * length, length), length)
        source = self.patches[p].astype(F32)
        gain0, gain1 = gains[0:1, :], gains[1:2, :]
        slot = lax.rem(p, 2)
        middle = self.mid[slot]
        inv = row_norm(middle)
        unit = middle * inv
        grad_mid = self.gmid[p]
        self.small_g[experts + 1 : experts + 2, :] += jnp.sum(grad_mid * unit, axis=0, keepdims=True)
        self.small_g[0:experts, :] += dot_nn(self.glog[p], self.nm[slot])
        grad_unit = grad_mid * gain1
        grad_middle = self.upstream[p].astype(F32) + inv * (
            grad_unit - unit * jnp.mean(grad_unit * unit, axis=1, keepdims=True)
        )
        self.patch_o[p] = grad_middle
        branch = grad_middle.astype(BF16)
        self.branch_s[rows, :] = branch
        self.datt_s[...] = dot_nt(branch, self.proj_s[...]).astype(BF16)
        dkv_s[...] = jnp.zeros(dkv_s.shape, F32)
        item_row = self.items[p].astype(F32)
        item_col, offset = positions(item_row, length)
        cos_row, sin_row = rope_rows(offset, self.table[...], length, width)
        for pair in range(pairs):
            if pair == 2:
                midway()
            lanes = slice(128 * pair, 128 * pair + 128)
            key_lanes = slice(width + 128 * pair, width + 128 * pair + 128)
            value_lanes = slice(2 * width + 128 * pair, 2 * width + 128 * pair + 128)
            keys_t = mixed[slot, :, key_lanes].astype(F32).T.astype(BF16)
            for block, (start, low, high) in enumerate(windows(length)):
                query = mixed[slot, start : start + QB, lanes] * 0.125
                query = jnp.concatenate([query * mask_a, query * mask_b], axis=0)
                datt = self.datt_s[start : start + QB, lanes]
                datt = jnp.concatenate([datt * mask_a, datt * mask_b], axis=0)
                prob = self.probs[slot, pair, block, : high - low]
                dprob = dot_nt(mixed[slot, low:high, value_lanes], datt)
                weight = prob.astype(F32)
                mean = jnp.sum(weight * dprob, axis=0, keepdims=True)
                dscore = (weight * (dprob - mean)).astype(BF16)
                dkv_s[low:high, key_lanes] += dot_nn(dscore, query)
                dkv_s[low:high, value_lanes] += dot_nn(prob, datt)
                dquery = dot_nn(keys_t[:, low:high], dscore)
                dquery = jnp.where(top_rows, dquery[:, :QB], dquery[:, QB:])
                dkv_s[start : start + QB, lanes] = dquery.T * 0.125
        dmix_s = self.dmix_s
        dmix_s[rows, :width] = turn(dkv_s[:, :width], cos_row, -sin_row, low_lane).astype(BF16)
        dmix_s[rows, width : 2 * width] = turn(
            dkv_s[:, width : 2 * width], cos_row, -sin_row, low_lane
        ).astype(BF16)
        dmix_s[rows, 2 * width :] = dkv_s[:, 2 * width :].astype(BF16)
        grad_normed = dot_nt(dmix_s[rows, :], self.qkv_s[...])
        inv_in = row_norm(source)
        unit_in = source * inv_in
        self.normed_s[rows, :] = (unit_in * gain0).astype(BF16)
        self.small_g[experts : experts + 1, :] += jnp.sum(grad_normed * unit_in, axis=0, keepdims=True)
        grad_unit_in = grad_normed * gain0
        self.patch_o[p] += inv_in * (
            grad_unit_in - unit_in * jnp.mean(grad_unit_in * unit_in, axis=1, keepdims=True)
        )

    def tail(self, att, tail):
        packs, length, width = self.patches.shape
        tail[...] = jnp.zeros(tail.shape, BF16)
        for block in range(4):
            if block < 3:
                grad = dot_tn(self.normed_s[...], self.dmix_s[:, block * width : block * width + width])
            else:
                flat = jnp.concatenate([att[p] for p in range(packs)], axis=0)
                grad = dot_tn(flat, self.branch_s[...])
            lay_tail(tail, block, grad.astype(BF16))
        tail[0, 0, 0, tail.shape[3] - 16 :, :] = self.small_g[...].astype(BF16)


def tail_rows(width, devices):
    return 4 * width // devices + 16


def lay_tail(tail, block, grad):
    _, dp, line, rows, width = tail.shape
    rows = rows - 16
    each = width // rows
    for piece in range(each):
        number = block * each + piece
        spot = (number // (dp * line), number // line % dp, number % line)
        tail[(*spot, slice(0, rows), slice(None))] = grad[piece * rows : piece * rows + rows]


def backward_kernel(
    line,
    kept, patches, upstream, items, qkv_w, proj_w, gains, table, gmid, glog, mixed_i, probs_i, att_i, mid_i, nm_i,
    patch_o, grad_o, tail_o,
    qkv_s, proj_s, mixed, probs, att, mid, nm,
    normed_s, branch_s, datt_s, dmix_s, dkv_s, small_g, tail, tail_low,
    owns, sides, diag_in, side_in, line_in,
    tsums, tcore_in, tsquare_in, tline_in,
    load_sem, own_sem, diag_send, diag_sem, side_send, side_sem, line_send, line_sem,
    *small_sems,
):
    packs = patches.shape[0]
    place = Place(line)
    place.greet()
    reduce = Close(
        place, kept, owns, sides, diag_in, side_in, line_in, own_sem,
        (diag_send, diag_sem, side_send, side_sem, line_send, line_sem),
    )
    half = tail_low.shape[0] // 2
    smalls = [
        Small(
            place, pl.ds(n * half, half), tail, tail_low, tail_o, tsums, tcore_in, tsquare_in, tline_in,
            small_sems[12 * n : 12 * n + 12],
        )
        for n in range(2)
    ]
    reduce.start()
    loads = ((mixed_i, mixed), (mid_i, mid), (nm_i, nm), (probs_i, probs), (att_i, att))

    def load(n, p):
        source, target = loads[n]
        return pltpu.make_async_copy(
            source.at[p], target.at[lax.rem(p, target.shape[0])], load_sem.at[n, p]
        )

    for p in range(packs):
        for n in range(len(loads)):
            if p < loads[n][1].shape[0]:
                load(n, p).start()
    qkv_s[...] = qkv_w[...].astype(BF16)
    proj_s[...] = proj_w[...].astype(BF16)
    small_g[...] = jnp.zeros(small_g.shape, F32)
    work = Backward((
        patches, upstream, items, gains, table, gmid, glog,
        qkv_s, proj_s, mixed, probs, mid, nm,
        patch_o, normed_s, branch_s, datt_s, dmix_s, dkv_s, small_g,
    ))
    def pack(p, carry):
        for n in range(len(loads)):
            load(n, p).wait()

        def midway():
            pl.when(p == 1)(lambda: reduce.send_side(2))

            def later():
                reduce.send_side(3)
                reduce.send_line(2)

            pl.when(p == packs - 1)(later)

        work.pack(p, midway)

        def ahead():
            for n in range(len(loads) - 1):
                load(n, p + 2).start()

        pl.when(p + 2 < packs)(ahead)

        def first():
            reduce.send_line(0)
            reduce.send_line(1)

        pl.when(p == 0)(first)
        return carry

    lax.fori_loop(0, packs, pack, 0)
    work.tail(att, tail)
    for small in smalls:
        small.start()
    chains = [small.stages() for small in smalls]
    for stage in range(6):
        for chain in chains:
            next(chain)
    reduce.finish(grad_o)
    for small in smalls:
        small.finish()


def run_backward(
    kept, patches, upstream, items, qkv_w, proj_w, gains, table, gmid, glog, mixed, probs, att, mid, nm, slot
):
    packs, length, width = patches.shape
    _, line, rows, _ = kept.shape
    dp, ex = lax.axis_size("dp"), lax.axis_size("expert")
    few = tail_rows(width, ex * dp)
    dma = pltpu.SemaphoreType.DMA
    here = pl.BlockSpec(memory_space=pltpu.VMEM)
    away = pl.BlockSpec(memory_space=pl.ANY)
    shapes = (
        ((packs, length, width), F32),
        ((rows, width), F32),
        ((ex // line, dp, line, few, width), BF16),
    )
    scratch = (
        ((width, 3 * width), BF16),
        ((width, width), BF16),
        ((2,) + mixed.shape[1:], BF16),
        ((2,) + probs.shape[1:], BF16),
        (att.shape, BF16),
        ((2,) + mid.shape[1:], F32),
        ((2,) + nm.shape[1:], BF16),
        ((packs * length, width), BF16),
        ((packs * length, width), BF16),
        ((length, width), BF16),
        ((packs * length, 3 * width), BF16),
        ((length, 3 * width), F32),
        ((16, width), F32),
        ((ex // line, dp, line, few, width), BF16),
        ((few, width), BF16),
        *([((line, rows, width), BF16)] * 5),
        ((4, line, few, width), BF16),
        ((4, line, few, width), BF16),
        ((3, line, few, width), BF16),
        ((line, few, width), BF16),
    )
    small_sems = [dma((n,)) for n in (4, 4, 3, 3, line, line, line, line, 3, 3, 4, 4) * 2]
    return pl.pallas_call(
        functools.partial(backward_kernel, line),
        out_shape=tuple(jax.ShapeDtypeStruct(*s) for s in shapes),
        in_specs=[away] + [here] * 9 + [away] * 5,
        out_specs=(here, here, here),
        scratch_shapes=[pltpu.VMEM(*s) for s in scratch]
        + [dma((5, packs)), dma((2, line))] + [dma((line,))] * 6 + small_sems,
        compiler_params=pltpu.CompilerParams(
            collective_id=slot, has_side_effects=True, vmem_limit_bytes=VMEM_BYTES
        ),
        name="backward",
    )(kept, patches, upstream, items, qkv_w, proj_w, gains, table, gmid, glog, mixed, probs, att, mid, nm)


def update_kernel(
    tail, inner_g, down_g,
    qkv_w, qkv_f, qkv_s, proj_w, proj_f, proj_s, router_w, router_f, router_s,
    gains_w, gains_f, gains_s, inner_w, inner_f, inner_s, down_w, down_f, down_s,
    qkv_wo, qkv_fo, qkv_so, proj_wo, proj_fo, proj_so, router_wo, router_fo, router_so,
    gains_wo, gains_fo, gains_so, inner_wo, inner_fo, inner_so, down_wo, down_fo, down_so,
):
    step = pl.program_id(0)
    ex, dp, few, width = tail.shape
    rows = few - 16
    experts = router_w.shape[0]
    attn = tail[:, :, :rows, :].reshape(ex * dp * rows, width).astype(F32)

    def write(outs, values):
        for out, value in zip(outs, values):
            out[...] = value

    def qkv():
        write((qkv_wo, qkv_fo, qkv_so), adamw(qkv_w[...], qkv_f[...], qkv_s[...], attn, 0.1, 0.1))

    def proj():
        write((proj_wo, proj_fo, proj_so), adamw(proj_w[...], proj_f[...], proj_s[...], attn, 0.4, 0.1))

    def rest():
        small = tail[0, 0, rows:, :].astype(F32)
        router_g = small[:experts]
        gains_g = small[experts : experts + 2]
        write(
            (router_wo, router_fo, router_so),
            adamw(router_w[...], router_f[...], router_s[...], router_g, 0.07, 0.1),
        )
        write(
            (gains_wo, gains_fo, gains_so),
            adamw(gains_w[...], gains_f[...], gains_s[...], gains_g, 0.4, 0.0),
        )

    pl.when(step < 3)(qkv)
    pl.when(step == 3)(proj)
    pl.when(step == 0)(rest)
    write(
        (inner_wo, inner_fo, inner_so),
        adamw(inner_w[...], inner_f[...], inner_s[...], inner_g[...], 0.1, 0.1),
    )
    write((down_wo, down_fo, down_so), adamw(down_w[...], down_f[...], down_s[...], down_g[...], 0.15, 0.1))


def run_update(tail, grad, weights):
    ex, dp, few, width = tail.shape
    qkv, router, inner, down = weights[0], weights[6], weights[12], weights[15]
    deep, span = inner.shape[0], down.shape[0] // 4
    of_qkv = pl.BlockSpec((width, width), lambda j: (0, jnp.minimum(j, 2)))
    of_proj = pl.BlockSpec((width, width), lambda j: (0, 0))
    of_router = pl.BlockSpec(router.shape, lambda j: (0, 0))
    of_gains = pl.BlockSpec((2, width), lambda j: (0, 0))
    of_inner = pl.BlockSpec((deep, width), lambda j: (0, j))
    of_down = pl.BlockSpec((span, width), lambda j: (j, 0))
    specs = []
    for spec in (of_qkv, of_proj, of_router, of_gains, of_inner, of_down):
        specs += [spec] * 3
    first_down = 4 * deep // span
    return pl.pallas_call(
        update_kernel,
        out_shape=tuple(jax.ShapeDtypeStruct(w.shape, F32) for w in weights),
        grid=(4,),
        in_specs=[
            pl.BlockSpec((ex // 4, dp, few, width), lambda j: (j, 0, 0, 0)),
            pl.BlockSpec((deep, width), lambda j: (j, 0)),
            pl.BlockSpec((span, width), lambda j: (first_down + j, 0)),
        ] + specs,
        out_specs=tuple(specs),
        compiler_params=pltpu.CompilerParams(vmem_limit_bytes=VMEM_BYTES),
        name="update",
    )(tail, grad, grad, *weights)


def fast(
    patches, out_grad, item_ids, expert_ids,
    qkv_master, qkv_first, qkv_second,
    proj_master, proj_first, proj_second,
    router_master, router_first, router_second,
    gains_master, gains_first, gains_second,
    inner_master, inner_first, inner_second,
    down_master, down_first, down_second,
):
    width = patches.shape[2]
    experts = router_master.shape[1]
    hidden = down_master.shape[1] * lax.axis_size("dp")
    deep = inner_master.shape[1]
    blocks = inner_master.shape[2] // width
    shard = jnp.concatenate(
        [
            jnp.swapaxes(inner_master[0].reshape(deep, blocks, width), 0, 1).reshape(blocks * deep, width),
            down_master[0],
        ],
        axis=0,
    ).astype(BF16)
    router_w = router_master.T.astype(BF16)
    ids = jnp.swapaxes(expert_ids, 1, 2)
    table = jnp.asarray(rope_table(QB))
    full, kept, mixed, probs, att, mid, nm, block_out, gmid, glog = run_forward(
        shard, patches, out_grad, item_ids, ids, qkv_master, proj_master, router_w, gains_master, table, hidden, 0
    )
    patch_grad, grad, tail = run_backward(
        kept, patches, out_grad, item_ids, qkv_master, proj_master, gains_master, table,
        gmid, glog, mixed, probs, att, mid, nm, 1,
    )
    weights = (
        qkv_master, qkv_first, qkv_second,
        proj_master, proj_first, proj_second,
        router_master.T, router_first.T, router_second.T,
        gains_master, gains_first, gains_second,
        inner_master[0], inner_first[0], inner_second[0],
        down_master[0], down_first[0], down_second[0],
    )
    tail = tail.reshape(-1, lax.axis_size("dp"), *tail.shape[3:])
    new = run_update(tail, grad, weights)
    return (
        block_out, patch_grad, *new[:6], *(value.T for value in new[6:9]), *new[9:12],
        *(value[None] for value in new[12:]),
    )


GATHER_LIMIT = 16 * 1024 * 1024


def step(*args):
    inner_master, down_master = args[16], args[19]
    experts = inner_master.shape[0] * lax.axis_size("expert")
    entries = inner_master.shape[1] * inner_master.shape[2] + down_master.shape[1] * down_master.shape[2]
    weight_bytes = 2 * experts * entries * lax.axis_size("dp")
    square = lax.axis_size("dp") == 4 and lax.axis_size("expert") == 8 and inner_master.shape[0] == 1 and lax.axis_size("expert") == experts
    return (fast if square and weight_bytes <= GATHER_LIMIT else local)(*args)


def solution(mesh):
    in_specs = (
        P(None, ("dp", "expert"), None),
        P(None, ("dp", "expert"), None),
        P(None, ("dp", "expert"), None),
        P(None, ("dp", "expert"), None),
        P(),
        P(),
        P(),
        P(),
        P(),
        P(),
        P(),
        P(),
        P(),
        P(),
        P(),
        P(),
        P("expert", "dp", None),
        P("expert", "dp", None),
        P("expert", "dp", None),
        P("expert", "dp", None),
        P("expert", "dp", None),
        P("expert", "dp", None),
    )
    out_specs = (
        P(None, ("dp", "expert"), None),
        P(None, ("dp", "expert"), None),
        P(),
        P(),
        P(),
        P(),
        P(),
        P(),
        P(),
        P(),
        P(),
        P(),
        P(),
        P(),
        P("expert", "dp", None),
        P("expert", "dp", None),
        P("expert", "dp", None),
        P("expert", "dp", None),
        P("expert", "dp", None),
        P("expert", "dp", None),
    )
    return jax.shard_map(step, mesh=mesh, in_specs=in_specs, out_specs=out_specs, check_vma=False)
```

```python
import functools

import jax
import jax.numpy as jnp
import numpy as np
from jax import lax
from jax.experimental import pallas as pl
from jax.experimental.pallas import tpu as pltpu
from jax.sharding import PartitionSpec as P

HEADS = 6
HEAD = 64


norm_eps = 1e-06
adam_eps = 1e-08
correction = 0.875


def rotary_tables(item_row):
    length = item_row.shape[0]
    places = jnp.arange(length, dtype=jnp.int32)
    starts = jnp.concatenate([jnp.ones((1,), dtype=bool), item_row[1:] != item_row[:-1]])
    first = lax.cummax(jnp.where(starts, places, 0), axis=0)
    offset = (places - first).astype(jnp.float32)
    half = HEAD // 2
    freqs = 10000.0 ** (-jnp.arange(half, dtype=jnp.float32) / half)
    angles = offset[:, None] * freqs[None, :]
    return (jnp.cos(angles), jnp.sin(angles))


def rotate(vectors, cosine, sine):
    half = vectors.shape[-1] // 2
    first_half = vectors[..., :half]
    second_half = vectors[..., half:]
    cos_part = cosine[:, None, :]
    sin_part = sine[:, None, :]
    return jnp.concatenate(
        [
            first_half * cos_part - second_half * sin_part,
            second_half * cos_part + first_half * sin_part,
        ],
        axis=-1,
    )


def masked_scores(query, keys, same_item):
    scores = jnp.einsum("qhe,khe->hqk", query, keys, preferred_element_type=jnp.float32) * 0.125
    return jnp.where(same_item[None], scores, -1e30)


def adamw(weight, first, second, grad, rate, decay):
    first_new = 0.5 * first + 0.5 * grad
    second_new = 0.5 * second + 0.5 * grad * grad
    update = first_new / correction / (jnp.sqrt(second_new / correction) + adam_eps)
    return (weight - rate * (update + decay * weight), first_new, second_new)


def local(
    patches,
    out_grad,
    item_ids,
    expert_ids,
    qkv_master,
    qkv_first,
    qkv_second,
    proj_master,
    proj_first,
    proj_second,
    router_master,
    router_first,
    router_second,
    gains_master,
    gains_first,
    gains_second,
    inner_master,
    inner_first,
    inner_second,
    down_master,
    down_first,
    down_second,
):
    expert_count = lax.axis_size("expert")
    local_experts = inner_master.shape[0]
    experts = expert_count * local_experts
    length = patches.shape[1]
    width = patches.shape[2]
    top = expert_ids.shape[2]
    capacity = 2 * length * top // experts
    hidden_width = down_master.shape[1] * lax.axis_size("dp")
    inner_low, down_low = (
        lax.all_gather(inner_master.astype(jnp.bfloat16), "dp", axis=1, tiled=True),
        lax.all_gather(down_master.astype(jnp.bfloat16), "dp", axis=1, tiled=True),
    )
    qkv_low = qkv_master.astype(jnp.bfloat16)
    proj_low = proj_master.astype(jnp.bfloat16)
    router_low = router_master.astype(jnp.bfloat16)
    gain_attn = gains_master[0]
    gain_ffn = gains_master[1]
    expert_numbers = jnp.arange(experts, dtype=jnp.int32)

    def expert_forward(received):
        count = received.shape[1]
        grid = received.reshape(expert_count, local_experts, count, width)
        both = jnp.einsum("sjcd,jdf->sjcf", grid, inner_low, preferred_element_type=jnp.float32)
        hidden = (jax.nn.silu(both[..., :hidden_width]) * both[..., hidden_width:]).astype(
            jnp.bfloat16
        )
        result = jnp.einsum("sjcf,jfd->sjcd", hidden, down_low, preferred_element_type=jnp.float32)
        result = result.astype(jnp.bfloat16).reshape(experts, count, width)
        returned = lax.all_to_all(result, "expert", split_axis=0, concat_axis=0, tiled=True)
        return (returned, received)

    def micro_step(carry, inputs):
        grad_qkv, grad_proj, grad_router, grad_gains, grad_inner, grad_down = carry
        patch, upstream, item_block, routes = inputs
        items = item_block[0]
        source = patch.astype(jnp.float32)
        inv_first = lax.rsqrt(jnp.mean(source * source, axis=1, keepdims=True) + norm_eps)
        unit_first = source * inv_first
        normed_in = (unit_first * gain_attn).astype(jnp.bfloat16)
        mixed = jnp.dot(normed_in, qkv_low, preferred_element_type=jnp.float32)
        cosine, sine = rotary_tables(items)
        query = rotate(mixed[:, :width].reshape(length, HEADS, HEAD), cosine, sine).astype(
            jnp.bfloat16
        )
        keys = rotate(
            mixed[:, width : 2 * width].reshape(length, HEADS, HEAD), cosine, sine
        ).astype(jnp.bfloat16)
        values = mixed[:, 2 * width :].reshape(length, HEADS, HEAD).astype(jnp.bfloat16)
        same_item = items[:, None] == items[None, :]
        scores = masked_scores(query, keys, same_item)
        peak = jnp.max(scores, axis=2, keepdims=True)
        weights = jnp.exp(scores - peak)
        totals = jnp.sum(weights, axis=2, keepdims=True)
        probs_low = (weights / totals).astype(jnp.bfloat16)
        log_total = peak + jnp.log(totals)
        attended = jnp.einsum("hqk,khe->qhe", probs_low, values, preferred_element_type=jnp.float32)
        attended = attended.reshape(length, width).astype(jnp.bfloat16)
        middle = source + jnp.dot(attended, proj_low, preferred_element_type=jnp.float32)
        inv_second = lax.rsqrt(jnp.mean(middle * middle, axis=1, keepdims=True) + norm_eps)
        unit_second = middle * inv_second
        normed_mid = (unit_second * gain_ffn).astype(jnp.bfloat16)
        logits = jnp.dot(normed_mid, router_low, preferred_element_type=jnp.float32)
        chosen = jnp.take_along_axis(logits, routes, axis=1)
        gates = jax.nn.softmax(chosen, axis=1)
        flat_ids = routes.reshape(length * top)
        hits = (flat_ids[:, None] == expert_numbers[None, :]).astype(jnp.int32)
        rank = jnp.sum(jnp.cumsum(hits, axis=0) * hits, axis=1) - 1
        slots = flat_ids * capacity + rank
        copies = jnp.repeat(normed_mid, top, axis=0)
        outgoing = jnp.zeros((experts * capacity, width), jnp.bfloat16).at[slots].set(copies)
        outgoing = outgoing.reshape(experts, capacity, width)
        returned, kept_inputs = expert_forward(
            lax.all_to_all(outgoing, "expert", split_axis=0, concat_axis=0, tiled=True)
        )
        picked = (
            returned.reshape(experts * capacity, width)[slots]
            .reshape(length, top, width)
            .astype(jnp.float32)
        )
        combined = jnp.sum(gates[:, :, None] * picked, axis=1)
        block_out = (middle + combined).astype(jnp.bfloat16)
        upstream_full = upstream.astype(jnp.float32)
        grad_gate = jnp.sum(upstream_full[:, None, :] * picked, axis=2)
        grad_chosen = gates * (grad_gate - jnp.sum(gates * grad_gate, axis=1, keepdims=True))
        route_hits = (routes[:, :, None] == expert_numbers[None, None, :]).astype(jnp.float32)
        grad_logits = jnp.sum(grad_chosen[:, :, None] * route_hits, axis=1).astype(jnp.bfloat16)
        grad_router_now = jnp.dot(normed_mid.T, grad_logits, preferred_element_type=jnp.float32)
        grad_mid = jnp.dot(grad_logits, router_low.T, preferred_element_type=jnp.float32)
        grad_slots = (
            (gates[:, :, None] * upstream_full[:, None, :])
            .astype(jnp.bfloat16)
            .reshape(length * top, width)
        )
        grad_outgoing = (
            jnp.zeros((experts * capacity, width), jnp.bfloat16).at[slots].set(grad_slots)
        )
        grad_outgoing = grad_outgoing.reshape(experts, capacity, width)
        incoming, inputs_back = (
            lax.all_to_all(grad_outgoing, "expert", split_axis=0, concat_axis=0, tiled=True),
            lax.all_to_all(outgoing, "expert", split_axis=0, concat_axis=0, tiled=True),
        )
        grid_in = inputs_back.reshape(expert_count, local_experts, capacity, width)
        grid_grad = incoming.reshape(expert_count, local_experts, capacity, width)
        both = jnp.einsum("sjcd,jdf->sjcf", grid_in, inner_low, preferred_element_type=jnp.float32)
        gate_part = both[..., :hidden_width]
        up_part = both[..., hidden_width:]
        sigma = jax.nn.sigmoid(gate_part)
        activated = jax.nn.silu(gate_part)
        hidden = (activated * up_part).astype(jnp.bfloat16)
        grad_hidden = jnp.einsum(
            "sjcd,jfd->sjcf", grid_grad, down_low, preferred_element_type=jnp.float32
        )
        grad_down_now = jnp.einsum(
            "sjcf,sjcd->jfd", hidden, grid_grad, preferred_element_type=jnp.float32
        )
        grad_both = jnp.concatenate(
            [
                grad_hidden * up_part * sigma * (1.0 + gate_part * (1.0 - sigma)),
                grad_hidden * activated,
            ],
            axis=3,
        ).astype(jnp.bfloat16)
        grad_inner_now = jnp.einsum(
            "sjcd,sjcf->jdf", grid_in, grad_both, preferred_element_type=jnp.float32
        )
        grad_copies = jnp.einsum(
            "sjcf,jdf->sjcd", grad_both, inner_low, preferred_element_type=jnp.float32
        )
        grad_copies = grad_copies.astype(jnp.bfloat16).reshape(experts, capacity, width)
        grad_back = lax.all_to_all(grad_copies, "expert", split_axis=0, concat_axis=0, tiled=True)
        grad_picked = grad_back.reshape(experts * capacity, width)[slots].reshape(
            length, top, width
        )
        grad_mid = grad_mid + jnp.sum(grad_picked.astype(jnp.float32), axis=1)
        grad_unit_second = grad_mid * gain_ffn
        grad_gain_ffn = jnp.sum(grad_mid * unit_second, axis=0)
        grad_middle = upstream_full + inv_second * (
            grad_unit_second
            - unit_second * jnp.mean(grad_unit_second * unit_second, axis=1, keepdims=True)
        )
        grad_branch = grad_middle.astype(jnp.bfloat16)
        grad_proj_now = jnp.dot(attended.T, grad_branch, preferred_element_type=jnp.float32)
        grad_attended = jnp.dot(grad_branch, proj_low.T, preferred_element_type=jnp.float32)
        grad_attended = grad_attended.astype(jnp.bfloat16).reshape(length, HEADS, HEAD)
        probs_again = jnp.exp(masked_scores(query, keys, same_item) - log_total)
        grad_probs = jnp.einsum(
            "qhe,khe->hqk", grad_attended, values, preferred_element_type=jnp.float32
        )
        grad_values = jnp.einsum(
            "hqk,qhe->khe", probs_low, grad_attended, preferred_element_type=jnp.float32
        )
        grad_scores = probs_again * (
            grad_probs - jnp.sum(probs_again * grad_probs, axis=2, keepdims=True)
        )
        grad_scores = grad_scores.astype(jnp.bfloat16)
        grad_query = (
            jnp.einsum("hqk,khe->qhe", grad_scores, keys, preferred_element_type=jnp.float32)
            * 0.125
        )
        grad_keys = (
            jnp.einsum("hqk,qhe->khe", grad_scores, query, preferred_element_type=jnp.float32)
            * 0.125
        )
        grad_mixed = jnp.concatenate(
            [
                rotate(grad_query, cosine, -sine).reshape(length, width),
                rotate(grad_keys, cosine, -sine).reshape(length, width),
                grad_values.reshape(length, width),
            ],
            axis=1,
        ).astype(jnp.bfloat16)
        grad_qkv_now = jnp.dot(normed_in.T, grad_mixed, preferred_element_type=jnp.float32)
        grad_normed = jnp.dot(grad_mixed, qkv_low.T, preferred_element_type=jnp.float32)
        grad_unit_first = grad_normed * gain_attn
        grad_gain_attn = jnp.sum(grad_normed * unit_first, axis=0)
        patch_grad = grad_middle + inv_first * (
            grad_unit_first
            - unit_first * jnp.mean(grad_unit_first * unit_first, axis=1, keepdims=True)
        )
        new_carry = (
            grad_qkv + grad_qkv_now,
            grad_proj + grad_proj_now,
            grad_router + grad_router_now,
            grad_gains + jnp.stack([grad_gain_attn, grad_gain_ffn]),
            grad_inner + grad_inner_now,
            grad_down + grad_down_now,
        )
        return (new_carry, (block_out, patch_grad))

    start = (
        jnp.zeros(qkv_master.shape, jnp.float32),
        jnp.zeros(proj_master.shape, jnp.float32),
        jnp.zeros(router_master.shape, jnp.float32),
        jnp.zeros(gains_master.shape, jnp.float32),
        jnp.zeros(inner_low.shape, jnp.float32),
        jnp.zeros(down_low.shape, jnp.float32),
    )
    totals, outputs = lax.scan(micro_step, start, (patches, out_grad, item_ids, expert_ids))
    grad_qkv, grad_proj, grad_router, grad_gains = lax.psum(
        (totals[0], totals[1], totals[2], totals[3]), ("dp", "expert")
    )
    grad_inner, grad_down = (
        lax.psum_scatter(totals[4], "dp", scatter_dimension=1, tiled=True),
        lax.psum_scatter(totals[5], "dp", scatter_dimension=1, tiled=True),
    )
    qkv_new = adamw(qkv_master, qkv_first, qkv_second, grad_qkv, 0.1, 0.1)
    proj_new = adamw(proj_master, proj_first, proj_second, grad_proj, 0.4, 0.1)
    router_new = adamw(router_master, router_first, router_second, grad_router, 0.07, 0.1)
    gains_new = adamw(gains_master, gains_first, gains_second, grad_gains, 0.4, 0.0)
    inner_new = adamw(inner_master, inner_first, inner_second, grad_inner, 0.1, 0.1)
    down_new = adamw(down_master, down_first, down_second, grad_down, 0.15, 0.1)
    return (
        outputs[0],
        outputs[1],
        qkv_new[0],
        qkv_new[1],
        qkv_new[2],
        proj_new[0],
        proj_new[1],
        proj_new[2],
        router_new[0],
        router_new[1],
        router_new[2],
        gains_new[0],
        gains_new[1],
        gains_new[2],
        inner_new[0],
        inner_new[1],
        inner_new[2],
        down_new[0],
        down_new[1],
        down_new[2],
    )


F32 = jnp.float32
BF16 = jnp.bfloat16
QB = 128


def iota(shape, axis):
    return lax.broadcasted_iota(jnp.int32, shape, axis)


def dot_nn(a, b):
    return jnp.dot(a, b, preferred_element_type=F32)


def dot_nt(a, b):
    return lax.dot_general(a, b, (((1,), (1,)), ((), ())), preferred_element_type=F32)


def dot_tn(a, b):
    return lax.dot_general(a, b, (((0,), (0,)), ((), ())), preferred_element_type=F32)


def swap_halves(v, low_lane):
    width = v.shape[1]
    half = HEAD // 2
    return jnp.where(low_lane, pltpu.roll(v, width - half, 1), pltpu.roll(v, half, 1))


def turn(v, cos_row, sin_row, low_lane):
    return v * cos_row + swap_halves(v, low_lane) * sin_row


def rope_table(item_max):
    half = HEAD // 2
    offset = np.arange(item_max, dtype=np.float32)
    freqs = np.float32(10000.0) ** (-np.arange(half, dtype=np.float32) / np.float32(half))
    angles = (offset[:, None] * freqs[None, :]).astype(np.float32)
    cosine, sine = np.cos(angles), np.sin(angles)
    return np.concatenate([cosine] * 4 + [-sine, sine] * 2, axis=1).astype(np.float32)


def windows(length):
    found = []
    for start in range(0, length, QB):
        low = max(0, start - QB)
        high = min(length, start + 2 * QB)
        found.append((start, low, high))
    return found


def row_norm(values):
    return lax.rsqrt(jnp.mean(values * values, axis=1, keepdims=True) + norm_eps)


def positions(item_row, length):
    eye = iota((length, length), 0) == iota((length, length), 1)
    col = jnp.sum(jnp.where(eye, item_row, 0.0), axis=1, keepdims=True)
    before = jnp.sum(jnp.where(item_row < col, 1.0, 0.0), axis=1, keepdims=True)
    offset = iota((length, 1), 0) - before.astype(jnp.int32)
    return col, offset


def rope_rows(offset, table, length, width):
    spots = table.shape[0]
    pick = jnp.where(iota((length, spots), 1) == offset, 1.0, 0.0)
    both = jnp.dot(pick, table, precision=lax.Precision.HIGHEST, preferred_element_type=F32)
    copies = width // 128
    return (
        jnp.concatenate([both[:, :128]] * copies, axis=1),
        jnp.concatenate([both[:, 128:]] * copies, axis=1),
    )


VMEM_BYTES = 64 * 1024 * 1024 - 512 * 1024


MESH_ID = pl.DeviceIdType.MESH


class Place:
    def __init__(self, line):
        self.line = line
        dp, ex = lax.axis_index("dp"), lax.axis_index("expert")
        self.x, self.core = lax.div(dp, 2), lax.rem(dp, 2)
        self.z, self.y = lax.div(ex, 2), lax.rem(ex, 2)

    def device(self, flip_x=0, flip_y=0, flip_core=0, z=None):
        x = 1 - self.x if flip_x else self.x
        y = 1 - self.y if flip_y else self.y
        core = 1 - self.core if flip_core else self.core
        return (2 * x + core, 2 * (self.z if z is None else z) + y)

    def levels(self):
        found = [(0, self.z, None, 0)]
        for away in range(1, self.line):
            found.append((away, self.z - away, lambda a=away: self.z >= a, -1))
            found.append((away, self.z + away, lambda a=away: self.z + a < self.line, 1))
        return found

    def up(self):
        return self.z + 1 < self.line

    def down(self):
        return self.z > 0

    def by_distance(self, i):
        found = 0
        for z in range(self.line):
            order = sorted(range(self.line), key=lambda level: (abs(level - z), level))
            for place, level in enumerate(order):
                hit = jnp.logical_and(self.z == z, i == place).astype(jnp.int32)
                found = found + hit * level
        return found

    def greet(self):
        barrier = pltpu.get_barrier_semaphore()

        def signal(device):
            pl.semaphore_signal(barrier, inc=1, device_id=device, device_id_type=MESH_ID)

        for device in (self.device(1), self.device(0, 1), self.device(1, 1), self.device(0, 0, 1)):
            signal(device)
        for step in range(1, self.line):
            signal(self.device(z=lax.rem(self.z + step, self.line)))
        pl.semaphore_wait(barrier, self.line + 3)


def both(*tests):
    tests = [t for t in tests if t is not None]

    def all_of():
        found = tests[0]()
        for t in tests[1:]:
            found = jnp.logical_and(found, t())
        return found

    return all_of if tests else None


def only(test, body):
    if test is None:
        body()
    else:
        pl.when(test())(body)


def remote(source, target, departure, arrival, device):
    return pltpu.make_async_remote_copy(
        src_ref=source,
        dst_ref=target,
        send_sem=departure,
        recv_sem=arrival,
        device_id=device,
        device_id_type=MESH_ID,
    )


class Wires:
    def __init__(self, send_sem, like):
        self.send_sem, self.like = send_sem, like
        self.sent = []

    def send(self, source, target, arrival, device, test=None):
        copy = pltpu.make_async_remote_copy(
            src_ref=source,
            dst_ref=target,
            send_sem=self.send_sem.at[len(self.sent)],
            recv_sem=arrival,
            device_id=device,
            device_id_type=MESH_ID,
        )
        only(test, copy.start)
        self.sent.append(test)

    def arrived(self, target, arrival, device, test=None):
        copy = pltpu.make_async_remote_copy(
            src_ref=target,
            dst_ref=target,
            send_sem=self.send_sem.at[0],
            recv_sem=arrival,
            device_id=device,
            device_id_type=MESH_ID,
        )
        only(test, copy.wait_recv)

    def finish(self):
        for number, test in enumerate(self.sent):
            copy = pltpu.make_async_remote_copy(
                src_ref=self.like,
                dst_ref=self.like,
                send_sem=self.send_sem.at[number],
                recv_sem=self.send_sem.at[number],
                device_id=(0, 0),
                device_id_type=MESH_ID,
            )
            only(test, copy.wait_send)


class Gather:
    def __init__(self, place, shard, full, send_sem, recv_sem, copy_sem):
        self.place, self.shard, self.full = place, shard, full
        self.recv_sem, self.copy_sem = recv_sem, copy_sem
        self.wires = Wires(send_sem, shard)

    def at(self, device):
        return self.full.at[device[1], device[0]]

    def ready(self, device):
        return self.recv_sem.at[device[1], device[0]]

    def pass_on(self, origin, to, test=None, source=None):
        source = self.at(origin) if source is None else source
        self.wires.send(source, self.at(origin), self.ready(origin), to, test)

    def wait(self, origin, test=None):
        self.wires.arrived(self.at(origin), self.ready(origin), self.place.device(0, 0, 1), test)

    def start(self):
        place = self.place
        me = place.device()
        self.pass_on(me, place.device(z=place.z + 1), place.up, self.shard)
        self.pass_on(me, place.device(z=place.z - 1), place.down, self.shard)
        self.pass_on(me, place.device(1), None, self.shard)
        self.pass_on(me, place.device(0, 1), None, self.shard)
        self.pass_on(me, place.device(0, 0, 1), None, self.shard)
        self.own = pltpu.make_async_copy(self.shard, self.at(me), self.copy_sem)
        self.own.start()

    def column(self, away):
        place = self.place
        for dist, level, test, way in place.levels():
            if dist != away:
                continue
            origin = place.device(z=level)
            self.wait(origin, test)
            if way < 0:
                self.pass_on(origin, place.device(z=place.z + 1), both(test, place.up))
            if way > 0:
                self.pass_on(origin, place.device(z=place.z - 1), both(test, place.down))
            self.pass_on(origin, place.device(1), test)
            self.pass_on(origin, place.device(0, 1), test)
            self.pass_on(origin, place.device(0, 0, 1), test)

    def square(self, away):
        place = self.place
        for dist, level, test, way in place.levels():
            if dist != away:
                continue
            over_x, over_y = place.device(1, z=level), place.device(0, 1, z=level)
            self.wait(over_x, test)
            if dist % 2 == 0:
                self.pass_on(over_x, place.device(0, 1), test)
            self.pass_on(over_x, place.device(0, 0, 1), test)
            self.wait(over_y, test)
            if dist % 2 == 1:
                self.pass_on(over_y, place.device(1), test)
            self.pass_on(over_y, place.device(0, 0, 1), test)

    def corner(self, away):
        place = self.place
        for dist, level, test, way in place.levels():
            if dist != away:
                continue
            across = place.device(1, 1, z=level)
            self.wait(across, test)
            self.pass_on(across, place.device(0, 0, 1), test)

    def partner(self, flip_x, flip_y, level):
        self.wait(self.place.device(flip_x, flip_y, 1, z=level))


OWN, OVER_X, OVER_Y, ACROSS = 0, 1, 2, 3
EARLY = 2


class Close:
    def __init__(self, place, kept, owns, sides, diag_in, side_in, line_in, load_sem, sems):
        self.place, self.kept, self.owns, self.sides = place, kept, owns, sides
        self.diag_in, self.side_in, self.line_in, self.load_sem = diag_in, side_in, line_in, load_sem
        self.diag_send, self.diag_sem, self.side_send, self.side_sem, self.line_send, self.line_sem = sems

    def level(self, slot):
        return self.place.by_distance(self.place.line - 1 - slot)

    def load(self, which, slot):
        target = self.owns if which == 0 else self.sides
        return pltpu.make_async_copy(
            self.kept.at[which, self.level(slot)], target.at[slot], self.load_sem.at[which, slot]
        )

    def across(self, slot):
        level = self.level(slot)
        return remote(
            self.kept.at[2, level], self.diag_in.at[slot], self.diag_send.at[slot], self.diag_sem.at[slot],
            self.place.device(1),
        )

    def aside(self, slot):
        level = self.level(slot)
        source = self.kept.at[1, level] if slot < EARLY else self.sides.at[slot]
        return remote(
            source, self.side_in.at[slot], self.side_send.at[slot], self.side_sem.at[slot],
            self.place.device(1) if slot == 0 else self.place.device(0, 1),
        )

    def along(self, slot):
        return remote(
            self.owns.at[slot], self.line_in.at[self.place.z], self.line_send.at[slot],
            self.line_sem.at[self.place.z], self.place.device(z=self.level(slot)),
        )

    def start(self):
        for slot in range(self.place.line):
            (self.aside(slot) if slot < EARLY else self.across(slot)).start()
            self.load(0, slot).start()
            if slot >= EARLY:
                self.load(1, slot).start()

    def send_side(self, slot):
        self.load(1, slot).wait()
        self.across(slot).wait_recv()
        self.sides[slot] = (self.sides[slot].astype(F32) + self.diag_in[slot].astype(F32)).astype(BF16)
        self.aside(slot).start()

    def collect(self, slot):
        self.load(0, slot).wait()
        self.aside(slot).wait_recv()
        return self.owns[slot].astype(F32) + self.side_in[slot].astype(F32)

    def send_line(self, slot):
        self.owns[slot] = self.collect(slot).astype(BF16)
        self.along(slot).start()

    def finish(self, out):
        place = self.place
        last = place.line - 1
        out[...] = self.collect(last)
        for step in range(1, place.line):
            z = lax.rem(place.z + step, place.line)
            remote(
                self.owns.at[0], self.line_in.at[z], self.line_send.at[0], self.line_sem.at[z],
                place.device(z=z),
            ).wait_recv()
            out[...] += self.line_in[z].astype(F32)
        for slot in range(place.line):
            self.aside(slot).wait_send()
            if slot >= EARLY:
                self.across(slot).wait_send()
            if slot < last:
                self.along(slot).wait_send()


class Small:
    def __init__(self, place, rows, part, low, out, sums, core_in, square_in, line_in, sems):
        self.place, self.rows = place, rows
        self.part, self.low, self.out = part, low, out
        self.sums, self.core_in, self.square_in, self.line_in = sums, core_in, square_in, line_in
        (
            self.core_send, self.core_sem, self.square_send, self.square_sem, self.line_send, self.line_sem,
            self.up_send, self.up_sem, self.back_send, self.back_sem, self.last_send, self.last_sem,
        ) = sems

    def lane(self, group, flip_core=0):
        place = self.place
        x = 1 - place.x if group in (OVER_X, ACROSS) else place.x
        y = 1 - place.y if group in (OVER_Y, ACROSS) else place.y
        core = 1 - place.core if flip_core else place.core
        return y, 2 * x + core

    def to(self, group):
        return self.place.device(int(group in (OVER_X, ACROSS)), int(group in (OVER_Y, ACROSS)))

    def core(self, group):
        y, d = self.lane(group, 1)
        return remote(
            self.part.at[y, d, :, self.rows], self.core_in.at[group, :, self.rows], self.core_send.at[group], self.core_sem.at[group],
            self.place.device(0, 0, 1),
        )

    def over(self, group):
        return remote(
            self.sums.at[group, :, self.rows], self.square_in.at[group - 1, :, self.rows], self.square_send.at[group - 1],
            self.square_sem.at[group - 1], self.to(group),
        )

    def along(self, z):
        return remote(
            self.sums.at[OWN, z, self.rows], self.line_in.at[self.place.z, self.rows], self.line_send.at[z],
            self.line_sem.at[self.place.z], self.place.device(z=z),
        )

    def landed(self, z):
        return remote(
            self.sums.at[OWN, z, self.rows], self.line_in.at[z, self.rows], self.line_send.at[z], self.line_sem.at[z],
            self.place.device(z=z),
        )

    def up(self, z):
        y, d = self.lane(OWN)
        return remote(
            self.low.at[self.rows], self.out.at[y, d, self.place.z, self.rows], self.up_send.at[z], self.up_sem.at[self.place.z],
            self.place.device(z=z),
        )

    def risen(self, z):
        y, d = self.lane(OWN)
        return remote(
            self.low.at[self.rows], self.out.at[y, d, z, self.rows], self.up_send.at[z], self.up_sem.at[z],
            self.place.device(z=z),
        )

    def back(self, group):
        y, d = self.lane(OWN)
        return remote(
            self.out.at[y, d, :, self.rows], self.out.at[y, d, :, self.rows], self.back_send.at[group - 1], self.back_sem.at[group - 1],
            self.to(group),
        )

    def last(self, group):
        y, d = self.lane(group)
        return remote(
            self.out.at[y, d, :, self.rows], self.out.at[y, d, :, self.rows], self.last_send.at[group], self.last_sem.at[group],
            self.place.device(0, 0, 1),
        )

    def others(self):
        return [lax.rem(self.place.z + step, self.place.line) for step in range(1, self.place.line)]

    def start(self):
        for group in (ACROSS, OVER_X, OVER_Y, OWN):
            self.core(group).start()

    def stages(self):
        place, rows = self.place, self.rows
        for group in (ACROSS, OVER_X, OVER_Y, OWN):
            self.core(group).wait_recv()
            y, d = self.lane(group)
            total = self.part[y, d, :, rows].astype(F32) + self.core_in[group, :, rows].astype(F32)
            self.sums[group, :, rows] = total.astype(BF16)
            if group != OWN:
                self.over(group).start()
        yield
        total = self.sums[OWN, :, rows].astype(F32)
        for group in (OVER_X, OVER_Y, ACROSS):
            self.over(group).wait_recv()
            total = total + self.square_in[group - 1, :, rows].astype(F32)
        self.sums[OWN, :, rows] = total.astype(BF16)
        for z in self.others():
            self.along(z).start()
        yield
        total = self.sums[OWN, place.z, rows].astype(F32)
        for z in self.others():
            self.landed(z).wait_recv()
            total = total + self.line_in[z, rows].astype(F32)
        self.low[rows] = total.astype(BF16)
        for z in self.others():
            self.up(z).start()
        y, d = self.lane(OWN)
        self.out[y, d, place.z, rows] = total.astype(BF16)
        yield
        for z in self.others():
            self.risen(z).wait_recv()
        for group in (ACROSS, OVER_X, OVER_Y):
            self.back(group).start()
        self.last(OWN).start()
        yield
        for group in (OVER_X, OVER_Y, ACROSS):
            self.back(group).wait_recv()
            self.last(group).start()
        yield
        for group in (OWN, OVER_X, OVER_Y, ACROSS):
            self.last(group).wait_recv()
        yield

    def finish(self):
        for group in (OWN, OVER_X, OVER_Y, ACROSS):
            self.core(group).wait_send()
            self.last(group).wait_send()
            if group != OWN:
                self.over(group).wait_send()
                self.back(group).wait_send()
        for z in self.others():
            self.along(z).wait_send()
            self.up(z).wait_send()


def copy_all(copies):
    for copy in copies:
        copy.start()


def attend_pack(p, patches, items, gains, table, qkv_s, proj_s, mixed_s, probs_s, att_s, mid_s, nm_s):
    _, length, width = patches.shape
    pairs = width // 128
    slot = lax.rem(p, mixed_s.shape[0])
    low_lane = iota((1, width), 1) % HEAD < HEAD // 2
    first_head = iota((1, 128), 1) < HEAD
    mask_a = jnp.where(first_head, 1.0, 0.0).astype(BF16)
    mask_b = jnp.where(first_head, 0.0, 1.0).astype(BF16)
    top_rows = iota((128, 1), 0) < HEAD
    source = patches[p].astype(F32)
    normed = (source * row_norm(source) * gains[0:1, :]).astype(BF16)
    mixed = dot_nn(normed, qkv_s[...])
    item_row = items[p].astype(F32)
    item_col, offset = positions(item_row, length)
    cos_row, sin_row = rope_rows(offset, table[...], length, width)
    mixed_s[slot, :, :width] = turn(mixed[:, :width], cos_row, sin_row, low_lane).astype(BF16)
    mixed_s[slot, :, width : 2 * width] = turn(
        mixed[:, width : 2 * width], cos_row, sin_row, low_lane
    ).astype(BF16)
    mixed_s[slot, :, 2 * width :] = mixed[:, 2 * width :].astype(BF16)
    for pair in range(pairs):
        lanes = slice(128 * pair, 128 * pair + 128)
        key_lanes = slice(width + 128 * pair, width + 128 * pair + 128)
        values_t = mixed[:, 2 * width + 128 * pair : 2 * width + 128 * pair + 128].T.astype(BF16)
        for block, (start, low, high) in enumerate(windows(length)):
            query = mixed_s[slot, start : start + QB, lanes] * 0.125
            query = jnp.concatenate([query * mask_a, query * mask_b], axis=0)
            scores = dot_nt(mixed_s[slot, low:high, key_lanes], query)
            here = item_row[:, start : start + QB]
            same = item_col[low:high] == jnp.concatenate([here, here], axis=1)
            scores = jnp.where(same, scores, -1e30)
            peak = jnp.max(scores, axis=0, keepdims=True)
            weights = jnp.exp(scores - peak)
            total = jnp.sum(weights, axis=0, keepdims=True)
            probs = (weights * (1.0 / total)).astype(BF16)
            probs_s[slot, pair, block, : high - low] = probs
            out = dot_nn(values_t[:, low:high], probs)
            out = jnp.where(top_rows, out[:, :QB], out[:, QB:])
            att_s[p, start : start + QB, lanes] = out.T.astype(BF16)
    middle = source + dot_nn(att_s[p], proj_s[...])
    mid_s[p] = middle
    nm_s[p] = (middle * row_norm(middle) * gains[1:2, :]).astype(BF16)


class Experts:
    def __init__(self, refs, cap):
        (
            self.nm, self.upstream, self.rank_s, self.gate_s, self.gg_s, self.x_s, self.hid_s, self.go_s,
            self.gb_s, self.y_s, self.inner_w, self.down_w,
        ) = refs
        self.cap = cap

    def prepare(self, p, ids, router_w):
        nm = self.nm
        _, length, width = nm.shape
        experts = router_w.shape[0]
        earlier = jnp.where(iota((length, length), 0) < iota((length, length), 1), 1.0, 0.0).astype(BF16)
        logits = dot_nt(router_w[...], nm[p])
        number = iota((experts, length), 0)
        hit0 = number == ids[p, 0:1, :]
        hit1 = number == ids[p, 1:2, :]
        chosen0 = jnp.sum(jnp.where(hit0, logits, 0.0), axis=0, keepdims=True)
        chosen1 = jnp.sum(jnp.where(hit1, logits, 0.0), axis=0, keepdims=True)
        peak = jnp.maximum(chosen0, chosen1)
        e0 = jnp.exp(chosen0 - peak)
        e1 = jnp.exp(chosen1 - peak)
        total = e0 + e1
        self.gate_s[p] = jnp.where(hit0, e0 / total, 0.0) + jnp.where(hit1, e1 / total, 0.0)
        named = jnp.where(hit0, 1.0, jnp.where(hit1, 1.0, 0.0))
        rank = dot_nn(named.astype(BF16), earlier)
        self.rank_s[p] = jnp.where(named > 0.5, rank, -1.0)

    def rows(self, p, expert):
        cap = self.cap
        _, length, width = self.nm.shape
        hidden_width = self.hid_s.shape[1]
        here = pl.ds(pl.multiple_of(p * cap, cap), cap)
        rank = self.rank_s[p, pl.ds(expert, 1), :]
        gate_row = self.gate_s[p, pl.ds(expert, 1), :]
        pick = iota((cap, length), 0).astype(F32) == rank
        chosen = jnp.where(pick, 1.0, 0.0).astype(BF16)
        taken = dot_nn(chosen, jnp.concatenate([self.nm[p], self.upstream[p]], axis=1))
        gate_col = jnp.sum(jnp.where(pick, gate_row, 0.0), axis=1, keepdims=True)
        x = taken[:, :width].astype(BF16)
        g = taken[:, width:]
        self.x_s[here, :] = x
        grad_out = (gate_col * g).astype(BF16)
        self.go_s[here, :] = grad_out
        gate = dot_nn(x, self.inner_w[:, :hidden_width])
        up = dot_nn(x, self.inner_w[:, hidden_width:])
        sigma = 1.0 / (1.0 + jnp.exp(-gate))
        active = gate * sigma
        hidden = (active * up).astype(BF16)
        self.hid_s[here, :] = hidden
        result = dot_nn(hidden, self.down_w[...]).astype(BF16).astype(F32)
        spot = pl.ds(pl.multiple_of(expert * cap, cap), cap)
        self.y_s[p, spot, :width] = (gate_col * result).astype(BF16)
        grad_gate = jnp.sum(g * result, axis=1, keepdims=True)
        self.gg_s[p, pl.ds(expert, 1), :] = jnp.sum(
            jnp.where(pick, grad_gate, 0.0), axis=0, keepdims=True
        )
        grad_hidden = dot_nt(grad_out, self.down_w[...])
        self.gb_s[here, :hidden_width] = (
            grad_hidden * up * sigma * (1.0 + gate * (1.0 - sigma))
        ).astype(BF16)
        self.gb_s[here, hidden_width:] = (grad_hidden * active).astype(BF16)
        self.y_s[p, spot, width:] = dot_nt(self.gb_s[here, :], self.inner_w[...]).astype(BF16)

    def grads(self, part):
        copies, _, width = part.shape
        hidden_width = self.hid_s.shape[1]
        deep, span = width // copies, hidden_width // copies
        for block in range(2 * hidden_width // width):
            lanes = slice(block * width, block * width + width)
            grad = dot_tn(self.x_s[...], self.gb_s[:, lanes]).astype(BF16)
            for d in range(copies):
                part[d, block * deep : block * deep + deep, :] = grad[d * deep : d * deep + deep]
        grad = dot_tn(self.hid_s[...], self.go_s[...]).astype(BF16)
        for d in range(copies):
            part[d, width:, :] = grad[d * span : d * span + span]

    def finish(self, p, router_w, mid, block_o, gmid_o, glog_o):
        cap = self.cap
        _, length, width = self.nm.shape
        experts = router_w.shape[0]
        ranks = self.rank_s[p].T
        slot = iota((length, cap), 1).astype(F32)
        pieces = [
            jnp.where(ranks[:, e : e + 1] == slot, 1.0, 0.0).astype(BF16) for e in range(experts)
        ]
        back = dot_nn(jnp.concatenate(pieces, axis=1), self.y_s[p])
        gate = self.gate_s[p]
        grad_gate = self.gg_s[p]
        mean = jnp.sum(gate * grad_gate, axis=0, keepdims=True)
        hit = self.rank_s[p] > -0.5
        grad_logits = jnp.where(hit, gate * (grad_gate - mean), 0.0).astype(BF16)
        glog_o[p] = grad_logits
        block_o[p] = (mid[p] + back[:, :width]).astype(BF16)
        gmid_o[p] = back[:, width:] + dot_tn(grad_logits, router_w[...])


def unpack(weights, inner_w, down_w):
    copies, _, width = weights.shape
    deep, span = width // copies, down_w.shape[0] // copies
    for d in range(copies):
        for block in range(inner_w.shape[1] // width):
            inner_w[d * deep : d * deep + deep, block * width : block * width + width] = weights[
                d, block * deep : block * deep + deep, :
            ]
        down_w[d * span : d * span + span, :] = weights[d, width:, :]


def forward_kernel(
    line, cap,
    shard, patches, upstream, items, ids, qkv_w, proj_w, router_w, gains, table,
    full, kept_o, mixed_o, probs_o, att_o, mid_o, nm_o, block_o, gmid_o, glog_o,
    qkv_s, proj_s, mixed_s, probs_s, att_s, mid_s, nm_s, wbuf, pbuf,
    rank_s, gate_s, gg_s, x_s, hid_s, go_s, gb_s, y_s, inner_s, down_s, block_s, gmid_s,
    sums, core_in, diag_in, side_in,
    send_sem, recv_sem, own_sem, save_sem, fetch_sem, keep_sem,
    core_send, core_sem, diag_send, diag_sem, side_send, side_sem, credit_sem,
):
    packs = patches.shape[0]
    experts = router_w.shape[0]
    place = Place(line)
    place.greet()
    gather = Gather(place, shard, full, send_sem, recv_sem, own_sem)
    gather.start()
    qkv_s[...] = qkv_w[...].astype(BF16)
    proj_s[...] = proj_w[...].astype(BF16)
    work = Experts(
        (nm_s, upstream, rank_s, gate_s, gg_s, x_s, hid_s, go_s, gb_s, y_s, inner_s, down_s), cap
    )
    saves = ((mixed_s, mixed_o), (probs_s, probs_o), (att_s, att_o), (mid_s, mid_o), (nm_s, nm_o))
    results = ((block_s, block_o), (gmid_s, gmid_o))

    def save(n, p):
        source, target = saves[n]
        return pltpu.make_async_copy(
            source.at[lax.rem(p, source.shape[0])], target.at[p], save_sem.at[n, p]
        )

    def result(n, p):
        return pltpu.make_async_copy(results[n][0].at[p], results[n][1].at[p], save_sem.at[len(saves) + n, p])

    def pack(p, carry):
        def reuse():
            save(0, p - 2).wait()
            save(1, p - 2).wait()

        pl.when(p >= 2)(reuse)
        attend_pack(p, patches, items, gains, table, qkv_s, proj_s, mixed_s, probs_s, att_s, mid_s, nm_s)
        for n in range(len(saves)):
            save(n, p).start()
        work.prepare(p, ids, router_w)
        for k in range(1, line - 1):

            def relay(k=k):
                gather.column(k)
                if k == 1:
                    gather.square(0)

            pl.when(p == min(k - 1, packs - 1))(relay)
        return carry

    lax.fori_loop(0, packs, pack, 0)

    def near(i):
        return int(i < line) if isinstance(i, int) else (i < line).astype(jnp.int32)

    def number(i):
        level = place.by_distance(near(i) * i + (1 - near(i)) * (2 * line - 1 - i))
        side = near(i) * place.y + (1 - near(i)) * (1 - place.y)
        return level, 2 * level + side

    def fetch(i):
        return pltpu.make_async_copy(full.at[number(i)[1]], wbuf.at[lax.rem(i, 2)], fetch_sem.at[lax.rem(i, 2)])

    def arrive(i):
        level = number(i)[0]

        def close():
            gather.partner(0, 0, level)
            gather.partner(1, 0, level)

        def far():
            gather.partner(0, 1, level)
            gather.partner(1, 1, level)

        if isinstance(i, int):
            (close if i < line else far)()
        else:
            pl.when(i < line)(close)
            pl.when(i >= line)(far)

    def piece(q, flip_core):
        return place.device(q, 0, flip_core)[0]

    def swap(i, q):
        slot = lax.rem(i, 2)
        return remote(
            pbuf.at[slot, piece(q, 1)], core_in.at[slot, q], core_send.at[slot, q], core_sem.at[slot, q],
            place.device(0, 0, 1),
        )

    def across(n):
        level = number(line + n)[0]
        return remote(
            sums.at[ACROSS, level], diag_in.at[n], diag_send.at[n], diag_sem.at[n],
            place.device(0, 1) if n == 0 else place.device(1),
        )

    def aside(level, group=OVER_X):
        return remote(
            sums.at[group, level], side_in.at[level], side_send.at[level], side_sem.at[level],
            place.device(1) if group == OVER_X else place.device(0, 1),
        )

    def keep(which, group, level):
        return pltpu.make_async_copy(sums.at[group, level], kept_o.at[which, level], keep_sem.at[which, level])

    def merge(i):
        slot = lax.rem(i, 2)
        level = number(i)[0]
        group = 2 * (1 - near(i))
        for q in range(2):
            swap(i, q).wait_recv()
            total = pbuf[slot, piece(q, 0)].astype(F32) + core_in[slot, q].astype(F32)
            sums[group + q, level] = total.astype(BF16)
        pl.semaphore_signal(credit_sem, inc=1, device_id=place.device(0, 0, 1), device_id_type=MESH_ID)
        pl.when(jnp.logical_and(i >= 2, i < line - 1))(lambda: aside(level).start())

        def early(n):
            across(n).start()
            if n == 0:
                aside(level, OVER_Y).start()

        for n in range(EARLY):
            pl.when(i == line + n)(lambda n=n: early(n))

        def put_away():
            keep(1, OVER_Y, level).start()
            keep(2, ACROSS, level).start()

        pl.when(i >= line + EARLY)(put_away)

    gather.own.wait()
    arrive(0)
    fetch(0).start()

    def last_square():
        gather.square(line - 1)
        for i in range(2):
            aside(number(i)[0]).start()

    def two_corners():
        gather.corner(0)
        gather.corner(1)

    def third():
        gather.column(line - 1)
        gather.square(1)

    events = (
        (0, 0, third),
        (1, 1, lambda: gather.square(line - 2)),
        (2, 1, last_square),
        (3, 0, two_corners),
        (3, 1, lambda: gather.corner(line - 2)),
        (3, packs - 1, lambda: gather.corner(line - 1)),
    )

    def one(i, carry):
        fetch(i).wait()
        unpack(wbuf.at[lax.rem(i, 2)], inner_s, down_s)
        expert = number(i)[1]

        def rows(p, inner_carry):
            work.rows(p, expert)
            pl.when(jnp.logical_and(p == 0, i >= 1))(lambda: merge(i - 1))
            for slot, turn_at, event in events:
                pl.when(jnp.logical_and(i == slot, p == turn_at))(event)
            return inner_carry

        lax.fori_loop(0, packs, rows, 0)

        def ahead():
            arrive(i + 1)
            fetch(i + 1).start()

        pl.when(i + 1 < experts)(ahead)

        def free():
            pl.semaphore_wait(credit_sem, 1)
            for q in range(2):
                swap(i, q).wait_send()

        pl.when(i >= 2)(free)
        work.grads(pbuf.at[lax.rem(i, 2)])
        for q in range(2):
            swap(i, q).start()
        return carry

    lax.fori_loop(0, experts, one, 0)

    def last(i, carry):
        merge(i)
        return carry

    lax.fori_loop(experts - 1, experts, last, 0)

    def finish(p, carry):
        work.finish(p, router_w, mid_s, block_s, gmid_s, glog_o)
        for n in range(len(results)):
            result(n, p).start()
        return carry

    lax.fori_loop(0, packs, finish, 0)

    def settle(level, carry):
        aside(level).wait_recv()
        sums[OWN, level] = (sums[OWN, level].astype(F32) + side_in[level].astype(F32)).astype(BF16)
        keep(0, OWN, level).start()
        return carry

    lax.fori_loop(0, line, settle, 0)
    for n in range(EARLY):
        level = number(line + n)[0]
        across(n).wait_recv()
        group = OVER_X if n == 0 else OVER_Y
        sums[group, level] = (sums[group, level].astype(F32) + diag_in[n].astype(F32)).astype(BF16)
        keep(1, group, level).start()
        across(n).wait_send()

    def drain(level, carry):
        keep(0, OWN, level).wait()
        keep(1, OVER_Y, level).wait()
        aside(level).wait_send()
        return carry

    lax.fori_loop(0, line, drain, 0)
    for n in range(EARLY, line):
        keep(2, ACROSS, number(line + n)[0]).wait()
    pl.semaphore_wait(credit_sem, 2)
    for i in range(experts - 2, experts):
        for q in range(2):
            swap(i, q).wait_send()
    for n in range(len(saves)):
        for p in range(packs - 2 if n < 2 else 0, packs):
            save(n, p).wait()
    for n in range(len(results)):
        for p in range(packs):
            result(n, p).wait()
    gather.wires.finish()


def run_forward(shard, patches, upstream, items, ids, qkv_w, proj_w, router_w, gains, table, hidden, slot):
    packs, length, width = patches.shape
    experts = router_w.shape[0]
    dp, ex = lax.axis_size("dp"), lax.axis_size("expert")
    line = ex // 2
    cap = 2 * length * ids.shape[1] // experts
    pairs, blocks = width // 128, length // QB
    rows = shard.shape[0]
    dma = pltpu.SemaphoreType.DMA
    here = pl.BlockSpec(memory_space=pltpu.VMEM)
    away = pl.BlockSpec(memory_space=pl.ANY)
    saved = (
        ((packs, length, 3 * width), BF16),
        ((packs, pairs, blocks, 3 * QB, 2 * QB), BF16),
        ((packs, length, width), BF16),
        ((packs, length, width), F32),
        ((packs, length, width), BF16),
    )
    shapes = (
        ((ex, dp, rows, width), BF16),
        ((3, line, rows, width), BF16),
        *saved,
        ((packs, length, width), BF16),
        ((packs, length, width), F32),
        ((packs, experts, length), BF16),
    )
    scratch = (
        ((width, 3 * width), BF16),
        ((width, width), BF16),
        ((2, length, 3 * width), BF16),
        ((2, pairs, blocks, 3 * QB, 2 * QB), BF16),
        *saved[2:],
        ((2, dp, rows, width), BF16),
        ((2, dp, rows, width), BF16),
        ((packs, experts, length), F32),
        ((packs, experts, length), F32),
        ((packs, experts, length), F32),
        ((packs * cap, width), BF16),
        ((packs * cap, hidden), BF16),
        ((packs * cap, width), BF16),
        ((packs * cap, 2 * hidden), BF16),
        ((packs, experts * cap, 2 * width), BF16),
        ((width, 2 * hidden), BF16),
        ((hidden, width), BF16),
        ((packs, length, width), BF16),
        ((packs, length, width), F32),
        ((4, line, rows, width), BF16),
        ((2, 2, rows, width), BF16),
        ((EARLY, rows, width), BF16),
        ((line, rows, width), BF16),
    )
    return pl.pallas_call(
        functools.partial(forward_kernel, line, cap),
        out_shape=tuple(jax.ShapeDtypeStruct(*s) for s in shapes),
        in_specs=[here] * 10,
        out_specs=(away,) * 9 + (here,),
        scratch_shapes=[pltpu.VMEM(*s) for s in scratch]
        + [dma((24 * line,)), dma((ex, dp)), dma, dma((7, packs)), dma((2,)), dma((3, line))]
        + [dma((2, 2))] * 2 + [dma((EARLY,))] * 2 + [dma((line,))] * 2 + [pltpu.SemaphoreType.REGULAR],
        compiler_params=pltpu.CompilerParams(
            collective_id=slot, has_side_effects=True, vmem_limit_bytes=VMEM_BYTES
        ),
        name="forward",
    )(shard, patches, upstream, items, ids, qkv_w, proj_w, router_w, gains, table)


class Backward:
    def __init__(self, refs):
        (
            self.patches, self.upstream, self.items, self.gains, self.table, self.gmid, self.glog,
            self.qkv_s, self.proj_s, self.mixed, self.probs, self.mid, self.nm,
            self.patch_o, self.normed_s, self.branch_s, self.datt_s, self.dmix_s, self.dkv_s, self.small_g,
        ) = refs

    def pack(self, p, midway):
        packs, length, width = self.patch_o.shape
        pairs = width // 128
        experts = self.glog.shape[1]
        gains, mixed, dkv_s = self.gains, self.mixed, self.dkv_s
        low_lane = iota((1, width), 1) % HEAD < HEAD // 2
        first_head = iota((1, 128), 1) < HEAD
        mask_a = jnp.where(first_head, 1.0, 0.0).astype(BF16)
        mask_b = jnp.where(first_head, 0.0, 1.0).astype(BF16)
        top_rows = iota((128, 1), 0) < HEAD
        rows = pl.ds(pl.multiple_of(p * length, length), length)
        slot = lax.rem(p, 2)
        source = self.patches[slot].astype(F32)
        gain0, gain1 = gains[0:1, :], gains[1:2, :]
        middle = self.mid[slot]
        inv = row_norm(middle)
        unit = middle * inv
        grad_mid = self.gmid[slot]
        self.small_g[experts + 1 : experts + 2, :] += jnp.sum(grad_mid * unit, axis=0, keepdims=True)
        self.small_g[0:experts, :] += dot_nn(self.glog[p], self.nm[slot])
        grad_unit = grad_mid * gain1
        grad_middle = self.upstream[slot].astype(F32) + inv * (
            grad_unit - unit * jnp.mean(grad_unit * unit, axis=1, keepdims=True)
        )
        self.patch_o[p] = grad_middle
        branch = grad_middle.astype(BF16)
        self.branch_s[rows, :] = branch
        self.datt_s[...] = dot_nt(branch, self.proj_s[...]).astype(BF16)
        dkv_s[...] = jnp.zeros(dkv_s.shape, F32)
        item_row = self.items[p].astype(F32)
        item_col, offset = positions(item_row, length)
        cos_row, sin_row = rope_rows(offset, self.table[...], length, width)
        for pair in range(pairs):
            if pair == 2:
                midway()
            lanes = slice(128 * pair, 128 * pair + 128)
            key_lanes = slice(width + 128 * pair, width + 128 * pair + 128)
            value_lanes = slice(2 * width + 128 * pair, 2 * width + 128 * pair + 128)
            keys_t = mixed[slot, :, key_lanes].astype(F32).T.astype(BF16)
            for block, (start, low, high) in enumerate(windows(length)):
                query = mixed[slot, start : start + QB, lanes] * 0.125
                query = jnp.concatenate([query * mask_a, query * mask_b], axis=0)
                datt = self.datt_s[start : start + QB, lanes]
                datt = jnp.concatenate([datt * mask_a, datt * mask_b], axis=0)
                prob = self.probs[slot, pair, block, : high - low]
                dprob = dot_nt(mixed[slot, low:high, value_lanes], datt)
                weight = prob.astype(F32)
                mean = jnp.sum(weight * dprob, axis=0, keepdims=True)
                dscore = (weight * (dprob - mean)).astype(BF16)
                dkv_s[low:high, key_lanes] += dot_nn(dscore, query)
                dkv_s[low:high, value_lanes] += dot_nn(prob, datt)
                dquery = dot_nn(keys_t[:, low:high], dscore)
                dquery = jnp.where(top_rows, dquery[:, :QB], dquery[:, QB:])
                dkv_s[start : start + QB, lanes] = dquery.T * 0.125
        dmix_s = self.dmix_s
        dmix_s[rows, :width] = turn(dkv_s[:, :width], cos_row, -sin_row, low_lane).astype(BF16)
        dmix_s[rows, width : 2 * width] = turn(
            dkv_s[:, width : 2 * width], cos_row, -sin_row, low_lane
        ).astype(BF16)
        dmix_s[rows, 2 * width :] = dkv_s[:, 2 * width :].astype(BF16)
        grad_normed = dot_nt(dmix_s[rows, :], self.qkv_s[...])
        inv_in = row_norm(source)
        unit_in = source * inv_in
        self.normed_s[rows, :] = (unit_in * gain0).astype(BF16)
        self.small_g[experts : experts + 1, :] += jnp.sum(grad_normed * unit_in, axis=0, keepdims=True)
        grad_unit_in = grad_normed * gain0
        self.patch_o[p] += inv_in * (
            grad_unit_in - unit_in * jnp.mean(grad_unit_in * unit_in, axis=1, keepdims=True)
        )

    def tail(self, att, tail):
        packs, length, width = self.patch_o.shape
        tail[...] = jnp.zeros(tail.shape, BF16)
        for block in range(4):
            if block < 3:
                grad = dot_tn(self.normed_s[...], self.dmix_s[:, block * width : block * width + width])
            else:
                flat = jnp.concatenate([att[p] for p in range(packs)], axis=0)
                grad = dot_tn(flat, self.branch_s[...])
            lay_tail(tail, block, grad.astype(BF16))
        tail[0, 0, 0, tail.shape[3] - 16 :, :] = self.small_g[...].astype(BF16)


def tail_rows(width, devices):
    return 4 * width // devices + 16


def lay_tail(tail, block, grad):
    _, dp, line, rows, width = tail.shape
    rows = rows - 16
    each = width // rows
    for piece in range(each):
        number = block * each + piece
        spot = (number // (dp * line), number // line % dp, number % line)
        tail[(*spot, slice(0, rows), slice(None))] = grad[piece * rows : piece * rows + rows]


def backward_kernel(
    line,
    kept, patches_i, upstream_i, items, qkv_w, proj_w, gains, table, gmid_i, glog, mixed_i, probs_i, att_i, mid_i, nm_i,
    patch_o, grad_o, tail_o,
    qkv_s, proj_s, mixed, probs, att, mid, nm, patches, upstream, gmid,
    normed_s, branch_s, datt_s, dmix_s, dkv_s, small_g, tail, tail_low,
    owns, sides, diag_in, side_in, line_in,
    tsums, tcore_in, tsquare_in, tline_in,
    load_sem, own_sem, diag_send, diag_sem, side_send, side_sem, line_send, line_sem,
    *small_sems,
):
    packs = patch_o.shape[0]
    place = Place(line)
    place.greet()
    reduce = Close(
        place, kept, owns, sides, diag_in, side_in, line_in, own_sem,
        (diag_send, diag_sem, side_send, side_sem, line_send, line_sem),
    )
    half = tail_low.shape[0] // 2
    smalls = [
        Small(
            place, pl.ds(n * half, half), tail, tail_low, tail_o, tsums, tcore_in, tsquare_in, tline_in,
            small_sems[12 * n : 12 * n + 12],
        )
        for n in range(2)
    ]
    reduce.start()
    loads = (
        (gmid_i, gmid), (mid_i, mid), (nm_i, nm), (upstream_i, upstream), (patches_i, patches),
        (mixed_i, mixed), (probs_i, probs), (att_i, att),
    )

    def load(n, p):
        source, target = loads[n]
        return pltpu.make_async_copy(
            source.at[p], target.at[lax.rem(p, target.shape[0])], load_sem.at[n, p]
        )

    for p in range(packs):
        for n in range(len(loads)):
            if p < loads[n][1].shape[0]:
                load(n, p).start()
    qkv_s[...] = qkv_w[...].astype(BF16)
    proj_s[...] = proj_w[...].astype(BF16)
    small_g[...] = jnp.zeros(small_g.shape, F32)
    work = Backward((
        patches, upstream, items, gains, table, gmid, glog,
        qkv_s, proj_s, mixed, probs, mid, nm,
        patch_o, normed_s, branch_s, datt_s, dmix_s, dkv_s, small_g,
    ))
    def pack(p, carry):
        for n in range(len(loads)):
            load(n, p).wait()

        def midway():
            pl.when(p == 1)(lambda: reduce.send_side(2))

            def later():
                reduce.send_side(3)
                reduce.send_line(2)

            pl.when(p == packs - 1)(later)

        work.pack(p, midway)

        def ahead():
            for n in range(len(loads) - 1):
                load(n, p + 2).start()

        pl.when(p + 2 < packs)(ahead)

        def first():
            reduce.send_line(0)
            reduce.send_line(1)

        pl.when(p == 0)(first)
        return carry

    lax.fori_loop(0, packs, pack, 0)
    work.tail(att, tail)
    for small in smalls:
        small.start()
    chains = [small.stages() for small in smalls]
    for stage in range(6):
        for chain in chains:
            next(chain)
    reduce.finish(grad_o)
    for small in smalls:
        small.finish()


def run_backward(
    kept, patches, upstream, items, qkv_w, proj_w, gains, table, gmid, glog, mixed, probs, att, mid, nm, slot
):
    packs, length, width = patches.shape
    _, line, rows, _ = kept.shape
    dp, ex = lax.axis_size("dp"), lax.axis_size("expert")
    few = tail_rows(width, ex * dp)
    dma = pltpu.SemaphoreType.DMA
    here = pl.BlockSpec(memory_space=pltpu.VMEM)
    away = pl.BlockSpec(memory_space=pl.ANY)
    shapes = (
        ((packs, length, width), F32),
        ((rows, width), F32),
        ((ex // line, dp, line, few, width), BF16),
    )
    scratch = (
        ((width, 3 * width), BF16),
        ((width, width), BF16),
        ((2,) + mixed.shape[1:], BF16),
        ((2,) + probs.shape[1:], BF16),
        (att.shape, BF16),
        ((2,) + mid.shape[1:], F32),
        ((2,) + nm.shape[1:], BF16),
        ((2, length, width), BF16),
        ((2, length, width), BF16),
        ((2, length, width), F32),
        ((packs * length, width), BF16),
        ((packs * length, width), BF16),
        ((length, width), BF16),
        ((packs * length, 3 * width), BF16),
        ((length, 3 * width), F32),
        ((16, width), F32),
        ((ex // line, dp, line, few, width), BF16),
        ((few, width), BF16),
        *([((line, rows, width), BF16)] * 5),
        ((4, line, few, width), BF16),
        ((4, line, few, width), BF16),
        ((3, line, few, width), BF16),
        ((line, few, width), BF16),
    )
    small_sems = [dma((n,)) for n in (4, 4, 3, 3, line, line, line, line, 3, 3, 4, 4) * 2]
    return pl.pallas_call(
        functools.partial(backward_kernel, line),
        out_shape=tuple(jax.ShapeDtypeStruct(*s) for s in shapes),
        in_specs=[away] * 3 + [here] * 5 + [away, here] + [away] * 5,
        out_specs=(here, here, here),
        scratch_shapes=[pltpu.VMEM(*s) for s in scratch]
        + [dma((8, packs)), dma((2, line))] + [dma((line,))] * 6 + small_sems,
        compiler_params=pltpu.CompilerParams(
            collective_id=slot, has_side_effects=True, vmem_limit_bytes=VMEM_BYTES
        ),
        name="backward",
    )(kept, patches, upstream, items, qkv_w, proj_w, gains, table, gmid, glog, mixed, probs, att, mid, nm)


def update_kernel(
    tail, inner_g, down_g,
    qkv_w, qkv_f, qkv_s, proj_w, proj_f, proj_s, router_w, router_f, router_s,
    gains_w, gains_f, gains_s, inner_w, inner_f, inner_s, down_w, down_f, down_s,
    qkv_wo, qkv_fo, qkv_so, proj_wo, proj_fo, proj_so, router_wo, router_fo, router_so,
    gains_wo, gains_fo, gains_so, inner_wo, inner_fo, inner_so, down_wo, down_fo, down_so,
):
    step = pl.program_id(0)
    ex, dp, few, width = tail.shape
    rows = few - 16
    experts = router_w.shape[0]
    attn = tail[:, :, :rows, :].reshape(ex * dp * rows, width).astype(F32)

    def write(outs, values):
        for out, value in zip(outs, values):
            out[...] = value

    def qkv():
        write((qkv_wo, qkv_fo, qkv_so), adamw(qkv_w[...], qkv_f[...], qkv_s[...], attn, 0.1, 0.1))

    def proj():
        write((proj_wo, proj_fo, proj_so), adamw(proj_w[...], proj_f[...], proj_s[...], attn, 0.4, 0.1))

    def rest():
        small = tail[0, 0, rows:, :].astype(F32)
        router_g = small[:experts]
        gains_g = small[experts : experts + 2]
        write(
            (router_wo, router_fo, router_so),
            adamw(router_w[...], router_f[...], router_s[...], router_g, 0.07, 0.1),
        )
        write(
            (gains_wo, gains_fo, gains_so),
            adamw(gains_w[...], gains_f[...], gains_s[...], gains_g, 0.4, 0.0),
        )

    pl.when(step < 3)(qkv)
    pl.when(step == 3)(proj)
    pl.when(step == 0)(rest)
    write(
        (inner_wo, inner_fo, inner_so),
        adamw(inner_w[...], inner_f[...], inner_s[...], inner_g[...], 0.1, 0.1),
    )
    write((down_wo, down_fo, down_so), adamw(down_w[...], down_f[...], down_s[...], down_g[...], 0.15, 0.1))


def run_update(tail, grad, weights):
    ex, dp, few, width = tail.shape
    qkv, router, inner, down = weights[0], weights[6], weights[12], weights[15]
    deep, span = inner.shape[0], down.shape[0] // 4
    of_qkv = pl.BlockSpec((width, width), lambda j: (0, jnp.minimum(j, 2)))
    of_proj = pl.BlockSpec((width, width), lambda j: (0, 0))
    of_router = pl.BlockSpec(router.shape, lambda j: (0, 0))
    of_gains = pl.BlockSpec((2, width), lambda j: (0, 0))
    of_inner = pl.BlockSpec((deep, width), lambda j: (0, j))
    of_down = pl.BlockSpec((span, width), lambda j: (j, 0))
    specs = []
    for spec in (of_qkv, of_proj, of_router, of_gains, of_inner, of_down):
        specs += [spec] * 3
    first_down = 4 * deep // span
    return pl.pallas_call(
        update_kernel,
        out_shape=tuple(jax.ShapeDtypeStruct(w.shape, F32) for w in weights),
        grid=(4,),
        in_specs=[
            pl.BlockSpec((ex // 4, dp, few, width), lambda j: (j, 0, 0, 0)),
            pl.BlockSpec((deep, width), lambda j: (j, 0)),
            pl.BlockSpec((span, width), lambda j: (first_down + j, 0)),
        ] + specs,
        out_specs=tuple(specs),
        compiler_params=pltpu.CompilerParams(vmem_limit_bytes=VMEM_BYTES),
        name="update",
    )(tail, grad, grad, *weights)


def fast(
    patches, out_grad, item_ids, expert_ids,
    qkv_master, qkv_first, qkv_second,
    proj_master, proj_first, proj_second,
    router_master, router_first, router_second,
    gains_master, gains_first, gains_second,
    inner_master, inner_first, inner_second,
    down_master, down_first, down_second,
):
    width = patches.shape[2]
    experts = router_master.shape[1]
    hidden = down_master.shape[1] * lax.axis_size("dp")
    deep = inner_master.shape[1]
    blocks = inner_master.shape[2] // width
    shard = jnp.concatenate(
        [
            jnp.swapaxes(inner_master[0].reshape(deep, blocks, width), 0, 1).reshape(blocks * deep, width),
            down_master[0],
        ],
        axis=0,
    ).astype(BF16)
    router_w = router_master.T.astype(BF16)
    ids = jnp.swapaxes(expert_ids, 1, 2)
    table = jnp.asarray(rope_table(QB))
    full, kept, mixed, probs, att, mid, nm, block_out, gmid, glog = run_forward(
        shard, patches, out_grad, item_ids, ids, qkv_master, proj_master, router_w, gains_master, table, hidden, 0
    )
    patch_grad, grad, tail = run_backward(
        kept, patches, out_grad, item_ids, qkv_master, proj_master, gains_master, table,
        gmid, glog, mixed, probs, att, mid, nm, 1,
    )
    weights = (
        qkv_master, qkv_first, qkv_second,
        proj_master, proj_first, proj_second,
        router_master.T, router_first.T, router_second.T,
        gains_master, gains_first, gains_second,
        inner_master[0], inner_first[0], inner_second[0],
        down_master[0], down_first[0], down_second[0],
    )
    tail = tail.reshape(-1, lax.axis_size("dp"), *tail.shape[3:])
    new = run_update(tail, grad, weights)
    return (
        block_out, patch_grad, *new[:6], *(value.T for value in new[6:9]), *new[9:12],
        *(value[None] for value in new[12:]),
    )


GATHER_LIMIT = 16 * 1024 * 1024


def step(*args):
    inner_master, down_master = args[16], args[19]
    experts = inner_master.shape[0] * lax.axis_size("expert")
    entries = inner_master.shape[1] * inner_master.shape[2] + down_master.shape[1] * down_master.shape[2]
    weight_bytes = 2 * experts * entries * lax.axis_size("dp")
    square = lax.axis_size("dp") == 4 and lax.axis_size("expert") == 8 and inner_master.shape[0] == 1 and lax.axis_size("expert") == experts
    return (fast if square and weight_bytes <= GATHER_LIMIT else local)(*args)


def solution(mesh):
    in_specs = (
        P(None, ("dp", "expert"), None),
        P(None, ("dp", "expert"), None),
        P(None, ("dp", "expert"), None),
        P(None, ("dp", "expert"), None),
        P(),
        P(),
        P(),
        P(),
        P(),
        P(),
        P(),
        P(),
        P(),
        P(),
        P(),
        P(),
        P("expert", "dp", None),
        P("expert", "dp", None),
        P("expert", "dp", None),
        P("expert", "dp", None),
        P("expert", "dp", None),
        P("expert", "dp", None),
    )
    out_specs = (
        P(None, ("dp", "expert"), None),
        P(None, ("dp", "expert"), None),
        P(),
        P(),
        P(),
        P(),
        P(),
        P(),
        P(),
        P(),
        P(),
        P(),
        P(),
        P(),
        P("expert", "dp", None),
        P("expert", "dp", None),
        P("expert", "dp", None),
        P("expert", "dp", None),
        P("expert", "dp", None),
        P("expert", "dp", None),
    )
    return jax.shard_map(step, mesh=mesh, in_specs=in_specs, out_specs=out_specs, check_vma=False)
```
